32 devices in a mesh: head: 4 (over x, core), blk: 8 (over z, y).
Axes of the slice: x: 2, y: 2, z: 4, core: 2. Of those that a mesh axis runs over, the one named last changes fastest.
Arguments:
- tokens: bfloat16 [16384, 768], P(('blk', 'head')), may hold values from -6 to 6
- first_values: bfloat16 [16384, 384], P(('blk', 'head')), may hold values from -6 to 6
- cotangent: bfloat16 [16384, 768], P(('blk', 'head')), may hold values from -6 to 6
- w_query: bfloat16 [768, 768], P('blk', 'head'), may hold values from -0.21875 to 0.21875
- w_key: bfloat16 [768, 768], P('blk', 'head'), may hold values from -0.21875 to 0.21875
- w_value: bfloat16 [768, 384], P('blk', 'head'), may hold values from -0.21875 to 0.21875
- w_out: bfloat16 [768, 768], P('head', 'blk'), may hold values from -3.5 to 3.5
- w_up: bfloat16 [768, 3072], P('blk', 'head'), may hold values from -0.21875 to 0.21875
- w_down: bfloat16 [3072, 768], P('head', 'blk'), may hold values from -0.109375 to 0.109375
- gain_attn: float32 [768], P('blk'), may hold values from 0.5 to 1.5
- gain_mlp: float32 [768], P('blk'), may hold values from 0.5 to 1.5
- doc_lengths: int32 [16], replicated, may hold values from 1 to 4096, 16384 in all
Outputs:
- layer_output: bfloat16 [16384, 768], P(('blk', 'head'))
- grad_tokens: float32 [16384, 768], P(('blk', 'head'))
- grad_first_values: float32 [16384, 384], P(('blk', 'head'))
- grad_w_query: float32 [768, 768], P('blk', 'head')
- grad_w_key: float32 [768, 768], P('blk', 'head')
- grad_w_value: float32 [768, 384], P('blk', 'head')
- grad_w_out: float32 [768, 768], P('head', 'blk')
- grad_w_up: float32 [768, 3072], P('blk', 'head')
- grad_w_down: float32 [3072, 768], P('head', 'blk')
- grad_gain_attn: float32 [768], P('blk')
- grad_gain_mlp: float32 [768], P('blk')
The draws below stay inside these ranges and needn't reach their ends.
Inputs may be any that keep to these rules, and one draw needn't show every extreme that they name: `doc_lengths`: the lengths sum to 16384 and the longest is exactly 4096.
All inputs are finite; a program needn't handle non-finite values.
Results may differ from the reference program's by a relative error of at most 0.03.
Values may be sent and summed in bfloat16 or wider, within the bound.
A program may use at most 192 MiB of HBM per device.

```python
import math
import jax
import jax.numpy as jnp
import numpy as np
from jax import lax

D = 768
HEADS = 12
HEAD_DIM = 64
FF = 3072
DOC_MAX = 4096
TOKENS = 16384
NDOCS = 16


def shard_levels(stream_key, extent, shards, least, largest):
    level = 1.0
    for dim, blocks in shards:
        heights = jax.random.uniform(jax.random.fold_in(jax.random.fold_in(stream_key, 6), dim), (blocks,), jnp.float32, least / len(shards), largest / len(shards))
        level = level * jnp.repeat(jnp.exp(heights), extent[dim] // blocks).reshape((-1,) + (1,) * (len(extent) - 1 - dim))
    return level


def length_profile(number_of, total, bound, lean):
    portions = [(1 << 20) // math.isqrt(rank ** lean) + 1 for rank in range(2, number_of + 1)]
    spare, holding = total - bound - (number_of - 1), [1] * (number_of - 1)
    while spare > 0:
        free = [i for i in range(number_of - 1) if holding[i] < bound]
        mass, remaining = sum([portions[i] for i in free]), spare
        for i in free:
            more = min(bound - holding[i], max(1, remaining * portions[i] // mass), spare)
            holding[i] = holding[i] + more
            spare = spare - more
    return np.array([bound] + holding)


def uneven_parts(key, number_of, total, limit, lean):
    if number_of == 2:
        one = jax.random.randint(key, (), max(1, total - limit), min(limit, total - 1) + 1)
        return jnp.stack([one, total - one])
    sizes = jnp.asarray(length_profile(number_of, total, limit, lean), jnp.int32)
    couples = (number_of - 1) // 2
    giver, sink = sizes[1:1 + 2 * couples:2], sizes[2:2 + 2 * couples:2]
    slack = jnp.minimum(giver - 1, limit - sink)
    moved = jax.random.randint(jax.random.fold_in(key, 1), (couples,), 0, 1 << 20) % (slack + 1)
    sizes = sizes.at[1:1 + 2 * couples:2].set(giver - moved).at[2:2 + 2 * couples:2].set(sink + moved)
    return sizes[jax.random.permutation(jax.random.fold_in(key, 2), number_of)]


def centred(stream_key, dims, width, limit, split=(), held_as=jnp.bfloat16):
    entries = jax.random.normal(stream_key, dims, jnp.float32) * width
    if len(split) > 0:
        entries = shard_levels(stream_key, dims, split, -0.22, 0.18) * entries
    return jnp.clip(entries, min=-limit, max=limit).astype(held_as)


def setup_inputs(seed: int = 0) -> dict:
    key_of = jax.random.split(jax.random.key(seed), 13)
    tokens = centred(key_of[0], (TOKENS, D), 1.0, 6.0, ((0, 32),))
    first_values = centred(key_of[1], (TOKENS, D // 2), 1.0, 6.0, ((0, 32),))
    cotangent = centred(key_of[2], (TOKENS, D), 1.0, 6.0, ((0, 32),))
    w_query = centred(key_of[3], (D, D), D ** -0.5, 0.21875, ((0, 8), (1, 4)))
    w_key = centred(key_of[4], (D, D), D ** -0.5, 0.21875, ((0, 8), (1, 4)))
    w_value = centred(key_of[5], (D, D // 2), D ** -0.5, 0.21875, ((0, 8), (1, 4)))
    w_out = centred(key_of[6], (D, D), 3 ** -0.5, 3.5, ((0, 4), (1, 8)))
    w_up = centred(key_of[7], (D, FF), D ** -0.5, 0.21875, ((0, 8), (1, 4)))
    w_down = centred(key_of[8], (FF, D), FF ** -0.5, 0.109375, ((0, 4), (1, 8)))
    gain_attn = jnp.clip(1.0 + 0.1 * jax.random.normal(key_of[9], (D,), jnp.float32), 0.5, 1.5)
    gain_mlp = jnp.clip(1.0 + 0.1 * jax.random.normal(key_of[10], (D,), jnp.float32), 0.5, 1.5)
    doc_lengths = uneven_parts(key_of[11], NDOCS, TOKENS, DOC_MAX, 2).astype(jnp.int32)
    return dict(tokens=tokens, first_values=first_values, cotangent=cotangent, w_query=w_query, w_key=w_key, w_value=w_value, w_out=w_out, w_up=w_up, w_down=w_down, gain_attn=gain_attn, gain_mlp=gain_mlp, doc_lengths=doc_lengths)


@jax.custom_vjp
def low(v):
    return lax.optimization_barrier(v.astype(jnp.bfloat16)).astype(jnp.float32)

@jax.custom_vjp
def low_back(v):
    return v

def low_keep(v):
    return (low(v), None)

def low_pass(kept, grad):
    return (grad,)

def back_keep(v):
    return (v, None)

def back_low(kept, grad):
    return (low(grad),)
low.defvjp(low_keep, low_pass)
low_back.defvjp(back_keep, back_low)
EPSILON = 1e-05
GELU_SCALE = 0.7978845608028654
EXCLUDED = -1e+30
HIGH = lax.Precision.HIGHEST

def layer_norm(values, norm_gain):
    center = values - lax.optimization_barrier(jnp.mean(values, axis=-1, keepdims=True))
    variance = lax.optimization_barrier(jnp.mean(jnp.square(center), axis=-1, keepdims=True))
    return center * lax.rsqrt(variance + EPSILON) * norm_gain

def gelu_tanh(values):
    return 0.5 * values * (1.0 + jnp.tanh(GELU_SCALE * (values + 0.044715 * values * values * values)))

def matmul(left_mat, right_mat):
    return jnp.dot(left_mat, right_mat, precision=HIGH, preferred_element_type=jnp.float32)

def segment_ids(doc_lengths):
    doc_ends = jnp.cumsum(doc_lengths).astype(jnp.int32)
    doc_starts = (doc_ends - doc_lengths).astype(jnp.int32)
    positions = jnp.arange(TOKENS, dtype=jnp.int32)
    counts = lax.optimization_barrier(jnp.sum((doc_starts[None, :] <= positions[:, None]).astype(jnp.int32), axis=1))
    return (counts - 1).astype(jnp.int32)

def attention(queries, keys_all, values, segments):
    block_rows = min(512, TOKENS)
    score_scale = HEAD_DIM ** (-0.5)
    key_pad = jnp.concatenate([jnp.zeros((DOC_MAX, HEADS, HEAD_DIM), jnp.float32), keys_all], axis=0)
    value_pad = jnp.concatenate([jnp.zeros((DOC_MAX, HEADS, HEAD_DIM), jnp.float32), values], axis=0)
    segment_pad = jnp.concatenate([jnp.full((DOC_MAX,), -1, jnp.int32), segments]).astype(jnp.int32)

    def one_block(row_start):
        query_blk = lax.dynamic_slice_in_dim(queries, row_start, block_rows, 0)
        key_win = lax.dynamic_slice_in_dim(key_pad, row_start, block_rows + DOC_MAX, 0)
        value_win = lax.dynamic_slice_in_dim(value_pad, row_start, block_rows + DOC_MAX, 0)
        query_seg = lax.dynamic_slice_in_dim(segments, row_start, block_rows, 0)
        key_seg = lax.dynamic_slice_in_dim(segment_pad, row_start, block_rows + DOC_MAX, 0)
        query_pos = row_start + jnp.arange(block_rows, dtype=jnp.int32)
        key_pos = row_start - DOC_MAX + jnp.arange(block_rows + DOC_MAX, dtype=jnp.int32)
        visible_mask = (key_seg[None, :] == query_seg[:, None]) & (key_pos[None, :] <= query_pos[:, None])
        scores = jnp.einsum('qhd,khd->hqk', query_blk, key_win, precision=HIGH) * score_scale
        scores = low_back(scores)
        scores = jnp.where(visible_mask[None], scores, EXCLUDED)
        soft_weights = jax.nn.softmax(scores, axis=-1)
        return jnp.einsum('hqk,khd->qhd', low(soft_weights), value_win, precision=HIGH)
    block_starts = (jnp.arange(TOKENS // block_rows, dtype=jnp.int32) * block_rows).astype(jnp.int32)
    blocks_out = lax.map(jax.checkpoint(one_block), block_starts)
    return blocks_out.reshape(TOKENS, HEADS * HEAD_DIM)

def forward(tokens_f, first_f, query_w, key_w, value_w, out_w, up_w, down_w, attn_g, mlp_g, segments):
    normed = low(layer_norm(tokens_f, attn_g))
    queries = low(low_back(matmul(normed, query_w)))
    keys_all = low(low_back(matmul(normed, key_w)))
    fresh = low(low_back(matmul(normed, value_w)))
    values = jnp.concatenate([fresh, low_back(first_f)], axis=1)
    head_shape = (TOKENS, HEADS, HEAD_DIM)
    mixed = attention(queries.reshape(head_shape), keys_all.reshape(head_shape), values.reshape(head_shape), segments)
    mixed = low(low_back(mixed))
    branch = low_back(matmul(mixed, out_w))
    resid = tokens_f + branch
    normed2 = low(layer_norm(resid, mlp_g))
    hidden_pre = low_back(matmul(normed2, up_w))
    hidden = low(gelu_tanh(hidden_pre))
    return resid + matmul(hidden, down_w)

def reference(tokens, first_values, cotangent, w_query, w_key, w_value, w_out, w_up, w_down, gain_attn, gain_mlp, doc_lengths):
    segments = segment_ids(doc_lengths)

    def closed(tokens_f, first_f, query_w, key_w, value_w, out_w, up_w, down_w, attn_g, mlp_g):
        return forward(tokens_f, first_f, query_w, key_w, value_w, out_w, up_w, down_w, attn_g, mlp_g, segments)
    primals = (tokens.astype(jnp.float32), first_values.astype(jnp.float32), w_query.astype(jnp.float32), w_key.astype(jnp.float32), w_value.astype(jnp.float32), w_out.astype(jnp.float32), w_up.astype(jnp.float32), w_down.astype(jnp.float32), gain_attn.astype(jnp.float32), gain_mlp.astype(jnp.float32))
    layer_out, pullback = jax.vjp(closed, *primals)
    gradients = pullback(cotangent.astype(jnp.float32))
    return (layer_out.astype(jnp.bfloat16), gradients[0], gradients[1], gradients[2], gradients[3], gradients[4], gradients[5], gradients[6], gradients[7], gradients[8], gradients[9])
```

```python
import functools

import jax
import jax.numpy as jnp
from jax import lax
from jax.experimental import pallas as pl
from jax.experimental.pallas import tpu as pltpu
from jax.sharding import PartitionSpec as P

HEADS = 12
HEAD_DIM = 64
DOC_MAX = 4096
EPSILON = 1e-05
GELU_SCALE = 0.7978845608028654
EXCLUDED = -1e30
WIDTH = 256
SPLITS = 3
BF16 = jnp.bfloat16
F32 = jnp.float32
MESH = pl.DeviceIdType.MESH
ANY = pl.BlockSpec(memory_space=pl.ANY)
WHOLE = pl.BlockSpec(memory_space=pltpu.VMEM)
NT = (((1,), (1,)), ((), ()))
TN = (((0,), (0,)), ((), ()))


def dotf(left, right, dims=None):
    if dims is None:
        dims = (((1,), (0,)), ((), ()))
    return lax.dot_general(left, right, dims, preferred_element_type=F32)


def remote(src, dst, send_sem, recv_sem, head, blk):
    return pltpu.make_async_remote_copy(
        src_ref=src,
        dst_ref=dst,
        send_sem=send_sem,
        recv_sem=recv_sem,
        device_id={"head": head, "blk": blk},
        device_id_type=MESH,
    )


def greet(partners):
    barrier = pltpu.get_barrier_semaphore()
    for head, blk in partners:
        pl.semaphore_signal(
            barrier, inc=1, device_id={"head": head, "blk": blk}, device_id_type=MESH
        )
    pl.semaphore_wait(barrier, len(partners))


def xor(value, bit):
    return value + bit - 2 * bit * (lax.div(value, bit) % 2)


def partners_of(head, blk, nblk, heads=True, blks=True):
    found = []
    if heads:
        found += [(xor(head, 1), blk), (xor(head, 2), blk), (3 - head, blk)]
    if blks:
        found += [(head, lax.rem(blk + d, nblk)) for d in range(1, nblk)]
    return found


def front_kernel(
    nblk, pieces, tok, first, w_q, w_k, w_v, gains,
    tok_all, first_all, q_all, k_all, v_own, v_all, gain_all,
    own_sem, send_x, recv_x, send_s, recv_s, send_f, recv_f, send_w, recv_w, send_v, recv_v,
):
    head, blk = lax.axis_index("head"), lax.axis_index("blk")
    side, core, far = xor(head, 2), xor(head, 1), 3 - head
    greet(partners_of(head, blk, nblk))
    moved = [(tok, tok_all), (first, first_all)]
    weights = [(w_q, q_all), (w_k, k_all), (w_v, v_own), (gains, gain_all)]
    rows = tok.shape[0] // pieces

    def part(ref, p):
        return ref.at[pl.ds(p * rows, rows)]

    def hop(sems, k, p, source, slot, target):
        dst = part(moved[k][1].at[slot], p)
        return remote(source, dst, sems[0].at[k, p], sems[1].at[k, p], target, blk)

    xs, ss, fs = (send_x, recv_x), (send_s, recv_s), (send_f, recv_f)
    order = [(k, p) for p in range(pieces) for k in range(2)]
    for k, p in order:
        hop(xs, k, p, part(moved[k][0], p), head, side).start()

    def spread(d):
        to = lax.rem(blk + d, nblk)
        return [
            remote(src, dst.at[blk], send_w.at[i, d], recv_w.at[i, d], head, to)
            for i, (src, dst) in enumerate(weights)
        ]

    def from_peer(d):
        source = lax.rem(blk - d + nblk, nblk)
        return [
            remote(src, dst.at[source], send_w.at[i, d], recv_w.at[i, d], head, source)
            for i, (src, dst) in enumerate(weights)
        ]

    for d in range(1, nblk):
        for copy in spread(d):
            copy.start()
    for k, p in order:
        hop(ss, k, p, part(moved[k][0], p), head, core).start()
    local = [
        pltpu.make_async_copy(moved[k][0], moved[k][1].at[head], own_sem.at[k]) for k in range(2)
    ] + [
        pltpu.make_async_copy(src, dst.at[blk], own_sem.at[2 + i])
        for i, (src, dst) in enumerate(weights)
    ]
    for copy in local:
        copy.start()
    for k, p in order:
        landed = part(moved[k][1].at[side], p)
        hop(xs, k, p, landed, side, side).wait_recv()
        hop(fs, k, p, landed, side, core).start()
    for copy in local:
        copy.wait()
    for d in range(1, nblk):
        for copy in from_peer(d):
            copy.wait_recv()
    half, kind = lax.div(head, 2), lax.rem(head, 2)
    for i in range(2):
        target = half + 2 * i

        @pl.when(target == head)
        def _():
            pltpu.make_async_copy(v_own, v_all.at[kind], own_sem.at[6]).start()

        @pl.when(target != head)
        def _():
            remote(v_own, v_all.at[kind], send_v.at[i], recv_v.at[kind], target, blk).start()

    for k, p in order:
        hop(ss, k, p, part(moved[k][1].at[core], p), core, core).wait_recv()
        hop(fs, k, p, part(moved[k][1].at[far], p), far, core).wait_recv()
    for c in range(2):
        source = 2 * kind + c

        @pl.when(source == head)
        def _():
            pltpu.make_async_copy(v_own, v_all.at[c], own_sem.at[6]).wait()

        @pl.when(source != head)
        def _():
            remote(v_own, v_all.at[c], send_v.at[0], recv_v.at[c], source, blk).wait_recv()

    for i in range(2):
        target = half + 2 * i

        @pl.when(target != head)
        def _():
            remote(v_own, v_all.at[kind], send_v.at[i], recv_v.at[kind], target, blk).wait_send()

    for k, p in order:
        hop(xs, k, p, part(moved[k][0], p), head, side).wait_send()
        hop(ss, k, p, part(moved[k][0], p), head, core).wait_send()
        hop(fs, k, p, part(moved[k][1].at[side], p), side, core).wait_send()
    for d in range(1, nblk):
        for copy in spread(d):
            copy.wait_send()


def front(nblk, tok, first, w_q, w_k, w_v, gains, pieces=4):
    def shape(lead, like):
        return jax.ShapeDtypeStruct(lead + like.shape, like.dtype)

    dma = pltpu.SemaphoreType.DMA
    return pl.pallas_call(
        functools.partial(front_kernel, nblk, pieces),
        out_shape=[
            shape((4,), tok),
            shape((4,), first),
            shape((nblk,), w_q),
            shape((nblk,), w_k),
            shape((nblk,), w_v),
            shape((2, nblk), w_v),
            shape((nblk,), gains),
        ],
        in_specs=[ANY] * 6,
        out_specs=[ANY] * 7,
        scratch_shapes=[dma((7,))]
        + [dma((2, pieces))] * 6
        + [dma((4, nblk))] * 2
        + [dma((2,))] * 2,
        compiler_params=pltpu.CompilerParams(collective_id=0, has_side_effects=True),
        name="front",
    )(tok, first, w_q, w_k, w_v, gains)


def halo_kernel(nblk, pieces, own, near_far, send_z, recv_z, send_y, recv_y):
    head, blk = lax.axis_index("head"), lax.axis_index("blk")
    odd = lax.rem(blk, 2)
    pair = blk + 1 - 2 * odd
    up, down = lax.rem(blk + 2, nblk), lax.rem(blk + nblk - 2, nblk)
    barrier = pltpu.get_barrier_semaphore()
    for to in (pair, up, down):
        pl.semaphore_signal(
            barrier, inc=1, device_id={"head": head, "blk": to}, device_id_type=MESH
        )
    pl.semaphore_wait(barrier, 3)
    rows = own.shape[0] // pieces

    def part(ref, p):
        return ref.at[pl.ds(p * rows, rows)]

    def far_copy(p, to):
        return remote(part(own, p), part(near_far.at[0], p), send_z.at[p], recv_z.at[p], head, to)

    def near_copy(p, src):
        return remote(src, part(near_far.at[1], p), send_y.at[p], recv_y.at[p], head, pair)

    for p in range(pieces):

        @pl.when(blk + 2 < nblk)
        def _():
            far_copy(p, up).start()

        @pl.when(odd == 0)
        def _():
            near_copy(p, part(own, p)).start()

    for p in range(pieces):

        @pl.when(blk >= 2)
        def _():
            far_copy(p, down).wait_recv()

        @pl.when((blk >= 2) & (odd == 1))
        def _():
            near_copy(p, part(near_far.at[0], p)).start()

    for p in range(pieces):

        @pl.when((blk >= 2) | (odd == 1))
        def _():
            near_copy(p, part(own, p)).wait_recv()

        @pl.when(blk + 2 < nblk)
        def _():
            far_copy(p, up).wait_send()

        @pl.when((blk >= 2) | (odd == 0))
        def _():
            near_copy(p, part(own, p)).wait_send()


def halo(nblk, own, pieces=8):
    dma = pltpu.SemaphoreType.DMA
    return pl.pallas_call(
        functools.partial(halo_kernel, nblk, pieces),
        out_shape=jax.ShapeDtypeStruct((2,) + own.shape, own.dtype),
        in_specs=[ANY],
        out_specs=ANY,
        scratch_shapes=[dma((pieces,))] * 4,
        compiler_params=pltpu.CompilerParams(collective_id=1, has_side_effects=True),
        name="halo",
    )(own)


def swap_kernel(nblk, parts, out, own_sem, send_sem, recv_sem):
    head, blk = lax.axis_index("head"), lax.axis_index("blk")
    others = [xor(head, 2), 3 - head, xor(head, 1)]
    greet(partners_of(head, blk, nblk, blks=False))
    copies = [
        remote(parts.at[to], out.at[head], send_sem.at[i], recv_sem.at[i], to, blk)
        for i, to in enumerate(others)
    ]
    for copy in copies:
        copy.start()
    local = pltpu.make_async_copy(parts.at[head], out.at[head], own_sem)
    local.start()
    local.wait()
    for i, to in enumerate(others):
        remote(parts.at[to], out.at[to], send_sem.at[i], recv_sem.at[i], to, blk).wait_recv()
    for copy in copies:
        copy.wait_send()


def swap(nblk, parts, collective_id):
    dma = pltpu.SemaphoreType.DMA
    return pl.pallas_call(
        functools.partial(swap_kernel, nblk),
        out_shape=jax.ShapeDtypeStruct(parts.shape, parts.dtype),
        in_specs=[ANY],
        out_specs=ANY,
        scratch_shapes=[dma, dma((3,)), dma((3,))],
        compiler_params=pltpu.CompilerParams(
            collective_id=collective_id, has_side_effects=True
        ),
        name="swap%d" % collective_id,
    )(parts)


def tail_kernel(
    nblk, pieces, grad, d_q, d_k, d_v, first, gains,
    out_grad, out_q, out_k, out_v, out_first, out_gain,
    core_buf, side_out, side_buf, q_buf, k_buf, v_buf, v_sum, v_got, gain_buf, gain_sum, gain_got,
    own_sem, send_s, recv_s, send_x, recv_x, send_w, recv_w, send_v, recv_v, send_f, recv_f,
    send_g, recv_g,
):
    head, blk = lax.axis_index("head"), lax.axis_index("blk")
    side, core, far = xor(head, 2), xor(head, 1), 3 - head
    greet(partners_of(head, blk, nblk))
    rows = grad.shape[1] // pieces

    def part(ref, p):
        return ref.at[pl.ds(p * rows, rows)]

    def to_core(i, p, slot):
        return remote(
            part(grad.at[slot], p), part(core_buf.at[i], p), send_s.at[i, p], recv_s.at[i, p],
            core, blk,
        )

    def to_side(p):
        return remote(
            part(side_out, p), part(side_buf, p), send_x.at[p], recv_x.at[p], side, blk
        )

    for p in range(pieces):
        to_core(0, p, far).start()
    for p in range(pieces):
        to_core(1, p, core).start()
    half, kind = lax.div(head, 2), lax.rem(head, 2)
    weights = [(d_q, q_buf), (d_k, k_buf), (d_v.at[0], v_buf.at[0]), (d_v.at[1], v_buf.at[1]),
               (gains, gain_buf)]

    def spread(d):
        to = lax.rem(blk + d, nblk)
        return [
            remote(src.at[to], dst.at[blk], send_w.at[i, d], recv_w.at[i, d], head, to)
            for i, (src, dst) in enumerate(weights)
        ]

    def from_peer(d):
        source = lax.rem(blk - d + nblk, nblk)
        return [
            remote(src.at[source], dst.at[source], send_w.at[i, d], recv_w.at[i, d], head, source)
            for i, (src, dst) in enumerate(weights)
        ]

    for d in range(1, nblk):
        for copy in spread(d):
            copy.start()
    local = [
        pltpu.make_async_copy(src.at[blk], dst.at[blk], own_sem.at[i])
        for i, (src, dst) in enumerate(weights)
    ]
    for copy in local:
        copy.start()

    def first_copy(i, to, slot):
        return remote(first.at[to], out_first.at[slot], send_f.at[i], recv_f.at[slot], to, blk)

    @pl.when(half == 1)
    def _():
        for i, to in enumerate((core, side, far)):
            first_copy(i, to, kind).start()
        pltpu.make_async_copy(first.at[head], out_first.at[kind], own_sem.at[5]).start()

    for p in range(pieces):
        to_core(0, p, far).wait_recv()
        part(side_out, p)[...] = (
            part(grad.at[side], p)[...].astype(F32) + part(core_buf.at[0], p)[...].astype(F32)
        ).astype(BF16)
        to_side(p).start()
    for copy in local:
        copy.wait()
    for d in range(1, nblk):
        for copy in from_peer(d):
            copy.wait_recv()
    out_q[...] = jnp.sum(q_buf[...].astype(F32), axis=0)
    out_k[...] = jnp.sum(k_buf[...].astype(F32), axis=0)
    v_sum[...] = jnp.sum(v_buf[...].astype(F32), axis=1)
    gain_sum[...] = jnp.sum(gain_buf[...], axis=0)
    peers = (core, side, far)
    for i, to in enumerate(peers):
        remote(gain_sum, gain_got.at[i], send_g.at[i], recv_g.at[i], to, blk).start()

    def give(c, to):
        return remote(v_sum.at[c], v_got, send_v.at[c], recv_v.at[0], to, blk)

    for c in range(2):
        to = 2 * head + c

        @pl.when((half == 0) & (to != head))
        def _():
            give(c, to).start()

    for p in range(pieces):
        to_core(1, p, core).wait_recv()
        to_side(p).wait_recv()
        part(out_grad, p)[...] = (
            part(grad.at[head], p)[...].astype(F32)
            + part(core_buf.at[1], p)[...].astype(F32)
            + part(side_buf, p)[...].astype(F32)
        )
    for i, to in enumerate(peers):
        remote(gain_sum, gain_got.at[i], send_g.at[i], recv_g.at[i], to, blk).wait_recv()
    out_gain[...] = gain_sum[...] + gain_got[0] + gain_got[1] + gain_got[2]

    @pl.when(head == 0)
    def _():
        out_v[...] = v_sum[0]

    @pl.when(head != 0)
    def _():
        give(0, half).wait_recv()
        out_v[...] = v_got[...]

    for slot in range(2):

        @pl.when(head == 2 + slot)
        def _():
            pltpu.make_async_copy(first.at[head], out_first.at[slot], own_sem.at[5]).wait()

        @pl.when(head != 2 + slot)
        def _():
            first_copy(0, 2 + slot, slot).wait_recv()

    @pl.when(half == 1)
    def _():
        for i, to in enumerate((core, side, far)):
            first_copy(i, to, kind).wait_send()

    for c in range(2):
        to = 2 * head + c

        @pl.when((half == 0) & (to != head))
        def _():
            give(c, to).wait_send()

    for i, to in enumerate(peers):
        remote(gain_sum, gain_got.at[i], send_g.at[i], recv_g.at[i], to, blk).wait_send()
    for p in range(pieces):
        to_core(0, p, far).wait_send()
        to_core(1, p, core).wait_send()
        to_side(p).wait_send()
    for d in range(1, nblk):
        for copy in spread(d):
            copy.wait_send()


def tail(nblk, grad, d_q, d_k, d_v, first, gains, pieces=4):
    dma = pltpu.SemaphoreType.DMA
    row, half = grad.shape[1:], d_v.shape[2:]
    piece = (2, pieces)
    return pl.pallas_call(
        functools.partial(tail_kernel, nblk, pieces),
        out_shape=[
            jax.ShapeDtypeStruct(row, F32),
            jax.ShapeDtypeStruct(d_q.shape[1:], F32),
            jax.ShapeDtypeStruct(d_k.shape[1:], F32),
            jax.ShapeDtypeStruct(half, F32),
            jax.ShapeDtypeStruct((2,) + first.shape[1:], BF16),
            jax.ShapeDtypeStruct(gains.shape[1:], F32),
        ],
        in_specs=[WHOLE] * 6,
        out_specs=[WHOLE] * 6,
        scratch_shapes=[
            pltpu.VMEM((2,) + row, BF16),
            pltpu.VMEM(row, BF16),
            pltpu.VMEM(row, BF16),
            pltpu.VMEM(d_q.shape, BF16),
            pltpu.VMEM(d_k.shape, BF16),
            pltpu.VMEM((2, nblk) + half, BF16),
            pltpu.VMEM((2,) + half, F32),
            pltpu.VMEM(half, F32),
            pltpu.VMEM(gains.shape, F32),
            pltpu.VMEM(gains.shape[1:], F32),
            pltpu.VMEM((3,) + gains.shape[1:], F32),
            dma((6,)),
            dma(piece), dma(piece),
            dma((pieces,)), dma((pieces,)),
            dma((5, nblk)), dma((5, nblk)),
            dma((2,)), dma((1,)),
            dma((3,)), dma((2,)),
            dma((3,)), dma((3,)),
        ],
        compiler_params=pltpu.CompilerParams(
            collective_id=4, has_side_effects=True, vmem_limit_bytes=48 << 20
        ),
        name="tail",
    )(grad, d_q, d_k, d_v, first, gains)


def head_mask(rows, h, heads, width, dtype=BF16):
    lane=lax.broadcasted_iota(jnp.int32,(rows,width),1)
    real=heads*HEAD_DIM
    m=((lane>=h*HEAD_DIM)&(lane<(h+1)*HEAD_DIM))|((lane>=real+3*h)&(lane<real+3*h+3))
    return m

def doc_start(meta, ndocs, t):
    def step(j,c):
        cum,best=c
        best=jnp.where(cum<=t,cum,best)
        return cum+meta[1+j],best
    return lax.fori_loop(0,ndocs,step,(jnp.int32(0),jnp.int32(0)))[1]

def doc_end(meta, ndocs, t):
    def step(j,c):
        cum,best,found=c
        cum=cum+meta[1+j]
        take=(cum>t)&(found==0)
        return cum,jnp.where(take,cum,best),jnp.where(take,1,found)
    return lax.fori_loop(0,ndocs,step,(jnp.int32(0),jnp.int32(0),jnp.int32(0)))[1]

def starts_vec(meta, ndocs, t):
    def step(j,c):
        cum,best=c
        return cum+meta[1+j],jnp.where(cum<=t,cum,best)
    return lax.fori_loop(0,ndocs,step,(jnp.int32(0),jnp.zeros(t.shape,jnp.int32)))[1]

def ends_vec(meta, ndocs, t):
    def step(j,c):
        cum,best=c
        ln=meta[1+j]
        return cum+ln,jnp.where(cum<=t,cum+ln,best)
    return lax.fori_loop(0,ndocs,step,(jnp.int32(0),jnp.zeros(t.shape,jnp.int32)))[1]

def three(lo,a,b,hi,body):
    lax.fori_loop(lo,a,lambda j,_: body(j,True),None)
    lax.fori_loop(a,b,lambda j,_: body(j,False),None)
    lax.fori_loop(b,hi,lambda j,_: body(j,True),None)

def fwd_kernel(heads,ndocs,tq,tk,reach, meta, q_ref,k_ref,v_ref,mix_ref,o32_ref,qaug_ref, qh, m_ref, acc_ref):
    i=pl.program_id(0)
    width=q_ref.shape[1]; real=heads*HEAD_DIM
    base=meta[0]; wbase=base-reach
    t0=base+i*tq
    lo=(doc_start(meta,ndocs,t0)-wbase)//tk
    f0=(doc_start(meta,ndocs,t0+tq-1)-wbase+tk-1)//tk
    f1=(t0-wbase)//tk
    hi=(t0+tq-1-wbase)//tk+1
    f0=jnp.minimum(f0,f1)
    q=q_ref[...]
    for h in range(heads):
        qh[h]=jnp.where(head_mask(tq,h,heads,width),q,jnp.zeros_like(q))
        m_ref[h]=jnp.full((tq,128),EXCLUDED,F32)
    acc_ref[...]=jnp.zeros_like(acc_ref)
    trow=t0+lax.broadcasted_iota(jnp.int32,(tq,128),0)
    srow=starts_vec(meta,ndocs,trow)
    lane=lax.broadcasted_iota(jnp.int32,(tq,width),1)
    def body(j,masked):
        off=pl.multiple_of(j*tk,tk)
        k=k_ref[pl.ds(off,tk),:]; v=v_ref[pl.ds(off,tk),:]
        if masked:
            u=wbase+off+lax.broadcasted_iota(jnp.int32,(tq,tk),1)
            vis=(u>=srow[:,:1])&(u<=trow[:,:1])
        pv=None; scale=None
        for h in range(heads):
            s=dotf(qh[h],k,NT)
            if masked: s=jnp.where(vis,s,EXCLUDED)
            mp=m_ref[h][:,:1]
            mn=jnp.maximum(mp,jnp.max(s,axis=1,keepdims=True))
            al=jnp.exp(mp-mn)
            p=jnp.exp(s-mn).astype(BF16)
            m_ref[h]=jnp.broadcast_to(mn,(tq,128))
            vh=jnp.where(head_mask(tk,h,heads,width),v,jnp.zeros_like(v))
            d=dotf(p,vh)
            pv=d if pv is None else pv+d
            scale=jnp.broadcast_to(al,(tq,width)) if scale is None else jnp.where(head_mask(tq,h,heads,width),al,scale)
        acc_ref[...]=acc_ref[...]*scale+pv
    three(lo,f0,f1,hi,body)
    acc=acc_ref[...]
    out=jnp.zeros((tq,width),F32); aug=q.astype(F32)
    for h in range(heads):
        l=acc[:,real+3*h:real+3*h+1]
        out=jnp.where(head_mask(tq,h,heads,width),acc/l,out)
        neg=-(m_ref[h][:,:1]+jnp.log(l))
        c0=neg.astype(BF16).astype(F32)
        c1=(neg-c0).astype(BF16).astype(F32)
        c2=neg-c0-c1
        aug=jnp.where(lane==real+3*h,c0,jnp.where(lane==real+3*h+1,c1,jnp.where(lane==real+3*h+2,c2,aug)))
    mix_ref[...]=out[:,:real].astype(BF16)
    o32_ref[...]=out
    qaug_ref[...]=aug.astype(BF16)

def attention_fwd(meta,q,k,v,heads,tq=256,tk=512):
    B,width=q.shape; W=k.shape[0]; ndocs=meta.shape[0]-1
    full=lambda: pl.BlockSpec((W,width),lambda i:(0,0),pipeline_mode=pl.Buffered(1))
    row=lambda w: pl.BlockSpec((tq,w),lambda i:(i,0))
    return pl.pallas_call(functools.partial(fwd_kernel,heads,ndocs,tq,tk,W-B),
        grid=(B//tq,),
        in_specs=[pl.BlockSpec(memory_space=pltpu.SMEM),row(width),full(),full()],
        out_specs=[row(heads*HEAD_DIM),row(width),row(width)],
        out_shape=[jax.ShapeDtypeStruct((B,heads*HEAD_DIM),BF16),jax.ShapeDtypeStruct((B,width),F32),jax.ShapeDtypeStruct((B,width),BF16)],
        scratch_shapes=[pltpu.VMEM((heads,tq,width),BF16),pltpu.VMEM((heads,tq,128),F32),pltpu.VMEM((tq,width),F32)],
        compiler_params=pltpu.CompilerParams(vmem_limit_bytes=56<<20),
        cost_estimate=pl.CostEstimate(flops=30_000_000_000,bytes_accessed=12<<20,transcendentals=20_000_000),
        name="attn_fwd")(meta,q,k,v)

def dq_kernel(heads,ndocs,tq,tk,reach, meta, q_ref,do_ref,k_ref,v_ref,dq_ref, qh, doh, acc_ref):
    i=pl.program_id(0)
    width=q_ref.shape[1]; real=heads*HEAD_DIM
    base=meta[0]; wbase=base-reach
    t0=base+i*tq
    lo=(doc_start(meta,ndocs,t0)-wbase)//tk
    f0=(doc_start(meta,ndocs,t0+tq-1)-wbase+tk-1)//tk
    f1=(t0-wbase)//tk
    hi=(t0+tq-1-wbase)//tk+1
    f0=jnp.minimum(f0,f1)
    q=q_ref[...]; do=do_ref[...]
    for h in range(heads):
        hm=head_mask(tq,h,heads,width)
        qh[h]=jnp.where(hm,q,jnp.zeros_like(q))
        doh[h]=jnp.where(hm,do,jnp.zeros_like(do))
    acc_ref[...]=jnp.zeros_like(acc_ref)
    trow=t0+lax.broadcasted_iota(jnp.int32,(tq,128),0)
    srow=starts_vec(meta,ndocs,trow)
    def body(j,masked):
        off=pl.multiple_of(j*tk,tk)
        k=k_ref[pl.ds(off,tk),:]; v=v_ref[pl.ds(off,tk),:]
        if masked:
            u=wbase+off+lax.broadcasted_iota(jnp.int32,(tq,tk),1)
            vis=(u>=srow[:,:1])&(u<=trow[:,:1])
        tot=None
        for h in range(heads):
            p=jnp.exp(dotf(qh[h],k,NT))
            if masked: p=jnp.where(vis,p,0.0)
            ds=(p*dotf(doh[h],v,NT)).astype(BF16)
            kh=jnp.where(head_mask(tk,h,heads,width),k,jnp.zeros_like(k))
            d=dotf(ds,kh)
            tot=d if tot is None else tot+d
        acc_ref[...]+=tot
    three(lo,f0,f1,hi,body)
    dq_ref[...]=(acc_ref[...]*(HEAD_DIM**-0.5)).astype(BF16)[:,:real]

def attention_dq(meta,q,do,k,v,heads,tq=256,tk=512):
    B,width=q.shape; W=k.shape[0]; ndocs=meta.shape[0]-1
    full=lambda: pl.BlockSpec((W,width),lambda i:(0,0),pipeline_mode=pl.Buffered(1))
    row=lambda w: pl.BlockSpec((tq,w),lambda i:(i,0))
    return pl.pallas_call(functools.partial(dq_kernel,heads,ndocs,tq,tk,W-B),
        grid=(B//tq,),
        in_specs=[pl.BlockSpec(memory_space=pltpu.SMEM),row(width),row(width),full(),full()],
        out_specs=row(heads*HEAD_DIM),
        out_shape=jax.ShapeDtypeStruct((B,heads*HEAD_DIM),BF16),
        scratch_shapes=[pltpu.VMEM((heads,tq,width),BF16)]*2+[pltpu.VMEM((tq,width),F32)],
        compiler_params=pltpu.CompilerParams(vmem_limit_bytes=56<<20),
        cost_estimate=pl.CostEstimate(flops=45_000_000_000,bytes_accessed=12<<20,transcendentals=20_000_000),
        name="attn_dq")(meta,q,do,k,v)

def dkv_kernel(heads,ndocs,tq,tk,meta, k_ref,v_ref,q_ref,do_ref,dk_ref,dv_ref, kh, vh, dk_acc, dv_acc):
    i=pl.program_id(0)
    width=k_ref.shape[1]; real=heads*HEAD_DIM
    base=meta[0]
    u0=base+i*tk
    lo=(u0-base)//tq
    f0=(u0+tk-1-base+tq-1)//tq
    e_first=doc_end(meta,ndocs,u0); e_last=doc_end(meta,ndocs,u0+tk-1)
    f1=(e_first-base)//tq
    hi=(e_last-1-base)//tq+1
    f0=jnp.minimum(f0,hi)
    f1=jnp.clip(f1,f0,hi)
    k=k_ref[...]; v=v_ref[...]
    for h in range(heads):
        hm=head_mask(tk,h,heads,width)
        kh[h]=jnp.where(hm,k,jnp.zeros_like(k))
        vh[h]=jnp.where(hm,v,jnp.zeros_like(v))
    dk_acc[...]=jnp.zeros_like(dk_acc); dv_acc[...]=jnp.zeros_like(dv_acc)
    urow=u0+lax.broadcasted_iota(jnp.int32,(tk,128),0)
    erow=ends_vec(meta,ndocs,urow)
    def body(j,masked):
        off=pl.multiple_of(j*tq,tq)
        q=q_ref[pl.ds(off,tq),:]; do=do_ref[pl.ds(off,tq),:]
        if masked:
            t=base+off+lax.broadcasted_iota(jnp.int32,(tk,tq),1)
            vis=(t>=urow[:,:1])&(t<erow[:,:1])
        a=None;b=None
        for h in range(heads):
            p=jnp.exp(dotf(kh[h],q,NT))
            if masked: p=jnp.where(vis,p,0.0)
            ds=(p*dotf(vh[h],do,NT)).astype(BF16)
            hm=head_mask(tq,h,heads,width)
            d=dotf(p.astype(BF16),jnp.where(hm,do,jnp.zeros_like(do)))
            a=d if a is None else a+d
            d=dotf(ds,jnp.where(hm,q,jnp.zeros_like(q)))
            b=d if b is None else b+d
        dv_acc[...]+=a
        dk_acc[...]+=b
    three(lo,f0,f1,hi,body)
    dk_ref[...]=dk_acc[...].astype(BF16)[:,:real]
    dv_ref[...]=dv_acc[...].astype(BF16)[:,:real]

def attention_dkv(meta,k,v,q,do,heads,tq=512,tk=256):
    B,width=k.shape; W=q.shape[0]; ndocs=meta.shape[0]-1
    full=lambda: pl.BlockSpec((W,width),lambda i:(0,0),pipeline_mode=pl.Buffered(1))
    row=lambda w: pl.BlockSpec((tk,w),lambda i:(i,0))
    return pl.pallas_call(functools.partial(dkv_kernel,heads,ndocs,tq,tk),
        grid=(B//tk,),
        in_specs=[pl.BlockSpec(memory_space=pltpu.SMEM),row(width),row(width),full(),full()],
        out_specs=[row(heads*HEAD_DIM)]*2,
        out_shape=[jax.ShapeDtypeStruct((B,heads*HEAD_DIM),BF16)]*2,
        scratch_shapes=[pltpu.VMEM((heads,tk,width),BF16)]*2+[pltpu.VMEM((tk,width),F32)]*2,
        compiler_params=pltpu.CompilerParams(vmem_limit_bytes=56<<20),
        cost_estimate=pl.CostEstimate(flops=60_000_000_000,bytes_accessed=12<<20,transcendentals=20_000_000),
        name="attn_dkv")(meta,k,v,q,do)


def statistics(values):
    center = values - jnp.mean(values, axis=-1, keepdims=True)
    scale = lax.rsqrt(jnp.mean(jnp.square(center), axis=-1, keepdims=True) + EPSILON)
    return center * scale, scale


def norm_back(grad, xhat, scale, gain):
    eg = grad * gain
    return scale * (
        eg
        - jnp.mean(eg, axis=-1, keepdims=True)
        - xhat * jnp.mean(eg * xhat, axis=-1, keepdims=True)
    )


def gelu_tanh(values):
    return (
        0.5 * values * (1.0 + jnp.tanh(GELU_SCALE * (values + 0.044715 * values * values * values)))
    )


def split_parts(values):
    high = values.astype(BF16)
    rest = values - high.astype(F32)
    middle = rest.astype(BF16)
    return high, middle, (rest - middle.astype(F32)).astype(BF16)


def widened(columns, extra):
    rows, width = columns.shape
    empty = jnp.zeros((rows, WIDTH - width - extra.shape[1]), BF16)
    return jnp.concatenate([columns, extra, empty], axis=1)


def on_device(
    tokens, first_values, cotangent, w_query, w_key, w_value, w_out, w_up, w_down,
    gain_attn, gain_mlp, doc_lengths,
):
    width = tokens.shape[1]
    heads_of = lax.axis_size("head")
    nblk = lax.axis_size("blk")
    head, blk = lax.axis_index("head"), lax.axis_index("blk")
    rows = tokens.shape[0]
    block = rows * heads_of
    heads = HEADS // heads_of
    cols = heads * HEAD_DIM
    part = width // nblk
    scale = HEAD_DIM**-0.5
    both = ("blk", "head")
    meta = jnp.concatenate([jnp.reshape(blk * block, (1,)).astype(jnp.int32), doc_lengths])

    packed = jnp.concatenate([w_up, w_down.T, w_out.T], axis=1)
    gathered = lax.all_gather(packed, both, axis=0).reshape(nblk, heads_of, part, packed.shape[1])

    def unpacked(lo, hi):
        return gathered[:, :, :, lo:hi].transpose(0, 2, 1, 3).reshape(width, heads_of * (hi - lo))

    up_cols = w_up.shape[1]
    full_up, down_t = unpacked(0, up_cols), unpacked(up_cols, 2 * up_cols)
    out_t = unpacked(2 * up_cols, packed.shape[1])

    gains = jnp.stack([gain_attn, gain_mlp])[:, None, :]
    tok_all, first_all, q_all, k_all, _, v_all, gain_all = front(
        nblk, tokens, first_values, w_query, w_key, w_value, gains
    )
    attn_gain = gain_all[:, 0].reshape(width)
    mlp_gain = gain_all[:, 1].reshape(width)
    wq, wk = q_all.reshape(width, cols), k_all.reshape(width, cols)
    v_halves = v_all.reshape(2, width, w_value.shape[1])
    wv = jnp.concatenate([v_halves[0], v_halves[1]], axis=1)
    xhat_all, _ = statistics(tok_all.reshape(block, width).astype(F32))
    normed = (xhat_all * attn_gain).astype(BF16)
    query = (dotf(normed, wq).astype(BF16).astype(F32) * scale).astype(BF16)
    key = dotf(normed, wk).astype(BF16)
    fresh = dotf(normed, wv).astype(BF16)
    kept = lax.dynamic_slice_in_dim(
        first_all.reshape(block, first_values.shape[1]), cols * (head % 2), cols, 1
    )
    value = jnp.where(head < 2, fresh, kept)

    pair = 2 * HEAD_DIM
    sent = jnp.concatenate([key[:, :pair], value[:, :pair], key[:, pair:], value[:, pair:]], axis=1)
    earlier = halo(nblk, sent)
    window = jnp.concatenate([earlier[0], earlier[1], sent], axis=0)
    ones = jnp.ones((window.shape[0], SPLITS * heads), BF16)
    key_win = widened(
        jnp.concatenate([window[:, :pair], window[:, 2 * pair : 2 * pair + HEAD_DIM]], axis=1), ones
    )
    value_win = widened(
        jnp.concatenate([window[:, pair : 2 * pair], window[:, 2 * pair + HEAD_DIM :]], axis=1), ones
    )
    no_extra = jnp.zeros((block, SPLITS * heads), BF16)
    mixed_heads, exact, query_wide = attention_fwd(
        meta, widened(query, no_extra), key_win, value_win, heads, 512, 1024
    )

    mixed = swap(nblk, mixed_heads.reshape(heads_of, rows, cols), 2)
    mixed = mixed.transpose(1, 0, 2).reshape(rows, width)
    token_f = tokens.astype(F32)
    resid = token_f + dotf(mixed, out_t, NT)
    xhat2, scale2 = statistics(resid)
    normed2 = (xhat2 * mlp_gain).astype(BF16)
    pre = dotf(normed2, full_up)
    hidden, gelu_back = jax.vjp(gelu_tanh, pre)
    hidden = hidden.astype(BF16)
    layer_output = (resid + dotf(hidden, down_t, NT)).astype(BF16)
    grad_hidden = dotf(cotangent, down_t)
    grad_pre = gelu_back(grad_hidden)[0].astype(BF16)
    grad_normed2 = dotf(grad_pre, full_up, NT)
    grad_resid = cotangent.astype(F32) + norm_back(grad_normed2, xhat2, scale2, mlp_gain)
    grad_branch = grad_resid.astype(BF16)
    grad_mixed = dotf(grad_branch, out_t).astype(BF16)
    grad_heads = swap(
        nblk, grad_mixed.reshape(rows, heads_of, cols).transpose(1, 0, 2), 3
    ).reshape(block, cols)

    gain_mlp_part = jnp.sum(grad_normed2 * xhat2, axis=0)
    whole_up = dotf(normed2, grad_pre, TN)
    whole_down = dotf(cotangent, hidden, TN)
    whole_out = dotf(grad_branch, mixed, TN)

    def repacked(whole):
        return (
            whole.astype(BF16)
            .reshape(nblk, part, heads_of, whole.shape[1] // heads_of)
            .transpose(0, 2, 1, 3)
        )

    grads = jnp.concatenate([repacked(whole_up), repacked(whole_down), repacked(whole_out)], axis=3)
    grads = grads.reshape(nblk * heads_of, part, packed.shape[1])
    reduced = lax.psum_scatter(grads, both, scatter_dimension=0, tiled=False).astype(F32)

    delta = jnp.sum(
        (grad_heads.astype(F32) * exact[:, :cols]).reshape(block, heads, HEAD_DIM), axis=2
    )
    delta_parts = jnp.stack(split_parts(-delta), axis=2).reshape(block, SPLITS * heads)
    grad_wide = widened(grad_heads, delta_parts)

    def from_later(array, distance):
        route = [(i, i - distance) for i in range(distance, nblk)]
        return lax.ppermute(array, "blk", route)

    def later_window(array):
        return jnp.concatenate([array, from_later(array, 1), from_later(array, 2)], axis=0)

    query_later, grad_later = later_window(query_wide), later_window(grad_wide)
    grad_query = attention_dq(meta, query_wide, grad_wide, key_win, value_win, heads, 512, 512)
    own = key_win.shape[0] - block
    grad_key, grad_value = attention_dkv(
        meta, key_win[own:], value_win[own:], query_later, grad_later, heads, 512, 512
    )

    whole_q, whole_k, whole_v = (
        dotf(normed, grad_query, TN),
        dotf(normed, grad_key, TN),
        dotf(normed, grad_value, TN),
    )
    fresh_grad = jnp.where(head < 2, grad_value, jnp.zeros_like(grad_value))
    grad_normed = dotf(grad_query, wq, NT) + dotf(grad_key, wk, NT) + dotf(fresh_grad, wv, NT)
    gain_attn_part = jnp.sum(grad_normed * xhat_all, axis=0)
    gain_parts = jnp.stack([gain_attn_part, gain_mlp_part]).reshape(2, nblk, 1, part)
    v_parts = whole_v.astype(BF16).reshape(nblk, part, 2, cols // 2).transpose(2, 0, 1, 3)
    grad_norm_sum, final_query, final_key, final_value, first_parts, gain_sums = tail(
        nblk,
        grad_normed.astype(BF16).reshape(heads_of, rows, width),
        whole_q.astype(BF16).reshape(nblk, part, cols),
        whole_k.astype(BF16).reshape(nblk, part, cols),
        v_parts,
        grad_value.reshape(heads_of, rows, cols),
        gain_parts.transpose(1, 0, 2, 3),
    )
    xhat, scale1 = statistics(token_f)
    grad_tokens = grad_resid + norm_back(grad_norm_sum, xhat, scale1, attn_gain)
    grad_first = jnp.concatenate([first_parts[0], first_parts[1]], axis=1).astype(F32)
    return (
        layer_output,
        grad_tokens,
        grad_first,
        final_query,
        final_key,
        final_value,
        reduced[:, 2 * up_cols :].T,
        reduced[:, :up_cols],
        reduced[:, up_cols : 2 * up_cols].T,
        gain_sums[0].reshape(part),
        gain_sums[1].reshape(part),
    )


def solution(mesh):
    rows = P(("blk", "head"), None)
    specs = (P("blk", "head"),) * 3 + (P("head", "blk"), P("blk", "head"), P("head", "blk"))
    gains = (P("blk"), P("blk"))
    return jax.shard_map(
        on_device,
        mesh=mesh,
        in_specs=(rows,) * 3 + specs + gains + (P(),),
        out_specs=(rows,) * 3 + specs + gains,
        check_vma=False,
    )
```

```python
import functools

import jax
import jax.numpy as jnp
from jax import lax
from jax.experimental import pallas as pl
from jax.experimental.pallas import tpu as pltpu
from jax.sharding import PartitionSpec as P

HEADS = 12
HEAD_DIM = 64
DOC_MAX = 4096
EPSILON = 1e-05
GELU_SCALE = 0.7978845608028654
EXCLUDED = -1e30
WIDTH = 256
SPLITS = 3
BF16 = jnp.bfloat16
F32 = jnp.float32
MESH = pl.DeviceIdType.MESH
ANY = pl.BlockSpec(memory_space=pl.ANY)
WHOLE = pl.BlockSpec(memory_space=pltpu.VMEM)
NT = (((1,), (1,)), ((), ()))
TN = (((0,), (0,)), ((), ()))


def dotf(left, right, dims=None):
    if dims is None:
        dims = (((1,), (0,)), ((), ()))
    return lax.dot_general(left, right, dims, preferred_element_type=F32)


def remote(src, dst, send_sem, recv_sem, head, blk):
    return pltpu.make_async_remote_copy(
        src_ref=src,
        dst_ref=dst,
        send_sem=send_sem,
        recv_sem=recv_sem,
        device_id={"head": head, "blk": blk},
        device_id_type=MESH,
    )


def greet(partners):
    barrier = pltpu.get_barrier_semaphore()
    for head, blk in partners:
        pl.semaphore_signal(
            barrier, inc=1, device_id={"head": head, "blk": blk}, device_id_type=MESH
        )
    pl.semaphore_wait(barrier, len(partners))


def xor(value, bit):
    return value + bit - 2 * bit * (lax.div(value, bit) % 2)


def partners_of(head, blk, nblk, heads=True, blks=True):
    found = []
    if heads:
        found += [(xor(head, 1), blk), (xor(head, 2), blk), (3 - head, blk)]
    if blks:
        found += [(head, lax.rem(blk + d, nblk)) for d in range(1, nblk)]
    return found


class Line:
    def __init__(self, nblk, head, blk, sources, targets, up, down, across):
        self.half, self.head, self.blk = nblk // 2, head, blk
        self.place, self.parity = lax.div(blk, 2), lax.rem(blk, 2)
        self.sources, self.targets = sources, targets
        self.sems = {"up": up, "down": down, "across": across}

    def copies(self, way, origin, step, fresh=False):
        slot = 2 * origin + self.parity
        to = {
            "up": lax.rem(self.blk + 2, 2 * self.half),
            "down": lax.rem(self.blk + 2 * self.half - 2, 2 * self.half),
            "across": self.blk + 1 - 2 * self.parity,
        }[way]
        send, recv = self.sems[way]
        return [
            remote(
                source if fresh else target.at[slot],
                target.at[slot],
                send.at[k, step],
                recv.at[k, step],
                self.head,
                to,
            )
            for k, (source, target) in enumerate(zip(self.sources, self.targets))
        ]

    def landing(self, way, origin, step, parity=None):
        slot = 2 * origin + (self.parity if parity is None else parity)
        send, recv = self.sems[way]
        other = self.blk + 1 - 2 * self.parity
        return [
            remote(
                target.at[slot], target.at[slot], send.at[k, step], recv.at[k, step], self.head, other
            )
            for k, target in enumerate(self.targets)
        ]

    def each(self, condition, copies, verb):
        @pl.when(condition)
        def _():
            for copy in copies():
                getattr(copy, verb)()

    def begin(self):
        self.each(self.place + 1 < self.half, lambda: self.copies("up", self.place, 0, True), "start")
        self.each(self.place > 0, lambda: self.copies("down", self.place, 0, True), "start")
        for copy in self.copies("across", self.place, self.place, True):
            copy.start()

    def step(self, s):
        low, high = self.place - 1 - s, self.place + 1 + s
        self.each(low >= 0, lambda: self.landing("up", low, s), "wait_recv")
        if s + 1 < self.half - 1:
            self.each(
                (low >= 0) & (self.place + 1 < self.half),
                lambda: self.copies("up", low, s + 1),
                "start",
            )
        self.each(low >= 0, lambda: self.copies("across", low, low), "start")
        self.each(high < self.half, lambda: self.landing("down", high, s), "wait_recv")
        if s + 1 < self.half - 1:
            self.each(
                (high < self.half) & (self.place > 0),
                lambda: self.copies("down", high, s + 1),
                "start",
            )
        self.each(high < self.half, lambda: self.copies("across", high, high), "start")

    def end(self):
        for o in range(self.half):
            for copy in self.landing("across", o, o, 1 - self.parity):
                copy.wait_recv()
            for copy in self.copies("across", o, o):
                copy.wait_send()
        for s in range(self.half - 1):
            self.each(
                (self.place - s >= 0) & (self.place + 1 < self.half),
                lambda: self.copies("up", self.place - s, s),
                "wait_send",
            )
            self.each(
                (self.place + s < self.half) & (self.place > 0),
                lambda: self.copies("down", self.place + s, s),
                "wait_send",
            )


def front_kernel(
    nblk, pieces, tok, first, w_qk, w_rest, w_v, gains,
    tok_all, first_all, qk_all, rest_all, v_own, v_all, gain_all,
    own_sem, send_x, recv_x, send_s, recv_s, send_f, recv_f, send_w, recv_w, send_v, recv_v,
    send_u, recv_u, send_d, recv_d, send_y, recv_y,
):
    head, blk = lax.axis_index("head"), lax.axis_index("blk")
    side, core, far = xor(head, 2), xor(head, 1), 3 - head
    greet(partners_of(head, blk, nblk))
    moved = [(tok, tok_all), (first, first_all)]
    weights = [(w_v, v_own), (gains, gain_all)]
    large = [(w_qk, qk_all), (w_rest, rest_all)]
    rows = tok.shape[0] // pieces
    line = Line(
        nblk, head, blk, [w_qk, w_rest], [qk_all, rest_all],
        (send_u, recv_u), (send_d, recv_d), (send_y, recv_y),
    )

    def part(ref, p):
        return ref.at[pl.ds(p * rows, rows)]

    def hop(sems, k, p, source, slot, target):
        dst = part(moved[k][1].at[slot], p)
        return remote(source, dst, sems[0].at[k, p], sems[1].at[k, p], target, blk)

    xs, ss, fs = (send_x, recv_x), (send_s, recv_s), (send_f, recv_f)
    order = [(k, p) for p in range(pieces) for k in range(2)]
    line.begin()
    for k, p in order:
        hop(xs, k, p, part(moved[k][0], p), head, side).start()

    def spread(d):
        to = lax.rem(blk + d, nblk)
        return [
            remote(src, dst.at[blk], send_w.at[i, d], recv_w.at[i, d], head, to)
            for i, (src, dst) in enumerate(weights)
        ]

    def from_peer(d):
        source = lax.rem(blk - d + nblk, nblk)
        return [
            remote(src, dst.at[source], send_w.at[i, d], recv_w.at[i, d], head, source)
            for i, (src, dst) in enumerate(weights)
        ]

    for d in range(1, nblk):
        for copy in spread(d):
            copy.start()
    for k, p in order:
        hop(ss, k, p, part(moved[k][0], p), head, core).start()
    local = [
        pltpu.make_async_copy(moved[k][0], moved[k][1].at[head], own_sem.at[k]) for k in range(2)
    ] + [
        pltpu.make_async_copy(src, dst.at[blk], own_sem.at[2 + i])
        for i, (src, dst) in enumerate(weights + large)
    ]
    for copy in local:
        copy.start()

    def pass_on(k, p):
        landed = part(moved[k][1].at[side], p)
        hop(xs, k, p, landed, side, side).wait_recv()
        hop(fs, k, p, landed, side, core).start()

    steps = nblk // 2 - 1
    for s in range(steps):
        line.step(s)
        for k, p in order[s * len(order) // steps : (s + 1) * len(order) // steps]:
            pass_on(k, p)
    for copy in local:
        copy.wait()
    for d in range(1, nblk):
        for copy in from_peer(d):
            copy.wait_recv()
    half, kind = lax.div(head, 2), lax.rem(head, 2)
    for i in range(2):
        target = half + 2 * i

        @pl.when(target == head)
        def _():
            pltpu.make_async_copy(v_own, v_all.at[kind], own_sem.at[6]).start()

        @pl.when(target != head)
        def _():
            remote(v_own, v_all.at[kind], send_v.at[i], recv_v.at[kind], target, blk).start()

    for k, p in order:
        hop(ss, k, p, part(moved[k][1].at[core], p), core, core).wait_recv()
        hop(fs, k, p, part(moved[k][1].at[far], p), far, core).wait_recv()
    for c in range(2):
        source = 2 * kind + c

        @pl.when(source == head)
        def _():
            pltpu.make_async_copy(v_own, v_all.at[c], own_sem.at[6]).wait()

        @pl.when(source != head)
        def _():
            remote(v_own, v_all.at[c], send_v.at[0], recv_v.at[c], source, blk).wait_recv()

    for i in range(2):
        target = half + 2 * i

        @pl.when(target != head)
        def _():
            remote(v_own, v_all.at[kind], send_v.at[i], recv_v.at[kind], target, blk).wait_send()

    for k, p in order:
        hop(xs, k, p, part(moved[k][0], p), head, side).wait_send()
        hop(ss, k, p, part(moved[k][0], p), head, core).wait_send()
        hop(fs, k, p, part(moved[k][1].at[side], p), side, core).wait_send()
    for d in range(1, nblk):
        for copy in spread(d):
            copy.wait_send()
    line.end()


def front(nblk, tok, first, w_qk, w_rest, w_v, gains, pieces=4):
    def shape(lead, like):
        return jax.ShapeDtypeStruct(lead + like.shape, like.dtype)

    dma = pltpu.SemaphoreType.DMA
    return pl.pallas_call(
        functools.partial(front_kernel, nblk, pieces),
        out_shape=[
            shape((4,), tok),
            shape((4,), first),
            shape((nblk,), w_qk),
            shape((nblk,), w_rest),
            shape((nblk,), w_v),
            shape((2, nblk), w_v),
            shape((nblk,), gains),
        ],
        in_specs=[WHOLE] * 6,
        out_specs=[ANY] * 7,
        scratch_shapes=[dma((7,))]
        + [dma((2, pieces))] * 6
        + [dma((2, nblk))] * 2
        + [dma((2,))] * 2
        + [dma((2, nblk // 2))] * 6,
        compiler_params=pltpu.CompilerParams(collective_id=0, has_side_effects=True),
        name="front",
    )(tok, first, w_qk, w_rest, w_v, gains)


def halo_kernel(
    nblk, pieces, own, rest, near_far, rest_all,
    send_z, recv_z, send_y, recv_y, send_x, recv_x, send_c, recv_c, send_f, recv_f,
):
    head, blk = lax.axis_index("head"), lax.axis_index("blk")
    side, core, beyond = xor(head, 2), xor(head, 1), 3 - head
    odd = lax.rem(blk, 2)
    pair = blk + 1 - 2 * odd
    up, down = lax.rem(blk + 2, nblk), lax.rem(blk + nblk - 2, nblk)
    greet(partners_of(head, blk, nblk, blks=False) + [(head, pair), (head, up), (head, down)])
    rows = own.shape[0] // pieces

    def part(ref, p):
        return ref.at[pl.ds(p * rows, rows)]

    def far_copy(p, to):
        return remote(part(own, p), part(near_far.at[0], p), send_z.at[p], recv_z.at[p], head, to)

    def near_copy(p, src):
        return remote(src, part(near_far.at[1], p), send_y.at[p], recv_y.at[p], head, pair)

    def chunk(sems, b, source, slot, to):
        return remote(
            source, rest_all.at[slot, b], sems[0].at[b], sems[1].at[b], to, blk
        )

    xs, cs, fs = (send_x, recv_x), (send_c, recv_c), (send_f, recv_f)
    for p in range(pieces):

        @pl.when(blk + 2 < nblk)
        def _():
            far_copy(p, up).start()

        @pl.when(odd == 0)
        def _():
            near_copy(p, part(own, p)).start()

    for b in range(nblk):
        chunk(xs, b, rest.at[b], head, side).start()
    for b in range(nblk):
        chunk(cs, b, rest.at[b], head, core).start()
    for n in range(max(pieces, nblk)):
        if n < pieces:

            @pl.when(blk >= 2)
            def _():
                far_copy(n, down).wait_recv()

            @pl.when((blk >= 2) & (odd == 1))
            def _():
                near_copy(n, part(near_far.at[0], n)).start()

        if n < nblk:
            landed = rest_all.at[side, n]
            chunk(xs, n, landed, side, side).wait_recv()
            chunk(fs, n, landed, side, core).start()
    for b in range(nblk):
        chunk(cs, b, rest.at[b], core, core).wait_recv()
        chunk(fs, b, rest.at[b], beyond, core).wait_recv()
    for b in range(nblk):
        chunk(xs, b, rest.at[b], head, side).wait_send()
        chunk(cs, b, rest.at[b], head, core).wait_send()
        chunk(fs, b, rest_all.at[side, b], side, core).wait_send()
    for p in range(pieces):

        @pl.when((blk >= 2) | (odd == 1))
        def _():
            near_copy(p, part(own, p)).wait_recv()

        @pl.when(blk + 2 < nblk)
        def _():
            far_copy(p, up).wait_send()

        @pl.when((blk >= 2) | (odd == 0))
        def _():
            near_copy(p, part(own, p)).wait_send()


def halo(nblk, own, rest, pieces=8):
    dma = pltpu.SemaphoreType.DMA
    return pl.pallas_call(
        functools.partial(halo_kernel, nblk, pieces),
        out_shape=[
            jax.ShapeDtypeStruct((2,) + own.shape, own.dtype),
            jax.ShapeDtypeStruct((4,) + rest.shape, rest.dtype),
        ],
        in_specs=[ANY] * 2,
        out_specs=[ANY] * 2,
        scratch_shapes=[dma((pieces,))] * 4 + [dma((nblk,))] * 6,
        compiler_params=pltpu.CompilerParams(collective_id=1, has_side_effects=True),
        name="halo",
    )(own, rest)


def tail_kernel(
    nblk, pieces, cols, grad, weights, first, gains, kept, got,
    out_grad, out_qk, out_v, out_first, out_gain, out_rest,
    core_buf, side_out, side_buf, pair_buf, line_out, line_in, v_sum, v_got,
    gain_buf, gain_sum, gain_got, up_out, up_in, down_out, down_in,
    own_sem, send_s, recv_s, send_x, recv_x, send_y, recv_y, send_l, recv_l,
    send_v, recv_v, send_f, recv_f, send_g, recv_g, send_h, recv_h, send_u, recv_u, send_d, recv_d,
):
    head, blk = lax.axis_index("head"), lax.axis_index("blk")
    side, core, far = xor(head, 2), xor(head, 1), 3 - head
    greet(partners_of(head, blk, nblk))
    rows = grad.shape[1] // pieces
    line, place, parity = nblk // 2, lax.div(blk, 2), lax.rem(blk, 2)
    pair = blk + 1 - 2 * parity
    above, below = lax.rem(blk + 2, nblk), lax.rem(blk + nblk - 2, nblk)

    def part(ref, p):
        return ref.at[pl.ds(p * rows, rows)]

    def to_core(i, p, slot):
        return remote(
            part(grad.at[slot], p), part(core_buf.at[i], p), send_s.at[i, p], recv_s.at[i, p],
            core, blk,
        )

    def to_side(p):
        return remote(
            part(side_out, p), part(side_buf, p), send_x.at[p], recv_x.at[p], side, blk
        )

    def sum_of(t):
        return kept[t].astype(F32) + got[t].astype(F32)

    def up_copy(t, to):
        return remote(up_out.at[t], up_in.at[t], send_u.at[t], recv_u.at[t], head, to)

    def down_copy(t, to):
        return remote(down_out.at[t], down_in.at[t], send_d.at[t], recv_d.at[t], head, to)

    def first_hops():
        for n in range(line - 1):
            t = line - 1 - n

            @pl.when((place == 0) & (place < t))
            def _():
                up_out[t] = sum_of(t).astype(BF16)
                up_copy(t, above).start()

            @pl.when((place == line - 1) & (place > n))
            def _():
                down_out[n] = sum_of(n).astype(BF16)
                down_copy(n, below).start()

    def next_hops(n):
        t = line - 1 - n

        @pl.when((place > 0) & (place < t))
        def _():
            up_copy(t, above).wait_recv()
            up_out[t] = (sum_of(t) + up_in[t].astype(F32)).astype(BF16)
            up_copy(t, above).start()

        @pl.when((place < line - 1) & (place > n))
        def _():
            down_copy(n, below).wait_recv()
            down_out[n] = (sum_of(n) + down_in[n].astype(F32)).astype(BF16)
            down_copy(n, below).start()

    for p in range(pieces):
        to_core(0, p, far).start()
    first_hops()
    for p in range(pieces):
        to_core(1, p, core).start()

    def across(n):
        return remote(
            weights.at[2 * n + 1 - parity], pair_buf.at[n], send_y.at[n], recv_y.at[n], head, pair
        )

    for n in range(line):
        across(n).start()
    half, kind = lax.div(head, 2), lax.rem(head, 2)

    def gain_to(d):
        to = lax.rem(blk + d, nblk)
        return remote(gains.at[to], gain_buf.at[blk], send_g.at[d], recv_g.at[d], head, to)

    def gain_from(d):
        source = lax.rem(blk - d + nblk, nblk)
        return remote(gains.at[0], gain_buf.at[source], send_g.at[d], recv_g.at[d], head, source)

    for d in range(1, nblk):
        gain_to(d).start()
    gain_buf[blk] = gains[blk]

    def first_copy(i, to, slot):
        return remote(first.at[to], out_first.at[slot], send_f.at[i], recv_f.at[slot], to, blk)

    @pl.when(half == 1)
    def _():
        for i, to in enumerate((core, side, far)):
            first_copy(i, to, kind).start()
        pltpu.make_async_copy(first.at[head], out_first.at[kind], own_sem).start()

    for p in range(pieces):
        to_core(0, p, far).wait_recv()
        part(side_out, p)[...] = (
            part(grad.at[side], p)[...].astype(F32) + part(core_buf.at[0], p)[...].astype(F32)
        ).astype(BF16)
        to_side(p).start()

    def along(d, to):
        return remote(
            line_out.at[to], line_in.at[d], send_l.at[d], recv_l.at[d], head, 2 * to + parity
        )

    for n in range(line):
        across(n).wait_recv()
        line_out[n] = (
            weights[2 * n + parity].astype(F32) + pair_buf[n].astype(F32)
        ).astype(BF16)
    for d in range(1, line):
        along(d, lax.rem(place + d, line)).start()
    for d in range(1, nblk):
        gain_from(d).wait_recv()
    gain_sum[...] = jnp.sum(gain_buf[...], axis=0)
    peers = (core, side, far)

    def gain_copy(i, to):
        return remote(gain_sum, gain_got.at[i], send_h.at[i], recv_h.at[i], to, blk)

    for i, to in enumerate(peers):
        gain_copy(i, to).start()
    for n in range(line - 1):
        next_hops(n)
    total = line_out[place].astype(F32)
    for d in range(1, line):
        along(d, lax.rem(place - d + line, line)).wait_recv()
        total = total + line_in[d].astype(F32)
    out_qk[...] = total[:, : 2 * cols]
    v_sum[0] = total[:, 2 * cols : 2 * cols + cols // 2]
    v_sum[1] = total[:, 2 * cols + cols // 2 : 3 * cols]

    def give(c, to):
        return remote(v_sum.at[c], v_got, send_v.at[c], recv_v.at[0], to, blk)

    for c in range(2):
        to = 2 * head + c

        @pl.when((half == 0) & (to != head))
        def _():
            give(c, to).start()

    for p in range(pieces):
        to_core(1, p, core).wait_recv()
        to_side(p).wait_recv()
        part(out_grad, p)[...] = (
            part(grad.at[head], p)[...].astype(F32)
            + part(core_buf.at[1], p)[...].astype(F32)
            + part(side_buf, p)[...].astype(F32)
        )
    out_rest[...] = sum_of(place)
    for t in range(line):

        @pl.when((place == t) & (place > 0))
        def _():
            up_copy(t, above).wait_recv()
            out_rest[...] += up_in[t].astype(F32)

        @pl.when((place == t) & (place < line - 1))
        def _():
            down_copy(t, below).wait_recv()
            out_rest[...] += down_in[t].astype(F32)

    for i, to in enumerate(peers):
        gain_copy(i, to).wait_recv()
    out_gain[...] = gain_sum[...] + gain_got[0] + gain_got[1] + gain_got[2]

    @pl.when(head == 0)
    def _():
        out_v[...] = v_sum[0]

    @pl.when(head != 0)
    def _():
        give(0, half).wait_recv()
        out_v[...] = v_got[...]

    for slot in range(2):

        @pl.when(head == 2 + slot)
        def _():
            pltpu.make_async_copy(first.at[head], out_first.at[slot], own_sem).wait()

        @pl.when(head != 2 + slot)
        def _():
            first_copy(0, 2 + slot, slot).wait_recv()

    @pl.when(half == 1)
    def _():
        for i, to in enumerate((core, side, far)):
            first_copy(i, to, kind).wait_send()

    for c in range(2):
        to = 2 * head + c

        @pl.when((half == 0) & (to != head))
        def _():
            give(c, to).wait_send()

    for i, to in enumerate(peers):
        gain_copy(i, to).wait_send()
    for p in range(pieces):
        to_core(0, p, far).wait_send()
        to_core(1, p, core).wait_send()
        to_side(p).wait_send()
    for d in range(1, nblk):
        gain_to(d).wait_send()
    for n in range(line):
        across(n).wait_send()
    for d in range(1, line):
        along(d, lax.rem(place + d, line)).wait_send()
    for t in range(line):

        @pl.when(place < t)
        def _():
            up_copy(t, above).wait_send()

        @pl.when(place > t)
        def _():
            down_copy(t, below).wait_send()


def tail(nblk, grad, weights, first, gains, kept, got, cols, pieces=4):
    dma = pltpu.SemaphoreType.DMA
    row, part = grad.shape[1:], weights.shape[1]
    half, line = (part, cols // 2), nblk // 2
    piece = (2, pieces)
    vmem = lambda *shape: pltpu.VMEM(shape, BF16)
    return pl.pallas_call(
        functools.partial(tail_kernel, nblk, pieces, cols),
        out_shape=[
            jax.ShapeDtypeStruct(row, F32),
            jax.ShapeDtypeStruct((part, 2 * cols), F32),
            jax.ShapeDtypeStruct(half, F32),
            jax.ShapeDtypeStruct((2,) + first.shape[1:], BF16),
            jax.ShapeDtypeStruct(gains.shape[1:], F32),
            jax.ShapeDtypeStruct(kept.shape[1:], F32),
        ],
        in_specs=[WHOLE] * 6,
        out_specs=[WHOLE] * 6,
        scratch_shapes=[
            vmem(2, *row), vmem(*row), vmem(*row),
            vmem(line, *weights.shape[1:]), vmem(line, *weights.shape[1:]),
            vmem(line, *weights.shape[1:]),
            pltpu.VMEM((2,) + half, F32),
            pltpu.VMEM(half, F32),
            pltpu.VMEM(gains.shape, F32),
            pltpu.VMEM(gains.shape[1:], F32),
            pltpu.VMEM((3,) + gains.shape[1:], F32),
            vmem(*kept.shape), vmem(*kept.shape), vmem(*kept.shape), vmem(*kept.shape),
            dma,
            dma(piece), dma(piece),
            dma((pieces,)), dma((pieces,)),
            dma((line,)), dma((line,)), dma((line,)), dma((line,)),
            dma((2,)), dma((1,)),
            dma((3,)), dma((2,)),
            dma((nblk,)), dma((nblk,)),
            dma((3,)), dma((3,)),
            dma((line,)), dma((line,)), dma((line,)), dma((line,)),
        ],
        compiler_params=pltpu.CompilerParams(
            collective_id=4, has_side_effects=True, vmem_limit_bytes=60 << 20
        ),
        name="tail",
    )(grad, weights, first, gains, kept, got)


def statistics(values):
    center = values - jnp.mean(values, axis=-1, keepdims=True)
    scale = lax.rsqrt(jnp.mean(jnp.square(center), axis=-1, keepdims=True) + EPSILON)
    return center * scale, scale


def norm_back(grad, xhat, scale, gain):
    eg = grad * gain
    return scale * (
        eg
        - jnp.mean(eg, axis=-1, keepdims=True)
        - xhat * jnp.mean(eg * xhat, axis=-1, keepdims=True)
    )


def split_parts(values):
    high = values.astype(BF16).astype(F32)
    middle = (values - high).astype(BF16).astype(F32)
    return high, middle, values - high - middle


def project_kernel(head_size, tok, first, w_qk, w_v, gain, normed, query, packed, weight):
    pair = 2 * head_size
    cols = 3 * head_size
    width = tok.shape[1]

    @pl.when(pl.program_id(0) == 0)
    def _():
        key, fresh = w_qk[:, cols:], jnp.concatenate([w_v[0], w_v[1]], axis=1)
        weight[:, :pair] = key[:, :pair]
        weight[:, pair : 2 * pair] = fresh[:, :pair]
        weight[:, 2 * pair : 3 * pair] = jnp.concatenate([key[:, pair:], fresh[:, pair:]], axis=1)
        weight[:, 3 * pair :] = jnp.concatenate(
            [w_qk[:, :cols], jnp.zeros((width, WIDTH - cols), BF16)], axis=1
        )

    head = lax.axis_index("head")
    xhat, _ = statistics(tok[...].astype(F32))
    rows = (xhat * gain[...]).astype(BF16)
    normed[...] = rows
    out = dotf(rows, weight[...])
    query[...] = (out[:, 3 * pair :].astype(BF16).astype(F32) * head_size**-0.5).astype(BF16)
    done = out[:, : 3 * pair].astype(BF16)
    kept = jnp.where(lax.rem(head, 2) == 0, first[:, :cols], first[:, cols:])
    given = jnp.concatenate([done[:, :pair], kept[:, :pair], done[:, 2 * pair : 2 * pair + head_size],
                             kept[:, pair:]], axis=1)
    packed[...] = jnp.where(head < 2, done, given)


def project(tok, first, w_qk, w_v, gain, rows=512):
    total, width = tok.shape
    cols = w_qk.shape[1] // 2
    fixed = lambda array: pl.BlockSpec(array.shape, lambda i: (0,) * array.ndim)
    row = lambda n: pl.BlockSpec((rows, n), lambda i: (i, 0))
    return pl.pallas_call(
        functools.partial(project_kernel, HEAD_DIM),
        grid=(total // rows,),
        in_specs=[row(width), row(first.shape[1])] + [fixed(a) for a in (w_qk, w_v, gain)],
        out_specs=[row(width), row(WIDTH), row(2 * cols)],
        out_shape=[
            jax.ShapeDtypeStruct((total, width), BF16),
            jax.ShapeDtypeStruct((total, WIDTH), BF16),
            jax.ShapeDtypeStruct((total, 2 * cols), BF16),
        ],
        scratch_shapes=[pltpu.VMEM((width, 2 * cols + WIDTH), BF16)],
        compiler_params=pltpu.CompilerParams(vmem_limit_bytes=48 << 20),
        cost_estimate=pl.CostEstimate(
            flops=2 * total * width * 640, bytes_accessed=16 << 20, transcendentals=0
        ),
        name="project",
    )(tok, first, w_qk, w_v, gain)


def gelu_both(pre):
    square = pre * pre
    inner = jnp.tanh(GELU_SCALE * (pre + 0.044715 * square * pre))
    slope = GELU_SCALE * (1.0 + 3.0 * 0.044715 * square)
    outer = 0.5 * (1.0 + inner)
    return pre * outer, outer + 0.5 * pre * (1.0 - inner * inner) * slope


def middle_kernel(
    nblk, up_cols, pieces, tok, mixed_parts, cot, gain, rest_own, gathered, query,
    out, grad_resid, grad_wide, gain_part, keep, give, query_later,
    up, down, w_out, up_grad, down_grad, out_grad, mixed, wide_parts, up_got, down_got, out_got,
    sems, out_sems, send_m, recv_m, send_g, recv_g, send_c, recv_c,
    send_z, recv_z, send_y, recv_y,
):
    head, blk = lax.axis_index("head"), lax.axis_index("blk")
    x, core_index = lax.div(head, 2), lax.rem(head, 2)
    core = xor(head, 1)
    others = [xor(head, 2), 3 - head, core]
    odd = lax.rem(blk, 2)
    pair = blk + 1 - 2 * odd
    above, below = lax.rem(blk + 2, nblk), lax.rem(blk + nblk - 2, nblk)
    greet(partners_of(head, blk, nblk, blks=False) + [(head, b) for b in (pair, above, below)])
    heads_of = 4
    part = gathered.shape[2]
    cols = mixed.shape[2]
    heads = cols // HEAD_DIM

    def mixed_copy(i, to, slot):
        return remote(
            mixed_parts.at[to], mixed.at[slot], send_m.at[i], recv_m.at[i], to, blk
        )

    for i, to in enumerate(others):
        mixed_copy(i, to, head).start()
    piece_rows = query.shape[0] // pieces

    def slab(ref, p):
        return ref.at[pl.ds(p * piece_rows, piece_rows)]

    def far_copy(p, to):
        dst = slab(query_later.at[1], p)
        return remote(slab(query, p), dst, send_z.at[p], recv_z.at[p], head, to)

    def near_copy(p, src):
        return remote(src, slab(query_later.at[0], p), send_y.at[p], recv_y.at[p], head, pair)

    for p in range(pieces):

        @pl.when(blk >= 2)
        def _():
            far_copy(p, below).start()

        @pl.when(odd == 1)
        def _():
            near_copy(p, slab(query, p)).start()

    def relay(p):
        @pl.when(blk + 2 < nblk)
        def _():
            far_copy(p, above).wait_recv()

        @pl.when((blk + 2 < nblk) & (odd == 0))
        def _():
            near_copy(p, slab(query_later.at[1], p)).start()

    chunks = [2 * n + 1 - core_index for n in range(2)] + [2 * n + core_index for n in range(2)]

    def load(i, which, own=False):
        target, lo, size = ((w_out, 2 * up_cols, cols), (up, 0, up_cols), (down, up_cols, up_cols))[
            which
        ]
        return [
            pltpu.make_async_copy(
                (rest_own.at[b] if own else gathered.at[chunks[i], b]).at[:, pl.ds(lo, size)],
                target.at[i, pl.ds(b * part, part)],
                sems.at[which, i, b],
            )
            for b in range(nblk)
        ]

    order = [(i, 0) for i in range(heads_of)] + [(i, w) for i in range(heads_of) for w in (1, 2)]
    for i, which in order:
        if i < 2:
            for copy in load(i, which):
                copy.start()
        else:

            @pl.when(x == i - 2)
            def _():
                for copy in load(i, which, True):
                    copy.start()

            @pl.when(x != i - 2)
            def _():
                for copy in load(i, which):
                    copy.start()

    mixed[head] = mixed_parts[head]
    for i in range(heads_of):
        for copy in load(i, 0):
            copy.wait()
    for i, to in enumerate(others):
        mixed_copy(i, to, to).wait_recv()
    branch = None
    for i in range(heads_of):
        term = dotf(mixed[chunks[i]], w_out[i], NT)
        branch = term if branch is None else branch + term
    resid = tok[...].astype(F32) + branch
    xhat, scale = statistics(resid)
    normed = (xhat * gain[...]).astype(BF16)
    cotangent = cot[...]
    total, grad_normed = resid, None

    def to_core(n, k):
        mine, theirs = ((up_grad, up_got), (down_grad, down_got), (out_grad, out_got))[k]
        return remote(mine.at[n], theirs.at[n], send_c.at[k, n], recv_c.at[k, n], core, blk)

    for i in range(heads_of):
        for copy in load(i, 1) + load(i, 2):
            copy.wait()
        pre = dotf(normed, up[i])
        hidden, slope = gelu_both(pre)
        hidden = hidden.astype(BF16)
        grad_pre = (slope * dotf(cotangent, down[i])).astype(BF16)
        total = total + dotf(hidden, down[i], NT)
        term = dotf(grad_pre, up[i], NT)
        grad_normed = term if grad_normed is None else grad_normed + term
        up_grad[i] = dotf(normed, grad_pre, TN).astype(BF16)
        down_grad[i] = dotf(cotangent, hidden, TN).astype(BF16)
        if i < 2:
            to_core(i, 0).start()
            to_core(i, 1).start()
        for p in range(i * pieces // heads_of, (i + 1) * pieces // heads_of):
            relay(p)
    out[...] = total.astype(BF16)
    gain_part[...] = jnp.sum(grad_normed * xhat, axis=0, keepdims=True)
    grad = cotangent.astype(F32) + norm_back(grad_normed, xhat, scale, gain[...])
    grad_resid[...] = grad
    branch_grad = grad.astype(BF16)
    lane = lax.broadcasted_iota(jnp.int32, (tok.shape[0], WIDTH), 1)
    for i in range(heads_of):
        h = chunks[i]
        rows = dotf(branch_grad, w_out[i]).astype(BF16).astype(F32)
        product = rows * mixed[h].astype(F32)
        wide = jnp.concatenate([rows, jnp.zeros((rows.shape[0], WIDTH - cols), F32)], axis=1)
        for k in range(heads):
            delta = jnp.sum(
                product[:, k * HEAD_DIM : (k + 1) * HEAD_DIM], axis=1, keepdims=True
            )
            for c, piece in enumerate(split_parts(-delta)):
                wide = jnp.where(lane == cols + SPLITS * k + c, piece, wide)
        wide_parts[h] = wide.astype(BF16)

    def wide_copy(i, to, slot):
        return remote(
            wide_parts.at[to], grad_wide.at[slot], send_g.at[i], recv_g.at[i], to, blk
        )

    for i, to in enumerate(others):
        wide_copy(i, to, head).start()
    grad_wide[head] = wide_parts[head]
    for i in range(heads_of):
        out_grad[i] = dotf(branch_grad, mixed[chunks[i]], TN).astype(BF16)
        if i < 2:
            to_core(i, 2).start()

    def store(n, k, target):
        mine = (up_grad, down_grad, out_grad)[k]
        lo, size = ((0, up_cols), (up_cols, up_cols), (2 * up_cols, cols))[k]
        return [
            pltpu.make_async_copy(
                mine.at[2 + n, pl.ds(b * part, part)],
                target.at[b].at[:, pl.ds(lo, size)],
                out_sems.at[k, n, b],
            )
            for b in range(nblk)
        ]

    for k in range(3):
        mine, theirs = ((up_grad, up_got), (down_grad, down_got), (out_grad, out_got))[k]
        for n in range(2):
            to_core(n, k).wait_recv()
            mine[2 + n] = (mine[2 + n].astype(F32) + theirs[n].astype(F32)).astype(BF16)

            @pl.when(x == n)
            def _():
                for copy in store(n, k, keep):
                    copy.start()

            @pl.when(x != n)
            def _():
                for copy in store(n, k, give):
                    copy.start()

    for k in range(3):
        for n in range(2):
            for copy in store(n, k, keep):
                copy.wait()
            to_core(n, k).wait_send()
    for i, to in enumerate(others):
        wide_copy(i, to, to).wait_recv()
    for i, to in enumerate(others):
        mixed_copy(i, to, head).wait_send()
        wide_copy(i, to, head).wait_send()
    for p in range(pieces):

        @pl.when((blk + 2 < nblk) | (odd == 0))
        def _():
            near_copy(p, slab(query, p)).wait_recv()

        @pl.when(blk >= 2)
        def _():
            far_copy(p, below).wait_send()

        @pl.when((blk + 2 < nblk) | (odd == 1))
        def _():
            near_copy(p, slab(query, p)).wait_send()


def middle(nblk, tok, mixed_parts, cot, gain, rest_own, gathered, query, up_cols, pieces=8):
    heads_of, rows, cols = mixed_parts.shape
    width = tok.shape[1]
    flops = 2 * rows * width * (6 * up_cols * heads_of + 3 * width)
    dma = pltpu.SemaphoreType.DMA
    vmem = lambda *shape: pltpu.VMEM(shape, BF16)
    return pl.pallas_call(
        functools.partial(middle_kernel, nblk, up_cols, pieces),
        out_shape=[
            jax.ShapeDtypeStruct((rows, width), BF16),
            jax.ShapeDtypeStruct((rows, width), F32),
            jax.ShapeDtypeStruct((heads_of, rows, WIDTH), BF16),
            jax.ShapeDtypeStruct((1, width), F32),
            jax.ShapeDtypeStruct(gathered.shape[1:], BF16),
            jax.ShapeDtypeStruct(gathered.shape[1:], BF16),
            jax.ShapeDtypeStruct((2,) + query.shape, BF16),
        ],
        in_specs=[WHOLE] * 4 + [ANY] * 3,
        out_specs=[WHOLE] * 4 + [ANY] * 3,
        scratch_shapes=[
            vmem(heads_of, width, up_cols), vmem(heads_of, width, up_cols),
            vmem(heads_of, width, cols),
            vmem(heads_of, width, up_cols), vmem(heads_of, width, up_cols),
            vmem(heads_of, width, cols),
            vmem(heads_of, rows, cols), vmem(heads_of, rows, WIDTH),
            vmem(2, width, up_cols), vmem(2, width, up_cols), vmem(2, width, cols),
            dma((3, heads_of, nblk)), dma((3, 2, nblk)),
            dma((3,)), dma((3,)), dma((3,)), dma((3,)), dma((3, 2)), dma((3, 2)),
            dma((pieces,)), dma((pieces,)), dma((pieces,)), dma((pieces,)),
        ],
        compiler_params=pltpu.CompilerParams(
            collective_id=2, has_side_effects=True, vmem_limit_bytes=62 << 20
        ),
        cost_estimate=pl.CostEstimate(
            flops=flops, bytes_accessed=24 << 20, transcendentals=rows * up_cols * heads_of
        ),
        name="middle",
    )(tok, mixed_parts, cot, gain, rest_own, gathered, query)


def pair_sum_kernel(ours, theirs, keep, give):
    odd = lax.rem(lax.axis_index("blk"), 2)
    sums = [(ours[n].astype(F32) + theirs[n].astype(F32)).astype(BF16) for n in range(2)]
    keep[0] = jnp.where(odd == 0, sums[0], sums[1])
    give[0] = jnp.where(odd == 0, sums[1], sums[0])


def pair_sum(ours, theirs):
    nblk, part, width = ours.shape
    both = pl.BlockSpec((2, part, width), lambda i: (i, 0, 0))
    one = pl.BlockSpec((1, part, width), lambda i: (i, 0, 0))
    return pl.pallas_call(
        pair_sum_kernel,
        grid=(nblk // 2,),
        in_specs=[both, both],
        out_specs=[one, one],
        out_shape=[jax.ShapeDtypeStruct((nblk // 2, part, width), BF16)] * 2,
        cost_estimate=pl.CostEstimate(
            flops=nblk * part * width, bytes_accessed=6 * nblk * part * width, transcendentals=0
        ),
        name="pair_sum",
    )(ours, theirs)


def unproject_kernel(
    nblk, d_q, d_k, d_v, normed, gain, w_qk, w_v,
    grad, out_all, gain_part, acc_q, acc_k, acc_v, acc_gain, fresh,
):
    step, last = pl.program_id(0), pl.num_programs(0) - 1
    part = normed.shape[1] // nblk
    cols = d_q.shape[1]

    @pl.when(step == 0)
    def _():
        mine = lax.axis_index("head") < 2
        weight = jnp.concatenate([w_v[0], w_v[1]], axis=1)
        fresh[...] = jnp.where(mine, weight, jnp.zeros_like(weight))
        acc_q[...] = jnp.zeros_like(acc_q)
        acc_k[...] = jnp.zeros_like(acc_k)
        acc_v[...] = jnp.zeros_like(acc_v)
        acc_gain[...] = jnp.zeros_like(acc_gain)

    rows = normed[...]
    mine = lax.axis_index("head") < 2
    d_fresh = jnp.where(mine, d_v[...], jnp.zeros_like(d_v[...]))
    both = jnp.concatenate([d_q[...], d_k[...]], axis=1)
    whole = dotf(both, w_qk[...], NT)
    whole = whole + dotf(d_fresh, fresh[...], NT)
    grad[...] = whole.astype(BF16)
    acc_gain[...] += jnp.sum(whole * rows.astype(F32), axis=0, keepdims=True)
    acc_q[...] += dotf(rows, d_q[...], TN)
    acc_k[...] += dotf(rows, d_k[...], TN)
    acc_v[...] += dotf(rows, d_v[...], TN)

    @pl.when(step == last)
    def _():
        gain_part[...] = acc_gain[...] / gain[...]
        empty = jnp.zeros((normed.shape[1], out_all.shape[2] - 3 * cols), F32)
        whole = jnp.concatenate([acc_q[...], acc_k[...], acc_v[...], empty], axis=1).astype(BF16)
        for b in range(nblk):
            out_all[b] = whole[b * part : (b + 1) * part]


def unproject(nblk, d_q, d_k, d_v, normed, gain, w_qk, w_v, rows=512):
    total, width = normed.shape
    cols = d_q.shape[1]
    part = width // nblk
    fixed = lambda array: pl.BlockSpec(array.shape, lambda i: (0,) * array.ndim)
    row = lambda n: pl.BlockSpec((rows, n), lambda i: (i, 0))
    outs = [
        jax.ShapeDtypeStruct((total, width), BF16),
        jax.ShapeDtypeStruct((nblk, part, -(-3 * cols // 128) * 128), BF16),
        jax.ShapeDtypeStruct((1, width), F32),
    ]
    return pl.pallas_call(
        functools.partial(unproject_kernel, nblk),
        grid=(total // rows,),
        in_specs=[row(cols)] * 3 + [row(width)] + [fixed(a) for a in (gain, w_qk, w_v)],
        out_specs=[row(width)] + [fixed(a) for a in outs[1:]],
        out_shape=outs,
        scratch_shapes=[
            pltpu.VMEM((width, cols), F32),
            pltpu.VMEM((width, cols), F32),
            pltpu.VMEM((width, cols), F32),
            pltpu.VMEM((1, width), F32),
            pltpu.VMEM((width, cols), BF16),
        ],
        compiler_params=pltpu.CompilerParams(vmem_limit_bytes=48 << 20),
        cost_estimate=pl.CostEstimate(
            flops=12 * total * width * cols, bytes_accessed=16 << 20, transcendentals=0
        ),
        name="unproject",
    )(d_q, d_k, d_v, normed, gain, w_qk, w_v)


def head_mask(rows, h, heads, width, dtype=BF16):
    lane=lax.broadcasted_iota(jnp.int32,(rows,width),1)
    real=heads*HEAD_DIM
    m=((lane>=h*HEAD_DIM)&(lane<(h+1)*HEAD_DIM))|((lane>=real+3*h)&(lane<real+3*h+3))
    return m

def doc_start(meta, ndocs, t):
    def step(j,c):
        cum,best=c
        best=jnp.where(cum<=t,cum,best)
        return cum+meta[1+j],best
    return lax.fori_loop(0,ndocs,step,(jnp.int32(0),jnp.int32(0)))[1]

def doc_end(meta, ndocs, t):
    def step(j,c):
        cum,best,found=c
        cum=cum+meta[1+j]
        take=(cum>t)&(found==0)
        return cum,jnp.where(take,cum,best),jnp.where(take,1,found)
    return lax.fori_loop(0,ndocs,step,(jnp.int32(0),jnp.int32(0),jnp.int32(0)))[1]

def starts_vec(meta, ndocs, t):
    def step(j,c):
        cum,best=c
        return cum+meta[1+j],jnp.where(cum<=t,cum,best)
    return lax.fori_loop(0,ndocs,step,(jnp.int32(0),jnp.zeros(t.shape,jnp.int32)))[1]

def ends_vec(meta, ndocs, t):
    def step(j,c):
        cum,best=c
        ln=meta[1+j]
        return cum+ln,jnp.where(cum<=t,cum+ln,best)
    return lax.fori_loop(0,ndocs,step,(jnp.int32(0),jnp.zeros(t.shape,jnp.int32)))[1]

def widened(columns, heads):
    rows, width = columns.shape
    ones = jnp.ones((rows, SPLITS * heads), BF16)
    empty = jnp.zeros((rows, WIDTH - width - SPLITS * heads), BF16)
    return jnp.concatenate([columns, ones, empty], axis=1)


def unpack_rows(packed, heads):
    pair = 2 * HEAD_DIM
    key = jnp.concatenate([packed[:, :pair], packed[:, 2 * pair : 2 * pair + HEAD_DIM]], axis=1)
    value = jnp.concatenate([packed[:, pair : 2 * pair], packed[:, 2 * pair + HEAD_DIM :]], axis=1)
    return widened(key, heads), widened(value, heads)


def build_window(heads, earlier, own, keys, values, step=512):
    block = own.shape[0]
    for j in range(earlier.shape[0] + 1):
        source = own if j == earlier.shape[0] else earlier.at[j]

        @pl.loop(0, block // step)
        def _(i):
            key, value = unpack_rows(source[pl.ds(i * step, step), :], heads)
            at = pl.ds(j * block + i * step, step)
            keys[at, :] = key
            values[at, :] = value


def three(lo,a,b,hi,body):
    lax.fori_loop(lo,a,lambda j,_: body(j,True),None)
    lax.fori_loop(a,b,lambda j,_: body(j,False),None)
    lax.fori_loop(b,hi,lambda j,_: body(j,True),None)

def fwd_kernel(heads, ndocs, tq, tk, meta, q_ref, earlier, own, mix_ref, wide_ref,
               k_ref, v_ref, qh, m_ref, acc_ref):
    i = pl.program_id(0)
    width = q_ref.shape[1]
    real = heads * HEAD_DIM
    base = meta[0]
    wbase = base - earlier.shape[0] * earlier.shape[1]

    @pl.when(i == 0)
    def _():
        build_window(heads, earlier, own, k_ref, v_ref)

    t0 = base + i * tq
    lo = (doc_start(meta, ndocs, t0) - wbase) // tk
    f0 = (doc_start(meta, ndocs, t0 + tq - 1) - wbase + tk - 1) // tk
    f1 = (t0 - wbase) // tk
    hi = (t0 + tq - 1 - wbase) // tk + 1
    f0 = jnp.minimum(f0, f1)
    q = q_ref[...]
    trow = t0 + lax.broadcasted_iota(jnp.int32, (tq, 128), 0)
    srow = starts_vec(meta, ndocs, trow)
    lane = lax.broadcasted_iota(jnp.int32, (tq, width), 1)

    def visible(off):
        u = wbase + off + lax.broadcasted_iota(jnp.int32, (tq, tk), 1)
        return (u >= srow[:, :1]) & (u <= trow[:, :1])

    def with_parts(values):
        wide = q.astype(F32)
        for h in range(heads):
            for c, piece in enumerate(split_parts(values[h])):
                wide = jnp.where(lane == real + SPLITS * h + c, piece, wide)
        return wide.astype(BF16)

    def finish(shifts):
        acc = acc_ref[...]
        out = jnp.zeros((tq, width), F32)
        negated = []
        for h in range(heads):
            total = acc[:, real + SPLITS * h : real + SPLITS * h + 1]
            out = jnp.where(head_mask(tq, h, heads, width), acc / total, out)
            negated.append(-(shifts[h] + jnp.log(total)))
        mix_ref[0] = out[:, :real].astype(BF16)
        wide_ref[...] = with_parts(negated)

    itself = q.astype(F32) * k_ref[pl.ds(pl.multiple_of(t0 - wbase, tq), tq), :].astype(F32)
    shifts = [
        jnp.sum(jnp.where(head_mask(tq, h, heads, width), itself, 0.0), axis=1, keepdims=True)
        for h in range(heads)
    ]
    shifted = with_parts([-x for x in shifts])
    for h in range(heads):
        qh[h] = jnp.where(head_mask(tq, h, heads, width), shifted, jnp.zeros_like(q))
    acc_ref[...] = jnp.zeros_like(acc_ref)

    def quick(j, masked):
        off = pl.multiple_of(j * tk, tk)
        k = k_ref[pl.ds(off, tk), :]
        v = v_ref[pl.ds(off, tk), :]
        if masked:
            vis = visible(off)
        pv = None
        for h in range(heads):
            p = jnp.exp(dotf(qh[h], k, NT))
            if masked:
                p = jnp.where(vis, p, 0.0)
            vh = jnp.where(head_mask(tk, h, heads, width), v, jnp.zeros_like(v))
            d = dotf(p.astype(BF16), vh)
            pv = d if pv is None else pv + d
        acc_ref[...] += pv

    three(lo, f0, f1, hi, quick)
    finish(shifts)
    sums = jnp.where(lane >= real, acc_ref[...], 0.0)
    fits = jnp.max(jnp.where(sums < 1e30, 0.0, 1.0)) == 0.0

    @pl.when(jnp.logical_not(fits))
    def _():
        for h in range(heads):
            qh[h] = jnp.where(head_mask(tq, h, heads, width), q, jnp.zeros_like(q))
            m_ref[h] = jnp.full((tq, 128), EXCLUDED, F32)
        acc_ref[...] = jnp.zeros_like(acc_ref)

        def body(j, carry):
            off = pl.multiple_of(j * tk, tk)
            k = k_ref[pl.ds(off, tk), :]
            v = v_ref[pl.ds(off, tk), :]
            vis = visible(off)
            pv = None
            scale = jnp.ones((tq, width), F32)
            for h in range(heads):
                s = jnp.where(vis, dotf(qh[h], k, NT), EXCLUDED)
                old = m_ref[h][:, :1]
                new = jnp.maximum(old, jnp.max(s, axis=1, keepdims=True))
                m_ref[h] = jnp.broadcast_to(new, (tq, 128))
                scale = jnp.where(head_mask(tq, h, heads, width), jnp.exp(old - new), scale)
                vh = jnp.where(head_mask(tk, h, heads, width), v, jnp.zeros_like(v))
                d = dotf(jnp.exp(s - new).astype(BF16), vh)
                pv = d if pv is None else pv + d
            acc_ref[...] = acc_ref[...] * scale + pv
            return carry

        lax.fori_loop(lo, hi, body, 0)
        finish([m_ref[h][:, :1] for h in range(heads)])


def whole_of(array):
    return pl.BlockSpec(
        array.shape, lambda i: (0,) * array.ndim, pipeline_mode=pl.Buffered(1)
    )


SCALARS = pl.BlockSpec(memory_space=pltpu.SMEM)


def attention_fwd(meta, q, earlier, own, heads, tq, tk):
    block, width = q.shape
    window = block * (1 + earlier.shape[0])
    ndocs = meta.shape[0] - 1
    return pl.pallas_call(
        functools.partial(fwd_kernel, heads, ndocs, tq, tk),
        grid=(block // tq,),
        in_specs=[
            SCALARS,
            pl.BlockSpec((tq, width), lambda i: (i, 0)),
            whole_of(earlier),
            whole_of(own),
        ],
        out_specs=[
            pl.BlockSpec((1, tq, heads * HEAD_DIM), lambda i: (i, 0, 0)),
            pl.BlockSpec((tq, width), lambda i: (i, 0)),
        ],
        out_shape=[
            jax.ShapeDtypeStruct((block // tq, tq, heads * HEAD_DIM), BF16),
            jax.ShapeDtypeStruct((block, width), BF16),
        ],
        scratch_shapes=[
            pltpu.VMEM((window, width), BF16),
            pltpu.VMEM((window, width), BF16),
            pltpu.VMEM((heads, tq, width), BF16),
            pltpu.VMEM((heads, tq, 128), F32),
            pltpu.VMEM((tq, width), F32),
        ],
        compiler_params=pltpu.CompilerParams(vmem_limit_bytes=56 << 20),
        cost_estimate=pl.CostEstimate(
            flops=30_000_000_000, bytes_accessed=12 << 20, transcendentals=20_000_000
        ),
        name="attn_fwd",
    )(meta, q, earlier, own)


def dq_kernel(heads, ndocs, tq, tk, meta, q_ref, do_ref, earlier, own, dq_ref,
              k_ref, v_ref, qh, doh, acc_ref):
    i = pl.program_id(0)
    width = q_ref.shape[1]
    real = heads * HEAD_DIM
    base = meta[0]
    wbase = base - earlier.shape[0] * earlier.shape[1]

    @pl.when(i == 0)
    def _():
        build_window(heads, earlier, own, k_ref, v_ref)

    t0 = base + i * tq
    lo = (doc_start(meta, ndocs, t0) - wbase) // tk
    f0 = (doc_start(meta, ndocs, t0 + tq - 1) - wbase + tk - 1) // tk
    f1 = (t0 - wbase) // tk
    hi = (t0 + tq - 1 - wbase) // tk + 1
    f0 = jnp.minimum(f0, f1)
    q = q_ref[...]
    do = do_ref[...]
    for h in range(heads):
        hm = head_mask(tq, h, heads, width)
        qh[h] = jnp.where(hm, q, jnp.zeros_like(q))
        doh[h] = jnp.where(hm, do, jnp.zeros_like(do))
    acc_ref[...] = jnp.zeros_like(acc_ref)
    trow = t0 + lax.broadcasted_iota(jnp.int32, (tq, 128), 0)
    srow = starts_vec(meta, ndocs, trow)

    def body(j, masked):
        off = pl.multiple_of(j * tk, tk)
        k = k_ref[pl.ds(off, tk), :]
        v = v_ref[pl.ds(off, tk), :]
        if masked:
            u = wbase + off + lax.broadcasted_iota(jnp.int32, (tq, tk), 1)
            vis = (u >= srow[:, :1]) & (u <= trow[:, :1])
        tot = None
        for h in range(heads):
            p = jnp.exp(dotf(qh[h], k, NT))
            if masked:
                p = jnp.where(vis, p, 0.0)
            ds = (p * dotf(doh[h], v, NT)).astype(BF16)
            kh = jnp.where(head_mask(tk, h, heads, width), k, jnp.zeros_like(k))
            d = dotf(ds, kh)
            tot = d if tot is None else tot + d
        acc_ref[...] += tot

    three(lo, f0, f1, hi, body)
    dq_ref[...] = (acc_ref[...] * (HEAD_DIM**-0.5)).astype(BF16)[:, :real]


def attention_dq(meta, q, do, earlier, own, heads, tq, tk):
    block, width = q.shape
    window = block * (1 + earlier.shape[0])
    ndocs = meta.shape[0] - 1
    row = lambda w: pl.BlockSpec((tq, w), lambda i: (i, 0))
    return pl.pallas_call(
        functools.partial(dq_kernel, heads, ndocs, tq, tk),
        grid=(block // tq,),
        in_specs=[SCALARS, row(width), row(width), whole_of(earlier), whole_of(own)],
        out_specs=row(heads * HEAD_DIM),
        out_shape=jax.ShapeDtypeStruct((block, heads * HEAD_DIM), BF16),
        scratch_shapes=[pltpu.VMEM((window, width), BF16)] * 2
        + [pltpu.VMEM((heads, tq, width), BF16)] * 2
        + [pltpu.VMEM((tq, width), F32)],
        compiler_params=pltpu.CompilerParams(vmem_limit_bytes=56 << 20),
        cost_estimate=pl.CostEstimate(
            flops=45_000_000_000, bytes_accessed=12 << 20, transcendentals=20_000_000
        ),
        name="attn_dq",
    )(meta, q, do, earlier, own)


def dkv_kernel(heads, ndocs, tq, tk, meta, own, q_parts, do_parts, dk_ref, dv_ref,
               q_ref, do_ref, kh, vh, dk_acc, dv_acc, sems):
    i = pl.program_id(0)
    width = q_ref.shape[1]
    real = heads * HEAD_DIM
    base = meta[0]

    @pl.when(i == 0)
    def _():
        copies = []
        for k, (parts, target) in enumerate(((q_parts, q_ref), (do_parts, do_ref))):
            row = 0
            for j, part in enumerate(parts):
                at = target.at[pl.ds(row, part.shape[0])]
                copies.append(pltpu.make_async_copy(part, at, sems.at[k, j]))
                row += part.shape[0]
        for copy in copies:
            copy.start()
        for copy in copies:
            copy.wait()

    u0 = base + i * tk
    lo = (u0 - base) // tq
    f0 = (u0 + tk - 1 - base + tq - 1) // tq
    e_first = doc_end(meta, ndocs, u0)
    e_last = doc_end(meta, ndocs, u0 + tk - 1)
    f1 = (e_first - base) // tq
    hi = (e_last - 1 - base) // tq + 1
    f0 = jnp.minimum(f0, hi)
    f1 = jnp.clip(f1, f0, hi)
    k, v = unpack_rows(own[...], heads)
    for h in range(heads):
        hm = head_mask(tk, h, heads, width)
        kh[h] = jnp.where(hm, k, jnp.zeros_like(k))
        vh[h] = jnp.where(hm, v, jnp.zeros_like(v))
    dk_acc[...] = jnp.zeros_like(dk_acc)
    dv_acc[...] = jnp.zeros_like(dv_acc)
    urow = u0 + lax.broadcasted_iota(jnp.int32, (tk, 128), 0)
    erow = ends_vec(meta, ndocs, urow)

    def body(j, masked):
        off = pl.multiple_of(j * tq, tq)
        q = q_ref[pl.ds(off, tq), :]
        do = do_ref[pl.ds(off, tq), :]
        if masked:
            t = base + off + lax.broadcasted_iota(jnp.int32, (tk, tq), 1)
            vis = (t >= urow[:, :1]) & (t < erow[:, :1])
        a = None
        b = None
        for h in range(heads):
            p = jnp.exp(dotf(kh[h], q, NT))
            if masked:
                p = jnp.where(vis, p, 0.0)
            ds = (p * dotf(vh[h], do, NT)).astype(BF16)
            hm = head_mask(tq, h, heads, width)
            d = dotf(p.astype(BF16), jnp.where(hm, do, jnp.zeros_like(do)))
            a = d if a is None else a + d
            d = dotf(ds, jnp.where(hm, q, jnp.zeros_like(q)))
            b = d if b is None else b + d
        dv_acc[...] += a
        dk_acc[...] += b

    three(lo, f0, f1, hi, body)
    dk_ref[...] = dk_acc[...].astype(BF16)[:, :real]
    dv_ref[...] = dv_acc[...].astype(BF16)[:, :real]


def attention_dkv(meta, own, q_parts, do_parts, heads, tq, tk):
    block, width = q_parts[0].shape
    window = sum(part.shape[0] for part in q_parts)
    ndocs = meta.shape[0] - 1
    row = lambda w: pl.BlockSpec((tk, w), lambda i: (i, 0))
    return pl.pallas_call(
        functools.partial(dkv_kernel, heads, ndocs, tq, tk),
        grid=(block // tk,),
        in_specs=[SCALARS, row(own.shape[1]), [ANY] * len(q_parts), [ANY] * len(do_parts)],
        out_specs=[row(heads * HEAD_DIM)] * 2,
        out_shape=[jax.ShapeDtypeStruct((block, heads * HEAD_DIM), BF16)] * 2,
        scratch_shapes=[pltpu.VMEM((window, width), BF16)] * 2
        + [pltpu.VMEM((heads, tk, width), BF16)] * 2
        + [pltpu.VMEM((tk, width), F32)] * 2
        + [pltpu.SemaphoreType.DMA((2, len(do_parts)))],
        compiler_params=pltpu.CompilerParams(vmem_limit_bytes=56 << 20),
        cost_estimate=pl.CostEstimate(
            flops=60_000_000_000, bytes_accessed=12 << 20, transcendentals=20_000_000
        ),
        name="attn_dkv",
    )(meta, own, q_parts, do_parts)


def on_device(
    tokens, first_values, cotangent, w_query, w_key, w_value, w_out, w_up, w_down,
    gain_attn, gain_mlp, doc_lengths,
):
    width = tokens.shape[1]
    heads_of = lax.axis_size("head")
    nblk = lax.axis_size("blk")
    blk = lax.axis_index("blk")
    rows = tokens.shape[0]
    block = rows * heads_of
    heads = HEADS // heads_of
    cols = heads * HEAD_DIM
    part = width // nblk
    meta = jnp.concatenate([jnp.reshape(blk * block, (1,)).astype(jnp.int32), doc_lengths])

    up_cols = w_up.shape[1]
    rest = jnp.concatenate([w_up, w_down.T, w_out.T], axis=1)
    gains = jnp.stack([gain_attn, gain_mlp])[:, None, :]
    tok_all, first_all, qk_all, rest_own, _, v_all, gain_all = front(
        nblk, tokens, first_values, jnp.concatenate([w_query, w_key], axis=1), rest, w_value, gains
    )
    attn_gain = gain_all[:, 0].reshape(1, width)
    mlp_gain = gain_all[:, 1].reshape(1, width)
    w_qk = qk_all.reshape(width, 2 * cols)
    w_v = v_all.reshape(2, width, w_value.shape[1])
    normed, query, own = project(
        tok_all.reshape(block, width), first_all.reshape(block, width // 2), w_qk, w_v, attn_gain
    )
    earlier, gathered = halo(nblk, own, rest_own)
    mixed_parts, query_wide = attention_fwd(meta, query, earlier, own, heads, rows, 2 * rows)
    layer_output, grad_resid, grad_parts, gain_mlp_part, keep, give, query_later = middle(
        nblk, tokens, mixed_parts, cotangent, mlp_gain, rest_own, gathered, query_wide, up_cols
    )
    grad_wide = grad_parts.reshape(block, WIDTH)
    taken = lax.ppermute(give, "head", [(h, (h + 2) % heads_of) for h in range(heads_of)])

    grads_later = [grad_wide] + [
        lax.ppermute(grad_wide, "blk", [(i, i - d) for i in range(d, nblk)]) for d in (1, 2)
    ]
    queries_later = [query_wide, query_later.reshape(2 * block, WIDTH)]
    grad_query = attention_dq(meta, query_wide, grad_wide, earlier, own, heads, rows, rows)
    taken, keep, grad_query = lax.optimization_barrier((taken, keep, grad_query))
    keep, give = pair_sum(keep, taken)
    taken = lax.ppermute(give, "blk", [(i, i + 1 - 2 * (i % 2)) for i in range(nblk)])
    keep, own = lax.optimization_barrier((keep, own))
    grad_key, grad_value = attention_dkv(
        meta, own, queries_later, grads_later, heads, rows, rows
    )
    grad_normed, part_weights, gain_attn_part = unproject(
        nblk, grad_query, grad_key, grad_value, normed, attn_gain, w_qk, w_v
    )
    gain_parts = jnp.concatenate([gain_attn_part, gain_mlp_part]).reshape(2, nblk, 1, part)
    grad_norm_sum, final_qk, final_value, first_parts, gain_sums, reduced = tail(
        nblk,
        grad_normed.reshape(heads_of, rows, width),
        part_weights,
        grad_value.reshape(heads_of, rows, cols),
        gain_parts.transpose(1, 0, 2, 3),
        keep,
        taken,
        cols,
    )
    xhat, scale1 = statistics(tokens.astype(F32))
    grad_tokens = grad_resid + norm_back(grad_norm_sum, xhat, scale1, attn_gain)
    grad_first = jnp.concatenate([first_parts[0], first_parts[1]], axis=1).astype(F32)
    return (
        layer_output,
        grad_tokens,
        grad_first,
        final_qk[:, :cols],
        final_qk[:, cols:],
        final_value,
        reduced[:, 2 * up_cols :].T,
        reduced[:, :up_cols],
        reduced[:, up_cols : 2 * up_cols].T,
        gain_sums[0].reshape(part),
        gain_sums[1].reshape(part),
    )


def solution(mesh):
    rows = P(("blk", "head"), None)
    specs = (P("blk", "head"),) * 3 + (P("head", "blk"), P("blk", "head"), P("head", "blk"))
    gains = (P("blk"), P("blk"))
    return jax.shard_map(
        on_device,
        mesh=mesh,
        in_specs=(rows,) * 3 + specs + gains + (P(),),
        out_specs=(rows,) * 3 + specs + gains,
        check_vma=False,
    )
```

```python
import functools

import jax
import jax.numpy as jnp
from jax import lax
from jax.experimental import pallas as pl
from jax.experimental.pallas import tpu as pltpu
from jax.sharding import PartitionSpec as P

HEADS = 12
HEAD_DIM = 64
DOC_MAX = 4096
EPSILON = 1e-05
GELU_SCALE = 0.7978845608028654
EXCLUDED = -1e30
WIDTH = 256
SPLITS = 3
BF16 = jnp.bfloat16
F32 = jnp.float32
MESH = pl.DeviceIdType.MESH
ANY = pl.BlockSpec(memory_space=pl.ANY)
WHOLE = pl.BlockSpec(memory_space=pltpu.VMEM)
NT = (((1,), (1,)), ((), ()))
TN = (((0,), (0,)), ((), ()))


def dotf(left, right, dims=None):
    if dims is None:
        dims = (((1,), (0,)), ((), ()))
    return lax.dot_general(left, right, dims, preferred_element_type=F32)


def remote(src, dst, send_sem, recv_sem, head, blk):
    return pltpu.make_async_remote_copy(
        src_ref=src,
        dst_ref=dst,
        send_sem=send_sem,
        recv_sem=recv_sem,
        device_id={"head": head, "blk": blk},
        device_id_type=MESH,
    )


def greet(partners):
    barrier = pltpu.get_barrier_semaphore()
    for head, blk in partners:
        pl.semaphore_signal(
            barrier, inc=1, device_id={"head": head, "blk": blk}, device_id_type=MESH
        )
    pl.semaphore_wait(barrier, len(partners))


def xor(value, bit):
    return value + bit - 2 * bit * (lax.div(value, bit) % 2)


def partners_of(head, blk, nblk, heads=True, blks=True):
    found = []
    if heads:
        found += [(xor(head, 1), blk), (xor(head, 2), blk), (3 - head, blk)]
    if blks:
        found += [(head, lax.rem(blk + d, nblk)) for d in range(1, nblk)]
    return found


class Line:
    def __init__(self, nblk, head, blk, sources, targets, up, down, across):
        self.half, self.head, self.blk = nblk // 2, head, blk
        self.place, self.parity = lax.div(blk, 2), lax.rem(blk, 2)
        self.sources, self.targets = sources, targets
        self.sems = {"up": up, "down": down, "across": across}

    def copies(self, way, origin, step, fresh=False):
        slot = 2 * origin + self.parity
        to = {
            "up": lax.rem(self.blk + 2, 2 * self.half),
            "down": lax.rem(self.blk + 2 * self.half - 2, 2 * self.half),
            "across": self.blk + 1 - 2 * self.parity,
        }[way]
        send, recv = self.sems[way]
        return [
            remote(
                source if fresh else target.at[slot],
                target.at[slot],
                send.at[k, step],
                recv.at[k, step],
                self.head,
                to,
            )
            for k, (source, target) in enumerate(zip(self.sources, self.targets))
        ]

    def landing(self, way, origin, step, parity=None):
        slot = 2 * origin + (self.parity if parity is None else parity)
        send, recv = self.sems[way]
        other = self.blk + 1 - 2 * self.parity
        return [
            remote(
                target.at[slot], target.at[slot], send.at[k, step], recv.at[k, step], self.head, other
            )
            for k, target in enumerate(self.targets)
        ]

    def each(self, condition, copies, verb):
        @pl.when(condition)
        def _():
            for copy in copies():
                getattr(copy, verb)()

    def begin(self):
        self.each(self.place + 1 < self.half, lambda: self.copies("up", self.place, 0, True), "start")
        self.each(self.place > 0, lambda: self.copies("down", self.place, 0, True), "start")
        for copy in self.copies("across", self.place, self.place, True):
            copy.start()

    def step(self, s):
        low, high = self.place - 1 - s, self.place + 1 + s
        self.each(low >= 0, lambda: self.landing("up", low, s), "wait_recv")
        if s + 1 < self.half - 1:
            self.each(
                (low >= 0) & (self.place + 1 < self.half),
                lambda: self.copies("up", low, s + 1),
                "start",
            )
        self.each(low >= 0, lambda: self.copies("across", low, low), "start")
        self.each(high < self.half, lambda: self.landing("down", high, s), "wait_recv")
        if s + 1 < self.half - 1:
            self.each(
                (high < self.half) & (self.place > 0),
                lambda: self.copies("down", high, s + 1),
                "start",
            )
        self.each(high < self.half, lambda: self.copies("across", high, high), "start")

    def arrived(self):
        for copy in self.landing("across", self.place, self.place, 1 - self.parity):
            copy.wait_recv()

    def end(self):
        for o in range(self.half):
            self.each(
                self.place != o, lambda: self.landing("across", o, o, 1 - self.parity), "wait_recv"
            )
            for copy in self.copies("across", o, o):
                copy.wait_send()
        for s in range(self.half - 1):
            self.each(
                (self.place - s >= 0) & (self.place + 1 < self.half),
                lambda: self.copies("up", self.place - s, s),
                "wait_send",
            )
            self.each(
                (self.place + s < self.half) & (self.place > 0),
                lambda: self.copies("down", self.place + s, s),
                "wait_send",
            )


def front_kernel(
    nblk, pieces, tok, first, w_q, w_k, w_v, w_up, w_down, w_out, gain_a, gain_m,
    tok_all, first_all, qk_all, rest_all, v_own, v_all, gain_all,
    w_qk, w_rest, gains,
    own_sem, send_x, recv_x, send_s, recv_s, send_f, recv_f, send_w, recv_w, send_v, recv_v,
    send_u, recv_u, send_d, recv_d, send_y, recv_y, send_r, recv_r,
):
    head, blk = lax.axis_index("head"), lax.axis_index("blk")
    side, core, far = xor(head, 2), xor(head, 1), 3 - head
    greet(partners_of(head, blk, nblk))
    moved = [(tok, tok_all), (first, first_all)]
    weights = [(w_v, v_own), (gains, gain_all)]
    large = [(w_qk, qk_all), (w_rest, rest_all.at[head])]
    rows = tok.shape[0] // pieces
    line = Line(
        nblk, head, blk, [w_qk, w_rest], [qk_all, rest_all.at[head]],
        (send_u, recv_u), (send_d, recv_d), (send_y, recv_y),
    )

    def part(ref, p):
        return ref.at[pl.ds(p * rows, rows)]

    def hop(sems, k, p, source, slot, target):
        dst = part(moved[k][1].at[slot], p)
        return remote(source, dst, sems[0].at[k, p], sems[1].at[k, p], target, blk)

    xs, ss, fs = (send_x, recv_x), (send_s, recv_s), (send_f, recv_f)
    order = [(k, p) for p in range(pieces) for k in range(2)]
    for k, p in order:
        hop(xs, k, p, part(moved[k][0], p), head, side).start()
    cols, inner = w_q.shape[1], w_up.shape[1]
    w_qk[:, :cols] = w_q[...]
    w_qk[:, cols:] = w_k[...]
    w_rest[:, :inner] = w_up[...]
    w_rest[:, inner : 2 * inner] = w_down[...]
    w_rest[:, 2 * inner :] = w_out[...].T
    gains[0] = gain_a[...]
    gains[1] = gain_m[...]
    line.begin()
    pair = blk + 1 - 2 * lax.rem(blk, 2)

    def cross(n, source, slot):
        return remote(
            source, rest_all.at[head, slot], send_r.at[n], recv_r.at[n], side, blk
        )

    cross(0, w_rest, blk).start()

    def spread(d):
        to = lax.rem(blk + d, nblk)
        return [
            remote(src, dst.at[blk], send_w.at[i, d], recv_w.at[i, d], head, to)
            for i, (src, dst) in enumerate(weights)
        ]

    def from_peer(d):
        source = lax.rem(blk - d + nblk, nblk)
        return [
            remote(src, dst.at[source], send_w.at[i, d], recv_w.at[i, d], head, source)
            for i, (src, dst) in enumerate(weights)
        ]

    for d in range(1, nblk):
        for copy in spread(d):
            copy.start()
    for k, p in order:
        hop(ss, k, p, part(moved[k][0], p), head, core).start()
    local = [
        pltpu.make_async_copy(moved[k][0], moved[k][1].at[head], own_sem.at[k]) for k in range(2)
    ] + [
        pltpu.make_async_copy(src, dst.at[blk], own_sem.at[2 + i])
        for i, (src, dst) in enumerate(weights + large)
    ]
    for copy in local:
        copy.start()

    def pass_on(k, p):
        landed = part(moved[k][1].at[side], p)
        hop(xs, k, p, landed, side, side).wait_recv()
        hop(fs, k, p, landed, side, core).start()

    steps = nblk // 2 - 1
    for s in range(steps):
        line.step(s)
        if s == 0:
            line.arrived()
            cross(1, rest_all.at[head, pair], pair).start()
        for k, p in order[s * len(order) // steps : (s + 1) * len(order) // steps]:
            pass_on(k, p)
    for copy in local:
        copy.wait()
    for d in range(1, nblk):
        for copy in from_peer(d):
            copy.wait_recv()
    half, kind = lax.div(head, 2), lax.rem(head, 2)
    for i in range(2):
        target = half + 2 * i

        @pl.when(target == head)
        def _():
            pltpu.make_async_copy(v_own, v_all.at[kind], own_sem.at[6]).start()

        @pl.when(target != head)
        def _():
            remote(v_own, v_all.at[kind], send_v.at[i], recv_v.at[kind], target, blk).start()

    for k, p in order:
        hop(ss, k, p, part(moved[k][1].at[core], p), core, core).wait_recv()
        hop(fs, k, p, part(moved[k][1].at[far], p), far, core).wait_recv()
    for c in range(2):
        source = 2 * kind + c

        @pl.when(source == head)
        def _():
            pltpu.make_async_copy(v_own, v_all.at[c], own_sem.at[6]).wait()

        @pl.when(source != head)
        def _():
            remote(v_own, v_all.at[c], send_v.at[0], recv_v.at[c], source, blk).wait_recv()

    for i in range(2):
        target = half + 2 * i

        @pl.when(target != head)
        def _():
            remote(v_own, v_all.at[kind], send_v.at[i], recv_v.at[kind], target, blk).wait_send()

    for k, p in order:
        hop(xs, k, p, part(moved[k][0], p), head, side).wait_send()
        hop(ss, k, p, part(moved[k][0], p), head, core).wait_send()
        hop(fs, k, p, part(moved[k][1].at[side], p), side, core).wait_send()
    for d in range(1, nblk):
        for copy in spread(d):
            copy.wait_send()
    line.end()
    for n, slot in enumerate((blk, pair)):
        cross(n, w_rest, slot).wait()


def front(nblk, tok, first, w_q, w_k, w_v, w_up, w_down, w_out, gain_a, gain_m, pieces=4):
    def shape(lead, like):
        return jax.ShapeDtypeStruct(lead + like.shape, like.dtype)

    dma = pltpu.SemaphoreType.DMA
    part = w_up.shape[0]
    qk = jax.ShapeDtypeStruct((part, w_q.shape[1] + w_k.shape[1]), BF16)
    rest = jax.ShapeDtypeStruct((part, w_up.shape[1] + w_down.shape[1] + w_out.shape[0]), BF16)
    gains = jax.ShapeDtypeStruct((2,) + gain_a.shape, F32)
    return pl.pallas_call(
        functools.partial(front_kernel, nblk, pieces),
        out_shape=[
            shape((4,), tok),
            shape((4,), first),
            shape((nblk,), qk),
            shape((4, nblk), rest),
            shape((nblk,), w_v),
            shape((2, nblk), w_v),
            shape((nblk,), gains),
        ],
        in_specs=[WHOLE] * 10,
        out_specs=[ANY] * 7,
        scratch_shapes=[pltpu.VMEM(a.shape, a.dtype) for a in (qk, rest, gains)]
        + [dma((7,))]
        + [dma((2, pieces))] * 6
        + [dma((2, nblk))] * 2
        + [dma((2,))] * 2
        + [dma((2, nblk // 2))] * 6
        + [dma((2,))] * 2,
        compiler_params=pltpu.CompilerParams(collective_id=0, has_side_effects=True),
        name="front",
    )(tok, first, w_q, w_k, w_v, w_up, w_down, w_out, gain_a, gain_m)


def tail_kernel(
    nblk, pieces, cols, grad, weights, first, gains, kept, got, tok, resid, gain,
    out_grad, out_q, out_k, out_v, out_first, out_gain, out_up, out_down, out_out,
    first_got, rest_sum,
    core_buf, side_out, side_buf, pair_buf, line_out, line_in, v_sum, v_got,
    gain_buf, gain_sum, gain_got, up_out, up_in, down_out, down_in,
    own_sem, send_s, recv_s, send_x, recv_x, send_y, recv_y, send_l, recv_l,
    send_v, recv_v, send_f, recv_f, send_g, recv_g, send_h, recv_h, send_u, recv_u, send_d, recv_d,
):
    head, blk = lax.axis_index("head"), lax.axis_index("blk")
    side, core, far = xor(head, 2), xor(head, 1), 3 - head
    greet(partners_of(head, blk, nblk))
    rows = grad.shape[1] // pieces
    line, place, parity = nblk // 2, lax.div(blk, 2), lax.rem(blk, 2)
    pair = blk + 1 - 2 * parity
    above, below = lax.rem(blk + 2, nblk), lax.rem(blk + nblk - 2, nblk)

    def part(ref, p):
        return ref.at[pl.ds(p * rows, rows)]

    def to_core(i, p, slot):
        return remote(
            part(grad.at[slot], p), part(core_buf.at[i], p), send_s.at[i, p], recv_s.at[i, p],
            core, blk,
        )

    def to_side(p):
        return remote(
            part(side_out, p), part(side_buf, p), send_x.at[p], recv_x.at[p], side, blk
        )

    def sum_of(t):
        return kept[t].astype(F32) + got[t].astype(F32)

    def up_copy(t, to):
        return remote(up_out.at[t], up_in.at[t], send_u.at[t], recv_u.at[t], head, to)

    def down_copy(t, to):
        return remote(down_out.at[t], down_in.at[t], send_d.at[t], recv_d.at[t], head, to)

    def first_hops():
        for n in range(line - 1):
            t = line - 1 - n

            @pl.when((place == 0) & (place < t))
            def _():
                up_out[t] = sum_of(t).astype(BF16)
                up_copy(t, above).start()

            @pl.when((place == line - 1) & (place > n))
            def _():
                down_out[n] = sum_of(n).astype(BF16)
                down_copy(n, below).start()

    def next_hops(n):
        t = line - 1 - n

        @pl.when((place > 0) & (place < t))
        def _():
            up_copy(t, above).wait_recv()
            up_out[t] = (sum_of(t) + up_in[t].astype(F32)).astype(BF16)
            up_copy(t, above).start()

        @pl.when((place < line - 1) & (place > n))
        def _():
            down_copy(n, below).wait_recv()
            down_out[n] = (sum_of(n) + down_in[n].astype(F32)).astype(BF16)
            down_copy(n, below).start()

    for p in range(pieces):
        to_core(0, p, far).start()
    first_hops()
    for p in range(pieces):
        to_core(1, p, core).start()

    def across(n):
        return remote(
            weights.at[2 * n + 1 - parity], pair_buf.at[n], send_y.at[n], recv_y.at[n], head, pair
        )

    for n in range(line):
        across(n).start()
    half, kind = lax.div(head, 2), lax.rem(head, 2)

    def gain_to(d):
        to = lax.rem(blk + d, nblk)
        return remote(gains.at[to], gain_buf.at[blk], send_g.at[d], recv_g.at[d], head, to)

    def gain_from(d):
        source = lax.rem(blk - d + nblk, nblk)
        return remote(gains.at[0], gain_buf.at[source], send_g.at[d], recv_g.at[d], head, source)

    for d in range(1, nblk):
        gain_to(d).start()
    gain_buf[blk] = gains[blk]

    def first_copy(i, to, slot):
        return remote(first.at[to], first_got.at[slot], send_f.at[i], recv_f.at[slot], to, blk)

    @pl.when(half == 1)
    def _():
        for i, to in enumerate((core, side, far)):
            first_copy(i, to, kind).start()
        pltpu.make_async_copy(first.at[head], first_got.at[kind], own_sem).start()

    for p in range(pieces):
        to_core(0, p, far).wait_recv()
        part(side_out, p)[...] = (
            part(grad.at[side], p)[...].astype(F32) + part(core_buf.at[0], p)[...].astype(F32)
        ).astype(BF16)
        to_side(p).start()

    def along(d, to):
        return remote(
            line_out.at[to], line_in.at[d], send_l.at[d], recv_l.at[d], head, 2 * to + parity
        )

    next_hops(0)
    for n in range(line):
        across(n).wait_recv()
        line_out[n] = (
            weights[2 * n + parity].astype(F32) + pair_buf[n].astype(F32)
        ).astype(BF16)
    for d in range(1, line):
        along(d, lax.rem(place + d, line)).start()
    for d in range(1, nblk):
        gain_from(d).wait_recv()
    gain_sum[...] = jnp.sum(gain_buf[...], axis=0)
    peers = (core, side, far)

    def gain_copy(i, to):
        return remote(gain_sum, gain_got.at[i], send_h.at[i], recv_h.at[i], to, blk)

    for i, to in enumerate(peers):
        gain_copy(i, to).start()
    for n in range(1, line - 1):
        next_hops(n)
    total = line_out[place].astype(F32)
    for d in range(1, line):
        along(d, lax.rem(place - d + line, line)).wait_recv()
        total = total + line_in[d].astype(F32)
    out_q[...] = total[:, :cols]
    out_k[...] = total[:, cols : 2 * cols]
    v_sum[0] = total[:, 2 * cols : 2 * cols + cols // 2]
    v_sum[1] = total[:, 2 * cols + cols // 2 : 3 * cols]

    def give(c, to):
        return remote(v_sum.at[c], v_got, send_v.at[c], recv_v.at[0], to, blk)

    for c in range(2):
        to = 2 * head + c

        @pl.when((half == 0) & (to != head))
        def _():
            give(c, to).start()

    for p in range(pieces):
        to_core(1, p, core).wait_recv()
        to_side(p).wait_recv()
        norm_grad = (
            part(grad.at[head], p)[...].astype(F32)
            + part(core_buf.at[1], p)[...].astype(F32)
            + part(side_buf, p)[...].astype(F32)
        )
        xhat, scale = statistics(part(tok, p)[...].astype(F32))
        part(out_grad, p)[...] = part(resid, p)[...] + norm_back(norm_grad, xhat, scale, gain[...])
    rest_sum[...] = sum_of(place)
    for t in range(line):

        @pl.when((place == t) & (place > 0))
        def _():
            up_copy(t, above).wait_recv()
            rest_sum[...] += up_in[t].astype(F32)

        @pl.when((place == t) & (place < line - 1))
        def _():
            down_copy(t, below).wait_recv()
            rest_sum[...] += down_in[t].astype(F32)

    inner = out_up.shape[1]
    out_up[...] = rest_sum[:, :inner]
    out_down[...] = rest_sum[:, inner : 2 * inner]
    out_out[...] = rest_sum[:, 2 * inner :].T
    for i, to in enumerate(peers):
        gain_copy(i, to).wait_recv()
    out_gain[...] = gain_sum[...] + gain_got[0] + gain_got[1] + gain_got[2]

    @pl.when(head == 0)
    def _():
        out_v[...] = v_sum[0]

    @pl.when(head != 0)
    def _():
        give(0, half).wait_recv()
        out_v[...] = v_got[...]

    for slot in range(2):

        @pl.when(head == 2 + slot)
        def _():
            pltpu.make_async_copy(first.at[head], first_got.at[slot], own_sem).wait()

        @pl.when(head != 2 + slot)
        def _():
            first_copy(0, 2 + slot, slot).wait_recv()

    out_first[...] = jnp.concatenate([first_got[0], first_got[1]], axis=1).astype(F32)

    @pl.when(half == 1)
    def _():
        for i, to in enumerate((core, side, far)):
            first_copy(i, to, kind).wait_send()

    for c in range(2):
        to = 2 * head + c

        @pl.when((half == 0) & (to != head))
        def _():
            give(c, to).wait_send()

    for i, to in enumerate(peers):
        gain_copy(i, to).wait_send()
    for p in range(pieces):
        to_core(0, p, far).wait_send()
        to_core(1, p, core).wait_send()
        to_side(p).wait_send()
    for d in range(1, nblk):
        gain_to(d).wait_send()
    for n in range(line):
        across(n).wait_send()
    for d in range(1, line):
        along(d, lax.rem(place + d, line)).wait_send()
    for t in range(line):

        @pl.when(place < t)
        def _():
            up_copy(t, above).wait_send()

        @pl.when(place > t)
        def _():
            down_copy(t, below).wait_send()


def tail(nblk, grad, weights, first, gains, kept, got, tok, resid, gain, cols, inner, pieces=4):
    dma = pltpu.SemaphoreType.DMA
    row, part = grad.shape[1:], weights.shape[1]
    half, line = (part, cols // 2), nblk // 2
    piece = (2, pieces)
    vmem = lambda *shape: pltpu.VMEM(shape, BF16)
    return pl.pallas_call(
        functools.partial(tail_kernel, nblk, pieces, cols),
        out_shape=[
            jax.ShapeDtypeStruct(row, F32),
            jax.ShapeDtypeStruct((part, cols), F32),
            jax.ShapeDtypeStruct((part, cols), F32),
            jax.ShapeDtypeStruct(half, F32),
            jax.ShapeDtypeStruct((row[0], 2 * cols), F32),
            jax.ShapeDtypeStruct(gains.shape[1:], F32),
            jax.ShapeDtypeStruct((part, inner), F32),
            jax.ShapeDtypeStruct((part, inner), F32),
            jax.ShapeDtypeStruct((cols, part), F32),
        ],
        in_specs=[WHOLE] * 9,
        out_specs=[WHOLE] * 9,
        scratch_shapes=[
            vmem(2, *first.shape[1:]), pltpu.VMEM(kept.shape[1:], F32),
            vmem(2, *row), vmem(*row), vmem(*row),
            vmem(line, *weights.shape[1:]), vmem(line, *weights.shape[1:]),
            vmem(line, *weights.shape[1:]),
            pltpu.VMEM((2,) + half, F32),
            pltpu.VMEM(half, F32),
            pltpu.VMEM(gains.shape, F32),
            pltpu.VMEM(gains.shape[1:], F32),
            pltpu.VMEM((3,) + gains.shape[1:], F32),
            vmem(*kept.shape), vmem(*kept.shape), vmem(*kept.shape), vmem(*kept.shape),
            dma,
            dma(piece), dma(piece),
            dma((pieces,)), dma((pieces,)),
            dma((line,)), dma((line,)), dma((line,)), dma((line,)),
            dma((2,)), dma((1,)),
            dma((3,)), dma((2,)),
            dma((nblk,)), dma((nblk,)),
            dma((3,)), dma((3,)),
            dma((line,)), dma((line,)), dma((line,)), dma((line,)),
        ],
        compiler_params=pltpu.CompilerParams(
            collective_id=4, has_side_effects=True, vmem_limit_bytes=60 << 20
        ),
        name="tail",
    )(grad, weights, first, gains, kept, got, tok, resid, gain)


def statistics(values):
    center = values - jnp.mean(values, axis=-1, keepdims=True)
    scale = lax.rsqrt(jnp.mean(jnp.square(center), axis=-1, keepdims=True) + EPSILON)
    return center * scale, scale


def norm_back(grad, xhat, scale, gain):
    eg = grad * gain
    return scale * (
        eg
        - jnp.mean(eg, axis=-1, keepdims=True)
        - xhat * jnp.mean(eg * xhat, axis=-1, keepdims=True)
    )


def split_parts(values):
    high = values.astype(BF16).astype(F32)
    middle = (values - high).astype(BF16).astype(F32)
    return high, middle, values - high - middle


def project_kernel(
    nblk, pieces, tok, first, w_qk, w_v, gain, rest_in,
    normed, query, own, near_far, rest,
    tok_buf, first_buf, weight, load_sem, normed_sem, normed_buf,
    send_z, recv_z, send_y, recv_y, send_x, recv_x, send_c, recv_c, send_f, recv_f,
):
    head, blk = lax.axis_index("head"), lax.axis_index("blk")
    side, core, beyond = xor(head, 2), xor(head, 1), 3 - head
    odd = lax.rem(blk, 2)
    near = blk + 1 - 2 * odd
    up, down = lax.rem(blk + 2, nblk), lax.rem(blk + nblk - 2, nblk)
    chunks = tok.shape[0]
    rows = tok.shape[1]
    loads = [
        [
            pltpu.make_async_copy(tok.at[t], tok_buf.at[t], load_sem.at[0, t]),
            pltpu.make_async_copy(first.at[t], first_buf.at[t], load_sem.at[1, t]),
        ]
        for t in range(chunks)
    ]
    for copies in loads:
        for copy in copies:
            copy.start()
    greet(partners_of(head, blk, nblk, blks=False) + [(head, near), (head, up), (head, down)])
    step = own.shape[0] // pieces

    def slab(ref, p):
        return ref.at[pl.ds(p * step, step)]

    def far_copy(p, to):
        return remote(slab(own, p), slab(near_far.at[0], p), send_z.at[p], recv_z.at[p], head, to)

    def near_copy(p, src):
        return remote(src, slab(near_far.at[1], p), send_y.at[p], recv_y.at[p], head, near)

    def chunk(sems, n, slot, to):
        b = lax.rem(lax.div(blk, 2) * 2 + n, nblk)
        return remote(rest.at[slot, b], rest.at[slot, b], sems[0].at[n], sems[1].at[n], to, blk)

    xs, cs, fs = (send_x, recv_x), (send_c, recv_c), (send_f, recv_f)
    for n in range(2, nblk):
        chunk(xs, n, head, side).start()
    for n in range(nblk):
        chunk(cs, n, head, core).start()
    for n in range(2):
        chunk(fs, n, side, core).start()

    size = HEAD_DIM
    pair = 2 * size
    cols = 3 * size
    width = tok.shape[2]
    key, fresh = w_qk[:, cols:], jnp.concatenate([w_v[0], w_v[1]], axis=1)
    weight[:, :pair] = key[:, :pair]
    weight[:, pair : 2 * pair] = fresh[:, :pair]
    weight[:, 2 * pair : 3 * pair] = jnp.concatenate([key[:, pair:], fresh[:, pair:]], axis=1)
    weight[:, 3 * pair :] = jnp.concatenate(
        [w_qk[:, :cols], jnp.zeros((width, WIDTH - cols), BF16)], axis=1
    )
    stores = []
    for t in range(chunks):
        for copy in loads[t]:
            copy.wait()
        xhat, _ = statistics(tok_buf[t].astype(F32))
        part = (xhat * gain[...]).astype(BF16)
        normed_buf[t] = part
        stores.append(
            pltpu.make_async_copy(
                normed_buf.at[t], normed.at[pl.ds(t * rows, rows)], normed_sem.at[t]
            )
        )
        stores[-1].start()
        out = dotf(part, weight[...])
        at = pl.ds(t * rows, rows)
        query[at, :] = (out[:, 3 * pair :].astype(BF16).astype(F32) * size**-0.5).astype(BF16)
        done = out[:, : 3 * pair].astype(BF16)
        given = first_buf[t]
        kept = jnp.where(lax.rem(head, 2) == 0, given[:, :cols], given[:, cols:])
        other = jnp.concatenate(
            [done[:, :pair], kept[:, :pair], done[:, 2 * pair : 2 * pair + size], kept[:, pair:]],
            axis=1,
        )
        own[at, :] = jnp.where(head < 2, done, other)
        for p in range(t * pieces // chunks, (t + 1) * pieces // chunks):

            @pl.when(blk + 2 < nblk)
            def _():
                far_copy(p, up).start()

            @pl.when(odd == 0)
            def _():
                near_copy(p, slab(own, p)).start()

    for n in range(max(pieces, nblk)):
        if n < pieces:

            @pl.when(blk >= 2)
            def _():
                far_copy(n, down).wait_recv()

            @pl.when((blk >= 2) & (odd == 1))
            def _():
                near_copy(n, slab(near_far.at[0], n)).start()

        if 2 <= n < nblk:
            chunk(xs, n, side, side).wait_recv()
            chunk(fs, n, side, core).start()
    for n in range(nblk):
        chunk(cs, n, core, core).wait_recv()
        chunk(fs, n, beyond, core).wait_recv()
    for n in range(nblk):
        if n >= 2:
            chunk(xs, n, head, side).wait_send()
        chunk(cs, n, head, core).wait_send()
        chunk(fs, n, side, core).wait_send()
    for copy in stores:
        copy.wait()
    for p in range(pieces):

        @pl.when((blk >= 2) | (odd == 1))
        def _():
            near_copy(p, slab(own, p)).wait_recv()

        @pl.when(blk + 2 < nblk)
        def _():
            far_copy(p, up).wait_send()

        @pl.when((blk >= 2) | (odd == 0))
        def _():
            near_copy(p, slab(own, p)).wait_send()


def project(nblk, tok, first, w_qk, w_v, gain, rest, pieces=8):
    chunks, rows, width = tok.shape
    total, cols = chunks * rows, w_qk.shape[1] // 2
    dma = pltpu.SemaphoreType.DMA
    return pl.pallas_call(
        functools.partial(project_kernel, nblk, pieces),
        out_shape=[
            jax.ShapeDtypeStruct((total, width), BF16),
            jax.ShapeDtypeStruct((total, WIDTH), BF16),
            jax.ShapeDtypeStruct((total, 2 * cols), BF16),
            jax.ShapeDtypeStruct((2, total, 2 * cols), BF16),
            jax.ShapeDtypeStruct(rest.shape, BF16),
        ],
        in_specs=[ANY] * 2 + [WHOLE] * 3 + [ANY],
        out_specs=[ANY, WHOLE, WHOLE, ANY, ANY],
        input_output_aliases={5: 4},
        scratch_shapes=[
            pltpu.VMEM(tok.shape, BF16),
            pltpu.VMEM(first.shape, BF16),
            pltpu.VMEM((width, 2 * cols + WIDTH), BF16),
            dma((2, chunks)),
            dma((chunks,)),
            pltpu.VMEM(tok.shape, BF16),
        ]
        + [dma((pieces,))] * 4
        + [dma((nblk,))] * 6,
        compiler_params=pltpu.CompilerParams(
            collective_id=1, has_side_effects=True, vmem_limit_bytes=48 << 20
        ),
        name="project",
    )(tok, first, w_qk, w_v, gain, rest)


def gelu_both(pre):
    square = pre * pre
    inner = jnp.tanh(GELU_SCALE * (pre + 0.044715 * square * pre))
    slope = GELU_SCALE * (1.0 + 3.0 * 0.044715 * square)
    outer = 0.5 * (1.0 + inner)
    return pre * outer, outer + 0.5 * pre * (1.0 - inner * inner) * slope


def middle_kernel(
    nblk, up_cols, cross, pieces, tok, mixed_parts, cot, gain, gathered, query,
    out, grad_resid, grad_wide, gain_part, keep_up, keep, give, query_later,
    up, down, w_out, up_grad, down_grad, out_grad, mixed, wide_parts, up_got, down_got, out_got,
    sems, out_sems, send_m, recv_m, send_g, recv_g, send_c, recv_c,
    send_z, recv_z, send_y, recv_y, up_side, up_side_got, send_x, recv_x, hidden_all, pre_all, normed_t, cot_t,
):
    head, blk = lax.axis_index("head"), lax.axis_index("blk")
    x, core_index = lax.div(head, 2), lax.rem(head, 2)
    core = xor(head, 1)
    others = [xor(head, 2), 3 - head, core]
    odd = lax.rem(blk, 2)
    pair = blk + 1 - 2 * odd
    above, below = lax.rem(blk + 2, nblk), lax.rem(blk + nblk - 2, nblk)
    greet(partners_of(head, blk, nblk, blks=False) + [(head, b) for b in (pair, above, below)])
    heads_of = 4
    part = gathered.shape[2]
    cols = mixed.shape[2]
    heads = cols // HEAD_DIM

    def mixed_copy(i, to, slot):
        return remote(
            mixed_parts.at[to], mixed.at[slot], send_m.at[i], recv_m.at[i], to, blk
        )

    for i, to in enumerate(others):
        mixed_copy(i, to, head).start()
    piece_rows = query.shape[0] // pieces

    def slab(ref, p):
        return ref.at[pl.ds(p * piece_rows, piece_rows)]

    def far_copy(p, to):
        dst = slab(query_later.at[1], p)
        return remote(slab(query, p), dst, send_z.at[p], recv_z.at[p], head, to)

    def near_copy(p, src):
        return remote(src, slab(query_later.at[0], p), send_y.at[p], recv_y.at[p], head, pair)

    for p in range(pieces):

        @pl.when(blk >= 2)
        def _():
            far_copy(p, below).start()

        @pl.when(odd == 1)
        def _():
            near_copy(p, slab(query, p)).start()

    def relay(p):
        @pl.when(blk + 2 < nblk)
        def _():
            far_copy(p, above).wait_recv()

        @pl.when((blk + 2 < nblk) & (odd == 0))
        def _():
            near_copy(p, slab(query_later.at[1], p)).start()

    chunks = [2 * n + c for n in (1 - x, x) for c in (1 - core_index, core_index)]
    side = others[0]
    sources = (3 - head, others[0], core)

    def load(i, which):
        target, lo, size = ((w_out, 2 * up_cols, cols), (up, 0, up_cols), (down, up_cols, up_cols))[
            which
        ]
        return [
            pltpu.make_async_copy(
                gathered.at[chunks[i], b].at[:, pl.ds(lo, size)],
                target.at[i, pl.ds(b * part, part)],
                sems.at[which, i, b],
            )
            for b in range(nblk)
        ]

    order = [(i, 0) for i in range(heads_of)] + [(i, w) for i in range(heads_of) for w in (1, 2)]
    for i, which in order:
        for copy in load(i, which):
            copy.start()
    mixed[head] = mixed_parts[head]
    for i in range(heads_of):
        for copy in load(i, 0):
            copy.wait()
    for i, to in enumerate(others):
        mixed_copy(i, to, to).wait_recv()
    branch = None
    for i in range(heads_of):
        term = dotf(mixed[chunks[i]], w_out[i], NT)
        branch = term if branch is None else branch + term
    resid = tok[...].astype(F32) + branch
    xhat, scale = statistics(resid)
    normed = (xhat * gain[...]).astype(BF16)
    cotangent = cot[...]
    total, grad_normed = resid, None

    def to_core(n, k):
        mine, theirs = ((up_grad, up_got), (down_grad, down_got), (out_grad, out_got))[k]
        return remote(mine.at[2 * n], theirs.at[n], send_c.at[k, n], recv_c.at[k, n], core, blk)

    def to_side():
        return remote(up_side, up_side_got, send_x, recv_x, side, blk)

    normed_t[...] = normed.T
    cot_t[...] = cotangent.T
    for i in range(heads_of):
        for copy in load(i, 1) + load(i, 2):
            copy.wait()
        hidden, slope = gelu_both(dotf(normed, up[i]))
        hidden_all[i] = hidden.astype(BF16)
        pre_all[i] = (slope * dotf(cotangent, down[i])).astype(BF16)
        total = total + dotf(hidden_all[i], down[i], NT)
        term = dotf(pre_all[i], up[i], NT)
        grad_normed = term if grad_normed is None else grad_normed + term
        for p in range(i * pieces // heads_of, (i + 1) * pieces // heads_of):
            relay(p)
    grad = cotangent.astype(F32) + norm_back(grad_normed, xhat, scale, gain[...])
    branch_grad = grad.astype(BF16)
    lane = lax.broadcasted_iota(jnp.int32, (tok.shape[0], WIDTH), 1)

    def wide_copy(i, to, slot):
        return remote(
            wide_parts.at[to], grad_wide.at[slot], send_g.at[i], recv_g.at[i], to, blk
        )

    for i in range(heads_of):
        h = chunks[i]
        rows = dotf(branch_grad, w_out[i]).astype(BF16).astype(F32)
        product = rows * mixed[h].astype(F32)
        wide = jnp.concatenate([rows, jnp.zeros((rows.shape[0], WIDTH - cols), F32)], axis=1)
        for k in range(heads):
            delta = jnp.sum(
                product[:, k * HEAD_DIM : (k + 1) * HEAD_DIM], axis=1, keepdims=True
            )
            for c, piece in enumerate(split_parts(-delta)):
                wide = jnp.where(lane == cols + SPLITS * k + c, piece, wide)
        wide_parts[h] = wide.astype(BF16)
        if i < 3:
            wide_copy(i, h, head).start()
    grad_wide[head] = wide_parts[head]
    out[...] = total.astype(BF16)
    gain_part[...] = jnp.sum(grad_normed * xhat, axis=0, keepdims=True)
    grad_resid[...] = grad
    for i in range(heads_of):
        up_grad[i] = dotf(normed_t[...], pre_all[i]).astype(BF16)
        down_grad[i] = dotf(cot_t[...], hidden_all[i]).astype(BF16)
        if i % 2 == 0:
            to_core(i // 2, 0).start()
            to_core(i // 2, 1).start()
        if i == 1:
            to_core(0, 0).wait_recv()
            up_side[...] = (
                up_grad[1, :, :cross].astype(F32) + up_got[0, :, :cross].astype(F32)
            ).astype(BF16)
            to_side().start()
    branch_t = branch_grad.T
    for i in range(heads_of):
        out_grad[i] = dotf(branch_t, mixed[chunks[i]]).astype(BF16)
        if i % 2 == 0:
            to_core(i // 2, 2).start()

    def store(k, source, target, lo):
        size = source.shape[1]
        return [
            pltpu.make_async_copy(
                source.at[pl.ds(b * part, part)],
                target.at[b].at[:, pl.ds(lo, size)],
                out_sems.at[k, b],
            )
            for b in range(nblk)
        ]

    stores = []
    far_up = up_cols - cross
    for n, target in enumerate((give, keep)):
        at = 2 * n + 1
        for k, (mine, theirs) in enumerate(
            ((up_grad, up_got), (down_grad, down_got), (out_grad, out_got))
        ):
            if n or k:
                to_core(n, k).wait_recv()
            mine[at] = (mine[at].astype(F32) + theirs[n].astype(F32)).astype(BF16)
        stores += store(3 * n, up_grad.at[at].at[:, pl.ds(cross, far_up)], target, 0)
        stores += store(3 * n + 1, down_grad.at[at], target, far_up)
        stores += store(3 * n + 2, out_grad.at[at], target, far_up + up_cols)
        for copy in stores[-3 * nblk :]:
            copy.start()
    to_side().wait()
    up_side[...] = (up_grad[3, :, :cross].astype(F32) + up_side_got[...].astype(F32)).astype(BF16)
    stores += store(6, up_side, keep_up, 0)
    for copy in stores[-nblk:]:
        copy.start()
    for copy in stores:
        copy.wait()
    for k in range(3):
        for n in range(2):
            to_core(n, k).wait_send()
    for i in range(3):
        wide_copy(i, chunks[i], sources[i]).wait_recv()
    for i, to in enumerate(others):
        mixed_copy(i, to, head).wait_send()
        wide_copy(i, chunks[i], head).wait_send()
    for p in range(pieces):

        @pl.when((blk + 2 < nblk) | (odd == 0))
        def _():
            near_copy(p, slab(query, p)).wait_recv()

        @pl.when(blk >= 2)
        def _():
            far_copy(p, below).wait_send()

        @pl.when((blk + 2 < nblk) | (odd == 1))
        def _():
            near_copy(p, slab(query, p)).wait_send()


def middle(nblk, tok, mixed_parts, cot, gain, gathered, query, up_cols, cross=256, pieces=8):
    heads_of, rows, cols = mixed_parts.shape
    width, part = tok.shape[1], gathered.shape[2]
    flops = 2 * rows * width * (6 * up_cols * heads_of + 3 * width)
    dma = pltpu.SemaphoreType.DMA
    vmem = lambda *shape: pltpu.VMEM(shape, BF16)
    return pl.pallas_call(
        functools.partial(middle_kernel, nblk, up_cols, cross, pieces),
        out_shape=[
            jax.ShapeDtypeStruct((rows, width), BF16),
            jax.ShapeDtypeStruct((rows, width), F32),
            jax.ShapeDtypeStruct((heads_of, rows, WIDTH), BF16),
            jax.ShapeDtypeStruct((1, width), F32),
            jax.ShapeDtypeStruct((nblk, part, cross), BF16),
            jax.ShapeDtypeStruct((nblk, part, gathered.shape[3] - cross), BF16),
            jax.ShapeDtypeStruct((nblk, part, gathered.shape[3] - cross), BF16),
            jax.ShapeDtypeStruct((2,) + query.shape, BF16),
        ],
        in_specs=[WHOLE] * 4 + [ANY] * 2,
        out_specs=[WHOLE] * 4 + [ANY] * 4,
        scratch_shapes=[
            vmem(heads_of, width, up_cols), vmem(heads_of, width, up_cols),
            vmem(heads_of, width, cols),
            vmem(heads_of, width, up_cols), vmem(heads_of, width, up_cols),
            vmem(heads_of, width, cols),
            vmem(heads_of, rows, cols), vmem(heads_of, rows, WIDTH),
            vmem(2, width, up_cols), vmem(2, width, up_cols), vmem(2, width, cols),
            dma((3, heads_of, nblk)), dma((7, nblk)),
            dma((3,)), dma((3,)), dma((3,)), dma((3,)), dma((3, 2)), dma((3, 2)),
            dma((pieces,)), dma((pieces,)), dma((pieces,)), dma((pieces,)),
            vmem(width, cross), vmem(width, cross), dma, dma,
            vmem(heads_of, rows, up_cols), vmem(heads_of, rows, up_cols),
            vmem(width, rows), vmem(width, rows),
        ],
        compiler_params=pltpu.CompilerParams(
            collective_id=2, has_side_effects=True, vmem_limit_bytes=62 << 20
        ),
        cost_estimate=pl.CostEstimate(
            flops=flops, bytes_accessed=24 << 20, transcendentals=rows * up_cols * heads_of
        ),
        name="middle",
    )(tok, mixed_parts, cot, gain, gathered, query)


def pair_sum_kernel(up, ours, theirs, keep, give):
    odd = lax.rem(lax.axis_index("blk"), 2)
    sums = [(ours[n].astype(F32) + theirs[n].astype(F32)).astype(BF16) for n in range(2)]
    cols = up.shape[2]
    keep[0, :, :cols] = jnp.where(odd == 0, up[0], up[1])
    give[0, :, :cols] = jnp.where(odd == 0, up[1], up[0])
    keep[0, :, cols:] = jnp.where(odd == 0, sums[0], sums[1])
    give[0, :, cols:] = jnp.where(odd == 0, sums[1], sums[0])


def pair_sum(up, ours, theirs):
    nblk, part, width = ours.shape
    total = width + up.shape[2]
    spec = lambda n, cols: pl.BlockSpec((n, part, cols), lambda i: (i, 0, 0))
    return pl.pallas_call(
        pair_sum_kernel,
        grid=(nblk // 2,),
        in_specs=[spec(2, up.shape[2]), spec(2, width), spec(2, width)],
        out_specs=[spec(1, total)] * 2,
        out_shape=[jax.ShapeDtypeStruct((nblk // 2, part, total), BF16)] * 2,
        cost_estimate=pl.CostEstimate(
            flops=nblk * part * width, bytes_accessed=6 * nblk * part * width, transcendentals=0
        ),
        name="pair_sum",
    )(up, ours, theirs)


def unproject_kernel(
    nblk, d_q, d_k, d_v, normed, gain, w_qk, w_v,
    grad, out_all, gain_part, acc_q, acc_k, acc_v, acc_gain, fresh,
):
    step, last = pl.program_id(0), pl.num_programs(0) - 1
    part = normed.shape[1] // nblk
    cols = d_q.shape[1]

    @pl.when(step == 0)
    def _():
        mine = lax.axis_index("head") < 2
        weight = jnp.concatenate([w_v[0], w_v[1]], axis=1)
        fresh[...] = jnp.where(mine, weight, jnp.zeros_like(weight))
        acc_q[...] = jnp.zeros_like(acc_q)
        acc_k[...] = jnp.zeros_like(acc_k)
        acc_v[...] = jnp.zeros_like(acc_v)
        acc_gain[...] = jnp.zeros_like(acc_gain)

    rows = normed[...]
    mine = lax.axis_index("head") < 2
    d_fresh = jnp.where(mine, d_v[...], jnp.zeros_like(d_v[...]))
    both = jnp.concatenate([d_q[...], d_k[...]], axis=1)
    whole = dotf(both, w_qk[...], NT)
    whole = whole + dotf(d_fresh, fresh[...], NT)
    grad[...] = whole.astype(BF16)
    acc_gain[...] += jnp.sum(whole * rows.astype(F32), axis=0, keepdims=True)
    acc_q[...] += dotf(rows, d_q[...], TN)
    acc_k[...] += dotf(rows, d_k[...], TN)
    acc_v[...] += dotf(rows, d_v[...], TN)

    @pl.when(step == last)
    def _():
        gain_part[...] = acc_gain[...] / gain[...]
        empty = jnp.zeros((normed.shape[1], out_all.shape[2] - 3 * cols), F32)
        whole = jnp.concatenate([acc_q[...], acc_k[...], acc_v[...], empty], axis=1).astype(BF16)
        for b in range(nblk):
            out_all[b] = whole[b * part : (b + 1) * part]


def unproject(nblk, d_q, d_k, d_v, normed, gain, w_qk, w_v, rows=512):
    total, width = normed.shape
    cols = d_q.shape[1]
    part = width // nblk
    fixed = lambda array: pl.BlockSpec(array.shape, lambda i: (0,) * array.ndim)
    row = lambda n: pl.BlockSpec((rows, n), lambda i: (i, 0))
    outs = [
        jax.ShapeDtypeStruct((total, width), BF16),
        jax.ShapeDtypeStruct((nblk, part, -(-3 * cols // 128) * 128), BF16),
        jax.ShapeDtypeStruct((1, width), F32),
    ]
    return pl.pallas_call(
        functools.partial(unproject_kernel, nblk),
        grid=(total // rows,),
        in_specs=[row(cols)] * 3 + [row(width)] + [fixed(a) for a in (gain, w_qk, w_v)],
        out_specs=[row(width)] + [fixed(a) for a in outs[1:]],
        out_shape=outs,
        scratch_shapes=[
            pltpu.VMEM((width, cols), F32),
            pltpu.VMEM((width, cols), F32),
            pltpu.VMEM((width, cols), F32),
            pltpu.VMEM((1, width), F32),
            pltpu.VMEM((width, cols), BF16),
        ],
        compiler_params=pltpu.CompilerParams(vmem_limit_bytes=48 << 20),
        cost_estimate=pl.CostEstimate(
            flops=12 * total * width * cols, bytes_accessed=16 << 20, transcendentals=0
        ),
        name="unproject",
    )(d_q, d_k, d_v, normed, gain, w_qk, w_v)


def head_rows(h, heads, shape):
    row = lax.broadcasted_iota(jnp.int32, shape, 0)
    real = heads * HEAD_DIM
    own = (row >= h * HEAD_DIM) & (row < (h + 1) * HEAD_DIM)
    return own | ((row >= real + SPLITS * h) & (row < real + SPLITS * (h + 1)))


def per_head(wide, heads, out):
    flipped = wide.T
    for h in range(heads):
        out[h] = jnp.where(head_rows(h, heads, flipped.shape), flipped, jnp.zeros_like(flipped))


def doc_start(meta, ndocs, t):
    def step(j,c):
        cum,best=c
        best=jnp.where(cum<=t,cum,best)
        return cum+meta[1+j],best
    return lax.fori_loop(0,ndocs,step,(jnp.int32(0),jnp.int32(0)),unroll=True)[1]

def doc_end(meta, ndocs, t):
    def step(j,c):
        cum,best,found=c
        cum=cum+meta[1+j]
        take=(cum>t)&(found==0)
        return cum,jnp.where(take,cum,best),jnp.where(take,1,found)
    return lax.fori_loop(0,ndocs,step,(jnp.int32(0),jnp.int32(0),jnp.int32(0)),unroll=True)[1]

def starts_vec(meta, ndocs, t):
    def step(j,c):
        cum,best=c
        return cum+meta[1+j],jnp.where(cum<=t,cum,best)
    return lax.fori_loop(0,ndocs,step,(jnp.int32(0),jnp.zeros(t.shape,jnp.int32)),unroll=True)[1]

def ends_vec(meta, ndocs, t):
    def step(j,c):
        cum,best=c
        ln=meta[1+j]
        return cum+ln,jnp.where(cum<=t,cum+ln,best)
    return lax.fori_loop(0,ndocs,step,(jnp.int32(0),jnp.zeros(t.shape,jnp.int32)),unroll=True)[1]

def widened(columns, heads):
    rows, width = columns.shape
    ones = jnp.ones((rows, SPLITS * heads), BF16)
    empty = jnp.zeros((rows, WIDTH - width - SPLITS * heads), BF16)
    return jnp.concatenate([columns, ones, empty], axis=1)


def unpack_rows(packed, heads):
    pair = 2 * HEAD_DIM
    key = jnp.concatenate([packed[:, :pair], packed[:, 2 * pair : 2 * pair + HEAD_DIM]], axis=1)
    value = jnp.concatenate([packed[:, pair : 2 * pair], packed[:, 2 * pair + HEAD_DIM :]], axis=1)
    return widened(key, heads), widened(value, heads)


STEP = 512


def build_window(heads, start, earlier, own, packed, sems, keys, values, key_rows, value_rows):
    before = earlier.shape[0] // STEP
    chunks = before + own.shape[0] // STEP

    def copy(n, source, row):
        return pltpu.make_async_copy(
            source.at[pl.ds(row * STEP, STEP)], packed.at[pl.ds(n * STEP, STEP)], sems.at[n]
        )

    def begin(n, carry):
        @pl.when(n < before)
        def _():
            copy(n, earlier, n).start()

        @pl.when(n >= before)
        def _():
            copy(n, own, n - before).start()

        return carry

    def build(n, carry):
        copy(n, own, 0).wait()
        at = pl.ds(pl.multiple_of(n * STEP, STEP), STEP)
        key, value = unpack_rows(packed[at, :], heads)
        for wide, rows, flipped in ((key, keys, key_rows), (value, values, value_rows)):
            if rows is not None:
                rows[at, :] = wide
            if flipped is not None:
                turned = wide.T
                for h in range(heads):
                    flipped[h, :HEAD_DIM, at] = turned[h * HEAD_DIM : (h + 1) * HEAD_DIM]
        return carry

    lax.fori_loop(start, chunks, begin, 0)
    lax.fori_loop(start, chunks, build, 0)


def three(lo,a,b,hi,body):
    lax.fori_loop(lo,a,lambda j,_: body(j,True),None)
    lax.fori_loop(a,b,lambda j,_: body(j,False),None)
    lax.fori_loop(b,hi,lambda j,_: body(j,True),None)

def query_tiles(meta, ndocs, t0, wbase, tq, tk):
    lo = (doc_start(meta, ndocs, t0) - wbase) // tk
    f0 = (doc_start(meta, ndocs, t0 + tq - 1) - wbase + tk - 1) // tk
    f1 = (t0 - wbase) // tk
    hi = (t0 + tq - 1 - wbase) // tk + 1
    return lo, jnp.minimum(f0, f1), f1, hi


def fwd_kernel(heads, ndocs, tq, tk, meta, q_ref, earlier, own, mix_ref, wide_ref,
               k_ref, vt_ref, qt, m_ref, acc_ref, packed, sems):
    i = pl.program_id(0)
    width = q_ref.shape[1]
    real = heads * HEAD_DIM
    base = meta[0]
    wbase = base - earlier.shape[0]

    @pl.when(i == 0)
    def _():
        vt_ref[:, HEAD_DIM:, :] = jnp.ones_like(vt_ref[:, HEAD_DIM:, :])
        start = (doc_start(meta, ndocs, base) - wbase) // tk * (tk // STEP)
        build_window(heads, start, earlier, own, packed, sems, k_ref, None, None, vt_ref)

    t0 = base + i * tq
    lo, f0, f1, hi = query_tiles(meta, ndocs, t0, wbase, tq, tk)
    q = q_ref[...]
    trow = t0 + lax.broadcasted_iota(jnp.int32, (8, tq), 1)
    srow = starts_vec(meta, ndocs, trow)[:1]
    trow = trow[:1]
    lane = lax.broadcasted_iota(jnp.int32, (tq, width), 1)

    def visible(off):
        u = wbase + off + lax.broadcasted_iota(jnp.int32, (tk, tq), 0)
        return (u >= srow) & (u <= trow)

    itself = q.astype(F32) * k_ref[pl.ds(pl.multiple_of(t0 - wbase, tq), tq), :].astype(F32)
    shifted = q.astype(F32)
    for h in range(heads):
        mine = (lane >= h * HEAD_DIM) & (lane < (h + 1) * HEAD_DIM)
        score = jnp.sum(jnp.where(mine, itself, 0.0), axis=1, keepdims=True)
        for c, piece in enumerate(split_parts(-score)):
            shifted = jnp.where(lane == real + SPLITS * h + c, piece, shifted)
    per_head(shifted.astype(BF16), heads, qt)
    acc_ref[...] = jnp.zeros_like(acc_ref)

    def quick(j, masked):
        off = pl.multiple_of(j * tk, tk)
        k = k_ref[pl.ds(off, tk), :]
        if masked:
            vis = visible(off)
        for h in range(heads):
            p = jnp.exp(dotf(k, qt[h]))
            if masked:
                p = jnp.where(vis, p, 0.0)
            acc_ref[h] += dotf(vt_ref[h, :, pl.ds(off, tk)], p.astype(BF16))

    def finish(extra):
        rows = []
        parts = []
        for h in range(heads):
            acc = acc_ref[h]
            total = acc[HEAD_DIM : HEAD_DIM + 1]
            rows.append(acc[:HEAD_DIM] / total)
            at = real + SPLITS * h
            shift = jnp.sum(qt[h, at : at + SPLITS, :].astype(F32), axis=0, keepdims=True)
            parts += split_parts(shift - extra[h] - jnp.log(total))
        rest = jnp.zeros((width - real - len(parts), tq), F32)
        turned = jnp.concatenate(rows + parts + [rest], axis=0).T
        mix_ref[0] = turned[:, :real].astype(BF16)
        wide_ref[...] = jnp.where(lane < real, q.astype(F32), turned).astype(BF16)

    three(lo, f0, f1, hi, quick)
    none = jnp.zeros((1, tq), F32)
    finish([none] * heads)
    sums = acc_ref[:, HEAD_DIM : HEAD_DIM + 1, :]
    fits = jnp.max(jnp.where(sums < 1e30, 0.0, 1.0)) == 0.0

    @pl.when(jnp.logical_not(fits))
    def _():
        acc_ref[...] = jnp.zeros_like(acc_ref)
        m_ref[...] = jnp.full_like(m_ref, EXCLUDED)

        def body(j, carry):
            off = pl.multiple_of(j * tk, tk)
            k = k_ref[pl.ds(off, tk), :]
            vis = visible(off)
            for h in range(heads):
                s = jnp.where(vis, dotf(k, qt[h]), EXCLUDED)
                old = m_ref[h, :1]
                new = jnp.maximum(old, jnp.max(s, axis=0, keepdims=True))
                m_ref[h, :1] = new
                p = jnp.exp(s - new).astype(BF16)
                acc_ref[h] = acc_ref[h] * jnp.exp(old - new) + dotf(
                    vt_ref[h, :, pl.ds(off, tk)], p
                )
            return carry

        lax.fori_loop(lo, hi, body, 0)
        finish([m_ref[h, :1] for h in range(heads)])


SCALARS = pl.BlockSpec(memory_space=pltpu.SMEM)


def attention_fwd(meta, q, earlier, own, heads, tq, tk):
    block, width = q.shape
    window = block + earlier.shape[0]
    ndocs = meta.shape[0] - 1
    return pl.pallas_call(
        functools.partial(fwd_kernel, heads, ndocs, tq, tk),
        grid=(block // tq,),
        in_specs=[
            SCALARS,
            pl.BlockSpec((tq, width), lambda i: (i, 0)),
            ANY,
            ANY,
        ],
        out_specs=[
            pl.BlockSpec((1, tq, heads * HEAD_DIM), lambda i: (i, 0, 0)),
            pl.BlockSpec((tq, width), lambda i: (i, 0)),
        ],
        out_shape=[
            jax.ShapeDtypeStruct((block // tq, tq, heads * HEAD_DIM), BF16),
            jax.ShapeDtypeStruct((block, width), BF16),
        ],
        scratch_shapes=[
            pltpu.VMEM((window, width), BF16),
            pltpu.VMEM((heads, HEAD_DIM + 16, window), BF16),
            pltpu.VMEM((heads, width, tq), BF16),
            pltpu.VMEM((heads, 8, tq), F32),
            pltpu.VMEM((heads, HEAD_DIM + 16, tq), F32),
            pltpu.VMEM((window, own.shape[1]), BF16),
            pltpu.SemaphoreType.DMA((window // STEP,)),
        ],
        compiler_params=pltpu.CompilerParams(vmem_limit_bytes=56 << 20),
        cost_estimate=pl.CostEstimate(
            flops=30_000_000_000, bytes_accessed=12 << 20, transcendentals=20_000_000
        ),
        name="attn_fwd",
    )(meta, q, earlier, own)


def dq_kernel(heads, ndocs, tq, tk, meta, q_ref, do_ref, earlier, own, dq_ref,
              k_ref, v_ref, kt_ref, qt, dot, acc_ref, packed, sems):
    i = pl.program_id(0)
    base = meta[0]
    wbase = base - earlier.shape[0]

    @pl.when(i == 0)
    def _():
        start = (doc_start(meta, ndocs, base) - wbase) // tk * (tk // STEP)
        build_window(heads, start, earlier, own, packed, sems, k_ref, v_ref, kt_ref, None)

    t0 = base + i * tq
    per_head(q_ref[...], heads, qt)
    per_head(do_ref[...], heads, dot)
    acc_ref[...] = jnp.zeros_like(acc_ref)
    trow = t0 + lax.broadcasted_iota(jnp.int32, (8, tq), 1)
    srow = starts_vec(meta, ndocs, trow)[:1]
    trow = trow[:1]

    def body(j, masked):
        off = pl.multiple_of(j * tk, tk)
        k = k_ref[pl.ds(off, tk), :]
        v = v_ref[pl.ds(off, tk), :]
        if masked:
            u = wbase + off + lax.broadcasted_iota(jnp.int32, (tk, tq), 0)
            vis = (u >= srow) & (u <= trow)
        for h in range(heads):
            p = jnp.exp(dotf(k, qt[h]))
            if masked:
                p = jnp.where(vis, p, 0.0)
            ds = (p * dotf(v, dot[h])).astype(BF16)
            acc_ref[h] += dotf(kt_ref[h, :, pl.ds(off, tk)], ds)

    three(*query_tiles(meta, ndocs, t0, wbase, tq, tk), body)
    turned = acc_ref[...].reshape(heads * HEAD_DIM, tq).T
    dq_ref[...] = (turned * (HEAD_DIM**-0.5)).astype(BF16)


def attention_dq(meta, q, do, earlier, own, heads, tq, tk):
    block, width = q.shape
    window = block + earlier.shape[0]
    ndocs = meta.shape[0] - 1
    row = lambda w: pl.BlockSpec((tq, w), lambda i: (i, 0))
    return pl.pallas_call(
        functools.partial(dq_kernel, heads, ndocs, tq, tk),
        grid=(block // tq,),
        in_specs=[SCALARS, row(width), row(width), ANY, ANY],
        out_specs=row(heads * HEAD_DIM),
        out_shape=jax.ShapeDtypeStruct((block, heads * HEAD_DIM), BF16),
        scratch_shapes=[pltpu.VMEM((window, width), BF16)] * 2
        + [pltpu.VMEM((heads, HEAD_DIM, window), BF16)]
        + [pltpu.VMEM((heads, width, tq), BF16)] * 2
        + [pltpu.VMEM((heads, HEAD_DIM, tq), F32)]
        + [pltpu.VMEM((window, own.shape[1]), BF16), pltpu.SemaphoreType.DMA((window // STEP,))],
        compiler_params=pltpu.CompilerParams(vmem_limit_bytes=56 << 20),
        cost_estimate=pl.CostEstimate(
            flops=45_000_000_000, bytes_accessed=12 << 20, transcendentals=20_000_000
        ),
        name="attn_dq",
    )(meta, q, do, earlier, own)


def dkv_kernel(heads, ndocs, tq, tk, meta, own, q_parts, do_parts, dk_ref, dv_ref,
               q_ref, do_ref, qt_ref, dot_ref, kt, vt, dk_acc, dv_acc, sems):
    i = pl.program_id(0)
    base = meta[0]

    @pl.when(i == 0)
    def _():
        block = pl.num_programs(0) * tk
        end = (doc_end(meta, ndocs, base + block - 1) - base + STEP - 1) // STEP
        sources = []
        for parts in (q_parts, do_parts):
            row, found = 0, []
            for part in parts:
                found.append((row // STEP, (row + part.shape[0]) // STEP, part))
                row += part.shape[0]
            sources.append(found)

        def copy(k, n, source, row):
            return pltpu.make_async_copy(
                source.at[pl.ds(row * STEP, STEP)],
                (q_ref, do_ref)[k].at[pl.ds(n * STEP, STEP)],
                sems.at[k, n],
            )

        def begin(n, carry):
            for k in range(2):
                for first, last, part in sources[k]:

                    @pl.when((n >= first) & (n < last))
                    def _():
                        copy(k, n, part, n - first).start()

            return carry

        def turn(n, carry):
            at = pl.ds(pl.multiple_of(n * STEP, STEP), STEP)
            for k, (rows, flipped) in enumerate(((q_ref, qt_ref), (do_ref, dot_ref))):
                copy(k, n, sources[k][0][2], 0).wait()
                turned = rows[at, :].T
                for h in range(heads):
                    flipped[h, :, at] = turned[h * HEAD_DIM : (h + 1) * HEAD_DIM]
            return carry

        lax.fori_loop(0, end, begin, 0)
        lax.fori_loop(0, end, turn, 0)

    u0 = base + i * tk
    lo = (u0 - base) // tq
    f0 = (u0 + tk - 1 - base + tq - 1) // tq
    e_first = doc_end(meta, ndocs, u0)
    e_last = doc_end(meta, ndocs, u0 + tk - 1)
    f1 = (e_first - base) // tq
    hi = (e_last - 1 - base) // tq + 1
    f0 = jnp.minimum(f0, hi)
    f1 = jnp.clip(f1, f0, hi)
    k, v = unpack_rows(own[...], heads)
    per_head(k, heads, kt)
    per_head(v, heads, vt)
    dk_acc[...] = jnp.zeros_like(dk_acc)
    dv_acc[...] = jnp.zeros_like(dv_acc)
    urow = u0 + lax.broadcasted_iota(jnp.int32, (8, tk), 1)
    erow = ends_vec(meta, ndocs, urow)[:1]
    urow = urow[:1]

    def body(j, masked):
        off = pl.multiple_of(j * tq, tq)
        at = pl.ds(off, tq)
        q = q_ref[at, :]
        do = do_ref[at, :]
        if masked:
            t = base + off + lax.broadcasted_iota(jnp.int32, (tq, tk), 0)
            vis = (t >= urow) & (t < erow)
        for h in range(heads):
            p = jnp.exp(dotf(q, kt[h]))
            if masked:
                p = jnp.where(vis, p, 0.0)
            ds = (p * dotf(do, vt[h])).astype(BF16)
            dv_acc[h] += dotf(dot_ref[h, :, at], p.astype(BF16))
            dk_acc[h] += dotf(qt_ref[h, :, at], ds)

    three(lo, f0, f1, hi, body)
    for acc, out in ((dk_acc, dk_ref), (dv_acc, dv_ref)):
        out[...] = acc[...].reshape(heads * HEAD_DIM, tk).T.astype(BF16)


def attention_dkv(meta, own, q_parts, do_parts, heads, tq, tk):
    block, width = q_parts[0].shape
    window = sum(part.shape[0] for part in q_parts)
    ndocs = meta.shape[0] - 1
    row = lambda w: pl.BlockSpec((tk, w), lambda i: (i, 0))
    return pl.pallas_call(
        functools.partial(dkv_kernel, heads, ndocs, tq, tk),
        grid=(block // tk,),
        in_specs=[SCALARS, row(own.shape[1]), [ANY] * len(q_parts), [ANY] * len(do_parts)],
        out_specs=[row(heads * HEAD_DIM)] * 2,
        out_shape=[jax.ShapeDtypeStruct((block, heads * HEAD_DIM), BF16)] * 2,
        scratch_shapes=[pltpu.VMEM((window, width), BF16)] * 2
        + [pltpu.VMEM((heads, HEAD_DIM, window), BF16)] * 2
        + [pltpu.VMEM((heads, width, tk), BF16)] * 2
        + [pltpu.VMEM((heads, HEAD_DIM, tk), F32)] * 2
        + [pltpu.SemaphoreType.DMA((2, window // STEP))],
        compiler_params=pltpu.CompilerParams(vmem_limit_bytes=56 << 20),
        cost_estimate=pl.CostEstimate(
            flops=60_000_000_000, bytes_accessed=12 << 20, transcendentals=20_000_000
        ),
        name="attn_dkv",
    )(meta, own, q_parts, do_parts)


def on_device(
    tokens, first_values, cotangent, w_query, w_key, w_value, w_out, w_up, w_down,
    gain_attn, gain_mlp, doc_lengths,
):
    width = tokens.shape[1]
    heads_of = lax.axis_size("head")
    nblk = lax.axis_size("blk")
    blk = lax.axis_index("blk")
    rows = tokens.shape[0]
    block = rows * heads_of
    heads = HEADS // heads_of
    cols = heads * HEAD_DIM
    part = width // nblk
    meta = jnp.concatenate([jnp.reshape(blk * block, (1,)).astype(jnp.int32), doc_lengths])

    up_cols = w_up.shape[1]
    tok_all, first_all, qk_all, gathered, _, v_all, gain_all = front(
        nblk, tokens, first_values, w_query, w_key, w_value, w_up, w_down.T, w_out,
        gain_attn.reshape(1, part), gain_mlp.reshape(1, part),
    )
    attn_gain = gain_all[:, 0].reshape(1, width)
    mlp_gain = gain_all[:, 1].reshape(1, width)
    w_qk = qk_all.reshape(width, 2 * cols)
    w_v = v_all.reshape(2, width, w_value.shape[1])
    normed, query, own, earlier, gathered = project(
        nblk, tok_all, first_all, w_qk, w_v, attn_gain, gathered
    )
    earlier = earlier.reshape(2 * block, 2 * cols)
    mixed_parts, query_wide = attention_fwd(
        meta, query, earlier, own, heads, rows, 2 * rows
    )
    layer_output, grad_resid, grad_parts, gain_mlp_part, keep_up, keep, give, query_later = middle(
        nblk, tokens, mixed_parts, cotangent, mlp_gain, gathered, query_wide, up_cols
    )
    grad_wide = grad_parts.reshape(block, WIDTH)
    taken = lax.ppermute(give, "head", [(h, (h + 2) % heads_of) for h in range(heads_of)])

    grads_later = [grad_wide] + [
        lax.ppermute(grad_wide, "blk", [(i, i - d) for i in range(d, nblk)]) for d in (1, 2)
    ]
    queries_later = [query_wide, query_later.reshape(2 * block, WIDTH)]
    grad_query = attention_dq(
        meta, query_wide, grad_wide, earlier, own, heads, rows, 2 * rows
    )
    taken, keep, grad_query = lax.optimization_barrier((taken, keep, grad_query))
    keep, give = pair_sum(keep_up, keep, taken)
    taken = lax.ppermute(give, "blk", [(i, i + 1 - 2 * (i % 2)) for i in range(nblk)])
    keep, own = lax.optimization_barrier((keep, own))
    grad_key, grad_value = attention_dkv(
        meta, own, queries_later, grads_later, heads, rows, rows
    )
    grad_normed, part_weights, gain_attn_part = unproject(
        nblk, grad_query, grad_key, grad_value, normed, attn_gain, w_qk, w_v
    )
    gain_parts = jnp.concatenate([gain_attn_part, gain_mlp_part]).reshape(2, nblk, 1, part)
    (
        grad_tokens, final_query, final_key, final_value, grad_first, gain_sums,
        final_up, final_down, final_out,
    ) = tail(
        nblk,
        grad_normed.reshape(heads_of, rows, width),
        part_weights,
        grad_value.reshape(heads_of, rows, cols),
        gain_parts.transpose(1, 0, 2, 3),
        keep,
        taken,
        tokens,
        grad_resid,
        attn_gain,
        cols,
        up_cols,
    )
    return (
        layer_output,
        grad_tokens,
        grad_first,
        final_query,
        final_key,
        final_value,
        final_out,
        final_up,
        final_down.T,
        gain_sums[0].reshape(part),
        gain_sums[1].reshape(part),
    )


def solution(mesh):
    rows = P(("blk", "head"), None)
    specs = (P("blk", "head"),) * 3 + (P("head", "blk"), P("blk", "head"), P("head", "blk"))
    gains = (P("blk"), P("blk"))
    return jax.shard_map(
        on_device,
        mesh=mesh,
        in_specs=(rows,) * 3 + specs + gains + (P(),),
        out_specs=(rows,) * 3 + specs + gains,
        check_vma=False,
    )
```

```python
import functools

import jax
import jax.numpy as jnp
from jax import lax
from jax.experimental import pallas as pl
from jax.experimental.pallas import tpu as pltpu
from jax.sharding import PartitionSpec as P

HEADS = 12
HEAD_DIM = 64
DOC_MAX = 4096
EPSILON = 1e-05
GELU_SCALE = 0.7978845608028654
EXCLUDED = -1e30
WIDTH = 256
SPLITS = 3
BF16 = jnp.bfloat16
F32 = jnp.float32
MESH = pl.DeviceIdType.MESH
ANY = pl.BlockSpec(memory_space=pl.ANY)
WHOLE = pl.BlockSpec(memory_space=pltpu.VMEM)
NT = (((1,), (1,)), ((), ()))
TN = (((0,), (0,)), ((), ()))


def dotf(left, right, dims=None):
    if dims is None:
        dims = (((1,), (0,)), ((), ()))
    return lax.dot_general(left, right, dims, preferred_element_type=F32)


def remote(src, dst, send_sem, recv_sem, head, blk):
    return pltpu.make_async_remote_copy(
        src_ref=src,
        dst_ref=dst,
        send_sem=send_sem,
        recv_sem=recv_sem,
        device_id={"head": head, "blk": blk},
        device_id_type=MESH,
    )


def greet(partners):
    barrier = pltpu.get_barrier_semaphore()
    for head, blk in partners:
        pl.semaphore_signal(
            barrier, inc=1, device_id={"head": head, "blk": blk}, device_id_type=MESH
        )
    pl.semaphore_wait(barrier, len(partners))


def xor(value, bit):
    return value + bit - 2 * bit * (lax.div(value, bit) % 2)


def partners_of(head, blk, nblk, heads=True, blks=True):
    found = []
    if heads:
        found += [(xor(head, 1), blk), (xor(head, 2), blk), (3 - head, blk)]
    if blks:
        found += [(head, lax.rem(blk + d, nblk)) for d in range(1, nblk)]
    return found


class Line:
    def __init__(self, nblk, head, blk, source, target, up, down, across):
        self.half, self.head, self.blk = nblk // 2, head, blk
        self.place, self.parity = lax.div(blk, 2), lax.rem(blk, 2)
        self.source, self.target = source, target
        self.sems = {"up": up, "down": down, "across": across}

    def copy(self, way, origin, step, fresh=False):
        slot = 2 * origin + self.parity
        to = {
            "up": lax.rem(self.blk + 2, 2 * self.half),
            "down": lax.rem(self.blk + 2 * self.half - 2, 2 * self.half),
            "across": self.blk + 1 - 2 * self.parity,
        }[way]
        send, recv = self.sems[way]
        return remote(
            self.source if fresh else self.target.at[slot],
            self.target.at[slot], send.at[step], recv.at[step], self.head, to,
        )

    def landing(self, way, slot, step):
        send, recv = self.sems[way]
        other = self.blk + 1 - 2 * self.parity
        at = self.target.at[slot]
        return remote(at, at, send.at[step], recv.at[step], self.head, other)

    def begin(self):
        @pl.when(self.place + 1 < self.half)
        def _():
            self.copy("up", self.place, 0, True).start()

        @pl.when(self.place > 0)
        def _():
            self.copy("down", self.place, 0, True).start()

        self.copy("across", self.place, self.place, True).start()

    def step(self, s, then=None):
        low, high = self.place - 1 - s, self.place + 1 + s

        @pl.when(low >= 0)
        def _():
            self.landing("up", 2 * low + self.parity, s).wait_recv()
            if s + 1 < self.half - 1:

                @pl.when(self.place + 1 < self.half)
                def _():
                    self.copy("up", low, s + 1).start()

            self.copy("across", low, low).start()
            if then:
                then(2 * low + self.parity)

        @pl.when(high < self.half)
        def _():
            self.landing("down", 2 * high + self.parity, s).wait_recv()
            if s + 1 < self.half - 1:

                @pl.when(self.place > 0)
                def _():
                    self.copy("down", high, s + 1).start()

            self.copy("across", high, high).start()
            if then:
                then(2 * high + self.parity)

    def land(self, origin):
        self.landing("across", 2 * origin + 1 - self.parity, origin).wait_recv()

    def finish(self):
        for o in range(self.half):
            self.copy("across", o, o).wait_send()
        for s in range(self.half - 1):

            @pl.when((self.place - s >= 0) & (self.place + 1 < self.half))
            def _():
                self.copy("up", self.place - s, s).wait_send()

            @pl.when((self.place + s < self.half) & (self.place > 0))
            def _():
                self.copy("down", self.place + s, s).wait_send()


def tail_kernel(
    nblk, pieces, cols, d_q, d_k, d_v, normed, w_qk, w_v, gain_m, kept, got, tok, resid, gain,
    out_grad, out_q, out_k, out_v, out_first, out_gain, out_up, out_down, out_out,
    grad, weights, gains, joined, weight, acc, first_got, rest_sum,
    core_buf, side_out, side_buf, pair_buf, line_out, line_in, v_sum, v_got,
    gain_buf, gain_sum, gain_got, up_out, up_in, down_out, down_in,
    own_sem, send_s, recv_s, send_x, recv_x, send_y, recv_y, send_l, recv_l,
    send_v, recv_v, send_f, recv_f, send_g, recv_g, send_h, recv_h, send_u, recv_u, send_d, recv_d,
):
    head, blk = lax.axis_index("head"), lax.axis_index("blk")
    side, core, far = xor(head, 2), xor(head, 1), 3 - head
    greet(partners_of(head, blk, nblk))
    rows = grad.shape[1] // pieces
    line, place, parity = nblk // 2, lax.div(blk, 2), lax.rem(blk, 2)
    pair = blk + 1 - 2 * parity
    above, below = lax.rem(blk + 2, nblk), lax.rem(blk + nblk - 2, nblk)

    def part(ref, p):
        return ref.at[pl.ds(p * rows, rows)]

    def to_core(i, p, slot):
        return remote(
            part(grad.at[slot], p), part(core_buf.at[i], p), send_s.at[i, p], recv_s.at[i, p],
            core, blk,
        )

    def to_side(p):
        return remote(
            part(side_out, p), part(side_buf, p), send_x.at[p], recv_x.at[p], side, blk
        )

    def sum_of(t):
        return kept[t].astype(F32) + got[t].astype(F32)

    def up_copy(t, to):
        return remote(up_out.at[t], up_in.at[t], send_u.at[t], recv_u.at[t], head, to)

    def down_copy(t, to):
        return remote(down_out.at[t], down_in.at[t], send_d.at[t], recv_d.at[t], head, to)

    def first_hops():
        for n in range(line - 1):
            t = line - 1 - n

            @pl.when((place == 0) & (place < t))
            def _():
                up_out[t] = sum_of(t).astype(BF16)
                up_copy(t, above).start()

            @pl.when((place == line - 1) & (place > n))
            def _():
                down_out[n] = sum_of(n).astype(BF16)
                down_copy(n, below).start()

    def next_hops(n):
        t = line - 1 - n

        @pl.when((place > 0) & (place < t))
        def _():
            up_copy(t, above).wait_recv()
            up_out[t] = (sum_of(t) + up_in[t].astype(F32)).astype(BF16)
            up_copy(t, above).start()

        @pl.when((place < line - 1) & (place > n))
        def _():
            down_copy(n, below).wait_recv()
            down_out[n] = (sum_of(n) + down_in[n].astype(F32)).astype(BF16)
            down_copy(n, below).start()

    first_hops()
    half, kind = lax.div(head, 2), lax.rem(head, 2)

    def first_copy(i, to, slot):
        source = d_v.at[pl.ds(to * grad.shape[1], grad.shape[1])]
        return remote(source, first_got.at[slot], send_f.at[i], recv_f.at[slot], to, blk)

    def own_first(slot):
        source = d_v.at[pl.ds(head * grad.shape[1], grad.shape[1])]
        return pltpu.make_async_copy(source, first_got.at[slot], own_sem)

    @pl.when(half == 1)
    def _():
        for i, to in enumerate((core, side, far)):
            first_copy(i, to, kind).start()
        own_first(kind).start()

    mine = half == 0
    weight[:, : 2 * cols] = w_qk[...]
    fresh = jnp.concatenate([w_v[0], w_v[1]], axis=1)
    weight[:, 2 * cols :] = jnp.where(mine, fresh, jnp.zeros_like(fresh))
    gain_row = None
    for i, t in enumerate((far, side, core, head)):
        at = pl.ds(pl.multiple_of(t * grad.shape[1], grad.shape[1]), grad.shape[1])
        joined[:, :cols] = d_q[at, :]
        joined[:, cols : 2 * cols] = d_k[at, :]
        joined[:, 2 * cols : 3 * cols] = d_v[at, :]
        joined[:, 3 * cols :] = jnp.zeros((grad.shape[1], joined.shape[1] - 3 * cols), BF16)
        given = joined[...]
        whole = dotf(given[:, : 3 * cols], weight[...], NT)
        grad[t] = whole.astype(BF16)
        if i == 0:
            for p in range(pieces):
                to_core(0, p, far).start()
        if i == 2:
            for p in range(pieces):
                to_core(1, p, core).start()
        rows_in = normed[at, :]
        term = jnp.sum(whole * rows_in.astype(F32), axis=0, keepdims=True)
        gain_row = term if gain_row is None else gain_row + term
        term = dotf(rows_in, given, TN)
        acc[...] = term if i == 0 else acc[...] + term
        if i == 2:
            for p in range(pieces):
                to_core(0, p, far).wait_recv()
                part(side_out, p)[...] = (
                    part(grad.at[side], p)[...].astype(F32)
                    + part(core_buf.at[0], p)[...].astype(F32)
                ).astype(BF16)
                to_side(p).start()
    whole_part = weights.shape[1]
    for b in range(nblk):
        weights[b] = acc[b * whole_part : (b + 1) * whole_part].astype(BF16)

    def across(n):
        return remote(
            weights.at[2 * n + 1 - parity], pair_buf.at[n], send_y.at[n], recv_y.at[n], head, pair
        )

    for n in range(line):
        across(n).start()
    gain_row = gain_row / gain[...]
    for b in range(nblk):
        gains[b, 0] = gain_row[:, b * whole_part : (b + 1) * whole_part]
        gains[b, 1] = gain_m[:, b * whole_part : (b + 1) * whole_part]

    def gain_to(d):
        to = lax.rem(blk + d, nblk)
        return remote(gains.at[to], gain_buf.at[blk], send_g.at[d], recv_g.at[d], head, to)

    def gain_from(d):
        source = lax.rem(blk - d + nblk, nblk)
        return remote(gains.at[0], gain_buf.at[source], send_g.at[d], recv_g.at[d], head, source)

    for d in range(1, nblk):
        gain_to(d).start()
    gain_buf[blk] = gains[blk]

    def along(d, to):
        return remote(
            line_out.at[to], line_in.at[d], send_l.at[d], recv_l.at[d], head, 2 * to + parity
        )

    next_hops(0)
    for n in range(line):
        across(n).wait_recv()
        line_out[n] = (
            weights[2 * n + parity].astype(F32) + pair_buf[n].astype(F32)
        ).astype(BF16)
    for d in range(1, line):
        along(d, lax.rem(place + d, line)).start()
    for d in range(1, nblk):
        gain_from(d).wait_recv()
    gain_sum[...] = jnp.sum(gain_buf[...], axis=0)
    peers = (core, side, far)

    def gain_copy(i, to):
        return remote(gain_sum, gain_got.at[i], send_h.at[i], recv_h.at[i], to, blk)

    for i, to in enumerate(peers):
        gain_copy(i, to).start()
    for n in range(1, line - 1):
        next_hops(n)
    total = line_out[place].astype(F32)
    for d in range(1, line):
        along(d, lax.rem(place - d + line, line)).wait_recv()
        total = total + line_in[d].astype(F32)
    out_q[...] = total[:, :cols]
    out_k[...] = total[:, cols : 2 * cols]
    v_sum[0] = total[:, 2 * cols : 2 * cols + cols // 2]
    v_sum[1] = total[:, 2 * cols + cols // 2 : 3 * cols]

    def give(c, to):
        return remote(v_sum.at[c], v_got, send_v.at[c], recv_v.at[0], to, blk)

    for c in range(2):
        to = 2 * head + c

        @pl.when((half == 0) & (to != head))
        def _():
            give(c, to).start()

    for p in range(pieces):
        to_core(1, p, core).wait_recv()
        to_side(p).wait_recv()
        norm_grad = (
            part(grad.at[head], p)[...].astype(F32)
            + part(core_buf.at[1], p)[...].astype(F32)
            + part(side_buf, p)[...].astype(F32)
        )
        xhat, scale = statistics(part(tok, p)[...].astype(F32))
        part(out_grad, p)[...] = part(resid, p)[...] + norm_back(norm_grad, xhat, scale, gain[...])
    rest_sum[...] = sum_of(place)
    for t in range(line):

        @pl.when((place == t) & (place > 0))
        def _():
            up_copy(t, above).wait_recv()
            rest_sum[...] += up_in[t].astype(F32)

        @pl.when((place == t) & (place < line - 1))
        def _():
            down_copy(t, below).wait_recv()
            rest_sum[...] += down_in[t].astype(F32)

    inner = out_up.shape[1]
    out_up[...] = rest_sum[:, :inner]
    out_down[...] = rest_sum[:, inner : 2 * inner]
    out_out[...] = rest_sum[:, 2 * inner :].T
    for i, to in enumerate(peers):
        gain_copy(i, to).wait_recv()
    out_gain[...] = gain_sum[...] + gain_got[0] + gain_got[1] + gain_got[2]

    @pl.when(head == 0)
    def _():
        out_v[...] = v_sum[0]

    @pl.when(head != 0)
    def _():
        give(0, half).wait_recv()
        out_v[...] = v_got[...]

    for slot in range(2):

        @pl.when(head == 2 + slot)
        def _():
            own_first(slot).wait()

        @pl.when(head != 2 + slot)
        def _():
            first_copy(0, 2 + slot, slot).wait_recv()

    out_first[...] = jnp.concatenate([first_got[0], first_got[1]], axis=1).astype(F32)

    @pl.when(half == 1)
    def _():
        for i, to in enumerate((core, side, far)):
            first_copy(i, to, kind).wait_send()

    for c in range(2):
        to = 2 * head + c

        @pl.when((half == 0) & (to != head))
        def _():
            give(c, to).wait_send()

    for i, to in enumerate(peers):
        gain_copy(i, to).wait_send()
    for p in range(pieces):
        to_core(0, p, far).wait_send()
        to_core(1, p, core).wait_send()
        to_side(p).wait_send()
    for d in range(1, nblk):
        gain_to(d).wait_send()
    for n in range(line):
        across(n).wait_send()
    for d in range(1, line):
        along(d, lax.rem(place + d, line)).wait_send()
    for t in range(line):

        @pl.when(place < t)
        def _():
            up_copy(t, above).wait_send()

        @pl.when(place > t)
        def _():
            down_copy(t, below).wait_send()


def tail(nblk, d_q, d_k, d_v, normed, w_qk, w_v, gain_m, kept, got, tok, resid, gain, pieces=4):
    dma = pltpu.SemaphoreType.DMA
    row, part, cols = tok.shape, w_v.shape[1] // nblk, d_q.shape[1]
    inner = (kept.shape[2] - cols) // 2
    padded = -(-3 * cols // 128) * 128
    gains = jax.ShapeDtypeStruct((nblk, 2, 1, part), F32)
    half, line = (part, cols // 2), nblk // 2
    piece = (2, pieces)
    vmem = lambda *shape: pltpu.VMEM(shape, BF16)
    return pl.pallas_call(
        functools.partial(tail_kernel, nblk, pieces, cols),
        out_shape=[
            jax.ShapeDtypeStruct(row, F32),
            jax.ShapeDtypeStruct((part, cols), F32),
            jax.ShapeDtypeStruct((part, cols), F32),
            jax.ShapeDtypeStruct(half, F32),
            jax.ShapeDtypeStruct((row[0], 2 * cols), F32),
            jax.ShapeDtypeStruct(gains.shape[1:], F32),
            jax.ShapeDtypeStruct((part, inner), F32),
            jax.ShapeDtypeStruct((part, inner), F32),
            jax.ShapeDtypeStruct((cols, part), F32),
        ],
        in_specs=[WHOLE] * 12,
        out_specs=[WHOLE] * 9,
        scratch_shapes=[
            vmem(4, *row), vmem(nblk, part, padded), pltpu.VMEM(gains.shape, F32),
            vmem(row[0], padded), vmem(row[1], 3 * cols), pltpu.VMEM((row[1], padded), F32),
            vmem(2, row[0], cols), pltpu.VMEM(kept.shape[1:], F32),
            vmem(2, *row), vmem(*row), vmem(*row),
            vmem(line, part, padded), vmem(line, part, padded),
            vmem(line, part, padded),
            pltpu.VMEM((2,) + half, F32),
            pltpu.VMEM(half, F32),
            pltpu.VMEM(gains.shape, F32),
            pltpu.VMEM(gains.shape[1:], F32),
            pltpu.VMEM((3,) + gains.shape[1:], F32),
            vmem(*kept.shape), vmem(*kept.shape), vmem(*kept.shape), vmem(*kept.shape),
            dma,
            dma(piece), dma(piece),
            dma((pieces,)), dma((pieces,)),
            dma((line,)), dma((line,)), dma((line,)), dma((line,)),
            dma((2,)), dma((1,)),
            dma((3,)), dma((2,)),
            dma((nblk,)), dma((nblk,)),
            dma((3,)), dma((3,)),
            dma((line,)), dma((line,)), dma((line,)), dma((line,)),
        ],
        compiler_params=pltpu.CompilerParams(
            collective_id=4, has_side_effects=True, vmem_limit_bytes=60 << 20
        ),
        name="tail",
    )(d_q, d_k, d_v, normed, w_qk, w_v, gain_m, kept, got, tok, resid, gain)


def settle_kernel(count, *refs):
    sources, targets, sems = refs[:count], refs[count : 2 * count], refs[2 * count]
    copies = [
        pltpu.make_async_copy(source, target, sems.at[i])
        for i, (source, target) in enumerate(zip(sources, targets))
    ]
    for copy in copies:
        copy.start()
    for copy in copies:
        copy.wait()


def settle(arrays):
    count = len(arrays)
    return pl.pallas_call(
        functools.partial(settle_kernel, count),
        out_shape=[jax.ShapeDtypeStruct(a.shape, a.dtype) for a in arrays],
        in_specs=[ANY] * count,
        out_specs=[WHOLE] * count,
        scratch_shapes=[pltpu.SemaphoreType.DMA((count,))],
        name="settle",
    )(*arrays)


def statistics(values):
    center = values - jnp.mean(values, axis=-1, keepdims=True)
    scale = lax.rsqrt(jnp.mean(jnp.square(center), axis=-1, keepdims=True) + EPSILON)
    return center * scale, scale


def norm_back(grad, xhat, scale, gain):
    eg = grad * gain
    return scale * (
        eg
        - jnp.mean(eg, axis=-1, keepdims=True)
        - xhat * jnp.mean(eg * xhat, axis=-1, keepdims=True)
    )


def split_parts(values):
    high = values.astype(BF16).astype(F32)
    middle = (values - high).astype(BF16).astype(F32)
    return high, middle, values - high - middle


def front_kernel(
    nblk, parts, pieces, early, tok, first, w_q, w_k, w_v, w_up, w_down, w_out, gain_a, gain_m,
    normed, query, own, near_far, rest, qk_all, v_all, attn_gain, mlp_gain,
    tok_all, first_all, v_own, gain_all, w_qk, w_rest, gains, weight, normed_buf,
    own_sem, normed_sem, send_t, recv_t, send_s, recv_s, send_p, recv_p, send_w, recv_w,
    send_v, recv_v, qk_u, qk_ur, qk_d, qk_dr, qk_a, qk_ar, up_u, up_ur, up_d, up_dr, up_a, up_ar,
    send_x, recv_x, send_c, recv_c, send_f, recv_f, send_z, recv_z, send_y, recv_y,
):
    head, blk = lax.axis_index("head"), lax.axis_index("blk")
    side, core, beyond = xor(head, 2), xor(head, 1), 3 - head
    odd, place = lax.rem(blk, 2), lax.div(blk, 2)
    near = blk + 1 - 2 * odd
    up, down = lax.rem(blk + 2, nblk), lax.rem(blk + nblk - 2, nblk)
    greet(partners_of(head, blk, nblk))
    moved = [(tok, tok_all), (first, first_all)]
    weights = [(w_v, v_own), (gains, gain_all)]
    rows = tok.shape[0] // parts

    def part(ref, n):
        return ref.at[pl.ds(n * rows, rows)]

    def hop(sems, k, n, source, slot, target):
        dst = part(moved[k][1].at[slot], n)
        return remote(source, dst, sems[0].at[k, n], sems[1].at[k, n], target, blk)

    ts, ss, ps = (send_t, recv_t), (send_s, recv_s), (send_p, recv_p)
    order = [(k, n) for n in range(parts) for k in range(2)]
    for k, n in order:
        hop(ts, k, n, part(moved[k][0], n), head, side).start()
    cols, inner = w_q.shape[1], w_up.shape[1]
    w_qk[:, :cols] = w_q[...]
    w_qk[:, cols:] = w_k[...]
    qk_line = Line(nblk, head, blk, w_qk, qk_all, (qk_u, qk_ur), (qk_d, qk_dr), (qk_a, qk_ar))
    qk_line.begin()
    w_rest[:, :inner] = w_up[...]
    w_rest[:, inner : 2 * inner] = w_down[...]
    w_rest[:, 2 * inner :] = w_out[...].T
    line = Line(
        nblk, head, blk, w_rest, rest.at[head], (up_u, up_ur), (up_d, up_dr), (up_a, up_ar)
    )
    line.begin()
    gains[0] = gain_a[...]
    gains[1] = gain_m[...]

    def chunk(sems, slot, b, to, source=None):
        at = rest.at[slot, b]
        return remote(at if source is None else source, at, sems[0].at[b], sems[1].at[b], to, blk)

    xs, cs, fs = (send_x, recv_x), (send_c, recv_c), (send_f, recv_f)

    def to_core(b, source=None):
        chunk(cs, head, b, core, source).start()

    def to_side(b, source=None):
        @pl.when(b < early)
        def _():
            chunk(xs, head, b, side, source).start()

    to_core(blk, w_rest)
    own_rest = pltpu.make_async_copy(w_rest, rest.at[head, blk], own_sem)
    own_rest.start()

    def spread(d):
        to = lax.rem(blk + d, nblk)
        return [
            remote(src, dst.at[blk], send_w.at[i, d], recv_w.at[i, d], head, to)
            for i, (src, dst) in enumerate(weights)
        ]

    def from_peer(d):
        source = lax.rem(blk - d + nblk, nblk)
        return [
            remote(src, dst.at[source], send_w.at[i, d], recv_w.at[i, d], head, source)
            for i, (src, dst) in enumerate(weights)
        ]

    for d in range(1, nblk):
        for copy in spread(d):
            copy.start()
    for k, n in order:
        hop(ss, k, n, part(moved[k][0], n), head, core).start()
    tok_all[head] = tok[...]
    first_all[head] = first[...]
    v_own[blk] = w_v[...]
    gain_all[blk] = gains[...]
    qk_all[blk] = w_qk[...]

    def pass_on(k, n):
        landed = part(moved[k][1].at[side], n)
        hop(ts, k, n, landed, side, side).wait_recv()
        hop(ps, k, n, landed, side, core).start()

    steps = nblk // 2 - 1
    for s in range(steps):
        qk_line.step(s)
    for s in range(steps):
        line.step(s, to_core)
        for k, n in order[s * len(order) // steps : (s + 1) * len(order) // steps]:
            pass_on(k, n)
    to_side(blk, w_rest)
    for s in range(steps):

        @pl.when(place - 1 - s >= 0)
        def _():
            to_side(blk - 2 - 2 * s)

        @pl.when(place + 1 + s < nblk // 2)
        def _():
            to_side(blk + 2 + 2 * s)

    for d in range(1, nblk):
        for copy in from_peer(d):
            copy.wait_recv()
    half, kind = lax.div(head, 2), lax.rem(head, 2)
    for i in range(2):
        target = half + 2 * i

        @pl.when(target == head)
        def _():
            v_all[kind] = v_own[...]

        @pl.when(target != head)
        def _():
            remote(v_own, v_all.at[kind], send_v.at[i], recv_v.at[kind], target, blk).start()

    for o in range(nblk // 2):
        qk_line.land(o)
    for c in range(2):
        source = 2 * kind + c

        @pl.when(source != head)
        def _():
            remote(v_own, v_all.at[c], send_v.at[0], recv_v.at[c], source, blk).wait_recv()

    attn_gain[...] = jnp.concatenate([gain_all[b, 0] for b in range(nblk)], axis=1)
    mlp_gain[...] = jnp.concatenate([gain_all[b, 1] for b in range(nblk)], axis=1)

    step = own.shape[0] // pieces

    def slab(ref, n):
        return ref.at[pl.ds(n * step, step)]

    def far_copy(n, to):
        return remote(slab(own, n), slab(near_far.at[0], n), send_z.at[n], recv_z.at[n], head, to)

    def near_copy(n, src):
        return remote(src, slab(near_far.at[1], n), send_y.at[n], recv_y.at[n], head, near)

    size = HEAD_DIM
    pair = 2 * size
    width = tok.shape[1]
    block = w_q.shape[0]
    for b in range(nblk):
        at = pl.ds(b * block, block)
        both, fresh = qk_all[b], jnp.concatenate([v_all[0, b], v_all[1, b]], axis=1)
        key = both[:, cols:]
        weight[at, :pair] = key[:, :pair]
        weight[at, pair : 2 * pair] = fresh[:, :pair]
        weight[at, 2 * pair : 3 * pair] = jnp.concatenate([key[:, pair:], fresh[:, pair:]], axis=1)
        weight[at, 3 * pair :] = jnp.concatenate(
            [both[:, :cols], jnp.zeros((block, WIDTH - cols), BF16)], axis=1
        )
    stores = []
    for i, t in enumerate((head, side, core, beyond)):
        if i == 2:
            for k, n in order:
                hop(ss, k, n, part(moved[k][1].at[core], n), core, core).wait_recv()
        if i == 3:
            for k, n in order:
                hop(ps, k, n, part(moved[k][1].at[beyond], n), beyond, core).wait_recv()
        total = tok.shape[0]
        at = pl.ds(pl.multiple_of(t * total, total), total)
        xhat, _ = statistics(tok_all[t].astype(F32))
        row = (xhat * attn_gain[...]).astype(BF16)
        normed_buf[t] = row
        stores.append(pltpu.make_async_copy(normed_buf.at[t], normed.at[at], normed_sem.at[i]))
        stores[-1].start()
        out = dotf(row, weight[...])
        query[at, :] = (out[:, 3 * pair :].astype(BF16).astype(F32) * size**-0.5).astype(BF16)
        done = out[:, : 3 * pair].astype(BF16)
        given = first_all[t]
        kept = jnp.where(kind == 0, given[:, :cols], given[:, cols:])
        other = jnp.concatenate(
            [done[:, :pair], kept[:, :pair], done[:, 2 * pair : 2 * pair + size], kept[:, pair:]],
            axis=1,
        )
        own[at, :] = jnp.where(half == 0, done, other)
        for n in range(pieces // 4):
            n = t * (pieces // 4) + n

            @pl.when(blk + 2 < nblk)
            def _():
                far_copy(n, up).start()

            @pl.when(odd == 0)
            def _():
                near_copy(n, slab(own, n)).start()

    for o in range(nblk // 2):

        line.land(o)
        to_core(2 * o + 1 - odd)
        to_side(2 * o + 1 - odd)

    for i, t in enumerate((head, side, core, beyond)):
        for n in range(pieces // 4):
            n = t * (pieces // 4) + n

            @pl.when(blk >= 2)
            def _():
                far_copy(n, down).wait_recv()

            @pl.when((blk >= 2) & (odd == 1))
            def _():
                near_copy(n, slab(near_far.at[0], n)).start()

    own_rest.wait()
    for b in range(early):
        chunk(xs, side, b, side).wait_recv()
        chunk(fs, side, b, core).start()
    for b in range(nblk):
        chunk(cs, core, b, core).wait_recv()
    for b in range(early):
        chunk(fs, beyond, b, core).wait_recv()
        chunk(xs, head, b, side).wait_send()
        chunk(fs, side, b, core).wait_send()
    for b in range(nblk):
        chunk(cs, head, b, core).wait_send()
    for copy in stores:
        copy.wait()
    for n in range(pieces):

        @pl.when((blk >= 2) | (odd == 1))
        def _():
            near_copy(n, slab(own, n)).wait_recv()

        @pl.when(blk + 2 < nblk)
        def _():
            far_copy(n, up).wait_send()

        @pl.when((blk >= 2) | (odd == 0))
        def _():
            near_copy(n, slab(own, n)).wait_send()

    for i in range(2):
        target = half + 2 * i

        @pl.when(target != head)
        def _():
            remote(v_own, v_all.at[kind], send_v.at[i], recv_v.at[kind], target, blk).wait_send()

    for k, n in order:
        hop(ts, k, n, part(moved[k][0], n), head, side).wait_send()
        hop(ss, k, n, part(moved[k][0], n), head, core).wait_send()
        hop(ps, k, n, part(moved[k][1].at[side], n), side, core).wait_send()
    for d in range(1, nblk):
        for copy in spread(d):
            copy.wait_send()
    qk_line.finish()
    line.finish()


def front(
    nblk, early, tok, first, w_q, w_k, w_v, w_up, w_down, w_out, gain_a, gain_m, parts=4, pieces=8
):
    dma = pltpu.SemaphoreType.DMA
    (rows, width), (part, cols) = tok.shape, w_q.shape
    total = 4 * rows
    both = w_up.shape[1] + w_down.shape[1] + w_out.shape[0]
    low = lambda *shape: jax.ShapeDtypeStruct(shape, BF16)
    vmem = lambda *shape: pltpu.VMEM(shape, BF16)
    line = [dma((nblk // 2,))] * 6
    return pl.pallas_call(
        functools.partial(front_kernel, nblk, parts, pieces, early),
        out_shape=[
            low(total, width),
            low(total, WIDTH),
            low(total, 2 * cols),
            low(2, total, 2 * cols),
            low(4, nblk, part, both),
            low(nblk, part, 2 * cols),
            low(2, nblk, *w_v.shape),
            jax.ShapeDtypeStruct((1, width), F32),
            jax.ShapeDtypeStruct((1, width), F32),
        ],
        in_specs=[WHOLE] * 10,
        out_specs=[ANY, WHOLE, WHOLE, ANY, ANY] + [WHOLE] * 4,
        scratch_shapes=[
            vmem(4, *tok.shape),
            vmem(4, *first.shape),
            vmem(nblk, *w_v.shape),
            pltpu.VMEM((nblk, 2) + gain_a.shape, F32),
            vmem(part, 2 * cols),
            vmem(part, both),
            pltpu.VMEM((2,) + gain_a.shape, F32),
            vmem(width, 2 * cols + WIDTH),
            vmem(4, *tok.shape),
            dma,
            dma((4,)),
        ]
        + [dma((2, parts))] * 6
        + [dma((2, nblk))] * 2
        + [dma((2,))] * 2
        + line * 2
        + [dma((nblk,))] * 6
        + [dma((pieces,))] * 4,
        compiler_params=pltpu.CompilerParams(
            collective_id=0, has_side_effects=True, vmem_limit_bytes=56 << 20
        ),
        name="front",
    )(tok, first, w_q, w_k, w_v, w_up, w_down, w_out, gain_a, gain_m)


def gelu_both(pre):
    square = pre * pre
    inner = jnp.tanh(GELU_SCALE * (pre + 0.044715 * square * pre))
    slope = GELU_SCALE * (1.0 + 3.0 * 0.044715 * square)
    outer = 0.5 * (1.0 + inner)
    return pre * outer, outer + 0.5 * pre * (1.0 - inner * inner) * slope


def middle_kernel(
    nblk, up_cols, cross, pieces, tok, mixed_parts, cot, gain, gathered, late, query,
    out, grad_resid, grad_wide, gain_part, keep_up, keep, give, query_later,
    up, down, w_out, up_grad, down_grad, out_grad, mixed, wide_parts, up_got, down_got, out_got,
    sems, out_sems, send_m, recv_m, send_g, recv_g, send_c, recv_c,
    send_z, recv_z, send_y, recv_y, up_side, up_side_got, send_x, recv_x, hidden_all, pre_all, normed_t, cot_t, late_far, send_l, recv_l,
):
    head, blk = lax.axis_index("head"), lax.axis_index("blk")
    x, core_index = lax.div(head, 2), lax.rem(head, 2)
    core = xor(head, 1)
    others = [xor(head, 2), 3 - head, core]
    odd = lax.rem(blk, 2)
    pair = blk + 1 - 2 * odd
    above, below = lax.rem(blk + 2, nblk), lax.rem(blk + nblk - 2, nblk)
    greet(partners_of(head, blk, nblk, blks=False) + [(head, b) for b in (pair, above, below)])
    heads_of = 4
    part = gathered.shape[2]
    cols = mixed.shape[2]
    heads = cols // HEAD_DIM

    def mixed_copy(i, to, slot):
        return remote(
            mixed_parts.at[to], mixed.at[slot], send_m.at[i], recv_m.at[i], to, blk
        )

    for i, to in enumerate(others):
        mixed_copy(i, to, head).start()
    late_copy = remote(late, late_far, send_l, recv_l, core, blk)
    late_copy.start()
    early = nblk - late.shape[0]
    piece_rows = query.shape[0] // pieces

    def slab(ref, p):
        return ref.at[pl.ds(p * piece_rows, piece_rows)]

    def far_copy(p, to):
        dst = slab(query_later.at[1], p)
        return remote(slab(query, p), dst, send_z.at[p], recv_z.at[p], head, to)

    def near_copy(p, src):
        return remote(src, slab(query_later.at[0], p), send_y.at[p], recv_y.at[p], head, pair)

    for p in range(pieces):

        @pl.when(blk >= 2)
        def _():
            far_copy(p, below).start()

        @pl.when(odd == 1)
        def _():
            near_copy(p, slab(query, p)).start()

    def relay(p):
        @pl.when(blk + 2 < nblk)
        def _():
            far_copy(p, above).wait_recv()

        @pl.when((blk + 2 < nblk) & (odd == 0))
        def _():
            near_copy(p, slab(query_later.at[1], p)).start()

    chunks = [2 * n + c for n in (1 - x, x) for c in (1 - core_index, core_index)]
    side = others[0]
    sources = (3 - head, others[0], core)

    def source(i, b):
        if b < early or i > 1:
            return gathered.at[chunks[i], b]
        return (late_far, late)[i].at[b - early]

    def load(i, which):
        target, lo, size = ((w_out, 2 * up_cols, cols), (up, 0, up_cols), (down, up_cols, up_cols))[
            which
        ]
        return [
            pltpu.make_async_copy(
                source(i, b).at[:, pl.ds(lo, size)],
                target.at[i, pl.ds(b * part, part)],
                sems.at[which, i, b],
            )
            for b in range(nblk)
        ]

    turns = (2, 3, 1, 0)
    order = [(i, 0) for i in turns] + [(i, w) for i in turns for w in (1, 2)]
    for i, which in order:
        for b, copy in enumerate(load(i, which)):
            if i or b < early:
                copy.start()
    mixed[head] = mixed_parts[head]
    late_copy.wait()
    for which in range(3):
        for copy in load(0, which)[early:]:
            copy.start()
    for i in range(heads_of):
        for copy in load(i, 0):
            copy.wait()
    for i, to in enumerate(others):
        mixed_copy(i, to, to).wait_recv()
    branch = None
    for i in range(heads_of):
        term = dotf(mixed[chunks[i]], w_out[i], NT)
        branch = term if branch is None else branch + term
    resid = tok[...].astype(F32) + branch
    xhat, scale = statistics(resid)
    normed = (xhat * gain[...]).astype(BF16)
    cotangent = cot[...]
    total, grad_normed = resid, None

    def to_core(n, k):
        mine, theirs = ((up_grad, up_got), (down_grad, down_got), (out_grad, out_got))[k]
        return remote(mine.at[2 * n], theirs.at[n], send_c.at[k, n], recv_c.at[k, n], core, blk)

    def to_side():
        return remote(up_side, up_side_got, send_x, recv_x, side, blk)

    normed_t[...] = normed.T
    cot_t[...] = cotangent.T
    for n, i in enumerate(turns):
        for copy in load(i, 1) + load(i, 2):
            copy.wait()
        hidden, slope = gelu_both(dotf(normed, up[i]))
        hidden_all[i] = hidden.astype(BF16)
        pre_all[i] = (slope * dotf(cotangent, down[i])).astype(BF16)
        total = total + dotf(hidden_all[i], down[i], NT)
        term = dotf(pre_all[i], up[i], NT)
        grad_normed = term if grad_normed is None else grad_normed + term
        for p in range(n * pieces // heads_of, (n + 1) * pieces // heads_of):
            relay(p)
    grad = cotangent.astype(F32) + norm_back(grad_normed, xhat, scale, gain[...])
    branch_grad = grad.astype(BF16)
    lane = lax.broadcasted_iota(jnp.int32, (tok.shape[0], WIDTH), 1)

    def wide_copy(i, to, slot):
        return remote(
            wide_parts.at[to], grad_wide.at[slot], send_g.at[i], recv_g.at[i], to, blk
        )

    for i in range(heads_of):
        h = chunks[i]
        rows = dotf(branch_grad, w_out[i]).astype(BF16).astype(F32)
        product = rows * mixed[h].astype(F32)
        wide = jnp.concatenate([rows, jnp.zeros((rows.shape[0], WIDTH - cols), F32)], axis=1)
        for k in range(heads):
            delta = jnp.sum(
                product[:, k * HEAD_DIM : (k + 1) * HEAD_DIM], axis=1, keepdims=True
            )
            for c, piece in enumerate(split_parts(-delta)):
                wide = jnp.where(lane == cols + SPLITS * k + c, piece, wide)
        wide_parts[h] = wide.astype(BF16)
        if i < 3:
            wide_copy(i, h, head).start()
    grad_wide[head] = wide_parts[head]
    out[...] = total.astype(BF16)
    gain_part[...] = jnp.sum(grad_normed * xhat, axis=0, keepdims=True)
    grad_resid[...] = grad
    for i in range(heads_of):
        up_grad[i] = dotf(normed_t[...], pre_all[i]).astype(BF16)
        down_grad[i] = dotf(cot_t[...], hidden_all[i]).astype(BF16)
        if i % 2 == 0:
            to_core(i // 2, 0).start()
            to_core(i // 2, 1).start()
        if i == 1:
            to_core(0, 0).wait_recv()
            up_side[...] = (
                up_grad[1, :, :cross].astype(F32) + up_got[0, :, :cross].astype(F32)
            ).astype(BF16)
            to_side().start()
    branch_t = branch_grad.T
    for i in range(heads_of):
        out_grad[i] = dotf(branch_t, mixed[chunks[i]]).astype(BF16)
        if i % 2 == 0:
            to_core(i // 2, 2).start()

    def store(k, source, target, lo):
        size = source.shape[1]
        return [
            pltpu.make_async_copy(
                source.at[pl.ds(b * part, part)],
                target.at[b].at[:, pl.ds(lo, size)],
                out_sems.at[k, b],
            )
            for b in range(nblk)
        ]

    stores = []
    far_up = up_cols - cross
    for n, target in enumerate((give, keep)):
        at = 2 * n + 1
        for k, (mine, theirs) in enumerate(
            ((up_grad, up_got), (down_grad, down_got), (out_grad, out_got))
        ):
            if n or k:
                to_core(n, k).wait_recv()
            mine[at] = (mine[at].astype(F32) + theirs[n].astype(F32)).astype(BF16)
        stores += store(3 * n, up_grad.at[at].at[:, pl.ds(cross, far_up)], target, 0)
        stores += store(3 * n + 1, down_grad.at[at], target, far_up)
        stores += store(3 * n + 2, out_grad.at[at], target, far_up + up_cols)
        for copy in stores[-3 * nblk :]:
            copy.start()
    to_side().wait()
    up_side[...] = (up_grad[3, :, :cross].astype(F32) + up_side_got[...].astype(F32)).astype(BF16)
    stores += store(6, up_side, keep_up, 0)
    for copy in stores[-nblk:]:
        copy.start()
    for copy in stores:
        copy.wait()
    for k in range(3):
        for n in range(2):
            to_core(n, k).wait_send()
    for i in range(3):
        wide_copy(i, chunks[i], sources[i]).wait_recv()
    for i, to in enumerate(others):
        mixed_copy(i, to, head).wait_send()
        wide_copy(i, chunks[i], head).wait_send()
    for p in range(pieces):

        @pl.when((blk + 2 < nblk) | (odd == 0))
        def _():
            near_copy(p, slab(query, p)).wait_recv()

        @pl.when(blk >= 2)
        def _():
            far_copy(p, below).wait_send()

        @pl.when((blk + 2 < nblk) | (odd == 1))
        def _():
            near_copy(p, slab(query, p)).wait_send()


def middle(nblk, tok, mixed_parts, cot, gain, gathered, late, query, up_cols, cross=256, pieces=8):
    heads_of, rows, cols = mixed_parts.shape
    width, part = tok.shape[1], gathered.shape[2]
    flops = 2 * rows * width * (6 * up_cols * heads_of + 3 * width)
    dma = pltpu.SemaphoreType.DMA
    vmem = lambda *shape: pltpu.VMEM(shape, BF16)
    return pl.pallas_call(
        functools.partial(middle_kernel, nblk, up_cols, cross, pieces),
        out_shape=[
            jax.ShapeDtypeStruct((rows, width), BF16),
            jax.ShapeDtypeStruct((rows, width), F32),
            jax.ShapeDtypeStruct((heads_of, rows, WIDTH), BF16),
            jax.ShapeDtypeStruct((1, width), F32),
            jax.ShapeDtypeStruct((nblk, part, cross), BF16),
            jax.ShapeDtypeStruct((nblk, part, gathered.shape[3] - cross), BF16),
            jax.ShapeDtypeStruct((nblk, part, gathered.shape[3] - cross), BF16),
            jax.ShapeDtypeStruct((2,) + query.shape, BF16),
        ],
        in_specs=[WHOLE] * 4 + [ANY] * 3,
        out_specs=[WHOLE] * 4 + [ANY] * 4,
        scratch_shapes=[
            vmem(heads_of, width, up_cols), vmem(heads_of, width, up_cols),
            vmem(heads_of, width, cols),
            vmem(heads_of, width, up_cols), vmem(heads_of, width, up_cols),
            vmem(heads_of, width, cols),
            vmem(heads_of, rows, cols), vmem(heads_of, rows, WIDTH),
            vmem(2, width, up_cols), vmem(2, width, up_cols), vmem(2, width, cols),
            dma((3, heads_of, nblk)), dma((7, nblk)),
            dma((3,)), dma((3,)), dma((3,)), dma((3,)), dma((3, 2)), dma((3, 2)),
            dma((pieces,)), dma((pieces,)), dma((pieces,)), dma((pieces,)),
            vmem(width, cross), vmem(width, cross), dma, dma,
            vmem(heads_of, rows, up_cols), vmem(heads_of, rows, up_cols),
            vmem(width, rows), vmem(width, rows),
            vmem(*late.shape), dma, dma,
        ],
        compiler_params=pltpu.CompilerParams(
            collective_id=2, has_side_effects=True, vmem_limit_bytes=62 << 20
        ),
        cost_estimate=pl.CostEstimate(
            flops=flops, bytes_accessed=24 << 20, transcendentals=rows * up_cols * heads_of
        ),
        name="middle",
    )(tok, mixed_parts, cot, gain, gathered, late, query)


def pair_sum_kernel(up, ours, theirs, keep, give):
    odd = lax.rem(lax.axis_index("blk"), 2)
    sums = [(ours[n].astype(F32) + theirs[n].astype(F32)).astype(BF16) for n in range(2)]
    cols = up.shape[2]
    keep[0, :, :cols] = jnp.where(odd == 0, up[0], up[1])
    give[0, :, :cols] = jnp.where(odd == 0, up[1], up[0])
    keep[0, :, cols:] = jnp.where(odd == 0, sums[0], sums[1])
    give[0, :, cols:] = jnp.where(odd == 0, sums[1], sums[0])


def pair_sum(up, ours, theirs):
    nblk, part, width = ours.shape
    total = width + up.shape[2]
    spec = lambda n, cols: pl.BlockSpec((n, part, cols), lambda i: (i, 0, 0))
    return pl.pallas_call(
        pair_sum_kernel,
        grid=(nblk // 2,),
        in_specs=[spec(2, up.shape[2]), spec(2, width), spec(2, width)],
        out_specs=[spec(1, total)] * 2,
        out_shape=[jax.ShapeDtypeStruct((nblk // 2, part, total), BF16)] * 2,
        cost_estimate=pl.CostEstimate(
            flops=nblk * part * width, bytes_accessed=6 * nblk * part * width, transcendentals=0
        ),
        name="pair_sum",
    )(up, ours, theirs)


def head_rows(h, heads, shape):
    row = lax.broadcasted_iota(jnp.int32, shape, 0)
    real = heads * HEAD_DIM
    own = (row >= h * HEAD_DIM) & (row < (h + 1) * HEAD_DIM)
    return own | ((row >= real + SPLITS * h) & (row < real + SPLITS * (h + 1)))


def per_head(wide, heads, out):
    flipped = wide.T
    for h in range(heads):
        out[h] = jnp.where(head_rows(h, heads, flipped.shape), flipped, jnp.zeros_like(flipped))


def doc_start(meta, ndocs, t):
    def step(j,c):
        cum,best=c
        best=jnp.where(cum<=t,cum,best)
        return cum+meta[1+j],best
    return lax.fori_loop(0,ndocs,step,(jnp.int32(0),jnp.int32(0)),unroll=True)[1]

def doc_end(meta, ndocs, t):
    def step(j,c):
        cum,best,found=c
        cum=cum+meta[1+j]
        take=(cum>t)&(found==0)
        return cum,jnp.where(take,cum,best),jnp.where(take,1,found)
    return lax.fori_loop(0,ndocs,step,(jnp.int32(0),jnp.int32(0),jnp.int32(0)),unroll=True)[1]

def starts_vec(meta, ndocs, t):
    def step(j,c):
        cum,best=c
        return cum+meta[1+j],jnp.where(cum<=t,cum,best)
    return lax.fori_loop(0,ndocs,step,(jnp.int32(0),jnp.zeros(t.shape,jnp.int32)),unroll=True)[1]

def ends_vec(meta, ndocs, t):
    def step(j,c):
        cum,best=c
        ln=meta[1+j]
        return cum+ln,jnp.where(cum<=t,cum+ln,best)
    return lax.fori_loop(0,ndocs,step,(jnp.int32(0),jnp.zeros(t.shape,jnp.int32)),unroll=True)[1]

def widened(columns, heads):
    rows, width = columns.shape
    ones = jnp.ones((rows, SPLITS * heads), BF16)
    empty = jnp.zeros((rows, WIDTH - width - SPLITS * heads), BF16)
    return jnp.concatenate([columns, ones, empty], axis=1)


def unpack_rows(packed, heads):
    pair = 2 * HEAD_DIM
    key = jnp.concatenate([packed[:, :pair], packed[:, 2 * pair : 2 * pair + HEAD_DIM]], axis=1)
    value = jnp.concatenate([packed[:, pair : 2 * pair], packed[:, 2 * pair + HEAD_DIM :]], axis=1)
    return widened(key, heads), widened(value, heads)


STEP = 512


def build_window(heads, start, earlier, own, packed, sems, keys, values, key_rows, value_rows):
    before = earlier.shape[0] // STEP
    chunks = before + own.shape[0] // STEP

    def copy(n, source, row):
        return pltpu.make_async_copy(
            source.at[pl.ds(row * STEP, STEP)], packed.at[pl.ds(n * STEP, STEP)], sems.at[n]
        )

    def begin(n, carry):
        @pl.when(n < before)
        def _():
            copy(n, earlier, n).start()

        @pl.when(n >= before)
        def _():
            copy(n, own, n - before).start()

        return carry

    def build(n, carry):
        copy(n, own, 0).wait()
        at = pl.ds(pl.multiple_of(n * STEP, STEP), STEP)
        key, value = unpack_rows(packed[at, :], heads)
        for wide, rows, flipped in ((key, keys, key_rows), (value, values, value_rows)):
            if rows is not None:
                rows[at, :] = wide
            if flipped is not None:
                turned = wide.T
                for h in range(heads):
                    flipped[h, :HEAD_DIM, at] = turned[h * HEAD_DIM : (h + 1) * HEAD_DIM]
        return carry

    lax.fori_loop(start, chunks, begin, 0)
    lax.fori_loop(start, chunks, build, 0)


def three(lo,a,b,hi,body):
    lax.fori_loop(lo,a,lambda j,_: body(j,True),None)
    lax.fori_loop(a,b,lambda j,_: body(j,False),None)
    lax.fori_loop(b,hi,lambda j,_: body(j,True),None)

def query_tiles(meta, ndocs, t0, wbase, tq, tk):
    lo = (doc_start(meta, ndocs, t0) - wbase) // tk
    f0 = (doc_start(meta, ndocs, t0 + tq - 1) - wbase + tk - 1) // tk
    f1 = (t0 - wbase) // tk
    hi = (t0 + tq - 1 - wbase) // tk + 1
    return lo, jnp.minimum(f0, f1), f1, hi


def fwd_kernel(heads, ndocs, tq, tk, meta, q_ref, earlier, own, mix_ref, wide_ref,
               k_ref, vt_ref, qt, m_ref, acc_ref, packed, sems):
    i = pl.program_id(0)
    width = q_ref.shape[1]
    real = heads * HEAD_DIM
    base = meta[0]
    wbase = base - earlier.shape[0]

    @pl.when(i == 0)
    def _():
        vt_ref[:, HEAD_DIM:, :] = jnp.ones_like(vt_ref[:, HEAD_DIM:, :])
        start = (doc_start(meta, ndocs, base) - wbase) // tk * (tk // STEP)
        build_window(heads, start, earlier, own, packed, sems, k_ref, None, None, vt_ref)

    t0 = base + i * tq
    lo, f0, f1, hi = query_tiles(meta, ndocs, t0, wbase, tq, tk)
    q = q_ref[...]
    trow = t0 + lax.broadcasted_iota(jnp.int32, (8, tq), 1)
    srow = starts_vec(meta, ndocs, trow)[:1]
    trow = trow[:1]
    lane = lax.broadcasted_iota(jnp.int32, (tq, width), 1)

    def visible(off):
        u = wbase + off + lax.broadcasted_iota(jnp.int32, (tk, tq), 0)
        return (u >= srow) & (u <= trow)

    itself = q.astype(F32) * k_ref[pl.ds(pl.multiple_of(t0 - wbase, tq), tq), :].astype(F32)
    shifted = q.astype(F32)
    for h in range(heads):
        mine = (lane >= h * HEAD_DIM) & (lane < (h + 1) * HEAD_DIM)
        score = jnp.sum(jnp.where(mine, itself, 0.0), axis=1, keepdims=True)
        for c, piece in enumerate(split_parts(-score)):
            shifted = jnp.where(lane == real + SPLITS * h + c, piece, shifted)
    per_head(shifted.astype(BF16), heads, qt)
    acc_ref[...] = jnp.zeros_like(acc_ref)

    def quick(j, masked):
        off = pl.multiple_of(j * tk, tk)
        k = k_ref[pl.ds(off, tk), :]
        if masked:
            vis = visible(off)
        for h in range(heads):
            p = jnp.exp(dotf(k, qt[h]))
            if masked:
                p = jnp.where(vis, p, 0.0)
            acc_ref[h] += dotf(vt_ref[h, :, pl.ds(off, tk)], p.astype(BF16))

    def finish(extra):
        rows = []
        parts = []
        for h in range(heads):
            acc = acc_ref[h]
            total = acc[HEAD_DIM : HEAD_DIM + 1]
            rows.append(acc[:HEAD_DIM] / total)
            at = real + SPLITS * h
            shift = jnp.sum(qt[h, at : at + SPLITS, :].astype(F32), axis=0, keepdims=True)
            parts += split_parts(shift - extra[h] - jnp.log(total))
        rest = jnp.zeros((width - real - len(parts), tq), F32)
        turned = jnp.concatenate(rows + parts + [rest], axis=0).T
        mix_ref[0] = turned[:, :real].astype(BF16)
        wide_ref[...] = jnp.where(lane < real, q.astype(F32), turned).astype(BF16)

    three(lo, f0, f1, hi, quick)
    none = jnp.zeros((1, tq), F32)
    finish([none] * heads)
    sums = acc_ref[:, HEAD_DIM : HEAD_DIM + 1, :]
    fits = jnp.max(jnp.where(sums < 1e30, 0.0, 1.0)) == 0.0

    @pl.when(jnp.logical_not(fits))
    def _():
        acc_ref[...] = jnp.zeros_like(acc_ref)
        m_ref[...] = jnp.full_like(m_ref, EXCLUDED)

        def body(j, carry):
            off = pl.multiple_of(j * tk, tk)
            k = k_ref[pl.ds(off, tk), :]
            vis = visible(off)
            for h in range(heads):
                s = jnp.where(vis, dotf(k, qt[h]), EXCLUDED)
                old = m_ref[h, :1]
                new = jnp.maximum(old, jnp.max(s, axis=0, keepdims=True))
                m_ref[h, :1] = new
                p = jnp.exp(s - new).astype(BF16)
                acc_ref[h] = acc_ref[h] * jnp.exp(old - new) + dotf(
                    vt_ref[h, :, pl.ds(off, tk)], p
                )
            return carry

        lax.fori_loop(lo, hi, body, 0)
        finish([m_ref[h, :1] for h in range(heads)])


SCALARS = pl.BlockSpec(memory_space=pltpu.SMEM)


def attention_fwd(meta, q, earlier, own, heads, tq, tk):
    block, width = q.shape
    window = block + earlier.shape[0]
    ndocs = meta.shape[0] - 1
    return pl.pallas_call(
        functools.partial(fwd_kernel, heads, ndocs, tq, tk),
        grid=(block // tq,),
        in_specs=[
            SCALARS,
            pl.BlockSpec((tq, width), lambda i: (i, 0)),
            ANY,
            ANY,
        ],
        out_specs=[
            pl.BlockSpec((1, tq, heads * HEAD_DIM), lambda i: (i, 0, 0)),
            pl.BlockSpec((tq, width), lambda i: (i, 0)),
        ],
        out_shape=[
            jax.ShapeDtypeStruct((block // tq, tq, heads * HEAD_DIM), BF16),
            jax.ShapeDtypeStruct((block, width), BF16),
        ],
        scratch_shapes=[
            pltpu.VMEM((window, width), BF16),
            pltpu.VMEM((heads, HEAD_DIM + 16, window), BF16),
            pltpu.VMEM((heads, width, tq), BF16),
            pltpu.VMEM((heads, 8, tq), F32),
            pltpu.VMEM((heads, HEAD_DIM + 16, tq), F32),
            pltpu.VMEM((window, own.shape[1]), BF16),
            pltpu.SemaphoreType.DMA((window // STEP,)),
        ],
        compiler_params=pltpu.CompilerParams(vmem_limit_bytes=56 << 20),
        cost_estimate=pl.CostEstimate(
            flops=30_000_000_000, bytes_accessed=12 << 20, transcendentals=20_000_000
        ),
        name="attn_fwd",
    )(meta, q, earlier, own)


def dq_kernel(heads, ndocs, tq, tk, meta, q_ref, do_ref, earlier, own, dq_ref,
              k_ref, v_ref, kt_ref, qt, dot, acc_ref, packed, sems):
    i = pl.program_id(0)
    base = meta[0]
    wbase = base - earlier.shape[0]

    @pl.when(i == 0)
    def _():
        start = (doc_start(meta, ndocs, base) - wbase) // tk * (tk // STEP)
        build_window(heads, start, earlier, own, packed, sems, k_ref, v_ref, kt_ref, None)

    t0 = base + i * tq
    per_head(q_ref[...], heads, qt)
    per_head(do_ref[...], heads, dot)
    acc_ref[...] = jnp.zeros_like(acc_ref)
    trow = t0 + lax.broadcasted_iota(jnp.int32, (8, tq), 1)
    srow = starts_vec(meta, ndocs, trow)[:1]
    trow = trow[:1]

    def body(j, masked):
        off = pl.multiple_of(j * tk, tk)
        k = k_ref[pl.ds(off, tk), :]
        v = v_ref[pl.ds(off, tk), :]
        if masked:
            u = wbase + off + lax.broadcasted_iota(jnp.int32, (tk, tq), 0)
            vis = (u >= srow) & (u <= trow)
        for h in range(heads):
            p = jnp.exp(dotf(k, qt[h]))
            if masked:
                p = jnp.where(vis, p, 0.0)
            ds = (p * dotf(v, dot[h])).astype(BF16)
            acc_ref[h] += dotf(kt_ref[h, :, pl.ds(off, tk)], ds)

    three(*query_tiles(meta, ndocs, t0, wbase, tq, tk), body)
    turned = acc_ref[...].reshape(heads * HEAD_DIM, tq).T
    dq_ref[...] = (turned * (HEAD_DIM**-0.5)).astype(BF16)


def attention_dq(meta, q, do, earlier, own, heads, tq, tk):
    block, width = q.shape
    window = block + earlier.shape[0]
    ndocs = meta.shape[0] - 1
    row = lambda w: pl.BlockSpec((tq, w), lambda i: (i, 0))
    return pl.pallas_call(
        functools.partial(dq_kernel, heads, ndocs, tq, tk),
        grid=(block // tq,),
        in_specs=[SCALARS, row(width), row(width), ANY, ANY],
        out_specs=row(heads * HEAD_DIM),
        out_shape=jax.ShapeDtypeStruct((block, heads * HEAD_DIM), BF16),
        scratch_shapes=[pltpu.VMEM((window, width), BF16)] * 2
        + [pltpu.VMEM((heads, HEAD_DIM, window), BF16)]
        + [pltpu.VMEM((heads, width, tq), BF16)] * 2
        + [pltpu.VMEM((heads, HEAD_DIM, tq), F32)]
        + [pltpu.VMEM((window, own.shape[1]), BF16), pltpu.SemaphoreType.DMA((window // STEP,))],
        compiler_params=pltpu.CompilerParams(vmem_limit_bytes=56 << 20),
        cost_estimate=pl.CostEstimate(
            flops=45_000_000_000, bytes_accessed=12 << 20, transcendentals=20_000_000
        ),
        name="attn_dq",
    )(meta, q, do, earlier, own)


def dkv_kernel(heads, ndocs, tq, tk, meta, own, q_parts, do_parts, dk_ref, dv_ref,
               q_ref, do_ref, qt_ref, dot_ref, kt, vt, dk_acc, dv_acc, sems):
    i = pl.program_id(0)
    base = meta[0]

    @pl.when(i == 0)
    def _():
        block = pl.num_programs(0) * tk
        end = (doc_end(meta, ndocs, base + block - 1) - base + STEP - 1) // STEP
        sources = []
        for parts in (q_parts, do_parts):
            row, found = 0, []
            for part in parts:
                found.append((row // STEP, (row + part.shape[0]) // STEP, part))
                row += part.shape[0]
            sources.append(found)

        def copy(k, n, source, row):
            return pltpu.make_async_copy(
                source.at[pl.ds(row * STEP, STEP)],
                (q_ref, do_ref)[k].at[pl.ds(n * STEP, STEP)],
                sems.at[k, n],
            )

        def begin(n, carry):
            for k in range(2):
                for first, last, part in sources[k]:

                    @pl.when((n >= first) & (n < last))
                    def _():
                        copy(k, n, part, n - first).start()

            return carry

        def turn(n, carry):
            at = pl.ds(pl.multiple_of(n * STEP, STEP), STEP)
            for k, (rows, flipped) in enumerate(((q_ref, qt_ref), (do_ref, dot_ref))):
                copy(k, n, sources[k][0][2], 0).wait()
                turned = rows[at, :].T
                for h in range(heads):
                    flipped[h, :, at] = turned[h * HEAD_DIM : (h + 1) * HEAD_DIM]
            return carry

        lax.fori_loop(0, end, begin, 0)
        lax.fori_loop(0, end, turn, 0)

    u0 = base + i * tk
    lo = (u0 - base) // tq
    f0 = (u0 + tk - 1 - base + tq - 1) // tq
    e_first = doc_end(meta, ndocs, u0)
    e_last = doc_end(meta, ndocs, u0 + tk - 1)
    f1 = (e_first - base) // tq
    hi = (e_last - 1 - base) // tq + 1
    f0 = jnp.minimum(f0, hi)
    f1 = jnp.clip(f1, f0, hi)
    k, v = unpack_rows(own[...], heads)
    per_head(k, heads, kt)
    per_head(v, heads, vt)
    dk_acc[...] = jnp.zeros_like(dk_acc)
    dv_acc[...] = jnp.zeros_like(dv_acc)
    urow = u0 + lax.broadcasted_iota(jnp.int32, (8, tk), 1)
    erow = ends_vec(meta, ndocs, urow)[:1]
    urow = urow[:1]

    def body(j, masked):
        off = pl.multiple_of(j * tq, tq)
        at = pl.ds(off, tq)
        q = q_ref[at, :]
        do = do_ref[at, :]
        if masked:
            t = base + off + lax.broadcasted_iota(jnp.int32, (tq, tk), 0)
            vis = (t >= urow) & (t < erow)
        for h in range(heads):
            p = jnp.exp(dotf(q, kt[h]))
            if masked:
                p = jnp.where(vis, p, 0.0)
            ds = (p * dotf(do, vt[h])).astype(BF16)
            dv_acc[h] += dotf(dot_ref[h, :, at], p.astype(BF16))
            dk_acc[h] += dotf(qt_ref[h, :, at], ds)

    three(lo, f0, f1, hi, body)
    for acc, out in ((dk_acc, dk_ref), (dv_acc, dv_ref)):
        out[...] = acc[...].reshape(heads * HEAD_DIM, tk).T.astype(BF16)


def attention_dkv(meta, own, q_parts, do_parts, heads, tq, tk):
    block, width = q_parts[0].shape
    window = sum(part.shape[0] for part in q_parts)
    ndocs = meta.shape[0] - 1
    row = lambda w: pl.BlockSpec((tk, w), lambda i: (i, 0))
    return pl.pallas_call(
        functools.partial(dkv_kernel, heads, ndocs, tq, tk),
        grid=(block // tk,),
        in_specs=[SCALARS, row(own.shape[1]), [ANY] * len(q_parts), [ANY] * len(do_parts)],
        out_specs=[row(heads * HEAD_DIM)] * 2,
        out_shape=[jax.ShapeDtypeStruct((block, heads * HEAD_DIM), BF16)] * 2,
        scratch_shapes=[pltpu.VMEM((window, width), BF16)] * 2
        + [pltpu.VMEM((heads, HEAD_DIM, window), BF16)] * 2
        + [pltpu.VMEM((heads, width, tk), BF16)] * 2
        + [pltpu.VMEM((heads, HEAD_DIM, tk), F32)] * 2
        + [pltpu.SemaphoreType.DMA((2, window // STEP))],
        compiler_params=pltpu.CompilerParams(vmem_limit_bytes=56 << 20),
        cost_estimate=pl.CostEstimate(
            flops=60_000_000_000, bytes_accessed=12 << 20, transcendentals=20_000_000
        ),
        name="attn_dkv",
    )(meta, own, q_parts, do_parts)


def on_device(
    tokens, first_values, cotangent, w_query, w_key, w_value, w_out, w_up, w_down,
    gain_attn, gain_mlp, doc_lengths,
):
    width = tokens.shape[1]
    heads_of = lax.axis_size("head")
    nblk = lax.axis_size("blk")
    blk = lax.axis_index("blk")
    rows = tokens.shape[0]
    block = rows * heads_of
    heads = HEADS // heads_of
    cols = heads * HEAD_DIM
    part = width // nblk
    meta = jnp.concatenate([jnp.reshape(blk * block, (1,)).astype(jnp.int32), doc_lengths])

    up_cols = w_up.shape[1]
    early = nblk - 3 * nblk // 8
    normed, query, own, earlier, gathered, qk_all, v_all, attn_gain, mlp_gain = front(
        nblk, early, tokens, first_values, w_query, w_key, w_value, w_up, w_down.T, w_out,
        gain_attn.reshape(1, part), gain_mlp.reshape(1, part),
    )
    w_qk = qk_all.reshape(width, 2 * cols)
    w_v = v_all.reshape(2, width, w_value.shape[1])
    earlier = earlier.reshape(2 * block, 2 * cols)
    beside = [(h, (h + 2) % heads_of) for h in range(heads_of)]
    mine = lax.dynamic_index_in_dim(gathered, lax.axis_index("head"), 0, keepdims=False)[early:]
    late = lax.ppermute(mine, "head", beside)
    mixed_parts, query_wide = attention_fwd(
        meta, query, earlier, own, heads, rows, 2 * rows
    )
    late, mixed_parts = lax.optimization_barrier((late, mixed_parts))
    layer_output, grad_resid, grad_parts, gain_mlp_part, keep_up, keep, give, query_later = middle(
        nblk, tokens, mixed_parts, cotangent, mlp_gain, gathered, late, query_wide, up_cols
    )
    grad_wide = grad_parts.reshape(block, WIDTH)
    taken = lax.ppermute(give, "head", beside)

    grads_later = [grad_wide] + [
        lax.ppermute(grad_wide, "blk", [(i, i - d) for i in range(d, nblk)]) for d in (1, 2)
    ]
    queries_later = [query_wide, query_later.reshape(2 * block, WIDTH)]
    grad_query = attention_dq(
        meta, query_wide, grad_wide, earlier, own, heads, rows, 2 * rows
    )
    taken, keep, grad_query = lax.optimization_barrier((taken, keep, grad_query))
    keep, give = pair_sum(keep_up, keep, taken)
    taken = lax.ppermute(give, "blk", [(i, i + 1 - 2 * (i % 2)) for i in range(nblk)])
    keep, own = lax.optimization_barrier((keep, own))
    grad_key, grad_value = attention_dkv(
        meta, own, queries_later, grads_later, heads, rows, rows
    )
    outs = tail(
        nblk, grad_query, grad_key, grad_value, normed, w_qk, w_v, gain_mlp_part, keep, taken,
        tokens, grad_resid, attn_gain,
    )
    (
        layer_output, grad_tokens, final_query, final_key, final_value, grad_first, gain_sums,
        final_up, final_down, final_out,
    ) = settle([layer_output] + list(outs))
    return (
        layer_output,
        grad_tokens,
        grad_first,
        final_query,
        final_key,
        final_value,
        final_out,
        final_up,
        final_down.T,
        gain_sums[0].reshape(part),
        gain_sums[1].reshape(part),
    )


def solution(mesh):
    rows = P(("blk", "head"), None)
    specs = (P("blk", "head"),) * 3 + (P("head", "blk"), P("blk", "head"), P("head", "blk"))
    gains = (P("blk"), P("blk"))
    return jax.shard_map(
        on_device,
        mesh=mesh,
        in_specs=(rows,) * 3 + specs + gains + (P(),),
        out_specs=(rows,) * 3 + specs + gains,
        check_vma=False,
    )
```

```python
import functools

import jax
import jax.numpy as jnp
from jax import lax
from jax.experimental import pallas as pl
from jax.experimental.pallas import tpu as pltpu
from jax.sharding import PartitionSpec as P

HEADS = 12
HEAD_DIM = 64
DOC_MAX = 4096
EPSILON = 1e-05
GELU_SCALE = 0.7978845608028654
EXCLUDED = -1e30
WIDTH = 256
SPLITS = 3
BF16 = jnp.bfloat16
F32 = jnp.float32
MESH = pl.DeviceIdType.MESH
ANY = pl.BlockSpec(memory_space=pl.ANY)
WHOLE = pl.BlockSpec(memory_space=pltpu.VMEM)
NT = (((1,), (1,)), ((), ()))
TN = (((0,), (0,)), ((), ()))


def dotf(left, right, dims=None):
    if dims is None:
        dims = (((1,), (0,)), ((), ()))
    return lax.dot_general(left, right, dims, preferred_element_type=F32)


def remote(src, dst, send_sem, recv_sem, head, blk):
    return pltpu.make_async_remote_copy(
        src_ref=src,
        dst_ref=dst,
        send_sem=send_sem,
        recv_sem=recv_sem,
        device_id={"head": head, "blk": blk},
        device_id_type=MESH,
    )


def greet(partners):
    barrier = pltpu.get_barrier_semaphore()
    for head, blk in partners:
        pl.semaphore_signal(
            barrier, inc=1, device_id={"head": head, "blk": blk}, device_id_type=MESH
        )
    pl.semaphore_wait(barrier, len(partners))


def xor(value, bit):
    return value + bit - 2 * bit * (lax.div(value, bit) % 2)


def partners_of(head, blk, nblk, heads=True, blks=True):
    found = []
    if heads:
        found += [(xor(head, 1), blk), (xor(head, 2), blk), (3 - head, blk)]
    if blks:
        found += [(head, lax.rem(blk + d, nblk)) for d in range(1, nblk)]
    return found


class Line:
    def __init__(self, nblk, head, blk, source, target, up, down, across):
        self.half, self.head, self.blk = nblk // 2, head, blk
        self.place, self.parity = lax.div(blk, 2), lax.rem(blk, 2)
        self.source, self.target = source, target
        self.sems = {"up": up, "down": down, "across": across}

    def copy(self, way, origin, step, fresh=False):
        slot = 2 * origin + self.parity
        to = {
            "up": lax.rem(self.blk + 2, 2 * self.half),
            "down": lax.rem(self.blk + 2 * self.half - 2, 2 * self.half),
            "across": self.blk + 1 - 2 * self.parity,
        }[way]
        send, recv = self.sems[way]
        return remote(
            self.source if fresh else self.target.at[slot],
            self.target.at[slot], send.at[step], recv.at[step], self.head, to,
        )

    def landing(self, way, slot, step):
        send, recv = self.sems[way]
        other = self.blk + 1 - 2 * self.parity
        at = self.target.at[slot]
        return remote(at, at, send.at[step], recv.at[step], self.head, other)

    def begin(self):
        @pl.when(self.place + 1 < self.half)
        def _():
            self.copy("up", self.place, 0, True).start()

        @pl.when(self.place > 0)
        def _():
            self.copy("down", self.place, 0, True).start()

        self.copy("across", self.place, self.place, True).start()

    def step(self, s, then=None):
        low, high = self.place - 1 - s, self.place + 1 + s

        @pl.when(low >= 0)
        def _():
            self.landing("up", 2 * low + self.parity, s).wait_recv()
            if s + 1 < self.half - 1:

                @pl.when(self.place + 1 < self.half)
                def _():
                    self.copy("up", low, s + 1).start()

            self.copy("across", low, low).start()
            if then:
                then(2 * low + self.parity)

        @pl.when(high < self.half)
        def _():
            self.landing("down", 2 * high + self.parity, s).wait_recv()
            if s + 1 < self.half - 1:

                @pl.when(self.place > 0)
                def _():
                    self.copy("down", high, s + 1).start()

            self.copy("across", high, high).start()
            if then:
                then(2 * high + self.parity)

    def land(self, origin):
        self.landing("across", 2 * origin + 1 - self.parity, origin).wait_recv()

    def finish(self):
        for o in range(self.half):
            self.copy("across", o, o).wait_send()
        for s in range(self.half - 1):

            @pl.when((self.place - s >= 0) & (self.place + 1 < self.half))
            def _():
                self.copy("up", self.place - s, s).wait_send()

            @pl.when((self.place + s < self.half) & (self.place > 0))
            def _():
                self.copy("down", self.place + s, s).wait_send()


def tail_kernel(
    nblk, pieces, cols, d_q, d_k, d_v, normed, w_qk, w_v, gain_m, kept_a, got_a, kept_b, got_b, tok, resid, gain,
    out_grad, out_q, out_k, out_v, out_first, out_gain, out_up, out_down, out_out,
    grad, weights, gains, joined, weight, acc, first_got, rest_sum,
    core_buf, side_out, side_buf, pair_buf, line_out, line_in, v_sum, v_got,
    gain_buf, gain_sum, gain_got, up_out, up_in, down_out, down_in,
    own_sem, send_s, recv_s, send_x, recv_x, send_y, recv_y, send_l, recv_l,
    send_v, recv_v, send_f, recv_f, send_g, recv_g, send_h, recv_h, send_u, recv_u, send_d, recv_d,
):
    head, blk = lax.axis_index("head"), lax.axis_index("blk")
    side, core, far = xor(head, 2), xor(head, 1), 3 - head
    greet(partners_of(head, blk, nblk))
    rows = grad.shape[1] // pieces
    line, place, parity = nblk // 2, lax.div(blk, 2), lax.rem(blk, 2)
    pair = blk + 1 - 2 * parity
    above, below = lax.rem(blk + 2, nblk), lax.rem(blk + nblk - 2, nblk)

    def part(ref, p):
        return ref.at[pl.ds(p * rows, rows)]

    def to_core(i, p, slot):
        return remote(
            part(grad.at[slot], p), part(core_buf.at[i], p), send_s.at[i, p], recv_s.at[i, p],
            core, blk,
        )

    def to_side(p):
        return remote(
            part(side_out, p), part(side_buf, p), send_x.at[p], recv_x.at[p], side, blk
        )

    def sum_of(t):
        first_part = kept_b[t].astype(F32) + got_b[t].astype(F32)
        return jnp.concatenate([first_part, kept_a[t].astype(F32) + got_a[t].astype(F32)], axis=1)

    def up_copy(t, to):
        return remote(up_out.at[t], up_in.at[t], send_u.at[t], recv_u.at[t], head, to)

    def down_copy(t, to):
        return remote(down_out.at[t], down_in.at[t], send_d.at[t], recv_d.at[t], head, to)

    def first_hops():
        for n in range(line - 1):
            t = line - 1 - n

            @pl.when((place == 0) & (place < t))
            def _():
                up_out[t] = sum_of(t).astype(BF16)
                up_copy(t, above).start()

            @pl.when((place == line - 1) & (place > n))
            def _():
                down_out[n] = sum_of(n).astype(BF16)
                down_copy(n, below).start()

    def next_hops(n):
        t = line - 1 - n

        @pl.when((place > 0) & (place < t))
        def _():
            up_copy(t, above).wait_recv()
            up_out[t] = (sum_of(t) + up_in[t].astype(F32)).astype(BF16)
            up_copy(t, above).start()

        @pl.when((place < line - 1) & (place > n))
        def _():
            down_copy(n, below).wait_recv()
            down_out[n] = (sum_of(n) + down_in[n].astype(F32)).astype(BF16)
            down_copy(n, below).start()

    first_hops()
    half, kind = lax.div(head, 2), lax.rem(head, 2)

    def first_copy(i, to, slot):
        source = d_v.at[pl.ds(to * grad.shape[1], grad.shape[1])]
        return remote(source, first_got.at[slot], send_f.at[i], recv_f.at[slot], to, blk)

    def own_first(slot):
        source = d_v.at[pl.ds(head * grad.shape[1], grad.shape[1])]
        return pltpu.make_async_copy(source, first_got.at[slot], own_sem)

    @pl.when(half == 1)
    def _():
        for i, to in enumerate((core, side, far)):
            first_copy(i, to, kind).start()
        own_first(kind).start()

    mine = half == 0
    weight[:, : 2 * cols] = w_qk[...]
    fresh = jnp.concatenate([w_v[0], w_v[1]], axis=1)
    weight[:, 2 * cols :] = jnp.where(mine, fresh, jnp.zeros_like(fresh))
    gain_row = None
    for i, t in enumerate((far, side, core, head)):
        at = pl.ds(pl.multiple_of(t * grad.shape[1], grad.shape[1]), grad.shape[1])
        joined[:, :cols] = d_q[at, :]
        joined[:, cols : 2 * cols] = d_k[at, :]
        joined[:, 2 * cols : 3 * cols] = d_v[at, :]
        joined[:, 3 * cols :] = jnp.zeros((grad.shape[1], joined.shape[1] - 3 * cols), BF16)
        given = joined[...]
        whole = dotf(given[:, : 3 * cols], weight[...], NT)
        grad[t] = whole.astype(BF16)
        if i == 0:
            for p in range(pieces):
                to_core(0, p, far).start()
        if i == 2:
            for p in range(pieces):
                to_core(1, p, core).start()
        rows_in = normed[at, :]
        term = jnp.sum(whole * rows_in.astype(F32), axis=0, keepdims=True)
        gain_row = term if gain_row is None else gain_row + term
        term = dotf(rows_in, given, TN)
        acc[...] = term if i == 0 else acc[...] + term
        if i == 2:
            for p in range(pieces):
                to_core(0, p, far).wait_recv()
                part(side_out, p)[...] = (
                    part(grad.at[side], p)[...].astype(F32)
                    + part(core_buf.at[0], p)[...].astype(F32)
                ).astype(BF16)
                to_side(p).start()
    whole_part = weights.shape[1]
    for b in range(nblk):
        weights[b] = acc[b * whole_part : (b + 1) * whole_part].astype(BF16)

    def across(n):
        return remote(
            weights.at[2 * n + 1 - parity], pair_buf.at[n], send_y.at[n], recv_y.at[n], head, pair
        )

    for n in range(line):
        across(n).start()
    gain_row = gain_row / gain[...]
    for b in range(nblk):
        gains[b, 0] = gain_row[:, b * whole_part : (b + 1) * whole_part]
        gains[b, 1] = gain_m[:, b * whole_part : (b + 1) * whole_part]

    def gain_to(d):
        to = lax.rem(blk + d, nblk)
        return remote(gains.at[to], gain_buf.at[blk], send_g.at[d], recv_g.at[d], head, to)

    def gain_from(d):
        source = lax.rem(blk - d + nblk, nblk)
        return remote(gains.at[0], gain_buf.at[source], send_g.at[d], recv_g.at[d], head, source)

    for d in range(1, nblk):
        gain_to(d).start()
    gain_buf[blk] = gains[blk]

    def along(d, to):
        return remote(
            line_out.at[to], line_in.at[d], send_l.at[d], recv_l.at[d], head, 2 * to + parity
        )

    next_hops(0)
    for n in range(line):
        across(n).wait_recv()
        line_out[n] = (
            weights[2 * n + parity].astype(F32) + pair_buf[n].astype(F32)
        ).astype(BF16)
    for d in range(1, line):
        along(d, lax.rem(place + d, line)).start()
    for d in range(1, nblk):
        gain_from(d).wait_recv()
    gain_sum[...] = jnp.sum(gain_buf[...], axis=0)
    peers = (core, side, far)

    def gain_copy(i, to):
        return remote(gain_sum, gain_got.at[i], send_h.at[i], recv_h.at[i], to, blk)

    for i, to in enumerate(peers):
        gain_copy(i, to).start()
    for n in range(1, line - 1):
        next_hops(n)
    total = line_out[place].astype(F32)
    for d in range(1, line):
        along(d, lax.rem(place - d + line, line)).wait_recv()
        total = total + line_in[d].astype(F32)
    out_q[...] = total[:, :cols]
    out_k[...] = total[:, cols : 2 * cols]
    v_sum[0] = total[:, 2 * cols : 2 * cols + cols // 2]
    v_sum[1] = total[:, 2 * cols + cols // 2 : 3 * cols]

    def give(c, to):
        return remote(v_sum.at[c], v_got, send_v.at[c], recv_v.at[0], to, blk)

    for c in range(2):
        to = 2 * head + c

        @pl.when((half == 0) & (to != head))
        def _():
            give(c, to).start()

    for p in range(pieces):
        to_core(1, p, core).wait_recv()
        to_side(p).wait_recv()
        norm_grad = (
            part(grad.at[head], p)[...].astype(F32)
            + part(core_buf.at[1], p)[...].astype(F32)
            + part(side_buf, p)[...].astype(F32)
        )
        xhat, scale = statistics(part(tok, p)[...].astype(F32))
        part(out_grad, p)[...] = part(resid, p)[...] + norm_back(norm_grad, xhat, scale, gain[...])
    rest_sum[...] = sum_of(place)
    for t in range(line):

        @pl.when((place == t) & (place > 0))
        def _():
            up_copy(t, above).wait_recv()
            rest_sum[...] += up_in[t].astype(F32)

        @pl.when((place == t) & (place < line - 1))
        def _():
            down_copy(t, below).wait_recv()
            rest_sum[...] += down_in[t].astype(F32)

    inner = out_up.shape[1]
    cut = kept_b.shape[2]
    out_up[...] = rest_sum[:, cut : cut + inner]
    out_down[:, :cut] = rest_sum[:, :cut]
    out_down[:, cut:] = rest_sum[:, cut + inner : 2 * inner]
    out_out[...] = rest_sum[:, 2 * inner :].T
    for i, to in enumerate(peers):
        gain_copy(i, to).wait_recv()
    out_gain[...] = gain_sum[...] + gain_got[0] + gain_got[1] + gain_got[2]

    @pl.when(head == 0)
    def _():
        out_v[...] = v_sum[0]

    @pl.when(head != 0)
    def _():
        give(0, half).wait_recv()
        out_v[...] = v_got[...]

    for slot in range(2):

        @pl.when(head == 2 + slot)
        def _():
            own_first(slot).wait()

        @pl.when(head != 2 + slot)
        def _():
            first_copy(0, 2 + slot, slot).wait_recv()

    out_first[...] = jnp.concatenate([first_got[0], first_got[1]], axis=1).astype(F32)

    @pl.when(half == 1)
    def _():
        for i, to in enumerate((core, side, far)):
            first_copy(i, to, kind).wait_send()

    for c in range(2):
        to = 2 * head + c

        @pl.when((half == 0) & (to != head))
        def _():
            give(c, to).wait_send()

    for i, to in enumerate(peers):
        gain_copy(i, to).wait_send()
    for p in range(pieces):
        to_core(0, p, far).wait_send()
        to_core(1, p, core).wait_send()
        to_side(p).wait_send()
    for d in range(1, nblk):
        gain_to(d).wait_send()
    for n in range(line):
        across(n).wait_send()
    for d in range(1, line):
        along(d, lax.rem(place + d, line)).wait_send()
    for t in range(line):

        @pl.when(place < t)
        def _():
            up_copy(t, above).wait_send()

        @pl.when(place > t)
        def _():
            down_copy(t, below).wait_send()


def tail(
    nblk, d_q, d_k, d_v, normed, w_qk, w_v, gain_m, kept_a, got_a, kept_b, got_b, tok, resid, gain,
    pieces=4,
):
    dma = pltpu.SemaphoreType.DMA
    row, part, cols = tok.shape, w_v.shape[1] // nblk, d_q.shape[1]
    rest = (nblk // 2, part, kept_a.shape[2] + kept_b.shape[2])
    inner = (rest[2] - cols) // 2
    padded = -(-3 * cols // 128) * 128
    gains = jax.ShapeDtypeStruct((nblk, 2, 1, part), F32)
    half, line = (part, cols // 2), nblk // 2
    piece = (2, pieces)
    vmem = lambda *shape: pltpu.VMEM(shape, BF16)
    return pl.pallas_call(
        functools.partial(tail_kernel, nblk, pieces, cols),
        out_shape=[
            jax.ShapeDtypeStruct(row, F32),
            jax.ShapeDtypeStruct((part, cols), F32),
            jax.ShapeDtypeStruct((part, cols), F32),
            jax.ShapeDtypeStruct(half, F32),
            jax.ShapeDtypeStruct((row[0], 2 * cols), F32),
            jax.ShapeDtypeStruct(gains.shape[1:], F32),
            jax.ShapeDtypeStruct((part, inner), F32),
            jax.ShapeDtypeStruct((part, inner), F32),
            jax.ShapeDtypeStruct((cols, part), F32),
        ],
        in_specs=[WHOLE] * 14,
        out_specs=[WHOLE] * 9,
        scratch_shapes=[
            vmem(4, *row), vmem(nblk, part, padded), pltpu.VMEM(gains.shape, F32),
            vmem(row[0], padded), vmem(row[1], 3 * cols), pltpu.VMEM((row[1], padded), F32),
            vmem(2, row[0], cols), pltpu.VMEM(rest[1:], F32),
            vmem(2, *row), vmem(*row), vmem(*row),
            vmem(line, part, padded), vmem(line, part, padded),
            vmem(line, part, padded),
            pltpu.VMEM((2,) + half, F32),
            pltpu.VMEM(half, F32),
            pltpu.VMEM(gains.shape, F32),
            pltpu.VMEM(gains.shape[1:], F32),
            pltpu.VMEM((3,) + gains.shape[1:], F32),
            vmem(*rest), vmem(*rest), vmem(*rest), vmem(*rest),
            dma,
            dma(piece), dma(piece),
            dma((pieces,)), dma((pieces,)),
            dma((line,)), dma((line,)), dma((line,)), dma((line,)),
            dma((2,)), dma((1,)),
            dma((3,)), dma((2,)),
            dma((nblk,)), dma((nblk,)),
            dma((3,)), dma((3,)),
            dma((line,)), dma((line,)), dma((line,)), dma((line,)),
        ],
        compiler_params=pltpu.CompilerParams(
            collective_id=4, has_side_effects=True, vmem_limit_bytes=60 << 20
        ),
        name="tail",
    )(d_q, d_k, d_v, normed, w_qk, w_v, gain_m, kept_a, got_a, kept_b, got_b, tok, resid, gain)


def settle_kernel(count, *refs):
    sources, targets, sems = refs[:count], refs[count : 2 * count], refs[2 * count]
    copies = [
        pltpu.make_async_copy(source, target, sems.at[i])
        for i, (source, target) in enumerate(zip(sources, targets))
    ]
    for copy in copies:
        copy.start()
    for copy in copies:
        copy.wait()


def settle(arrays):
    count = len(arrays)
    return pl.pallas_call(
        functools.partial(settle_kernel, count),
        out_shape=[jax.ShapeDtypeStruct(a.shape, a.dtype) for a in arrays],
        in_specs=[ANY] * count,
        out_specs=[WHOLE] * count,
        scratch_shapes=[pltpu.SemaphoreType.DMA((count,))],
        name="settle",
    )(*arrays)


def statistics(values):
    center = values - jnp.mean(values, axis=-1, keepdims=True)
    scale = lax.rsqrt(jnp.mean(jnp.square(center), axis=-1, keepdims=True) + EPSILON)
    return center * scale, scale


def norm_back(grad, xhat, scale, gain):
    eg = grad * gain
    return scale * (
        eg
        - jnp.mean(eg, axis=-1, keepdims=True)
        - xhat * jnp.mean(eg * xhat, axis=-1, keepdims=True)
    )


def split_parts(values):
    high = values.astype(BF16).astype(F32)
    middle = (values - high).astype(BF16).astype(F32)
    return high, middle, values - high - middle


def front_kernel(
    nblk, parts, pieces, early, tok, first, w_q, w_k, w_v, w_up, w_down, w_out, gain_a, gain_m,
    normed, query, own, near_far, rest, qk_all, v_all, attn_gain, mlp_gain,
    tok_all, first_all, v_own, gain_all, w_qk, w_rest, gains, weight, normed_buf,
    own_sem, normed_sem, send_t, recv_t, send_s, recv_s, send_p, recv_p, send_w, recv_w,
    send_v, recv_v, qk_u, qk_ur, qk_d, qk_dr, qk_a, qk_ar, up_u, up_ur, up_d, up_dr, up_a, up_ar,
    send_x, recv_x, send_c, recv_c, send_f, recv_f, send_z, recv_z, send_y, recv_y,
):
    head, blk = lax.axis_index("head"), lax.axis_index("blk")
    side, core, beyond = xor(head, 2), xor(head, 1), 3 - head
    odd, place = lax.rem(blk, 2), lax.div(blk, 2)
    near = blk + 1 - 2 * odd
    up, down = lax.rem(blk + 2, nblk), lax.rem(blk + nblk - 2, nblk)
    greet(partners_of(head, blk, nblk))
    moved = [(tok, tok_all), (first, first_all)]
    weights = [(w_v, v_own), (gains, gain_all)]
    rows = tok.shape[0] // parts

    def part(ref, n):
        return ref.at[pl.ds(n * rows, rows)]

    def hop(sems, k, n, source, slot, target):
        dst = part(moved[k][1].at[slot], n)
        return remote(source, dst, sems[0].at[k, n], sems[1].at[k, n], target, blk)

    ts, ss, ps = (send_t, recv_t), (send_s, recv_s), (send_p, recv_p)
    order = [(k, n) for n in range(parts) for k in range(2)]
    for k, n in order:
        hop(ts, k, n, part(moved[k][0], n), head, side).start()
    cols, inner = w_q.shape[1], w_up.shape[1]
    w_qk[:, :cols] = w_q[...]
    w_qk[:, cols:] = w_k[...]
    qk_line = Line(nblk, head, blk, w_qk, qk_all, (qk_u, qk_ur), (qk_d, qk_dr), (qk_a, qk_ar))
    qk_line.begin()
    w_rest[:, :inner] = w_up[...]
    w_rest[:, inner : 2 * inner] = w_down[...]
    w_rest[:, 2 * inner :] = w_out[...].T
    line = Line(
        nblk, head, blk, w_rest, rest.at[head], (up_u, up_ur), (up_d, up_dr), (up_a, up_ar)
    )
    line.begin()
    gains[0] = gain_a[...]
    gains[1] = gain_m[...]

    def chunk(sems, slot, b, to, source=None):
        at = rest.at[slot, b]
        return remote(at if source is None else source, at, sems[0].at[b], sems[1].at[b], to, blk)

    xs, cs, fs = (send_x, recv_x), (send_c, recv_c), (send_f, recv_f)

    def to_core(b, source=None):
        chunk(cs, head, b, core, source).start()

    def to_side(b, source=None):
        @pl.when(b < early)
        def _():
            chunk(xs, head, b, side, source).start()

    to_core(blk, w_rest)
    own_rest = pltpu.make_async_copy(w_rest, rest.at[head, blk], own_sem)
    own_rest.start()

    def spread(d):
        to = lax.rem(blk + d, nblk)
        return [
            remote(src, dst.at[blk], send_w.at[i, d], recv_w.at[i, d], head, to)
            for i, (src, dst) in enumerate(weights)
        ]

    def from_peer(d):
        source = lax.rem(blk - d + nblk, nblk)
        return [
            remote(src, dst.at[source], send_w.at[i, d], recv_w.at[i, d], head, source)
            for i, (src, dst) in enumerate(weights)
        ]

    for d in range(1, nblk):
        for copy in spread(d):
            copy.start()
    for k, n in order:
        hop(ss, k, n, part(moved[k][0], n), head, core).start()
    tok_all[head] = tok[...]
    first_all[head] = first[...]
    v_own[blk] = w_v[...]
    gain_all[blk] = gains[...]
    qk_all[blk] = w_qk[...]

    def pass_on(k, n):
        landed = part(moved[k][1].at[side], n)
        hop(ts, k, n, landed, side, side).wait_recv()
        hop(ps, k, n, landed, side, core).start()

    steps = nblk // 2 - 1
    for s in range(steps):
        qk_line.step(s)
    for s in range(steps):
        line.step(s, to_core)
        for k, n in order[s * len(order) // steps : (s + 1) * len(order) // steps]:
            pass_on(k, n)
    to_side(blk, w_rest)
    for s in range(steps):

        @pl.when(place - 1 - s >= 0)
        def _():
            to_side(blk - 2 - 2 * s)

        @pl.when(place + 1 + s < nblk // 2)
        def _():
            to_side(blk + 2 + 2 * s)

    for d in range(1, nblk):
        for copy in from_peer(d):
            copy.wait_recv()
    half, kind = lax.div(head, 2), lax.rem(head, 2)
    for i in range(2):
        target = half + 2 * i

        @pl.when(target == head)
        def _():
            v_all[kind] = v_own[...]

        @pl.when(target != head)
        def _():
            remote(v_own, v_all.at[kind], send_v.at[i], recv_v.at[kind], target, blk).start()

    for o in range(nblk // 2):
        qk_line.land(o)
    for c in range(2):
        source = 2 * kind + c

        @pl.when(source != head)
        def _():
            remote(v_own, v_all.at[c], send_v.at[0], recv_v.at[c], source, blk).wait_recv()

    attn_gain[...] = jnp.concatenate([gain_all[b, 0] for b in range(nblk)], axis=1)
    mlp_gain[...] = jnp.concatenate([gain_all[b, 1] for b in range(nblk)], axis=1)

    step = own.shape[0] // pieces

    def slab(ref, n):
        return ref.at[pl.ds(n * step, step)]

    def far_copy(n, to):
        return remote(slab(own, n), slab(near_far.at[0], n), send_z.at[n], recv_z.at[n], head, to)

    def near_copy(n, src):
        return remote(src, slab(near_far.at[1], n), send_y.at[n], recv_y.at[n], head, near)

    size = HEAD_DIM
    pair = 2 * size
    width = tok.shape[1]
    block = w_q.shape[0]
    for b in range(nblk):
        at = pl.ds(b * block, block)
        both, fresh = qk_all[b], jnp.concatenate([v_all[0, b], v_all[1, b]], axis=1)
        key = both[:, cols:]
        weight[at, :pair] = key[:, :pair]
        weight[at, pair : 2 * pair] = fresh[:, :pair]
        weight[at, 2 * pair : 3 * pair] = jnp.concatenate([key[:, pair:], fresh[:, pair:]], axis=1)
        weight[at, 3 * pair :] = jnp.concatenate(
            [both[:, :cols], jnp.zeros((block, WIDTH - cols), BF16)], axis=1
        )
    stores = []
    for i, t in enumerate((head, side, core, beyond)):
        if i == 2:
            for k, n in order:
                hop(ss, k, n, part(moved[k][1].at[core], n), core, core).wait_recv()
        if i == 3:
            for k, n in order:
                hop(ps, k, n, part(moved[k][1].at[beyond], n), beyond, core).wait_recv()
        total = tok.shape[0]
        at = pl.ds(pl.multiple_of(t * total, total), total)
        xhat, _ = statistics(tok_all[t].astype(F32))
        row = (xhat * attn_gain[...]).astype(BF16)
        normed_buf[t] = row
        stores.append(pltpu.make_async_copy(normed_buf.at[t], normed.at[at], normed_sem.at[i]))
        stores[-1].start()
        out = dotf(row, weight[...])
        query[at, :] = (out[:, 3 * pair :].astype(BF16).astype(F32) * size**-0.5).astype(BF16)
        done = out[:, : 3 * pair].astype(BF16)
        given = first_all[t]
        kept = jnp.where(kind == 0, given[:, :cols], given[:, cols:])
        other = jnp.concatenate(
            [done[:, :pair], kept[:, :pair], done[:, 2 * pair : 2 * pair + size], kept[:, pair:]],
            axis=1,
        )
        own[at, :] = jnp.where(half == 0, done, other)
        for n in range(pieces // 4):
            n = t * (pieces // 4) + n

            @pl.when(blk + 2 < nblk)
            def _():
                far_copy(n, up).start()

            @pl.when(odd == 0)
            def _():
                near_copy(n, slab(own, n)).start()

    for o in range(nblk // 2):

        line.land(o)
        to_core(2 * o + 1 - odd)
        to_side(2 * o + 1 - odd)

    for i, t in enumerate((head, side, core, beyond)):
        for n in range(pieces // 4):
            n = t * (pieces // 4) + n

            @pl.when(blk >= 2)
            def _():
                far_copy(n, down).wait_recv()

            @pl.when((blk >= 2) & (odd == 1))
            def _():
                near_copy(n, slab(near_far.at[0], n)).start()

    own_rest.wait()
    for b in range(early):
        chunk(xs, side, b, side).wait_recv()
        chunk(fs, side, b, core).start()
    for b in range(nblk):
        chunk(cs, core, b, core).wait_recv()
    for b in range(early):
        chunk(fs, beyond, b, core).wait_recv()
        chunk(xs, head, b, side).wait_send()
        chunk(fs, side, b, core).wait_send()
    for b in range(nblk):
        chunk(cs, head, b, core).wait_send()
    for copy in stores:
        copy.wait()
    for n in range(pieces):

        @pl.when((blk >= 2) | (odd == 1))
        def _():
            near_copy(n, slab(own, n)).wait_recv()

        @pl.when(blk + 2 < nblk)
        def _():
            far_copy(n, up).wait_send()

        @pl.when((blk >= 2) | (odd == 0))
        def _():
            near_copy(n, slab(own, n)).wait_send()

    for i in range(2):
        target = half + 2 * i

        @pl.when(target != head)
        def _():
            remote(v_own, v_all.at[kind], send_v.at[i], recv_v.at[kind], target, blk).wait_send()

    for k, n in order:
        hop(ts, k, n, part(moved[k][0], n), head, side).wait_send()
        hop(ss, k, n, part(moved[k][0], n), head, core).wait_send()
        hop(ps, k, n, part(moved[k][1].at[side], n), side, core).wait_send()
    for d in range(1, nblk):
        for copy in spread(d):
            copy.wait_send()
    qk_line.finish()
    line.finish()


def front(
    nblk, early, tok, first, w_q, w_k, w_v, w_up, w_down, w_out, gain_a, gain_m, parts=4, pieces=8
):
    dma = pltpu.SemaphoreType.DMA
    (rows, width), (part, cols) = tok.shape, w_q.shape
    total = 4 * rows
    both = w_up.shape[1] + w_down.shape[1] + w_out.shape[0]
    low = lambda *shape: jax.ShapeDtypeStruct(shape, BF16)
    vmem = lambda *shape: pltpu.VMEM(shape, BF16)
    line = [dma((nblk // 2,))] * 6
    return pl.pallas_call(
        functools.partial(front_kernel, nblk, parts, pieces, early),
        out_shape=[
            low(total, width),
            low(total, WIDTH),
            low(total, 2 * cols),
            low(2, total, 2 * cols),
            low(4, nblk, part, both),
            low(nblk, part, 2 * cols),
            low(2, nblk, *w_v.shape),
            jax.ShapeDtypeStruct((1, width), F32),
            jax.ShapeDtypeStruct((1, width), F32),
        ],
        in_specs=[WHOLE] * 10,
        out_specs=[ANY, WHOLE, WHOLE, ANY, ANY] + [WHOLE] * 4,
        scratch_shapes=[
            vmem(4, *tok.shape),
            vmem(4, *first.shape),
            vmem(nblk, *w_v.shape),
            pltpu.VMEM((nblk, 2) + gain_a.shape, F32),
            vmem(part, 2 * cols),
            vmem(part, both),
            pltpu.VMEM((2,) + gain_a.shape, F32),
            vmem(width, 2 * cols + WIDTH),
            vmem(4, *tok.shape),
            dma,
            dma((4,)),
        ]
        + [dma((2, parts))] * 6
        + [dma((2, nblk))] * 2
        + [dma((2,))] * 2
        + line * 2
        + [dma((nblk,))] * 6
        + [dma((pieces,))] * 4,
        compiler_params=pltpu.CompilerParams(
            collective_id=0, has_side_effects=True, vmem_limit_bytes=56 << 20
        ),
        name="front",
    )(tok, first, w_q, w_k, w_v, w_up, w_down, w_out, gain_a, gain_m)


def gelu_both(pre):
    square = pre * pre
    inner = jnp.tanh(GELU_SCALE * (pre + 0.044715 * square * pre))
    slope = GELU_SCALE * (1.0 + 3.0 * 0.044715 * square)
    outer = 0.5 * (1.0 + inner)
    return pre * outer, outer + 0.5 * pre * (1.0 - inner * inner) * slope


def middle_kernel(
    nblk, up_cols, cut, pieces, tok, mixed_parts, cot, gain, gathered, late, query,
    out, grad_resid, grad_wide, gain_part, keep_a, give_a, keep_b, give_b, query_later,
    up, down, w_out, up_grad, down_grad, out_grad, mixed, wide_parts, up_got, down_got, out_got,
    sems, out_sems, send_m, recv_m, send_g, recv_g, send_c, recv_c,
    send_z, recv_z, send_y, recv_y, hidden_all, pre_all, normed_t, cot_t, late_far, send_l, recv_l,
):
    head, blk = lax.axis_index("head"), lax.axis_index("blk")
    x, core_index = lax.div(head, 2), lax.rem(head, 2)
    core = xor(head, 1)
    others = [xor(head, 2), 3 - head, core]
    odd = lax.rem(blk, 2)
    pair = blk + 1 - 2 * odd
    above, below = lax.rem(blk + 2, nblk), lax.rem(blk + nblk - 2, nblk)
    greet(partners_of(head, blk, nblk, blks=False) + [(head, b) for b in (pair, above, below)])
    heads_of = 4
    part = gathered.shape[2]
    cols = mixed.shape[2]
    heads = cols // HEAD_DIM

    def mixed_copy(i, to, slot):
        return remote(
            mixed_parts.at[to], mixed.at[slot], send_m.at[i], recv_m.at[i], to, blk
        )

    for i, to in enumerate(others):
        mixed_copy(i, to, head).start()
    late_copy = remote(late, late_far, send_l, recv_l, core, blk)
    late_copy.start()
    early = nblk - late.shape[0]
    piece_rows = query.shape[0] // pieces

    def slab(ref, p):
        return ref.at[pl.ds(p * piece_rows, piece_rows)]

    def far_copy(p, to):
        dst = slab(query_later.at[1], p)
        return remote(slab(query, p), dst, send_z.at[p], recv_z.at[p], head, to)

    def near_copy(p, src):
        return remote(src, slab(query_later.at[0], p), send_y.at[p], recv_y.at[p], head, pair)

    for p in range(pieces):

        @pl.when(blk >= 2)
        def _():
            far_copy(p, below).start()

        @pl.when(odd == 1)
        def _():
            near_copy(p, slab(query, p)).start()

    def relay(p):
        @pl.when(blk + 2 < nblk)
        def _():
            far_copy(p, above).wait_recv()

        @pl.when((blk + 2 < nblk) & (odd == 0))
        def _():
            near_copy(p, slab(query_later.at[1], p)).start()

    chunks = [2 * n + c for n in (1 - x, x) for c in (1 - core_index, core_index)]
    side = others[0]
    sources = (3 - head, others[0], core)

    def source(i, b):
        if b < early or i > 1:
            return gathered.at[chunks[i], b]
        return (late_far, late)[i].at[b - early]

    def load(i, which):
        target, lo, size = ((w_out, 2 * up_cols, cols), (up, 0, up_cols), (down, up_cols, up_cols))[
            which
        ]
        return [
            pltpu.make_async_copy(
                source(i, b).at[:, pl.ds(lo, size)],
                target.at[i, pl.ds(b * part, part)],
                sems.at[which, i, b],
            )
            for b in range(nblk)
        ]

    turns = (2, 3, 1, 0)
    order = [(i, 0) for i in turns] + [(i, w) for i in turns for w in (1, 2)]
    for i, which in order:
        for b, copy in enumerate(load(i, which)):
            if i or b < early:
                copy.start()
    mixed[head] = mixed_parts[head]
    late_copy.wait()
    for which in range(3):
        for copy in load(0, which)[early:]:
            copy.start()
    for i in range(heads_of):
        for copy in load(i, 0):
            copy.wait()
    for i, to in enumerate(others):
        mixed_copy(i, to, to).wait_recv()
    branch = None
    for i in range(heads_of):
        term = dotf(mixed[chunks[i]], w_out[i], NT)
        branch = term if branch is None else branch + term
    resid = tok[...].astype(F32) + branch
    xhat, scale = statistics(resid)
    normed = (xhat * gain[...]).astype(BF16)
    cotangent = cot[...]
    total, grad_normed = resid, None

    def to_core(n, k):
        mine, theirs = ((up_grad, up_got), (down_grad, down_got), (out_grad, out_got))[k]
        return remote(mine.at[2 * n], theirs.at[n], send_c.at[k, n], recv_c.at[k, n], core, blk)

    normed_t[...] = normed.T
    cot_t[...] = cotangent.T
    for n, i in enumerate(turns):
        for copy in load(i, 1) + load(i, 2):
            copy.wait()
        hidden, slope = gelu_both(dotf(normed, up[i]))
        hidden_all[i] = hidden.astype(BF16)
        pre_all[i] = (slope * dotf(cotangent, down[i])).astype(BF16)
        total = total + dotf(hidden_all[i], down[i], NT)
        term = dotf(pre_all[i], up[i], NT)
        grad_normed = term if grad_normed is None else grad_normed + term
        for p in range(n * pieces // heads_of, (n + 1) * pieces // heads_of):
            relay(p)
    grad = cotangent.astype(F32) + norm_back(grad_normed, xhat, scale, gain[...])
    branch_grad = grad.astype(BF16)
    lane = lax.broadcasted_iota(jnp.int32, (tok.shape[0], WIDTH), 1)

    def wide_copy(i, to, slot):
        return remote(
            wide_parts.at[to], grad_wide.at[slot], send_g.at[i], recv_g.at[i], to, blk
        )

    for i in range(heads_of):
        h = chunks[i]
        rows = dotf(branch_grad, w_out[i]).astype(BF16).astype(F32)
        product = rows * mixed[h].astype(F32)
        wide = jnp.concatenate([rows, jnp.zeros((rows.shape[0], WIDTH - cols), F32)], axis=1)
        for k in range(heads):
            delta = jnp.sum(
                product[:, k * HEAD_DIM : (k + 1) * HEAD_DIM], axis=1, keepdims=True
            )
            for c, piece in enumerate(split_parts(-delta)):
                wide = jnp.where(lane == cols + SPLITS * k + c, piece, wide)
        wide_parts[h] = wide.astype(BF16)
        if i < 3:
            wide_copy(i, h, head).start()
    grad_wide[head] = wide_parts[head]
    out[...] = total.astype(BF16)
    gain_part[...] = jnp.sum(grad_normed * xhat, axis=0, keepdims=True)
    grad_resid[...] = grad
    for i in range(heads_of):
        up_grad[i] = dotf(normed_t[...], pre_all[i]).astype(BF16)
        down_grad[i] = dotf(cot_t[...], hidden_all[i]).astype(BF16)
        if i % 2 == 0:
            to_core(i // 2, 0).start()
            to_core(i // 2, 1).start()
    branch_t = branch_grad.T
    for i in range(heads_of):
        out_grad[i] = dotf(branch_t, mixed[chunks[i]]).astype(BF16)
        if i % 2 == 0:
            to_core(i // 2, 2).start()

    def store(k, source, target, lo):
        size = source.shape[1]
        return [
            pltpu.make_async_copy(
                source.at[pl.ds(b * part, part)],
                target(b).at[:, pl.ds(lo, size)],
                out_sems.at[k, b],
            )
            for b in range(nblk)
        ]

    stores = []
    for n, target in enumerate((give_a, keep_a)):
        at = 2 * n + 1
        for k, (mine, theirs) in enumerate(
            ((up_grad, up_got), (down_grad, down_got), (out_grad, out_got))
        ):
            to_core(n, k).wait_recv()
            mine[at] = (mine[at].astype(F32) + theirs[n].astype(F32)).astype(BF16)
        first_part = store(3 * n, up_grad.at[at], lambda b: target.at[b], 0)
        far_down = down_grad.at[at].at[:, pl.ds(cut, up_cols - cut)]
        first_part += store(6 + n, far_down, lambda b: target.at[b], up_cols)
        first_part += store(3 * n + 1, out_grad.at[at], lambda b: target.at[b], 2 * up_cols - cut)
        for copy in first_part:
            copy.start()
        kept = store(3 * n + 2, down_grad.at[at].at[:, pl.ds(0, cut)], lambda b: keep_b.at[n, b // 2], 0)
        given = store(3 * n + 2, down_grad.at[at].at[:, pl.ds(0, cut)], lambda b: give_b.at[n, b // 2], 0)
        for b in range(nblk):

            @pl.when(odd == b % 2)
            def _():
                kept[b].start()

            @pl.when(odd != b % 2)
            def _():
                given[b].start()

        stores += first_part + kept
    for copy in stores:
        copy.wait()
    for k in range(3):
        for n in range(2):
            to_core(n, k).wait_send()
    for i in range(3):
        wide_copy(i, chunks[i], sources[i]).wait_recv()
    for i, to in enumerate(others):
        mixed_copy(i, to, head).wait_send()
        wide_copy(i, chunks[i], head).wait_send()
    for p in range(pieces):

        @pl.when((blk + 2 < nblk) | (odd == 0))
        def _():
            near_copy(p, slab(query, p)).wait_recv()

        @pl.when(blk >= 2)
        def _():
            far_copy(p, below).wait_send()

        @pl.when((blk + 2 < nblk) | (odd == 1))
        def _():
            near_copy(p, slab(query, p)).wait_send()


def middle(nblk, tok, mixed_parts, cot, gain, gathered, late, query, up_cols, cut=512, pieces=8):
    heads_of, rows, cols = mixed_parts.shape
    width, part = tok.shape[1], gathered.shape[2]
    flops = 2 * rows * width * (6 * up_cols * heads_of + 3 * width)
    dma = pltpu.SemaphoreType.DMA
    vmem = lambda *shape: pltpu.VMEM(shape, BF16)
    return pl.pallas_call(
        functools.partial(middle_kernel, nblk, up_cols, cut, pieces),
        out_shape=[
            jax.ShapeDtypeStruct((rows, width), BF16),
            jax.ShapeDtypeStruct((rows, width), F32),
            jax.ShapeDtypeStruct((heads_of, rows, WIDTH), BF16),
            jax.ShapeDtypeStruct((1, width), F32),
            jax.ShapeDtypeStruct((nblk, part, 2 * up_cols - cut + cols), BF16),
            jax.ShapeDtypeStruct((nblk, part, 2 * up_cols - cut + cols), BF16),
            jax.ShapeDtypeStruct((2, nblk // 2, part, cut), BF16),
            jax.ShapeDtypeStruct((2, nblk // 2, part, cut), BF16),
            jax.ShapeDtypeStruct((2,) + query.shape, BF16),
        ],
        in_specs=[WHOLE] * 4 + [ANY] * 3,
        out_specs=[WHOLE] * 4 + [ANY] * 5,
        scratch_shapes=[
            vmem(heads_of, width, up_cols), vmem(heads_of, width, up_cols),
            vmem(heads_of, width, cols),
            vmem(heads_of, width, up_cols), vmem(heads_of, width, up_cols),
            vmem(heads_of, width, cols),
            vmem(heads_of, rows, cols), vmem(heads_of, rows, WIDTH),
            vmem(2, width, up_cols), vmem(2, width, up_cols), vmem(2, width, cols),
            dma((3, heads_of, nblk)), dma((8, nblk)),
            dma((3,)), dma((3,)), dma((3,)), dma((3,)), dma((3, 2)), dma((3, 2)),
            dma((pieces,)), dma((pieces,)), dma((pieces,)), dma((pieces,)),
            vmem(heads_of, rows, up_cols), vmem(heads_of, rows, up_cols),
            vmem(width, rows), vmem(width, rows),
            vmem(*late.shape), dma, dma,
        ],
        compiler_params=pltpu.CompilerParams(
            collective_id=2, has_side_effects=True, vmem_limit_bytes=62 << 20
        ),
        cost_estimate=pl.CostEstimate(
            flops=flops, bytes_accessed=24 << 20, transcendentals=rows * up_cols * heads_of
        ),
        name="middle",
    )(tok, mixed_parts, cot, gain, gathered, late, query)


def pair_sum_kernel(ours_a, got_a, ours_b, got_b, keep_a, give_a, keep_b, give_b):
    odd = lax.rem(lax.axis_index("blk"), 2)
    sums = [(ours_a[n].astype(F32) + got_a[n].astype(F32)).astype(BF16) for n in range(2)]
    keep_a[0] = jnp.where(odd == 0, sums[0], sums[1])
    give_a[0] = jnp.where(odd == 0, sums[1], sums[0])
    give_b[0] = (ours_b[0, 0].astype(F32) + got_b[0, 0].astype(F32)).astype(BF16)
    keep_b[0] = (ours_b[1, 0].astype(F32) + got_b[1, 0].astype(F32)).astype(BF16)


def pair_sum(ours_a, got_a, ours_b, got_b):
    nblk, part, width = ours_a.shape
    other = ours_b.shape[3]
    a_in = pl.BlockSpec((2, part, width), lambda i: (i, 0, 0))
    b_in = pl.BlockSpec((2, 1, part, other), lambda i: (0, i, 0, 0))
    out = lambda cols: pl.BlockSpec((1, part, cols), lambda i: (i, 0, 0))
    shape = lambda cols: jax.ShapeDtypeStruct((nblk // 2, part, cols), BF16)
    return pl.pallas_call(
        pair_sum_kernel,
        grid=(nblk // 2,),
        in_specs=[a_in, a_in, b_in, b_in],
        out_specs=[out(width)] * 2 + [out(other)] * 2,
        out_shape=[shape(width)] * 2 + [shape(other)] * 2,
        cost_estimate=pl.CostEstimate(
            flops=nblk * part * width, bytes_accessed=12 * nblk * part * width, transcendentals=0
        ),
        name="pair_sum",
    )(ours_a, got_a, ours_b, got_b)


def head_rows(h, heads, shape):
    row = lax.broadcasted_iota(jnp.int32, shape, 0)
    real = heads * HEAD_DIM
    own = (row >= h * HEAD_DIM) & (row < (h + 1) * HEAD_DIM)
    return own | ((row >= real + SPLITS * h) & (row < real + SPLITS * (h + 1)))


def per_head(wide, heads, out):
    flipped = wide.T
    for h in range(heads):
        out[h] = jnp.where(head_rows(h, heads, flipped.shape), flipped, jnp.zeros_like(flipped))


def doc_start(meta, ndocs, t):
    def step(j,c):
        cum,best=c
        best=jnp.where(cum<=t,cum,best)
        return cum+meta[1+j],best
    return lax.fori_loop(0,ndocs,step,(jnp.int32(0),jnp.int32(0)),unroll=True)[1]

def doc_end(meta, ndocs, t):
    def step(j,c):
        cum,best,found=c
        cum=cum+meta[1+j]
        take=(cum>t)&(found==0)
        return cum,jnp.where(take,cum,best),jnp.where(take,1,found)
    return lax.fori_loop(0,ndocs,step,(jnp.int32(0),jnp.int32(0),jnp.int32(0)),unroll=True)[1]

def starts_vec(meta, ndocs, t):
    def step(j,c):
        cum,best=c
        return cum+meta[1+j],jnp.where(cum<=t,cum,best)
    return lax.fori_loop(0,ndocs,step,(jnp.int32(0),jnp.zeros(t.shape,jnp.int32)),unroll=True)[1]

def ends_vec(meta, ndocs, t):
    def step(j,c):
        cum,best=c
        ln=meta[1+j]
        return cum+ln,jnp.where(cum<=t,cum+ln,best)
    return lax.fori_loop(0,ndocs,step,(jnp.int32(0),jnp.zeros(t.shape,jnp.int32)),unroll=True)[1]

def widened(columns, heads):
    rows, width = columns.shape
    ones = jnp.ones((rows, SPLITS * heads), BF16)
    empty = jnp.zeros((rows, WIDTH - width - SPLITS * heads), BF16)
    return jnp.concatenate([columns, ones, empty], axis=1)


def unpack_rows(packed, heads):
    pair = 2 * HEAD_DIM
    key = jnp.concatenate([packed[:, :pair], packed[:, 2 * pair : 2 * pair + HEAD_DIM]], axis=1)
    value = jnp.concatenate([packed[:, pair : 2 * pair], packed[:, 2 * pair + HEAD_DIM :]], axis=1)
    return widened(key, heads), widened(value, heads)


STEP = 512


def build_window(heads, start, earlier, own, packed, sems, keys, values, key_rows, value_rows):
    before = earlier.shape[0] // STEP
    chunks = before + own.shape[0] // STEP

    def copy(n, source, row):
        return pltpu.make_async_copy(
            source.at[pl.ds(row * STEP, STEP)], packed.at[pl.ds(n * STEP, STEP)], sems.at[n]
        )

    def begin(n, carry):
        @pl.when(n < before)
        def _():
            copy(n, earlier, n).start()

        @pl.when(n >= before)
        def _():
            copy(n, own, n - before).start()

        return carry

    def build(n, carry):
        copy(n, own, 0).wait()
        at = pl.ds(pl.multiple_of(n * STEP, STEP), STEP)
        key, value = unpack_rows(packed[at, :], heads)
        for wide, rows, flipped in ((key, keys, key_rows), (value, values, value_rows)):
            if rows is not None:
                rows[at, :] = wide
            if flipped is not None:
                turned = wide.T
                for h in range(heads):
                    flipped[h, :HEAD_DIM, at] = turned[h * HEAD_DIM : (h + 1) * HEAD_DIM]
        return carry

    lax.fori_loop(start, chunks, begin, 0)
    lax.fori_loop(start, chunks, build, 0)


def three(lo,a,b,hi,body):
    lax.fori_loop(lo,a,lambda j,_: body(j,True),None)
    lax.fori_loop(a,b,lambda j,_: body(j,False),None)
    lax.fori_loop(b,hi,lambda j,_: body(j,True),None)

def query_tiles(meta, ndocs, t0, wbase, tq, tk):
    lo = (doc_start(meta, ndocs, t0) - wbase) // tk
    f0 = (doc_start(meta, ndocs, t0 + tq - 1) - wbase + tk - 1) // tk
    f1 = (t0 - wbase) // tk
    hi = (t0 + tq - 1 - wbase) // tk + 1
    return lo, jnp.minimum(f0, f1), f1, hi


def fwd_kernel(heads, ndocs, tq, tk, meta, q_ref, earlier, own, mix_ref, wide_ref,
               k_ref, vt_ref, qt, m_ref, acc_ref, packed, sems):
    i = pl.program_id(0)
    width = q_ref.shape[1]
    real = heads * HEAD_DIM
    base = meta[0]
    wbase = base - earlier.shape[0]

    @pl.when(i == 0)
    def _():
        vt_ref[:, HEAD_DIM:, :] = jnp.ones_like(vt_ref[:, HEAD_DIM:, :])
        start = (doc_start(meta, ndocs, base) - wbase) // tk * (tk // STEP)
        build_window(heads, start, earlier, own, packed, sems, k_ref, None, None, vt_ref)

    t0 = base + i * tq
    lo, f0, f1, hi = query_tiles(meta, ndocs, t0, wbase, tq, tk)
    q = q_ref[...]
    trow = t0 + lax.broadcasted_iota(jnp.int32, (8, tq), 1)
    srow = starts_vec(meta, ndocs, trow)[:1]
    trow = trow[:1]
    lane = lax.broadcasted_iota(jnp.int32, (tq, width), 1)

    def visible(off):
        u = wbase + off + lax.broadcasted_iota(jnp.int32, (tk, tq), 0)
        return (u >= srow) & (u <= trow)

    itself = q.astype(F32) * k_ref[pl.ds(pl.multiple_of(t0 - wbase, tq), tq), :].astype(F32)
    shifted = q.astype(F32)
    for h in range(heads):
        mine = (lane >= h * HEAD_DIM) & (lane < (h + 1) * HEAD_DIM)
        score = jnp.sum(jnp.where(mine, itself, 0.0), axis=1, keepdims=True)
        for c, piece in enumerate(split_parts(-score)):
            shifted = jnp.where(lane == real + SPLITS * h + c, piece, shifted)
    per_head(shifted.astype(BF16), heads, qt)
    acc_ref[...] = jnp.zeros_like(acc_ref)

    def quick(j, masked):
        off = pl.multiple_of(j * tk, tk)
        k = k_ref[pl.ds(off, tk), :]
        if masked:
            vis = visible(off)
        for h in range(heads):
            p = jnp.exp(dotf(k, qt[h]))
            if masked:
                p = jnp.where(vis, p, 0.0)
            acc_ref[h] += dotf(vt_ref[h, :, pl.ds(off, tk)], p.astype(BF16))

    def finish(extra):
        rows = []
        parts = []
        for h in range(heads):
            acc = acc_ref[h]
            total = acc[HEAD_DIM : HEAD_DIM + 1]
            rows.append(acc[:HEAD_DIM] / total)
            at = real + SPLITS * h
            shift = jnp.sum(qt[h, at : at + SPLITS, :].astype(F32), axis=0, keepdims=True)
            parts += split_parts(shift - extra[h] - jnp.log(total))
        rest = jnp.zeros((width - real - len(parts), tq), F32)
        turned = jnp.concatenate(rows + parts + [rest], axis=0).T
        mix_ref[0] = turned[:, :real].astype(BF16)
        wide_ref[...] = jnp.where(lane < real, q.astype(F32), turned).astype(BF16)

    three(lo, f0, f1, hi, quick)
    none = jnp.zeros((1, tq), F32)
    finish([none] * heads)
    sums = acc_ref[:, HEAD_DIM : HEAD_DIM + 1, :]
    fits = jnp.max(jnp.where(sums < 1e30, 0.0, 1.0)) == 0.0

    @pl.when(jnp.logical_not(fits))
    def _():
        acc_ref[...] = jnp.zeros_like(acc_ref)
        m_ref[...] = jnp.full_like(m_ref, EXCLUDED)

        def body(j, carry):
            off = pl.multiple_of(j * tk, tk)
            k = k_ref[pl.ds(off, tk), :]
            vis = visible(off)
            for h in range(heads):
                s = jnp.where(vis, dotf(k, qt[h]), EXCLUDED)
                old = m_ref[h, :1]
                new = jnp.maximum(old, jnp.max(s, axis=0, keepdims=True))
                m_ref[h, :1] = new
                p = jnp.exp(s - new).astype(BF16)
                acc_ref[h] = acc_ref[h] * jnp.exp(old - new) + dotf(
                    vt_ref[h, :, pl.ds(off, tk)], p
                )
            return carry

        lax.fori_loop(lo, hi, body, 0)
        finish([m_ref[h, :1] for h in range(heads)])


SCALARS = pl.BlockSpec(memory_space=pltpu.SMEM)


def attention_fwd(meta, q, earlier, own, heads, tq, tk):
    block, width = q.shape
    window = block + earlier.shape[0]
    ndocs = meta.shape[0] - 1
    return pl.pallas_call(
        functools.partial(fwd_kernel, heads, ndocs, tq, tk),
        grid=(block // tq,),
        in_specs=[
            SCALARS,
            pl.BlockSpec((tq, width), lambda i: (i, 0)),
            ANY,
            ANY,
        ],
        out_specs=[
            pl.BlockSpec((1, tq, heads * HEAD_DIM), lambda i: (i, 0, 0)),
            pl.BlockSpec((tq, width), lambda i: (i, 0)),
        ],
        out_shape=[
            jax.ShapeDtypeStruct((block // tq, tq, heads * HEAD_DIM), BF16),
            jax.ShapeDtypeStruct((block, width), BF16),
        ],
        scratch_shapes=[
            pltpu.VMEM((window, width), BF16),
            pltpu.VMEM((heads, HEAD_DIM + 16, window), BF16),
            pltpu.VMEM((heads, width, tq), BF16),
            pltpu.VMEM((heads, 8, tq), F32),
            pltpu.VMEM((heads, HEAD_DIM + 16, tq), F32),
            pltpu.VMEM((window, own.shape[1]), BF16),
            pltpu.SemaphoreType.DMA((window // STEP,)),
        ],
        compiler_params=pltpu.CompilerParams(vmem_limit_bytes=56 << 20),
        cost_estimate=pl.CostEstimate(
            flops=30_000_000_000, bytes_accessed=12 << 20, transcendentals=20_000_000
        ),
        name="attn_fwd",
    )(meta, q, earlier, own)


def dq_kernel(heads, ndocs, tq, tk, meta, q_ref, do_ref, earlier, own, dq_ref,
              k_ref, v_ref, kt_ref, qt, dot, acc_ref, packed, sems):
    i = pl.program_id(0)
    base = meta[0]
    wbase = base - earlier.shape[0]

    @pl.when(i == 0)
    def _():
        start = (doc_start(meta, ndocs, base) - wbase) // tk * (tk // STEP)
        build_window(heads, start, earlier, own, packed, sems, k_ref, v_ref, kt_ref, None)

    t0 = base + i * tq
    per_head(q_ref[...], heads, qt)
    per_head(do_ref[...], heads, dot)
    acc_ref[...] = jnp.zeros_like(acc_ref)
    trow = t0 + lax.broadcasted_iota(jnp.int32, (8, tq), 1)
    srow = starts_vec(meta, ndocs, trow)[:1]
    trow = trow[:1]

    def body(j, masked):
        off = pl.multiple_of(j * tk, tk)
        k = k_ref[pl.ds(off, tk), :]
        v = v_ref[pl.ds(off, tk), :]
        if masked:
            u = wbase + off + lax.broadcasted_iota(jnp.int32, (tk, tq), 0)
            vis = (u >= srow) & (u <= trow)
        for h in range(heads):
            p = jnp.exp(dotf(k, qt[h]))
            if masked:
                p = jnp.where(vis, p, 0.0)
            ds = (p * dotf(v, dot[h])).astype(BF16)
            acc_ref[h] += dotf(kt_ref[h, :, pl.ds(off, tk)], ds)

    three(*query_tiles(meta, ndocs, t0, wbase, tq, tk), body)
    turned = acc_ref[...].reshape(heads * HEAD_DIM, tq).T
    dq_ref[...] = (turned * (HEAD_DIM**-0.5)).astype(BF16)


def attention_dq(meta, q, do, earlier, own, heads, tq, tk):
    block, width = q.shape
    window = block + earlier.shape[0]
    ndocs = meta.shape[0] - 1
    row = lambda w: pl.BlockSpec((tq, w), lambda i: (i, 0))
    return pl.pallas_call(
        functools.partial(dq_kernel, heads, ndocs, tq, tk),
        grid=(block // tq,),
        in_specs=[SCALARS, row(width), row(width), ANY, ANY],
        out_specs=row(heads * HEAD_DIM),
        out_shape=jax.ShapeDtypeStruct((block, heads * HEAD_DIM), BF16),
        scratch_shapes=[pltpu.VMEM((window, width), BF16)] * 2
        + [pltpu.VMEM((heads, HEAD_DIM, window), BF16)]
        + [pltpu.VMEM((heads, width, tq), BF16)] * 2
        + [pltpu.VMEM((heads, HEAD_DIM, tq), F32)]
        + [pltpu.VMEM((window, own.shape[1]), BF16), pltpu.SemaphoreType.DMA((window // STEP,))],
        compiler_params=pltpu.CompilerParams(vmem_limit_bytes=56 << 20),
        cost_estimate=pl.CostEstimate(
            flops=45_000_000_000, bytes_accessed=12 << 20, transcendentals=20_000_000
        ),
        name="attn_dq",
    )(meta, q, do, earlier, own)


def dkv_kernel(heads, ndocs, tq, tk, meta, own, q_parts, do_parts, dk_ref, dv_ref,
               q_ref, do_ref, qt_ref, dot_ref, kt, vt, dk_acc, dv_acc, sems):
    i = pl.program_id(0)
    base = meta[0]

    @pl.when(i == 0)
    def _():
        block = pl.num_programs(0) * tk
        end = (doc_end(meta, ndocs, base + block - 1) - base + STEP - 1) // STEP
        sources = []
        for parts in (q_parts, do_parts):
            row, found = 0, []
            for part in parts:
                found.append((row // STEP, (row + part.shape[0]) // STEP, part))
                row += part.shape[0]
            sources.append(found)

        def copy(k, n, source, row):
            return pltpu.make_async_copy(
                source.at[pl.ds(row * STEP, STEP)],
                (q_ref, do_ref)[k].at[pl.ds(n * STEP, STEP)],
                sems.at[k, n],
            )

        def begin(n, carry):
            for k in range(2):
                for first, last, part in sources[k]:

                    @pl.when((n >= first) & (n < last))
                    def _():
                        copy(k, n, part, n - first).start()

            return carry

        def turn(n, carry):
            at = pl.ds(pl.multiple_of(n * STEP, STEP), STEP)
            for k, (rows, flipped) in enumerate(((q_ref, qt_ref), (do_ref, dot_ref))):
                copy(k, n, sources[k][0][2], 0).wait()
                turned = rows[at, :].T
                for h in range(heads):
                    flipped[h, :, at] = turned[h * HEAD_DIM : (h + 1) * HEAD_DIM]
            return carry

        lax.fori_loop(0, end, begin, 0)
        lax.fori_loop(0, end, turn, 0)

    u0 = base + i * tk
    lo = (u0 - base) // tq
    f0 = (u0 + tk - 1 - base + tq - 1) // tq
    e_first = doc_end(meta, ndocs, u0)
    e_last = doc_end(meta, ndocs, u0 + tk - 1)
    f1 = (e_first - base) // tq
    hi = (e_last - 1 - base) // tq + 1
    f0 = jnp.minimum(f0, hi)
    f1 = jnp.clip(f1, f0, hi)
    k, v = unpack_rows(own[...], heads)
    per_head(k, heads, kt)
    per_head(v, heads, vt)
    dk_acc[...] = jnp.zeros_like(dk_acc)
    dv_acc[...] = jnp.zeros_like(dv_acc)
    urow = u0 + lax.broadcasted_iota(jnp.int32, (8, tk), 1)
    erow = ends_vec(meta, ndocs, urow)[:1]
    urow = urow[:1]

    def body(j, masked):
        off = pl.multiple_of(j * tq, tq)
        at = pl.ds(off, tq)
        q = q_ref[at, :]
        do = do_ref[at, :]
        if masked:
            t = base + off + lax.broadcasted_iota(jnp.int32, (tq, tk), 0)
            vis = (t >= urow) & (t < erow)
        for h in range(heads):
            p = jnp.exp(dotf(q, kt[h]))
            if masked:
                p = jnp.where(vis, p, 0.0)
            ds = (p * dotf(do, vt[h])).astype(BF16)
            dv_acc[h] += dotf(dot_ref[h, :, at], p.astype(BF16))
            dk_acc[h] += dotf(qt_ref[h, :, at], ds)

    three(lo, f0, f1, hi, body)
    for acc, out in ((dk_acc, dk_ref), (dv_acc, dv_ref)):
        out[...] = acc[...].reshape(heads * HEAD_DIM, tk).T.astype(BF16)


def attention_dkv(meta, own, q_parts, do_parts, heads, tq, tk):
    block, width = q_parts[0].shape
    window = sum(part.shape[0] for part in q_parts)
    ndocs = meta.shape[0] - 1
    row = lambda w: pl.BlockSpec((tk, w), lambda i: (i, 0))
    return pl.pallas_call(
        functools.partial(dkv_kernel, heads, ndocs, tq, tk),
        grid=(block // tk,),
        in_specs=[SCALARS, row(own.shape[1]), [ANY] * len(q_parts), [ANY] * len(do_parts)],
        out_specs=[row(heads * HEAD_DIM)] * 2,
        out_shape=[jax.ShapeDtypeStruct((block, heads * HEAD_DIM), BF16)] * 2,
        scratch_shapes=[pltpu.VMEM((window, width), BF16)] * 2
        + [pltpu.VMEM((heads, HEAD_DIM, window), BF16)] * 2
        + [pltpu.VMEM((heads, width, tk), BF16)] * 2
        + [pltpu.VMEM((heads, HEAD_DIM, tk), F32)] * 2
        + [pltpu.SemaphoreType.DMA((2, window // STEP))],
        compiler_params=pltpu.CompilerParams(vmem_limit_bytes=56 << 20),
        cost_estimate=pl.CostEstimate(
            flops=60_000_000_000, bytes_accessed=12 << 20, transcendentals=20_000_000
        ),
        name="attn_dkv",
    )(meta, own, q_parts, do_parts)


def on_device(
    tokens, first_values, cotangent, w_query, w_key, w_value, w_out, w_up, w_down,
    gain_attn, gain_mlp, doc_lengths,
):
    width = tokens.shape[1]
    heads_of = lax.axis_size("head")
    nblk = lax.axis_size("blk")
    blk = lax.axis_index("blk")
    rows = tokens.shape[0]
    block = rows * heads_of
    heads = HEADS // heads_of
    cols = heads * HEAD_DIM
    part = width // nblk
    meta = jnp.concatenate([jnp.reshape(blk * block, (1,)).astype(jnp.int32), doc_lengths])

    up_cols = w_up.shape[1]
    early = nblk - 3 * nblk // 8
    normed, query, own, earlier, gathered, qk_all, v_all, attn_gain, mlp_gain = front(
        nblk, early, tokens, first_values, w_query, w_key, w_value, w_up, w_down.T, w_out,
        gain_attn.reshape(1, part), gain_mlp.reshape(1, part),
    )
    w_qk = qk_all.reshape(width, 2 * cols)
    w_v = v_all.reshape(2, width, w_value.shape[1])
    earlier = earlier.reshape(2 * block, 2 * cols)
    beside = [(h, (h + 2) % heads_of) for h in range(heads_of)]
    mine = lax.dynamic_index_in_dim(gathered, lax.axis_index("head"), 0, keepdims=False)[early:]
    late = lax.ppermute(mine, "head", beside)
    mixed_parts, query_wide = attention_fwd(
        meta, query, earlier, own, heads, rows, 2 * rows
    )
    late, mixed_parts = lax.optimization_barrier((late, mixed_parts))
    layer_output, grad_resid, grad_parts, gain_mlp_part, keep_a, give_a, keep_b, give_b, query_later = middle(
        nblk, tokens, mixed_parts, cotangent, mlp_gain, gathered, late, query_wide, up_cols
    )
    grad_wide = grad_parts.reshape(block, WIDTH)
    across = [(i, i + 1 - 2 * (i % 2)) for i in range(nblk)]
    got_a = lax.ppermute(give_a, "head", beside)
    got_b = lax.ppermute(give_b, "blk", across)

    grads_later = [grad_wide] + [
        lax.ppermute(grad_wide, "blk", [(i, i - d) for i in range(d, nblk)]) for d in (1, 2)
    ]
    queries_later = [query_wide, query_later.reshape(2 * block, WIDTH)]
    grad_query = attention_dq(
        meta, query_wide, grad_wide, earlier, own, heads, rows, 2 * rows
    )
    got_a, got_b, grad_query = lax.optimization_barrier((got_a, got_b, grad_query))
    keep_a, give_a, keep_b, give_b = pair_sum(keep_a, got_a, keep_b, got_b)
    got_a = lax.ppermute(give_a, "blk", across)
    got_b = lax.ppermute(give_b, "head", beside)
    keep_a, own = lax.optimization_barrier((keep_a, own))
    grad_key, grad_value = attention_dkv(
        meta, own, queries_later, grads_later, heads, rows, rows
    )
    outs = tail(
        nblk, grad_query, grad_key, grad_value, normed, w_qk, w_v, gain_mlp_part,
        keep_a, got_a, keep_b, got_b, tokens, grad_resid, attn_gain,
    )
    (
        layer_output, grad_tokens, final_query, final_key, final_value, grad_first, gain_sums,
        final_up, final_down, final_out,
    ) = settle([layer_output] + list(outs))
    return (
        layer_output,
        grad_tokens,
        grad_first,
        final_query,
        final_key,
        final_value,
        final_out,
        final_up,
        final_down.T,
        gain_sums[0].reshape(part),
        gain_sums[1].reshape(part),
    )


def solution(mesh):
    rows = P(("blk", "head"), None)
    specs = (P("blk", "head"),) * 3 + (P("head", "blk"), P("blk", "head"), P("head", "blk"))
    gains = (P("blk"), P("blk"))
    return jax.shard_map(
        on_device,
        mesh=mesh,
        in_specs=(rows,) * 3 + specs + gains + (P(),),
        out_specs=(rows,) * 3 + specs + gains,
        check_vma=False,
    )
```

```python
import functools

import jax
import jax.numpy as jnp
from jax import lax
from jax.experimental import pallas as pl
from jax.experimental.pallas import tpu as pltpu
from jax.sharding import PartitionSpec as P

HEADS = 12
HEAD_DIM = 64
DOC_MAX = 4096
EPSILON = 1e-05
GELU_SCALE = 0.7978845608028654
EXCLUDED = -1e30
WIDTH = 256
SPLITS = 3
BF16 = jnp.bfloat16
F32 = jnp.float32
MESH = pl.DeviceIdType.MESH
ANY = pl.BlockSpec(memory_space=pl.ANY)
WHOLE = pl.BlockSpec(memory_space=pltpu.VMEM)
NT = (((1,), (1,)), ((), ()))
TN = (((0,), (0,)), ((), ()))


def dotf(left, right, dims=None):
    if dims is None:
        dims = (((1,), (0,)), ((), ()))
    return lax.dot_general(left, right, dims, preferred_element_type=F32)


def remote(src, dst, send_sem, recv_sem, head, blk):
    return pltpu.make_async_remote_copy(
        src_ref=src,
        dst_ref=dst,
        send_sem=send_sem,
        recv_sem=recv_sem,
        device_id={"head": head, "blk": blk},
        device_id_type=MESH,
    )


def greet(partners):
    barrier = pltpu.get_barrier_semaphore()
    for head, blk in partners:
        pl.semaphore_signal(
            barrier, inc=1, device_id={"head": head, "blk": blk}, device_id_type=MESH
        )
    pl.semaphore_wait(barrier, len(partners))


def xor(value, bit):
    return value + bit - 2 * bit * (lax.div(value, bit) % 2)


def partners_of(head, blk, nblk, heads=True, blks=True):
    found = []
    if heads:
        found += [(xor(head, 1), blk), (xor(head, 2), blk), (3 - head, blk)]
    if blks:
        found += [(head, lax.rem(blk + d, nblk)) for d in range(1, nblk)]
    return found


class Line:
    def __init__(self, nblk, head, blk, source, target, up, down, across):
        self.half, self.head, self.blk = nblk // 2, head, blk
        self.place, self.parity = lax.div(blk, 2), lax.rem(blk, 2)
        self.source, self.target = source, target
        self.sems = {"up": up, "down": down, "across": across}

    def copy(self, way, origin, step, fresh=False):
        slot = 2 * origin + self.parity
        to = {
            "up": lax.rem(self.blk + 2, 2 * self.half),
            "down": lax.rem(self.blk + 2 * self.half - 2, 2 * self.half),
            "across": self.blk + 1 - 2 * self.parity,
        }[way]
        send, recv = self.sems[way]
        return remote(
            self.source if fresh else self.target.at[slot],
            self.target.at[slot], send.at[step], recv.at[step], self.head, to,
        )

    def landing(self, way, slot, step):
        send, recv = self.sems[way]
        other = self.blk + 1 - 2 * self.parity
        at = self.target.at[slot]
        return remote(at, at, send.at[step], recv.at[step], self.head, other)

    def begin(self):
        @pl.when(self.place + 1 < self.half)
        def _():
            self.copy("up", self.place, 0, True).start()

        @pl.when(self.place > 0)
        def _():
            self.copy("down", self.place, 0, True).start()

        self.copy("across", self.place, self.place, True).start()

    def step(self, s, then=None):
        low, high = self.place - 1 - s, self.place + 1 + s

        @pl.when(low >= 0)
        def _():
            self.landing("up", 2 * low + self.parity, s).wait_recv()
            if s + 1 < self.half - 1:

                @pl.when(self.place + 1 < self.half)
                def _():
                    self.copy("up", low, s + 1).start()

            self.copy("across", low, low).start()
            if then:
                then(2 * low + self.parity)

        @pl.when(high < self.half)
        def _():
            self.landing("down", 2 * high + self.parity, s).wait_recv()
            if s + 1 < self.half - 1:

                @pl.when(self.place > 0)
                def _():
                    self.copy("down", high, s + 1).start()

            self.copy("across", high, high).start()
            if then:
                then(2 * high + self.parity)

    def land(self, origin):
        self.landing("across", 2 * origin + 1 - self.parity, origin).wait_recv()

    def finish(self):
        for o in range(self.half):
            self.copy("across", o, o).wait_send()
        for s in range(self.half - 1):

            @pl.when((self.place - s >= 0) & (self.place + 1 < self.half))
            def _():
                self.copy("up", self.place - s, s).wait_send()

            @pl.when((self.place + s < self.half) & (self.place > 0))
            def _():
                self.copy("down", self.place + s, s).wait_send()


def tail_kernel(
    nblk, pieces, cols, d_q, d_k, d_v, normed, w_qk, w_v, gain_m, kept_a, got_a, kept_b, got_b, tok, resid, gain,
    out_grad, out_q, out_k, out_v, out_first, out_gain, out_up, out_down, out_out,
    grad, weights, gains, joined, weight, acc,
    tok_buf, resid_buf, normed_buf, load_sem, first_got, rest_sum,
    core_buf, side_out, side_buf, pair_buf, line_out, line_in, v_sum, v_got,
    gain_buf, gain_sum, gain_got, up_out, up_in, down_out, down_in,
    own_sem, send_s, recv_s, send_x, recv_x, send_y, recv_y, send_l, recv_l,
    send_v, recv_v, send_f, recv_f, send_g, recv_g, send_h, recv_h, send_u, recv_u, send_d, recv_d,
):
    head, blk = lax.axis_index("head"), lax.axis_index("blk")
    side, core, far = xor(head, 2), xor(head, 1), 3 - head
    size = grad.shape[1]
    turns = (far, side, core, head)
    loads = [
        pltpu.make_async_copy(
            normed.at[pl.ds(pl.multiple_of(t * size, size), size)], normed_buf.at[i], load_sem.at[i]
        )
        for i, t in enumerate(turns)
    ]
    loads += [
        pltpu.make_async_copy(tok, tok_buf, load_sem.at[4]),
        pltpu.make_async_copy(resid, resid_buf, load_sem.at[5]),
    ]
    for copy in loads:
        copy.start()
    greet(partners_of(head, blk, nblk))
    rows = grad.shape[1] // pieces
    line, place, parity = nblk // 2, lax.div(blk, 2), lax.rem(blk, 2)
    pair = blk + 1 - 2 * parity
    above, below = lax.rem(blk + 2, nblk), lax.rem(blk + nblk - 2, nblk)

    def part(ref, p):
        return ref.at[pl.ds(p * rows, rows)]

    def to_core(i, p, slot):
        return remote(
            part(grad.at[slot], p), part(core_buf.at[i], p), send_s.at[i, p], recv_s.at[i, p],
            core, blk,
        )

    def to_side(p):
        return remote(
            part(side_out, p), part(side_buf, p), send_x.at[p], recv_x.at[p], side, blk
        )

    def sum_of(t):
        first_part = kept_b[t].astype(F32) + got_b[t].astype(F32)
        return jnp.concatenate([first_part, kept_a[t].astype(F32) + got_a[t].astype(F32)], axis=1)

    def up_copy(t, to):
        return remote(up_out.at[t], up_in.at[t], send_u.at[t], recv_u.at[t], head, to)

    def down_copy(t, to):
        return remote(down_out.at[t], down_in.at[t], send_d.at[t], recv_d.at[t], head, to)

    def first_hops():
        for n in range(line - 1):
            t = line - 1 - n

            @pl.when((place == 0) & (place < t))
            def _():
                up_out[t] = sum_of(t).astype(BF16)
                up_copy(t, above).start()

            @pl.when((place == line - 1) & (place > n))
            def _():
                down_out[n] = sum_of(n).astype(BF16)
                down_copy(n, below).start()

    def next_hops(n):
        t = line - 1 - n

        @pl.when((place > 0) & (place < t))
        def _():
            up_copy(t, above).wait_recv()
            up_out[t] = (sum_of(t) + up_in[t].astype(F32)).astype(BF16)
            up_copy(t, above).start()

        @pl.when((place < line - 1) & (place > n))
        def _():
            down_copy(n, below).wait_recv()
            down_out[n] = (sum_of(n) + down_in[n].astype(F32)).astype(BF16)
            down_copy(n, below).start()

    first_hops()
    half, kind = lax.div(head, 2), lax.rem(head, 2)

    def first_copy(i, to, slot):
        source = d_v.at[pl.ds(to * grad.shape[1], grad.shape[1])]
        return remote(source, first_got.at[slot], send_f.at[i], recv_f.at[slot], to, blk)

    def own_first(slot):
        source = d_v.at[pl.ds(head * grad.shape[1], grad.shape[1])]
        return pltpu.make_async_copy(source, first_got.at[slot], own_sem)

    @pl.when(half == 1)
    def _():
        for i, to in enumerate((core, side, far)):
            first_copy(i, to, kind).start()
        own_first(kind).start()

    mine = half == 0
    weight[:, : 2 * cols] = w_qk[...]
    fresh = jnp.concatenate([w_v[0], w_v[1]], axis=1)
    weight[:, 2 * cols :] = jnp.where(mine, fresh, jnp.zeros_like(fresh))
    gain_row = None
    for i, t in enumerate(turns):
        at = pl.ds(pl.multiple_of(t * grad.shape[1], grad.shape[1]), grad.shape[1])
        joined[:, :cols] = d_q[at, :]
        joined[:, cols : 2 * cols] = d_k[at, :]
        joined[:, 2 * cols : 3 * cols] = d_v[at, :]
        joined[:, 3 * cols :] = jnp.zeros((grad.shape[1], joined.shape[1] - 3 * cols), BF16)
        given = joined[...]
        whole = dotf(given[:, : 3 * cols], weight[...], NT)
        grad[t] = whole.astype(BF16)
        if i == 0:
            for p in range(pieces):
                to_core(0, p, far).start()
        if i == 2:
            for p in range(pieces):
                to_core(1, p, core).start()
        loads[i].wait()
        rows_in = normed_buf[i]
        term = jnp.sum(whole * rows_in.astype(F32), axis=0, keepdims=True)
        gain_row = term if gain_row is None else gain_row + term
        term = dotf(rows_in, given, TN)
        acc[...] = term if i == 0 else acc[...] + term
        if i == 2:
            for p in range(pieces):
                to_core(0, p, far).wait_recv()
                part(side_out, p)[...] = (
                    part(grad.at[side], p)[...].astype(F32)
                    + part(core_buf.at[0], p)[...].astype(F32)
                ).astype(BF16)
                to_side(p).start()
    whole_part = weights.shape[1]
    for b in range(nblk):
        weights[b] = acc[b * whole_part : (b + 1) * whole_part].astype(BF16)

    def across(n):
        return remote(
            weights.at[2 * n + 1 - parity], pair_buf.at[n], send_y.at[n], recv_y.at[n], head, pair
        )

    for n in range(line):
        across(n).start()
    gain_row = gain_row / gain[...]
    for b in range(nblk):
        gains[b, 0] = gain_row[:, b * whole_part : (b + 1) * whole_part]
        gains[b, 1] = gain_m[:, b * whole_part : (b + 1) * whole_part]

    def gain_to(d):
        to = lax.rem(blk + d, nblk)
        return remote(gains.at[to], gain_buf.at[blk], send_g.at[d], recv_g.at[d], head, to)

    def gain_from(d):
        source = lax.rem(blk - d + nblk, nblk)
        return remote(gains.at[0], gain_buf.at[source], send_g.at[d], recv_g.at[d], head, source)

    for d in range(1, nblk):
        gain_to(d).start()
    gain_buf[blk] = gains[blk]

    def along(d, to):
        return remote(
            line_out.at[to], line_in.at[d], send_l.at[d], recv_l.at[d], head, 2 * to + parity
        )

    next_hops(0)
    for n in range(line):
        across(n).wait_recv()
        line_out[n] = (
            weights[2 * n + parity].astype(F32) + pair_buf[n].astype(F32)
        ).astype(BF16)
    for d in range(1, line):
        along(d, lax.rem(place + d, line)).start()
    for d in range(1, nblk):
        gain_from(d).wait_recv()
    gain_sum[...] = jnp.sum(gain_buf[...], axis=0)
    peers = (core, side, far)

    def gain_copy(i, to):
        return remote(gain_sum, gain_got.at[i], send_h.at[i], recv_h.at[i], to, blk)

    for i, to in enumerate(peers):
        gain_copy(i, to).start()
    for n in range(1, line - 1):
        next_hops(n)
    total = line_out[place].astype(F32)
    for d in range(1, line):
        along(d, lax.rem(place - d + line, line)).wait_recv()
        total = total + line_in[d].astype(F32)
    out_q[...] = total[:, :cols]
    out_k[...] = total[:, cols : 2 * cols]
    v_sum[0] = total[:, 2 * cols : 2 * cols + cols // 2]
    v_sum[1] = total[:, 2 * cols + cols // 2 : 3 * cols]

    def give(c, to):
        return remote(v_sum.at[c], v_got, send_v.at[c], recv_v.at[0], to, blk)

    for c in range(2):
        to = 2 * head + c

        @pl.when((half == 0) & (to != head))
        def _():
            give(c, to).start()

    for copy in loads[4:]:
        copy.wait()
    for p in range(pieces):
        to_core(1, p, core).wait_recv()
        to_side(p).wait_recv()
        norm_grad = (
            part(grad.at[head], p)[...].astype(F32)
            + part(core_buf.at[1], p)[...].astype(F32)
            + part(side_buf, p)[...].astype(F32)
        )
        xhat, scale = statistics(part(tok_buf, p)[...].astype(F32))
        part(out_grad, p)[...] = part(resid_buf, p)[...] + norm_back(norm_grad, xhat, scale, gain[...])
    rest_sum[...] = sum_of(place)
    for t in range(line):

        @pl.when((place == t) & (place > 0))
        def _():
            up_copy(t, above).wait_recv()
            rest_sum[...] += up_in[t].astype(F32)

        @pl.when((place == t) & (place < line - 1))
        def _():
            down_copy(t, below).wait_recv()
            rest_sum[...] += down_in[t].astype(F32)

    inner = out_up.shape[1]
    cut = kept_b.shape[2]
    out_up[...] = rest_sum[:, cut : cut + inner]
    out_down[:, :cut] = rest_sum[:, :cut]
    out_down[:, cut:] = rest_sum[:, cut + inner : 2 * inner]
    out_out[...] = rest_sum[:, 2 * inner :].T
    for i, to in enumerate(peers):
        gain_copy(i, to).wait_recv()
    out_gain[...] = gain_sum[...] + gain_got[0] + gain_got[1] + gain_got[2]

    @pl.when(head == 0)
    def _():
        out_v[...] = v_sum[0]

    @pl.when(head != 0)
    def _():
        give(0, half).wait_recv()
        out_v[...] = v_got[...]

    for slot in range(2):

        @pl.when(head == 2 + slot)
        def _():
            own_first(slot).wait()

        @pl.when(head != 2 + slot)
        def _():
            first_copy(0, 2 + slot, slot).wait_recv()

    out_first[...] = jnp.concatenate([first_got[0], first_got[1]], axis=1).astype(F32)

    @pl.when(half == 1)
    def _():
        for i, to in enumerate((core, side, far)):
            first_copy(i, to, kind).wait_send()

    for c in range(2):
        to = 2 * head + c

        @pl.when((half == 0) & (to != head))
        def _():
            give(c, to).wait_send()

    for i, to in enumerate(peers):
        gain_copy(i, to).wait_send()
    for p in range(pieces):
        to_core(0, p, far).wait_send()
        to_core(1, p, core).wait_send()
        to_side(p).wait_send()
    for d in range(1, nblk):
        gain_to(d).wait_send()
    for n in range(line):
        across(n).wait_send()
    for d in range(1, line):
        along(d, lax.rem(place + d, line)).wait_send()
    for t in range(line):

        @pl.when(place < t)
        def _():
            up_copy(t, above).wait_send()

        @pl.when(place > t)
        def _():
            down_copy(t, below).wait_send()


def tail(
    nblk, d_q, d_k, d_v, normed, w_qk, w_v, gain_m, kept_a, got_a, kept_b, got_b, tok, resid, gain,
    pieces=4,
):
    dma = pltpu.SemaphoreType.DMA
    row, part, cols = tok.shape, w_v.shape[1] // nblk, d_q.shape[1]
    rest = (nblk // 2, part, kept_a.shape[2] + kept_b.shape[2])
    inner = (rest[2] - cols) // 2
    padded = -(-3 * cols // 128) * 128
    gains = jax.ShapeDtypeStruct((nblk, 2, 1, part), F32)
    half, line = (part, cols // 2), nblk // 2
    piece = (2, pieces)
    vmem = lambda *shape: pltpu.VMEM(shape, BF16)
    return pl.pallas_call(
        functools.partial(tail_kernel, nblk, pieces, cols),
        out_shape=[
            jax.ShapeDtypeStruct(row, F32),
            jax.ShapeDtypeStruct((part, cols), F32),
            jax.ShapeDtypeStruct((part, cols), F32),
            jax.ShapeDtypeStruct(half, F32),
            jax.ShapeDtypeStruct((row[0], 2 * cols), F32),
            jax.ShapeDtypeStruct(gains.shape[1:], F32),
            jax.ShapeDtypeStruct((part, inner), F32),
            jax.ShapeDtypeStruct((part, inner), F32),
            jax.ShapeDtypeStruct((cols, part), F32),
        ],
        in_specs=[WHOLE] * 3 + [ANY] + [WHOLE] * 7 + [ANY] * 2 + [WHOLE],
        out_specs=[WHOLE] * 9,
        scratch_shapes=[
            vmem(4, *row), vmem(nblk, part, padded), pltpu.VMEM(gains.shape, F32),
            vmem(row[0], padded), vmem(row[1], 3 * cols), pltpu.VMEM((row[1], padded), F32),
            vmem(*row), pltpu.VMEM(row, F32), vmem(4, *row), dma((6,)),
            vmem(2, row[0], cols), pltpu.VMEM(rest[1:], F32),
            vmem(2, *row), vmem(*row), vmem(*row),
            vmem(line, part, padded), vmem(line, part, padded),
            vmem(line, part, padded),
            pltpu.VMEM((2,) + half, F32),
            pltpu.VMEM(half, F32),
            pltpu.VMEM(gains.shape, F32),
            pltpu.VMEM(gains.shape[1:], F32),
            pltpu.VMEM((3,) + gains.shape[1:], F32),
            vmem(*rest), vmem(*rest), vmem(*rest), vmem(*rest),
            dma,
            dma(piece), dma(piece),
            dma((pieces,)), dma((pieces,)),
            dma((line,)), dma((line,)), dma((line,)), dma((line,)),
            dma((2,)), dma((1,)),
            dma((3,)), dma((2,)),
            dma((nblk,)), dma((nblk,)),
            dma((3,)), dma((3,)),
            dma((line,)), dma((line,)), dma((line,)), dma((line,)),
        ],
        compiler_params=pltpu.CompilerParams(
            collective_id=4, has_side_effects=True, vmem_limit_bytes=60 << 20
        ),
        name="tail",
    )(d_q, d_k, d_v, normed, w_qk, w_v, gain_m, kept_a, got_a, kept_b, got_b, tok, resid, gain)


def settle_kernel(count, *refs):
    sources, targets, sems = refs[:count], refs[count : 2 * count], refs[2 * count]
    copies = [
        pltpu.make_async_copy(source, target, sems.at[i])
        for i, (source, target) in enumerate(zip(sources, targets))
    ]
    for copy in copies:
        copy.start()
    for copy in copies:
        copy.wait()


def settle(arrays):
    count = len(arrays)
    return pl.pallas_call(
        functools.partial(settle_kernel, count),
        out_shape=[jax.ShapeDtypeStruct(a.shape, a.dtype) for a in arrays],
        in_specs=[ANY] * count,
        out_specs=[WHOLE] * count,
        scratch_shapes=[pltpu.SemaphoreType.DMA((count,))],
        name="settle",
    )(*arrays)


def statistics(values):
    center = values - jnp.mean(values, axis=-1, keepdims=True)
    scale = lax.rsqrt(jnp.mean(jnp.square(center), axis=-1, keepdims=True) + EPSILON)
    return center * scale, scale


def norm_back(grad, xhat, scale, gain):
    eg = grad * gain
    return scale * (
        eg
        - jnp.mean(eg, axis=-1, keepdims=True)
        - xhat * jnp.mean(eg * xhat, axis=-1, keepdims=True)
    )


def split_parts(values):
    high = values.astype(BF16).astype(F32)
    middle = (values - high).astype(BF16).astype(F32)
    return high, middle, values - high - middle


def front_kernel(
    nblk, parts, pieces, early, tok, first, w_q, w_k, w_v, w_up, w_down, w_out, gain_a, gain_m,
    normed, query, own, near_far, rest, qk_all, v_all, attn_gain, mlp_gain,
    tok_all, first_all, v_own, gain_all, w_qk, w_rest, gains, weight, normed_buf,
    own_sem, normed_sem, send_t, recv_t, send_s, recv_s, send_p, recv_p, send_w, recv_w,
    send_v, recv_v, qk_u, qk_ur, qk_d, qk_dr, qk_a, qk_ar, up_u, up_ur, up_d, up_dr, up_a, up_ar,
    send_x, recv_x, send_c, recv_c, send_f, recv_f, send_z, recv_z, send_y, recv_y,
):
    head, blk = lax.axis_index("head"), lax.axis_index("blk")
    side, core, beyond = xor(head, 2), xor(head, 1), 3 - head
    odd, place = lax.rem(blk, 2), lax.div(blk, 2)
    near = blk + 1 - 2 * odd
    up, down = lax.rem(blk + 2, nblk), lax.rem(blk + nblk - 2, nblk)
    greet(partners_of(head, blk, nblk))
    moved = [(tok, tok_all), (first, first_all)]
    weights = [(w_v, v_own), (gains, gain_all)]
    rows = tok.shape[0] // parts

    def part(ref, n):
        return ref.at[pl.ds(n * rows, rows)]

    def hop(sems, k, n, source, slot, target):
        dst = part(moved[k][1].at[slot], n)
        return remote(source, dst, sems[0].at[k, n], sems[1].at[k, n], target, blk)

    ts, ss, ps = (send_t, recv_t), (send_s, recv_s), (send_p, recv_p)
    order = [(k, n) for n in range(parts) for k in range(2)]
    for k, n in order:
        hop(ts, k, n, part(moved[k][0], n), head, side).start()
    cols, inner = w_q.shape[1], w_up.shape[1]
    w_qk[:, :cols] = w_q[...]
    w_qk[:, cols:] = w_k[...]
    qk_line = Line(nblk, head, blk, w_qk, qk_all, (qk_u, qk_ur), (qk_d, qk_dr), (qk_a, qk_ar))
    qk_line.begin()
    w_rest[:, :inner] = w_up[...]
    w_rest[:, inner : 2 * inner] = w_down[...]
    w_rest[:, 2 * inner :] = w_out[...].T
    line = Line(
        nblk, head, blk, w_rest, rest.at[head], (up_u, up_ur), (up_d, up_dr), (up_a, up_ar)
    )
    line.begin()
    gains[0] = gain_a[...]
    gains[1] = gain_m[...]

    def chunk(sems, slot, b, to, source=None):
        at = rest.at[slot, b]
        return remote(at if source is None else source, at, sems[0].at[b], sems[1].at[b], to, blk)

    xs, cs, fs = (send_x, recv_x), (send_c, recv_c), (send_f, recv_f)

    def to_core(b, source=None):
        chunk(cs, head, b, core, source).start()

    def to_side(b, source=None):
        @pl.when(b < early)
        def _():
            chunk(xs, head, b, side, source).start()

    to_core(blk, w_rest)
    own_rest = pltpu.make_async_copy(w_rest, rest.at[head, blk], own_sem)
    own_rest.start()

    def spread(d):
        to = lax.rem(blk + d, nblk)
        return [
            remote(src, dst.at[blk], send_w.at[i, d], recv_w.at[i, d], head, to)
            for i, (src, dst) in enumerate(weights)
        ]

    def from_peer(d):
        source = lax.rem(blk - d + nblk, nblk)
        return [
            remote(src, dst.at[source], send_w.at[i, d], recv_w.at[i, d], head, source)
            for i, (src, dst) in enumerate(weights)
        ]

    for d in range(1, nblk):
        for copy in spread(d):
            copy.start()
    for k, n in order:
        hop(ss, k, n, part(moved[k][0], n), head, core).start()
    tok_all[head] = tok[...]
    first_all[head] = first[...]
    v_own[blk] = w_v[...]
    gain_all[blk] = gains[...]
    qk_all[blk] = w_qk[...]

    def pass_on(k, n):
        landed = part(moved[k][1].at[side], n)
        hop(ts, k, n, landed, side, side).wait_recv()
        hop(ps, k, n, landed, side, core).start()

    steps = nblk // 2 - 1
    for s in range(steps):
        qk_line.step(s)
    for s in range(steps):
        line.step(s, to_core)
        for k, n in order[s * len(order) // steps : (s + 1) * len(order) // steps]:
            pass_on(k, n)
    to_side(blk, w_rest)
    for s in range(steps):

        @pl.when(place - 1 - s >= 0)
        def _():
            to_side(blk - 2 - 2 * s)

        @pl.when(place + 1 + s < nblk // 2)
        def _():
            to_side(blk + 2 + 2 * s)

    for d in range(1, nblk):
        for copy in from_peer(d):
            copy.wait_recv()
    half, kind = lax.div(head, 2), lax.rem(head, 2)
    for i in range(2):
        target = half + 2 * i

        @pl.when(target == head)
        def _():
            v_all[kind] = v_own[...]

        @pl.when(target != head)
        def _():
            remote(v_own, v_all.at[kind], send_v.at[i], recv_v.at[kind], target, blk).start()

    for o in range(nblk // 2):
        qk_line.land(o)
    for c in range(2):
        source = 2 * kind + c

        @pl.when(source != head)
        def _():
            remote(v_own, v_all.at[c], send_v.at[0], recv_v.at[c], source, blk).wait_recv()

    attn_gain[...] = jnp.concatenate([gain_all[b, 0] for b in range(nblk)], axis=1)
    mlp_gain[...] = jnp.concatenate([gain_all[b, 1] for b in range(nblk)], axis=1)

    step = own.shape[0] // pieces

    def slab(ref, n):
        return ref.at[pl.ds(n * step, step)]

    def far_copy(n, to):
        return remote(slab(own, n), slab(near_far.at[0], n), send_z.at[n], recv_z.at[n], head, to)

    def near_copy(n, src):
        return remote(src, slab(near_far.at[1], n), send_y.at[n], recv_y.at[n], head, near)

    size = HEAD_DIM
    pair = 2 * size
    width = tok.shape[1]
    block = w_q.shape[0]
    for b in range(nblk):
        at = pl.ds(b * block, block)
        both, fresh = qk_all[b], jnp.concatenate([v_all[0, b], v_all[1, b]], axis=1)
        key = both[:, cols:]
        weight[at, :pair] = key[:, :pair]
        weight[at, pair : 2 * pair] = fresh[:, :pair]
        weight[at, 2 * pair : 3 * pair] = jnp.concatenate([key[:, pair:], fresh[:, pair:]], axis=1)
        weight[at, 3 * pair :] = jnp.concatenate(
            [both[:, :cols], jnp.zeros((block, WIDTH - cols), BF16)], axis=1
        )
    def make_rows(i, carry):
        t = jnp.where(i == 0, head, jnp.where(i == 1, side, jnp.where(i == 2, core, beyond)))

        @pl.when(i == 2)
        def _():
            for k, n in order:
                hop(ss, k, n, part(moved[k][1].at[core], n), core, core).wait_recv()

        @pl.when(i == 3)
        def _():
            for k, n in order:
                hop(ps, k, n, part(moved[k][1].at[beyond], n), beyond, core).wait_recv()
        total = tok.shape[0]
        at = pl.ds(pl.multiple_of(t * total, total), total)
        xhat, _ = statistics(tok_all[t].astype(F32))
        row = (xhat * attn_gain[...]).astype(BF16)
        normed_buf[t] = row
        pltpu.make_async_copy(normed_buf.at[t], normed.at[at], normed_sem.at[i]).start()
        out = dotf(row, weight[...])
        query[at, :] = (out[:, 3 * pair :].astype(BF16).astype(F32) * size**-0.5).astype(BF16)
        done = out[:, : 3 * pair].astype(BF16)
        given = first_all[t]
        kept = jnp.where(kind == 0, given[:, :cols], given[:, cols:])
        other = jnp.concatenate(
            [done[:, :pair], kept[:, :pair], done[:, 2 * pair : 2 * pair + size], kept[:, pair:]],
            axis=1,
        )
        own[at, :] = jnp.where(half == 0, done, other)
        for n in range(pieces // 4):
            n = t * (pieces // 4) + n

            @pl.when(blk + 2 < nblk)
            def _():
                far_copy(n, up).start()

            @pl.when(odd == 0)
            def _():
                near_copy(n, slab(own, n)).start()

        return carry

    lax.fori_loop(0, 4, make_rows, 0)
    for o in range(nblk // 2):

        line.land(o)
        to_core(2 * o + 1 - odd)
        to_side(2 * o + 1 - odd)

    for i, t in enumerate((head, side, core, beyond)):
        for n in range(pieces // 4):
            n = t * (pieces // 4) + n

            @pl.when(blk >= 2)
            def _():
                far_copy(n, down).wait_recv()

            @pl.when((blk >= 2) & (odd == 1))
            def _():
                near_copy(n, slab(near_far.at[0], n)).start()

    own_rest.wait()
    for b in range(early):
        chunk(xs, side, b, side).wait_recv()
        chunk(fs, side, b, core).start()
    for b in range(nblk):
        chunk(cs, core, b, core).wait_recv()
    for b in range(early):
        chunk(fs, beyond, b, core).wait_recv()
        chunk(xs, head, b, side).wait_send()
        chunk(fs, side, b, core).wait_send()
    for b in range(nblk):
        chunk(cs, head, b, core).wait_send()
    for i in range(4):
        at = pl.ds(0, tok.shape[0])
        pltpu.make_async_copy(normed_buf.at[i], normed.at[at], normed_sem.at[i]).wait()
    for n in range(pieces):

        @pl.when((blk >= 2) | (odd == 1))
        def _():
            near_copy(n, slab(own, n)).wait_recv()

        @pl.when(blk + 2 < nblk)
        def _():
            far_copy(n, up).wait_send()

        @pl.when((blk >= 2) | (odd == 0))
        def _():
            near_copy(n, slab(own, n)).wait_send()

    for i in range(2):
        target = half + 2 * i

        @pl.when(target != head)
        def _():
            remote(v_own, v_all.at[kind], send_v.at[i], recv_v.at[kind], target, blk).wait_send()

    for k, n in order:
        hop(ts, k, n, part(moved[k][0], n), head, side).wait_send()
        hop(ss, k, n, part(moved[k][0], n), head, core).wait_send()
        hop(ps, k, n, part(moved[k][1].at[side], n), side, core).wait_send()
    for d in range(1, nblk):
        for copy in spread(d):
            copy.wait_send()
    qk_line.finish()
    line.finish()


def front(
    nblk, early, tok, first, w_q, w_k, w_v, w_up, w_down, w_out, gain_a, gain_m, parts=4, pieces=8
):
    dma = pltpu.SemaphoreType.DMA
    (rows, width), (part, cols) = tok.shape, w_q.shape
    total = 4 * rows
    both = w_up.shape[1] + w_down.shape[1] + w_out.shape[0]
    low = lambda *shape: jax.ShapeDtypeStruct(shape, BF16)
    vmem = lambda *shape: pltpu.VMEM(shape, BF16)
    line = [dma((nblk // 2,))] * 6
    return pl.pallas_call(
        functools.partial(front_kernel, nblk, parts, pieces, early),
        out_shape=[
            low(total, width),
            low(total, WIDTH),
            low(total, 2 * cols),
            low(2, total, 2 * cols),
            low(4, nblk, part, both),
            low(nblk, part, 2 * cols),
            low(2, nblk, *w_v.shape),
            jax.ShapeDtypeStruct((1, width), F32),
            jax.ShapeDtypeStruct((1, width), F32),
        ],
        in_specs=[WHOLE] * 10,
        out_specs=[ANY, WHOLE, WHOLE, ANY, ANY] + [WHOLE] * 4,
        scratch_shapes=[
            vmem(4, *tok.shape),
            vmem(4, *first.shape),
            vmem(nblk, *w_v.shape),
            pltpu.VMEM((nblk, 2) + gain_a.shape, F32),
            vmem(part, 2 * cols),
            vmem(part, both),
            pltpu.VMEM((2,) + gain_a.shape, F32),
            vmem(width, 2 * cols + WIDTH),
            vmem(4, *tok.shape),
            dma,
            dma((4,)),
        ]
        + [dma((2, parts))] * 6
        + [dma((2, nblk))] * 2
        + [dma((2,))] * 2
        + line * 2
        + [dma((nblk,))] * 6
        + [dma((pieces,))] * 4,
        compiler_params=pltpu.CompilerParams(
            collective_id=0, has_side_effects=True, vmem_limit_bytes=56 << 20
        ),
        name="front",
    )(tok, first, w_q, w_k, w_v, w_up, w_down, w_out, gain_a, gain_m)


def gelu_both(pre):
    square = pre * pre
    inner = jnp.tanh(GELU_SCALE * (pre + 0.044715 * square * pre))
    slope = GELU_SCALE * (1.0 + 3.0 * 0.044715 * square)
    outer = 0.5 * (1.0 + inner)
    return pre * outer, outer + 0.5 * pre * (1.0 - inner * inner) * slope


def middle_kernel(
    nblk, up_cols, cut, pieces, tok, mixed_parts, cot, gain, gathered, late, query,
    out, grad_resid, grad_wide, gain_part, keep_a, give_a, keep_b, give_b, query_later,
    up, down, w_out, up_grad, down_grad, out_grad, mixed, wide_parts, up_got, down_got, out_got,
    sems, out_sems, send_m, recv_m, send_g, recv_g, send_c, recv_c,
    send_z, recv_z, send_y, recv_y, hidden_all, pre_all, normed_t, cot_t, total, grad_normed, normed_rows, branch_rows, branch_t, late_far, send_l, recv_l,
):
    head, blk = lax.axis_index("head"), lax.axis_index("blk")
    x, core_index = lax.div(head, 2), lax.rem(head, 2)
    core = xor(head, 1)
    others = [xor(head, 2), 3 - head, core]
    odd = lax.rem(blk, 2)
    pair = blk + 1 - 2 * odd
    above, below = lax.rem(blk + 2, nblk), lax.rem(blk + nblk - 2, nblk)
    greet(partners_of(head, blk, nblk, blks=False) + [(head, b) for b in (pair, above, below)])
    heads_of = 4
    part = gathered.shape[2]
    cols = mixed.shape[2]
    heads = cols // HEAD_DIM

    def mixed_copy(i, to, slot):
        return remote(
            mixed_parts.at[to], mixed.at[slot], send_m.at[i], recv_m.at[i], to, blk
        )

    for i, to in enumerate(others):
        mixed_copy(i, to, head).start()
    late_copy = remote(late, late_far, send_l, recv_l, core, blk)
    late_copy.start()
    early = nblk - late.shape[0]
    piece_rows = query.shape[0] // pieces

    def slab(ref, p):
        return ref.at[pl.ds(p * piece_rows, piece_rows)]

    def far_copy(p, to):
        dst = slab(query_later.at[1], p)
        return remote(slab(query, p), dst, send_z.at[p], recv_z.at[p], head, to)

    def near_copy(p, src):
        return remote(src, slab(query_later.at[0], p), send_y.at[p], recv_y.at[p], head, pair)

    for p in range(pieces):

        @pl.when(blk >= 2)
        def _():
            far_copy(p, below).start()

        @pl.when(odd == 1)
        def _():
            near_copy(p, slab(query, p)).start()

    def relay(p):
        @pl.when(blk + 2 < nblk)
        def _():
            far_copy(p, above).wait_recv()

        @pl.when((blk + 2 < nblk) & (odd == 0))
        def _():
            near_copy(p, slab(query_later.at[1], p)).start()

    chunks = [2 * n + c for n in (1 - x, x) for c in (1 - core_index, core_index)]
    side = others[0]
    sources = (3 - head, others[0], core)

    def source(i, b):
        if b < early or i > 1:
            return gathered.at[chunks[i], b]
        return (late_far, late)[i].at[b - early]

    def load(i, which):
        target, lo, size = ((w_out, 2 * up_cols, cols), (up, 0, up_cols), (down, up_cols, up_cols))[
            which
        ]
        return [
            pltpu.make_async_copy(
                source(i, b).at[:, pl.ds(lo, size)],
                target.at[i, pl.ds(b * part, part)],
                sems.at[which, i, b],
            )
            for b in range(nblk)
        ]

    turns = (2, 3, 1, 0)
    order = [(i, 0) for i in turns] + [(i, w) for i in turns for w in (1, 2)]
    for i, which in order:
        for b, copy in enumerate(load(i, which)):
            if i or b < early:
                copy.start()
    mixed[head] = mixed_parts[head]
    late_copy.wait()
    for which in range(3):
        for copy in load(0, which)[early:]:
            copy.start()
    for i in range(heads_of):
        for copy in load(i, 0):
            copy.wait()
    for i, to in enumerate(others):
        mixed_copy(i, to, to).wait_recv()
    branch = None
    for i in range(heads_of):
        term = dotf(mixed[chunks[i]], w_out[i], NT)
        branch = term if branch is None else branch + term
    resid = tok[...].astype(F32) + branch
    xhat, scale = statistics(resid)
    normed = (xhat * gain[...]).astype(BF16)
    cotangent = cot[...]
    total[...] = resid
    grad_normed[...] = jnp.zeros_like(resid)

    def chunk_of(i):
        far = jnp.where(i < 2, 1 - x, x)
        return 2 * far + jnp.where(lax.rem(i, 2) == 0, 1 - core_index, core_index)

    def to_core(n, k):
        mine, theirs = ((up_grad, up_got), (down_grad, down_got), (out_grad, out_got))[k]
        return remote(mine.at[2 * n], theirs.at[n], send_c.at[k, n], recv_c.at[k, n], core, blk)

    normed_rows[...] = normed
    normed_t[...] = normed.T
    cot_t[...] = cotangent.T
    def arrived(which, i):
        target = (w_out, up, down)[which].at[i, pl.ds(0, part)]
        for b in range(nblk):
            pltpu.make_async_copy(target, target, sems.at[which, i, b]).wait()

    def forward(n, carry):
        i = jnp.where(n < 2, n + 2, 3 - n)
        arrived(1, i)
        arrived(2, i)
        hidden, slope = gelu_both(dotf(normed_rows[...], up[i]))
        hidden_all[i] = hidden.astype(BF16)
        pre_all[i] = (slope * dotf(cot[...], down[i])).astype(BF16)
        total[...] += dotf(hidden_all[i], down[i], NT)
        grad_normed[...] += dotf(pre_all[i], up[i], NT)

        @pl.loop(0, pieces // heads_of)
        def _(p):
            relay(n * (pieces // heads_of) + p)

        return carry

    lax.fori_loop(0, heads_of, forward, 0)
    grad = cotangent.astype(F32) + norm_back(grad_normed[...], xhat, scale, gain[...])
    branch_grad = grad.astype(BF16)
    lane = lax.broadcasted_iota(jnp.int32, (tok.shape[0], WIDTH), 1)

    def wide_copy(i, to, slot):
        return remote(
            wide_parts.at[to], grad_wide.at[slot], send_g.at[i], recv_g.at[i], to, blk
        )

    branch_rows[...] = branch_grad

    def widen(i, carry):
        h = chunk_of(i)
        rows = dotf(branch_rows[...], w_out[i]).astype(BF16).astype(F32)
        product = rows * mixed[h].astype(F32)
        wide = jnp.concatenate([rows, jnp.zeros((rows.shape[0], WIDTH - cols), F32)], axis=1)
        for k in range(heads):
            delta = jnp.sum(
                product[:, k * HEAD_DIM : (k + 1) * HEAD_DIM], axis=1, keepdims=True
            )
            for c, piece in enumerate(split_parts(-delta)):
                wide = jnp.where(lane == cols + SPLITS * k + c, piece, wide)
        wide_parts[h] = wide.astype(BF16)

        @pl.when(i < 3)
        def _():
            wide_copy(i, h, head).start()

        return carry

    lax.fori_loop(0, heads_of, widen, 0)
    grad_wide[head] = wide_parts[head]
    out[...] = total[...].astype(BF16)
    gain_part[...] = jnp.sum(grad_normed[...] * xhat, axis=0, keepdims=True)
    grad_resid[...] = grad
    branch_t[...] = branch_grad.T

    def weigh(i, carry):
        up_grad[i] = dotf(normed_t[...], pre_all[i]).astype(BF16)
        down_grad[i] = dotf(cot_t[...], hidden_all[i]).astype(BF16)
        out_grad[i] = dotf(branch_t[...], mixed[chunk_of(i)]).astype(BF16)

        @pl.when(lax.rem(i, 2) == 0)
        def _():
            for k in range(3):
                to_core(lax.div(i, 2), k).start()

        return carry

    lax.fori_loop(0, heads_of, weigh, 0)

    def store(k, source, target, lo):
        size = source.shape[1]
        return [
            pltpu.make_async_copy(
                source.at[pl.ds(b * part, part)],
                target(b).at[:, pl.ds(lo, size)],
                out_sems.at[k, b],
            )
            for b in range(nblk)
        ]

    stores = []
    for n, target in enumerate((give_a, keep_a)):
        at = 2 * n + 1
        for k, (mine, theirs) in enumerate(
            ((up_grad, up_got), (down_grad, down_got), (out_grad, out_got))
        ):
            to_core(n, k).wait_recv()
            mine[at] = (mine[at].astype(F32) + theirs[n].astype(F32)).astype(BF16)
        first_part = store(3 * n, up_grad.at[at], lambda b: target.at[b], 0)
        far_down = down_grad.at[at].at[:, pl.ds(cut, up_cols - cut)]
        first_part += store(6 + n, far_down, lambda b: target.at[b], up_cols)
        first_part += store(3 * n + 1, out_grad.at[at], lambda b: target.at[b], 2 * up_cols - cut)
        for copy in first_part:
            copy.start()
        kept = store(3 * n + 2, down_grad.at[at].at[:, pl.ds(0, cut)], lambda b: keep_b.at[n, b // 2], 0)
        given = store(3 * n + 2, down_grad.at[at].at[:, pl.ds(0, cut)], lambda b: give_b.at[n, b // 2], 0)
        for b in range(nblk):

            @pl.when(odd == b % 2)
            def _():
                kept[b].start()

            @pl.when(odd != b % 2)
            def _():
                given[b].start()

        stores += first_part + kept
    for copy in stores:
        copy.wait()
    for k in range(3):
        for n in range(2):
            to_core(n, k).wait_send()
    for i in range(3):
        wide_copy(i, chunks[i], sources[i]).wait_recv()
    for i, to in enumerate(others):
        mixed_copy(i, to, head).wait_send()
        wide_copy(i, chunks[i], head).wait_send()
    for p in range(pieces):

        @pl.when((blk + 2 < nblk) | (odd == 0))
        def _():
            near_copy(p, slab(query, p)).wait_recv()

        @pl.when(blk >= 2)
        def _():
            far_copy(p, below).wait_send()

        @pl.when((blk + 2 < nblk) | (odd == 1))
        def _():
            near_copy(p, slab(query, p)).wait_send()


def middle(nblk, tok, mixed_parts, cot, gain, gathered, late, query, up_cols, cut=512, pieces=8):
    heads_of, rows, cols = mixed_parts.shape
    width, part = tok.shape[1], gathered.shape[2]
    flops = 2 * rows * width * (6 * up_cols * heads_of + 3 * width)
    dma = pltpu.SemaphoreType.DMA
    vmem = lambda *shape: pltpu.VMEM(shape, BF16)
    return pl.pallas_call(
        functools.partial(middle_kernel, nblk, up_cols, cut, pieces),
        out_shape=[
            jax.ShapeDtypeStruct((rows, width), BF16),
            jax.ShapeDtypeStruct((rows, width), F32),
            jax.ShapeDtypeStruct((heads_of, rows, WIDTH), BF16),
            jax.ShapeDtypeStruct((1, width), F32),
            jax.ShapeDtypeStruct((nblk, part, 2 * up_cols - cut + cols), BF16),
            jax.ShapeDtypeStruct((nblk, part, 2 * up_cols - cut + cols), BF16),
            jax.ShapeDtypeStruct((2, nblk // 2, part, cut), BF16),
            jax.ShapeDtypeStruct((2, nblk // 2, part, cut), BF16),
            jax.ShapeDtypeStruct((2,) + query.shape, BF16),
        ],
        in_specs=[WHOLE] * 4 + [ANY] * 3,
        out_specs=[WHOLE] * 4 + [ANY] * 5,
        scratch_shapes=[
            vmem(heads_of, width, up_cols), vmem(heads_of, width, up_cols),
            vmem(heads_of, width, cols),
            vmem(heads_of, width, up_cols), vmem(heads_of, width, up_cols),
            vmem(heads_of, width, cols),
            vmem(heads_of, rows, cols), vmem(heads_of, rows, WIDTH),
            vmem(2, width, up_cols), vmem(2, width, up_cols), vmem(2, width, cols),
            dma((3, heads_of, nblk)), dma((8, nblk)),
            dma((3,)), dma((3,)), dma((3,)), dma((3,)), dma((3, 2)), dma((3, 2)),
            dma((pieces,)), dma((pieces,)), dma((pieces,)), dma((pieces,)),
            vmem(heads_of, rows, up_cols), vmem(heads_of, rows, up_cols),
            vmem(width, rows), vmem(width, rows),
            pltpu.VMEM((rows, width), F32), pltpu.VMEM((rows, width), F32),
            vmem(rows, width), vmem(rows, width), vmem(width, rows),
            vmem(*late.shape), dma, dma,
        ],
        compiler_params=pltpu.CompilerParams(
            collective_id=2, has_side_effects=True, vmem_limit_bytes=62 << 20
        ),
        cost_estimate=pl.CostEstimate(
            flops=flops, bytes_accessed=24 << 20, transcendentals=rows * up_cols * heads_of
        ),
        name="middle",
    )(tok, mixed_parts, cot, gain, gathered, late, query)


def pair_sum_kernel(ours_a, got_a, ours_b, got_b, keep_a, give_a, keep_b, give_b):
    odd = lax.rem(lax.axis_index("blk"), 2)
    sums = [(ours_a[n].astype(F32) + got_a[n].astype(F32)).astype(BF16) for n in range(2)]
    keep_a[0] = jnp.where(odd == 0, sums[0], sums[1])
    give_a[0] = jnp.where(odd == 0, sums[1], sums[0])
    give_b[0] = (ours_b[0, 0].astype(F32) + got_b[0, 0].astype(F32)).astype(BF16)
    keep_b[0] = (ours_b[1, 0].astype(F32) + got_b[1, 0].astype(F32)).astype(BF16)


def pair_sum(ours_a, got_a, ours_b, got_b):
    nblk, part, width = ours_a.shape
    other = ours_b.shape[3]
    a_in = pl.BlockSpec((2, part, width), lambda i: (i, 0, 0))
    b_in = pl.BlockSpec((2, 1, part, other), lambda i: (0, i, 0, 0))
    out = lambda cols: pl.BlockSpec((1, part, cols), lambda i: (i, 0, 0))
    shape = lambda cols: jax.ShapeDtypeStruct((nblk // 2, part, cols), BF16)
    return pl.pallas_call(
        pair_sum_kernel,
        grid=(nblk // 2,),
        in_specs=[a_in, a_in, b_in, b_in],
        out_specs=[out(width)] * 2 + [out(other)] * 2,
        out_shape=[shape(width)] * 2 + [shape(other)] * 2,
        cost_estimate=pl.CostEstimate(
            flops=nblk * part * width, bytes_accessed=12 * nblk * part * width, transcendentals=0
        ),
        name="pair_sum",
    )(ours_a, got_a, ours_b, got_b)


def head_rows(h, heads, shape):
    row = lax.broadcasted_iota(jnp.int32, shape, 0)
    real = heads * HEAD_DIM
    own = (row >= h * HEAD_DIM) & (row < (h + 1) * HEAD_DIM)
    return own | ((row >= real + SPLITS * h) & (row < real + SPLITS * (h + 1)))


def per_head(wide, heads, out):
    flipped = wide.T
    for h in range(heads):
        out[h] = jnp.where(head_rows(h, heads, flipped.shape), flipped, jnp.zeros_like(flipped))


def doc_start(meta, ndocs, t):
    def step(j,c):
        cum,best=c
        best=jnp.where(cum<=t,cum,best)
        return cum+meta[1+j],best
    return lax.fori_loop(0,ndocs,step,(jnp.int32(0),jnp.int32(0)),unroll=True)[1]

def doc_end(meta, ndocs, t):
    def step(j,c):
        cum,best,found=c
        cum=cum+meta[1+j]
        take=(cum>t)&(found==0)
        return cum,jnp.where(take,cum,best),jnp.where(take,1,found)
    return lax.fori_loop(0,ndocs,step,(jnp.int32(0),jnp.int32(0),jnp.int32(0)),unroll=True)[1]

def starts_vec(meta, ndocs, t):
    def step(j,c):
        cum,best=c
        return cum+meta[1+j],jnp.where(cum<=t,cum,best)
    return lax.fori_loop(0,ndocs,step,(jnp.int32(0),jnp.zeros(t.shape,jnp.int32)))[1]

def ends_vec(meta, ndocs, t):
    def step(j,c):
        cum,best=c
        ln=meta[1+j]
        return cum+ln,jnp.where(cum<=t,cum+ln,best)
    return lax.fori_loop(0,ndocs,step,(jnp.int32(0),jnp.zeros(t.shape,jnp.int32)))[1]

def widened(columns, heads):
    rows, width = columns.shape
    ones = jnp.ones((rows, SPLITS * heads), BF16)
    empty = jnp.zeros((rows, WIDTH - width - SPLITS * heads), BF16)
    return jnp.concatenate([columns, ones, empty], axis=1)


def unpack_rows(packed, heads):
    pair = 2 * HEAD_DIM
    key = jnp.concatenate([packed[:, :pair], packed[:, 2 * pair : 2 * pair + HEAD_DIM]], axis=1)
    value = jnp.concatenate([packed[:, pair : 2 * pair], packed[:, 2 * pair + HEAD_DIM :]], axis=1)
    return widened(key, heads), widened(value, heads)


STEP = 512


def build_window(heads, start, earlier, own, packed, sems, keys, values, key_rows, value_rows):
    before = earlier.shape[0] // STEP
    chunks = before + own.shape[0] // STEP

    def copy(n, source, row):
        return pltpu.make_async_copy(
            source.at[pl.ds(row * STEP, STEP)], packed.at[pl.ds(n * STEP, STEP)], sems.at[n]
        )

    def begin(n, carry):
        @pl.when(n < before)
        def _():
            copy(n, earlier, n).start()

        @pl.when(n >= before)
        def _():
            copy(n, own, n - before).start()

        return carry

    def build(n, carry):
        copy(n, own, 0).wait()
        at = pl.ds(pl.multiple_of(n * STEP, STEP), STEP)
        key, value = unpack_rows(packed[at, :], heads)
        for wide, rows, flipped in ((key, keys, key_rows), (value, values, value_rows)):
            if rows is not None:
                rows[at, :] = wide
            if flipped is not None:
                turned = wide.T
                for h in range(heads):
                    flipped[h, :HEAD_DIM, at] = turned[h * HEAD_DIM : (h + 1) * HEAD_DIM]
        return carry

    lax.fori_loop(start, chunks, begin, 0)
    lax.fori_loop(start, chunks, build, 0)


def three(lo, a, b, hi, body):
    edge = a - lo

    def masked(n, carry):
        body(jnp.where(n < edge, lo + n, b + n - edge), True)
        return carry

    def free(n, carry):
        body(n, False)
        return carry

    lax.fori_loop(0, edge + hi - b, masked, 0)
    lax.fori_loop(a, b, free, 0)


def query_tiles(meta, ndocs, t0, wbase, tq, tk):
    lo = (doc_start(meta, ndocs, t0) - wbase) // tk
    f0 = (doc_start(meta, ndocs, t0 + tq - 1) - wbase + tk - 1) // tk
    f1 = (t0 - wbase) // tk
    hi = (t0 + tq - 1 - wbase) // tk + 1
    return lo, jnp.minimum(f0, f1), f1, hi


def fwd_kernel(heads, ndocs, tq, tk, meta, q_ref, earlier, own, mix_ref, wide_ref,
               k_ref, vt_ref, qt, m_ref, acc_ref, packed, sems):
    i = pl.program_id(0)
    width = q_ref.shape[1]
    real = heads * HEAD_DIM
    base = meta[0]
    wbase = base - earlier.shape[0]

    @pl.when(i == 0)
    def _():
        vt_ref[:, HEAD_DIM:, :] = jnp.ones_like(vt_ref[:, HEAD_DIM:, :])
        start = (doc_start(meta, ndocs, base) - wbase) // tk * (tk // STEP)
        build_window(heads, start, earlier, own, packed, sems, k_ref, None, None, vt_ref)

    t0 = base + i * tq
    lo, f0, f1, hi = query_tiles(meta, ndocs, t0, wbase, tq, tk)
    q = q_ref[...]
    trow = t0 + lax.broadcasted_iota(jnp.int32, (8, tq), 1)
    srow = starts_vec(meta, ndocs, trow)[:1]
    trow = trow[:1]
    lane = lax.broadcasted_iota(jnp.int32, (tq, width), 1)

    def visible(off):
        u = wbase + off + lax.broadcasted_iota(jnp.int32, (tk, tq), 0)
        return (u >= srow) & (u <= trow)

    itself = q.astype(F32) * k_ref[pl.ds(pl.multiple_of(t0 - wbase, tq), tq), :].astype(F32)
    shifted = q.astype(F32)
    for h in range(heads):
        mine = (lane >= h * HEAD_DIM) & (lane < (h + 1) * HEAD_DIM)
        score = jnp.sum(jnp.where(mine, itself, 0.0), axis=1, keepdims=True)
        for c, piece in enumerate(split_parts(-score)):
            shifted = jnp.where(lane == real + SPLITS * h + c, piece, shifted)
    per_head(shifted.astype(BF16), heads, qt)
    acc_ref[...] = jnp.zeros_like(acc_ref)

    def quick(j, masked):
        off = pl.multiple_of(j * tk, tk)
        k = k_ref[pl.ds(off, tk), :]
        if masked:
            vis = visible(off)
        scores = [dotf(k, qt[h]) for h in range(heads)]
        for h in range(heads):
            p = jnp.exp(scores[h])
            if masked:
                p = jnp.where(vis, p, 0.0)
            acc_ref[h] += dotf(vt_ref[h, :, pl.ds(off, tk)], p.astype(BF16))

    def finish(extra):
        rows = []
        parts = []
        for h in range(heads):
            acc = acc_ref[h]
            total = acc[HEAD_DIM : HEAD_DIM + 1]
            rows.append(acc[:HEAD_DIM] / total)
            at = real + SPLITS * h
            shift = jnp.sum(qt[h, at : at + SPLITS, :].astype(F32), axis=0, keepdims=True)
            parts += split_parts(shift - extra[h] - jnp.log(total))
        rest = jnp.zeros((width - real - len(parts), tq), F32)
        turned = jnp.concatenate(rows + parts + [rest], axis=0).T
        mix_ref[0] = turned[:, :real].astype(BF16)
        wide_ref[...] = jnp.where(lane < real, q.astype(F32), turned).astype(BF16)

    three(lo, f0, f1, hi, quick)
    none = jnp.zeros((1, tq), F32)
    finish([none] * heads)
    sums = acc_ref[:, HEAD_DIM : HEAD_DIM + 1, :]
    fits = jnp.max(jnp.where(sums < 1e30, 0.0, 1.0)) == 0.0

    @pl.when(jnp.logical_not(fits))
    def _():
        acc_ref[...] = jnp.zeros_like(acc_ref)
        m_ref[...] = jnp.full_like(m_ref, EXCLUDED)

        def body(j, carry):
            off = pl.multiple_of(j * tk, tk)
            k = k_ref[pl.ds(off, tk), :]
            vis = visible(off)
            for h in range(heads):
                s = jnp.where(vis, dotf(k, qt[h]), EXCLUDED)
                old = m_ref[h, :1]
                new = jnp.maximum(old, jnp.max(s, axis=0, keepdims=True))
                m_ref[h, :1] = new
                p = jnp.exp(s - new).astype(BF16)
                acc_ref[h] = acc_ref[h] * jnp.exp(old - new) + dotf(
                    vt_ref[h, :, pl.ds(off, tk)], p
                )
            return carry

        lax.fori_loop(lo, hi, body, 0)
        finish([m_ref[h, :1] for h in range(heads)])


SCALARS = pl.BlockSpec(memory_space=pltpu.SMEM)


def attention_fwd(meta, q, earlier, own, heads, tq, tk):
    block, width = q.shape
    window = block + earlier.shape[0]
    ndocs = meta.shape[0] - 1
    return pl.pallas_call(
        functools.partial(fwd_kernel, heads, ndocs, tq, tk),
        grid=(block // tq,),
        in_specs=[
            SCALARS,
            pl.BlockSpec((tq, width), lambda i: (i, 0)),
            ANY,
            ANY,
        ],
        out_specs=[
            pl.BlockSpec((1, tq, heads * HEAD_DIM), lambda i: (i, 0, 0)),
            pl.BlockSpec((tq, width), lambda i: (i, 0)),
        ],
        out_shape=[
            jax.ShapeDtypeStruct((block // tq, tq, heads * HEAD_DIM), BF16),
            jax.ShapeDtypeStruct((block, width), BF16),
        ],
        scratch_shapes=[
            pltpu.VMEM((window, width), BF16),
            pltpu.VMEM((heads, HEAD_DIM + 16, window), BF16),
            pltpu.VMEM((heads, width, tq), BF16),
            pltpu.VMEM((heads, 8, tq), F32),
            pltpu.VMEM((heads, HEAD_DIM + 16, tq), F32),
            pltpu.VMEM((window, own.shape[1]), BF16),
            pltpu.SemaphoreType.DMA((window // STEP,)),
        ],
        compiler_params=pltpu.CompilerParams(vmem_limit_bytes=56 << 20),
        cost_estimate=pl.CostEstimate(
            flops=30_000_000_000, bytes_accessed=12 << 20, transcendentals=20_000_000
        ),
        name="attn_fwd",
    )(meta, q, earlier, own)


def dq_kernel(heads, ndocs, tq, tk, meta, q_ref, do_ref, earlier, own, dq_ref,
              k_ref, v_ref, kt_ref, qt, dot, acc_ref, packed, sems):
    i = pl.program_id(0)
    base = meta[0]
    wbase = base - earlier.shape[0]

    @pl.when(i == 0)
    def _():
        start = (doc_start(meta, ndocs, base) - wbase) // tk * (tk // STEP)
        build_window(heads, start, earlier, own, packed, sems, k_ref, v_ref, kt_ref, None)

    t0 = base + i * tq
    per_head(q_ref[...], heads, qt)
    per_head(do_ref[...], heads, dot)
    acc_ref[...] = jnp.zeros_like(acc_ref)
    trow = t0 + lax.broadcasted_iota(jnp.int32, (8, tq), 1)
    srow = starts_vec(meta, ndocs, trow)[:1]
    trow = trow[:1]

    def body(j, masked):
        off = pl.multiple_of(j * tk, tk)
        k = k_ref[pl.ds(off, tk), :]
        v = v_ref[pl.ds(off, tk), :]
        if masked:
            u = wbase + off + lax.broadcasted_iota(jnp.int32, (tk, tq), 0)
            vis = (u >= srow) & (u <= trow)
        made = [(dotf(k, qt[h]), dotf(v, dot[h])) for h in range(heads)]
        for h in range(heads):
            p = jnp.exp(made[h][0])
            if masked:
                p = jnp.where(vis, p, 0.0)
            ds = (p * made[h][1]).astype(BF16)
            acc_ref[h] += dotf(kt_ref[h, :, pl.ds(off, tk)], ds)

    three(*query_tiles(meta, ndocs, t0, wbase, tq, tk), body)
    turned = acc_ref[...].reshape(heads * HEAD_DIM, tq).T
    dq_ref[...] = (turned * (HEAD_DIM**-0.5)).astype(BF16)


def attention_dq(meta, q, do, earlier, own, heads, tq, tk):
    block, width = q.shape
    window = block + earlier.shape[0]
    ndocs = meta.shape[0] - 1
    row = lambda w: pl.BlockSpec((tq, w), lambda i: (i, 0))
    return pl.pallas_call(
        functools.partial(dq_kernel, heads, ndocs, tq, tk),
        grid=(block // tq,),
        in_specs=[SCALARS, row(width), row(width), ANY, ANY],
        out_specs=row(heads * HEAD_DIM),
        out_shape=jax.ShapeDtypeStruct((block, heads * HEAD_DIM), BF16),
        scratch_shapes=[pltpu.VMEM((window, width), BF16)] * 2
        + [pltpu.VMEM((heads, HEAD_DIM, window), BF16)]
        + [pltpu.VMEM((heads, width, tq), BF16)] * 2
        + [pltpu.VMEM((heads, HEAD_DIM, tq), F32)]
        + [pltpu.VMEM((window, own.shape[1]), BF16), pltpu.SemaphoreType.DMA((window // STEP,))],
        compiler_params=pltpu.CompilerParams(vmem_limit_bytes=56 << 20),
        cost_estimate=pl.CostEstimate(
            flops=45_000_000_000, bytes_accessed=12 << 20, transcendentals=20_000_000
        ),
        name="attn_dq",
    )(meta, q, do, earlier, own)


def dkv_kernel(heads, ndocs, tq, tk, meta, own, q_parts, do_parts, dk_ref, dv_ref,
               q_ref, do_ref, qt_ref, dot_ref, kt, vt, dk_acc, dv_acc, sems):
    i = pl.program_id(0)
    base = meta[0]

    @pl.when(i == 0)
    def _():
        block = pl.num_programs(0) * tk
        end = (doc_end(meta, ndocs, base + block - 1) - base + STEP - 1) // STEP
        sources = []
        for parts in (q_parts, do_parts):
            row, found = 0, []
            for part in parts:
                found.append((row // STEP, (row + part.shape[0]) // STEP, part))
                row += part.shape[0]
            sources.append(found)

        def copy(k, n, source, row):
            return pltpu.make_async_copy(
                source.at[pl.ds(row * STEP, STEP)],
                (q_ref, do_ref)[k].at[pl.ds(n * STEP, STEP)],
                sems.at[k, n],
            )

        def begin(n, carry):
            for k in range(2):
                for first, last, part in sources[k]:

                    @pl.when((n >= first) & (n < last))
                    def _():
                        copy(k, n, part, n - first).start()

            return carry

        def turn(n, carry):
            at = pl.ds(pl.multiple_of(n * STEP, STEP), STEP)
            for k, (rows, flipped) in enumerate(((q_ref, qt_ref), (do_ref, dot_ref))):
                copy(k, n, sources[k][0][2], 0).wait()
                turned = rows[at, :].T
                for h in range(heads):
                    flipped[h, :, at] = turned[h * HEAD_DIM : (h + 1) * HEAD_DIM]
            return carry

        lax.fori_loop(0, end, begin, 0)
        lax.fori_loop(0, end, turn, 0)

    u0 = base + i * tk
    lo = (u0 - base) // tq
    f0 = (u0 + tk - 1 - base + tq - 1) // tq
    e_first = doc_end(meta, ndocs, u0)
    e_last = doc_end(meta, ndocs, u0 + tk - 1)
    f1 = (e_first - base) // tq
    hi = (e_last - 1 - base) // tq + 1
    f0 = jnp.minimum(f0, hi)
    f1 = jnp.clip(f1, f0, hi)
    k, v = unpack_rows(own[...], heads)
    per_head(k, heads, kt)
    per_head(v, heads, vt)
    dk_acc[...] = jnp.zeros_like(dk_acc)
    dv_acc[...] = jnp.zeros_like(dv_acc)
    urow = u0 + lax.broadcasted_iota(jnp.int32, (8, tk), 1)
    erow = ends_vec(meta, ndocs, urow)[:1]
    urow = urow[:1]

    def body(j, masked):
        off = pl.multiple_of(j * tq, tq)
        at = pl.ds(off, tq)
        q = q_ref[at, :]
        do = do_ref[at, :]
        if masked:
            t = base + off + lax.broadcasted_iota(jnp.int32, (tq, tk), 0)
            vis = (t >= urow) & (t < erow)
        for h in range(heads):
            p = jnp.exp(dotf(q, kt[h]))
            if masked:
                p = jnp.where(vis, p, 0.0)
            ds = (p * dotf(do, vt[h])).astype(BF16)
            dv_acc[h] += dotf(dot_ref[h, :, at], p.astype(BF16))
            dk_acc[h] += dotf(qt_ref[h, :, at], ds)

    three(lo, f0, f1, hi, body)
    for acc, out in ((dk_acc, dk_ref), (dv_acc, dv_ref)):
        out[...] = acc[...].reshape(heads * HEAD_DIM, tk).T.astype(BF16)


def attention_dkv(meta, own, q_parts, do_parts, heads, tq, tk):
    block, width = q_parts[0].shape
    window = sum(part.shape[0] for part in q_parts)
    ndocs = meta.shape[0] - 1
    row = lambda w: pl.BlockSpec((tk, w), lambda i: (i, 0))
    return pl.pallas_call(
        functools.partial(dkv_kernel, heads, ndocs, tq, tk),
        grid=(block // tk,),
        in_specs=[SCALARS, row(own.shape[1]), [ANY] * len(q_parts), [ANY] * len(do_parts)],
        out_specs=[row(heads * HEAD_DIM)] * 2,
        out_shape=[jax.ShapeDtypeStruct((block, heads * HEAD_DIM), BF16)] * 2,
        scratch_shapes=[pltpu.VMEM((window, width), BF16)] * 2
        + [pltpu.VMEM((heads, HEAD_DIM, window), BF16)] * 2
        + [pltpu.VMEM((heads, width, tk), BF16)] * 2
        + [pltpu.VMEM((heads, HEAD_DIM, tk), F32)] * 2
        + [pltpu.SemaphoreType.DMA((2, window // STEP))],
        compiler_params=pltpu.CompilerParams(vmem_limit_bytes=56 << 20),
        cost_estimate=pl.CostEstimate(
            flops=60_000_000_000, bytes_accessed=12 << 20, transcendentals=20_000_000
        ),
        name="attn_dkv",
    )(meta, own, q_parts, do_parts)


def on_device(
    tokens, first_values, cotangent, w_query, w_key, w_value, w_out, w_up, w_down,
    gain_attn, gain_mlp, doc_lengths,
):
    width = tokens.shape[1]
    heads_of = lax.axis_size("head")
    nblk = lax.axis_size("blk")
    blk = lax.axis_index("blk")
    rows = tokens.shape[0]
    block = rows * heads_of
    heads = HEADS // heads_of
    cols = heads * HEAD_DIM
    part = width // nblk
    meta = jnp.concatenate([jnp.reshape(blk * block, (1,)).astype(jnp.int32), doc_lengths])

    up_cols = w_up.shape[1]
    early = nblk - 3 * nblk // 8
    normed, query, own, earlier, gathered, qk_all, v_all, attn_gain, mlp_gain = front(
        nblk, early, tokens, first_values, w_query, w_key, w_value, w_up, w_down.T, w_out,
        gain_attn.reshape(1, part), gain_mlp.reshape(1, part),
    )
    w_qk = qk_all.reshape(width, 2 * cols)
    w_v = v_all.reshape(2, width, w_value.shape[1])
    earlier = earlier.reshape(2 * block, 2 * cols)
    beside = [(h, (h + 2) % heads_of) for h in range(heads_of)]
    mine = lax.dynamic_index_in_dim(gathered, lax.axis_index("head"), 0, keepdims=False)[early:]
    late = lax.ppermute(mine, "head", beside)
    mixed_parts, query_wide = attention_fwd(
        meta, query, earlier, own, heads, rows, rows
    )
    late, mixed_parts = lax.optimization_barrier((late, mixed_parts))
    layer_output, grad_resid, grad_parts, gain_mlp_part, keep_a, give_a, keep_b, give_b, query_later = middle(
        nblk, tokens, mixed_parts, cotangent, mlp_gain, gathered, late, query_wide, up_cols
    )
    grad_wide = grad_parts.reshape(block, WIDTH)
    across = [(i, i + 1 - 2 * (i % 2)) for i in range(nblk)]
    got_a = lax.ppermute(give_a, "head", beside)
    got_b = lax.ppermute(give_b, "blk", across)

    grads_later = [grad_wide] + [
        lax.ppermute(grad_wide, "blk", [(i, i - d) for i in range(d, nblk)]) for d in (1, 2)
    ]
    queries_later = [query_wide, query_later.reshape(2 * block, WIDTH)]
    grad_query = attention_dq(
        meta, query_wide, grad_wide, earlier, own, heads, rows, rows
    )
    got_a, got_b, grad_query = lax.optimization_barrier((got_a, got_b, grad_query))
    keep_a, give_a, keep_b, give_b = pair_sum(keep_a, got_a, keep_b, got_b)
    got_a = lax.ppermute(give_a, "blk", across)
    got_b = lax.ppermute(give_b, "head", beside)
    keep_a, own = lax.optimization_barrier((keep_a, own))
    grad_key, grad_value = attention_dkv(
        meta, own, queries_later, grads_later, heads, rows, rows
    )
    outs = tail(
        nblk, grad_query, grad_key, grad_value, normed, w_qk, w_v, gain_mlp_part,
        keep_a, got_a, keep_b, got_b, tokens, grad_resid, attn_gain,
    )
    (
        layer_output, grad_tokens, final_query, final_key, final_value, grad_first, gain_sums,
        final_up, final_down, final_out,
    ) = settle([layer_output] + list(outs))
    return (
        layer_output,
        grad_tokens,
        grad_first,
        final_query,
        final_key,
        final_value,
        final_out,
        final_up,
        final_down.T,
        gain_sums[0].reshape(part),
        gain_sums[1].reshape(part),
    )


def solution(mesh):
    rows = P(("blk", "head"), None)
    specs = (P("blk", "head"),) * 3 + (P("head", "blk"), P("blk", "head"), P("head", "blk"))
    gains = (P("blk"), P("blk"))
    return jax.shard_map(
        on_device,
        mesh=mesh,
        in_specs=(rows,) * 3 + specs + gains + (P(),),
        out_specs=(rows,) * 3 + specs + gains,
        check_vma=False,
    )
```

```python
import functools

import jax
import jax.numpy as jnp
from jax import lax
from jax.experimental import pallas as pl
from jax.experimental.pallas import tpu as pltpu
from jax.sharding import PartitionSpec as P

HEADS = 12
HEAD_DIM = 64
DOC_MAX = 4096
EPSILON = 1e-05
GELU_SCALE = 0.7978845608028654
EXCLUDED = -1e30
WIDTH = 256
SPLITS = 3
BF16 = jnp.bfloat16
F32 = jnp.float32
MESH = pl.DeviceIdType.MESH
ANY = pl.BlockSpec(memory_space=pl.ANY)
WHOLE = pl.BlockSpec(memory_space=pltpu.VMEM)
NT = (((1,), (1,)), ((), ()))
TN = (((0,), (0,)), ((), ()))


def dotf(left, right, dims=None):
    if dims is None:
        dims = (((1,), (0,)), ((), ()))
    return lax.dot_general(left, right, dims, preferred_element_type=F32)


def remote(src, dst, send_sem, recv_sem, head, blk):
    return pltpu.make_async_remote_copy(
        src_ref=src,
        dst_ref=dst,
        send_sem=send_sem,
        recv_sem=recv_sem,
        device_id={"head": head, "blk": blk},
        device_id_type=MESH,
    )


def greet(partners):
    barrier = pltpu.get_barrier_semaphore()
    for head, blk in partners:
        pl.semaphore_signal(
            barrier, inc=1, device_id={"head": head, "blk": blk}, device_id_type=MESH
        )
    pl.semaphore_wait(barrier, len(partners))


def xor(value, bit):
    return value + bit - 2 * bit * (lax.div(value, bit) % 2)


def partners_of(head, blk, nblk, heads=True, blks=True):
    found = []
    if heads:
        found += [(xor(head, 1), blk), (xor(head, 2), blk), (3 - head, blk)]
    if blks:
        found += [(head, lax.rem(blk + d, nblk)) for d in range(1, nblk)]
    return found


class Line:
    def __init__(self, nblk, head, blk, source, target, up, down, across):
        self.half, self.head, self.blk = nblk // 2, head, blk
        self.place, self.parity = lax.div(blk, 2), lax.rem(blk, 2)
        self.source, self.target = source, target
        self.sems = {"up": up, "down": down, "across": across}

    def copy(self, way, origin, step, fresh=False):
        slot = 2 * origin + self.parity
        to = {
            "up": lax.rem(self.blk + 2, 2 * self.half),
            "down": lax.rem(self.blk + 2 * self.half - 2, 2 * self.half),
            "across": self.blk + 1 - 2 * self.parity,
        }[way]
        send, recv = self.sems[way]
        return remote(
            self.source if fresh else self.target.at[slot],
            self.target.at[slot], send.at[step], recv.at[step], self.head, to,
        )

    def landing(self, way, slot, step):
        send, recv = self.sems[way]
        other = self.blk + 1 - 2 * self.parity
        at = self.target.at[slot]
        return remote(at, at, send.at[step], recv.at[step], self.head, other)

    def begin(self):
        @pl.when(self.place + 1 < self.half)
        def _():
            self.copy("up", self.place, 0, True).start()

        @pl.when(self.place > 0)
        def _():
            self.copy("down", self.place, 0, True).start()

        self.copy("across", self.place, self.place, True).start()

    def step(self, s, then=None):
        low, high = self.place - 1 - s, self.place + 1 + s

        @pl.when(low >= 0)
        def _():
            self.landing("up", 2 * low + self.parity, s).wait_recv()
            if s + 1 < self.half - 1:

                @pl.when(self.place + 1 < self.half)
                def _():
                    self.copy("up", low, s + 1).start()

            self.copy("across", low, low).start()
            if then:
                then(2 * low + self.parity)

        @pl.when(high < self.half)
        def _():
            self.landing("down", 2 * high + self.parity, s).wait_recv()
            if s + 1 < self.half - 1:

                @pl.when(self.place > 0)
                def _():
                    self.copy("down", high, s + 1).start()

            self.copy("across", high, high).start()
            if then:
                then(2 * high + self.parity)

    def land(self, origin):
        self.landing("across", 2 * origin + 1 - self.parity, origin).wait_recv()

    def finish(self):
        for o in range(self.half):
            self.copy("across", o, o).wait_send()
        for s in range(self.half - 1):

            @pl.when((self.place - s >= 0) & (self.place + 1 < self.half))
            def _():
                self.copy("up", self.place - s, s).wait_send()

            @pl.when((self.place + s < self.half) & (self.place > 0))
            def _():
                self.copy("down", self.place + s, s).wait_send()


def tail_kernel(
    nblk, pieces, cols, d_q, d_k, d_v, normed, w_qk, w_v, gain_m, kept_a, got_a, kept_b, got_b, tok, resid, gain,
    out_grad, out_q, out_k, out_v, out_first, out_gain_a, out_gain_m, out_up, out_down, out_out,
    grad, weights, gains, joined, weight, acc,
    tok_buf, resid_buf, normed_buf, load_sem, first_got, rest_sum,
    core_buf, side_out, side_buf, pair_buf, line_out, line_in, v_sum, v_got,
    gain_buf, gain_sum, gain_got, up_out, up_in, down_out, down_in,
    own_sem, send_s, recv_s, send_x, recv_x, send_y, recv_y, send_l, recv_l,
    send_v, recv_v, send_f, recv_f, send_g, recv_g, send_h, recv_h, send_u, recv_u, send_d, recv_d,
):
    head, blk = lax.axis_index("head"), lax.axis_index("blk")
    side, core, far = xor(head, 2), xor(head, 1), 3 - head
    size = grad.shape[1]
    turns = (far, side, core, head)
    loads = [
        pltpu.make_async_copy(
            normed.at[pl.ds(pl.multiple_of(t * size, size), size)], normed_buf.at[i], load_sem.at[i]
        )
        for i, t in enumerate(turns)
    ]
    loads += [
        pltpu.make_async_copy(tok, tok_buf, load_sem.at[4]),
        pltpu.make_async_copy(resid, resid_buf, load_sem.at[5]),
    ]
    for copy in loads:
        copy.start()
    greet(partners_of(head, blk, nblk))
    rows = grad.shape[1] // pieces
    line, place, parity = nblk // 2, lax.div(blk, 2), lax.rem(blk, 2)
    pair = blk + 1 - 2 * parity
    above, below = lax.rem(blk + 2, nblk), lax.rem(blk + nblk - 2, nblk)

    def part(ref, p):
        return ref.at[pl.ds(p * rows, rows)]

    def to_core(i, p, slot):
        return remote(
            part(grad.at[slot], p), part(core_buf.at[i], p), send_s.at[i, p], recv_s.at[i, p],
            core, blk,
        )

    def to_side(p):
        return remote(
            part(side_out, p), part(side_buf, p), send_x.at[p], recv_x.at[p], side, blk
        )

    def sum_of(t):
        first_part = kept_b[t].astype(F32) + got_b[t].astype(F32)
        return jnp.concatenate([first_part, kept_a[t].astype(F32) + got_a[t].astype(F32)], axis=1)

    def up_copy(t, to):
        return remote(up_out.at[t], up_in.at[t], send_u.at[t], recv_u.at[t], head, to)

    def down_copy(t, to):
        return remote(down_out.at[t], down_in.at[t], send_d.at[t], recv_d.at[t], head, to)

    def first_hops():
        for n in range(line - 1):
            t = line - 1 - n

            @pl.when((place == 0) & (place < t))
            def _():
                up_out[t] = sum_of(t).astype(BF16)
                up_copy(t, above).start()

            @pl.when((place == line - 1) & (place > n))
            def _():
                down_out[n] = sum_of(n).astype(BF16)
                down_copy(n, below).start()

    def next_hops(n):
        t = line - 1 - n

        @pl.when((place > 0) & (place < t))
        def _():
            up_copy(t, above).wait_recv()
            up_out[t] = (sum_of(t) + up_in[t].astype(F32)).astype(BF16)
            up_copy(t, above).start()

        @pl.when((place < line - 1) & (place > n))
        def _():
            down_copy(n, below).wait_recv()
            down_out[n] = (sum_of(n) + down_in[n].astype(F32)).astype(BF16)
            down_copy(n, below).start()

    first_hops()
    half, kind = lax.div(head, 2), lax.rem(head, 2)

    def first_copy(i, to, slot):
        source = d_v.at[pl.ds(to * grad.shape[1], grad.shape[1])]
        return remote(source, first_got.at[slot], send_f.at[i], recv_f.at[slot], to, blk)

    def own_first(slot):
        source = d_v.at[pl.ds(head * grad.shape[1], grad.shape[1])]
        return pltpu.make_async_copy(source, first_got.at[slot], own_sem)

    @pl.when(half == 1)
    def _():
        for i, to in enumerate((core, side, far)):
            first_copy(i, to, kind).start()
        own_first(kind).start()

    mine = half == 0
    weight[:, : 2 * cols] = w_qk[...]
    fresh = jnp.concatenate([w_v[0], w_v[1]], axis=1)
    weight[:, 2 * cols :] = jnp.where(mine, fresh, jnp.zeros_like(fresh))
    gain_row = None
    for i, t in enumerate(turns):
        at = pl.ds(pl.multiple_of(t * grad.shape[1], grad.shape[1]), grad.shape[1])
        joined[:, :cols] = d_q[at, :]
        joined[:, cols : 2 * cols] = d_k[at, :]
        joined[:, 2 * cols : 3 * cols] = d_v[at, :]
        joined[:, 3 * cols :] = jnp.zeros((grad.shape[1], joined.shape[1] - 3 * cols), BF16)
        given = joined[...]
        whole = dotf(given[:, : 3 * cols], weight[...], NT)
        grad[t] = whole.astype(BF16)
        if i == 0:
            for p in range(pieces):
                to_core(0, p, far).start()
        if i == 2:
            for p in range(pieces):
                to_core(1, p, core).start()
        loads[i].wait()
        rows_in = normed_buf[i]
        term = jnp.sum(whole * rows_in.astype(F32), axis=0, keepdims=True)
        gain_row = term if gain_row is None else gain_row + term
        term = dotf(rows_in, given, TN)
        acc[...] = term if i == 0 else acc[...] + term
        if i == 2:
            for p in range(pieces):
                to_core(0, p, far).wait_recv()
                part(side_out, p)[...] = (
                    part(grad.at[side], p)[...].astype(F32)
                    + part(core_buf.at[0], p)[...].astype(F32)
                ).astype(BF16)
                to_side(p).start()
    whole_part = weights.shape[1]
    for b in range(nblk):
        weights[b] = acc[b * whole_part : (b + 1) * whole_part].astype(BF16)

    def across(n):
        return remote(
            weights.at[2 * n + 1 - parity], pair_buf.at[n], send_y.at[n], recv_y.at[n], head, pair
        )

    for n in range(line):
        across(n).start()
    gain_row = gain_row / gain[...]
    for b in range(nblk):
        gains[b, 0] = gain_row[:, b * whole_part : (b + 1) * whole_part]
        gains[b, 1] = gain_m[:, b * whole_part : (b + 1) * whole_part]

    def gain_to(d):
        to = lax.rem(blk + d, nblk)
        return remote(gains.at[to], gain_buf.at[blk], send_g.at[d], recv_g.at[d], head, to)

    def gain_from(d):
        source = lax.rem(blk - d + nblk, nblk)
        return remote(gains.at[0], gain_buf.at[source], send_g.at[d], recv_g.at[d], head, source)

    for d in range(1, nblk):
        gain_to(d).start()
    gain_buf[blk] = gains[blk]

    def along(d, to):
        return remote(
            line_out.at[to], line_in.at[d], send_l.at[d], recv_l.at[d], head, 2 * to + parity
        )

    next_hops(0)
    for n in range(line):
        across(n).wait_recv()
        line_out[n] = (
            weights[2 * n + parity].astype(F32) + pair_buf[n].astype(F32)
        ).astype(BF16)
    for d in range(1, line):
        along(d, lax.rem(place + d, line)).start()
    for d in range(1, nblk):
        gain_from(d).wait_recv()
    gain_sum[...] = jnp.sum(gain_buf[...], axis=0)
    peers = (core, side, far)

    def gain_copy(i, to):
        return remote(gain_sum, gain_got.at[i], send_h.at[i], recv_h.at[i], to, blk)

    for i, to in enumerate(peers):
        gain_copy(i, to).start()
    for n in range(1, line - 1):
        next_hops(n)
    total = line_out[place].astype(F32)
    for d in range(1, line):
        along(d, lax.rem(place - d + line, line)).wait_recv()
        total = total + line_in[d].astype(F32)
    out_q[...] = total[:, :cols]
    out_k[...] = total[:, cols : 2 * cols]
    v_sum[0] = total[:, 2 * cols : 2 * cols + cols // 2]
    v_sum[1] = total[:, 2 * cols + cols // 2 : 3 * cols]

    def give(c, to):
        return remote(v_sum.at[c], v_got, send_v.at[c], recv_v.at[0], to, blk)

    for c in range(2):
        to = 2 * head + c

        @pl.when((half == 0) & (to != head))
        def _():
            give(c, to).start()

    for copy in loads[4:]:
        copy.wait()
    for p in range(pieces):
        to_core(1, p, core).wait_recv()
        to_side(p).wait_recv()
        norm_grad = (
            part(grad.at[head], p)[...].astype(F32)
            + part(core_buf.at[1], p)[...].astype(F32)
            + part(side_buf, p)[...].astype(F32)
        )
        xhat, scale = statistics(part(tok_buf, p)[...].astype(F32))
        part(out_grad, p)[...] = part(resid_buf, p)[...] + norm_back(norm_grad, xhat, scale, gain[...])
    rest_sum[...] = sum_of(place)
    for t in range(line):

        @pl.when((place == t) & (place > 0))
        def _():
            up_copy(t, above).wait_recv()
            rest_sum[...] += up_in[t].astype(F32)

        @pl.when((place == t) & (place < line - 1))
        def _():
            down_copy(t, below).wait_recv()
            rest_sum[...] += down_in[t].astype(F32)

    inner = out_up.shape[1]
    cut = kept_b.shape[2]
    out_up[...] = rest_sum[:, cut : cut + inner]
    out_down[:, :cut] = rest_sum[:, :cut]
    out_down[:, cut:] = rest_sum[:, cut + inner : 2 * inner]
    out_out[...] = rest_sum[:, 2 * inner :].T
    for i, to in enumerate(peers):
        gain_copy(i, to).wait_recv()
    gain_total = gain_sum[...] + gain_got[0] + gain_got[1] + gain_got[2]
    out_gain_a[...] = gain_total[0]
    out_gain_m[...] = gain_total[1]

    @pl.when(head == 0)
    def _():
        out_v[...] = v_sum[0]

    @pl.when(head != 0)
    def _():
        give(0, half).wait_recv()
        out_v[...] = v_got[...]

    for slot in range(2):

        @pl.when(head == 2 + slot)
        def _():
            own_first(slot).wait()

        @pl.when(head != 2 + slot)
        def _():
            first_copy(0, 2 + slot, slot).wait_recv()

    out_first[...] = jnp.concatenate([first_got[0], first_got[1]], axis=1).astype(F32)

    @pl.when(half == 1)
    def _():
        for i, to in enumerate((core, side, far)):
            first_copy(i, to, kind).wait_send()

    for c in range(2):
        to = 2 * head + c

        @pl.when((half == 0) & (to != head))
        def _():
            give(c, to).wait_send()

    for i, to in enumerate(peers):
        gain_copy(i, to).wait_send()
    for p in range(pieces):
        to_core(0, p, far).wait_send()
        to_core(1, p, core).wait_send()
        to_side(p).wait_send()
    for d in range(1, nblk):
        gain_to(d).wait_send()
    for n in range(line):
        across(n).wait_send()
    for d in range(1, line):
        along(d, lax.rem(place + d, line)).wait_send()
    for t in range(line):

        @pl.when(place < t)
        def _():
            up_copy(t, above).wait_send()

        @pl.when(place > t)
        def _():
            down_copy(t, below).wait_send()


def tail(
    nblk, d_q, d_k, d_v, normed, w_qk, w_v, gain_m, kept_a, got_a, kept_b, got_b, tok, resid, gain,
    pieces=4,
):
    dma = pltpu.SemaphoreType.DMA
    row, part, cols = tok.shape, w_v.shape[1] // nblk, d_q.shape[1]
    rest = (nblk // 2, part, kept_a.shape[2] + kept_b.shape[2])
    inner = (rest[2] - cols) // 2
    padded = -(-3 * cols // 128) * 128
    gains = jax.ShapeDtypeStruct((nblk, 2, 1, part), F32)
    half, line = (part, cols // 2), nblk // 2
    piece = (2, pieces)
    vmem = lambda *shape: pltpu.VMEM(shape, BF16)
    return pl.pallas_call(
        functools.partial(tail_kernel, nblk, pieces, cols),
        out_shape=[
            jax.ShapeDtypeStruct(row, F32),
            jax.ShapeDtypeStruct((part, cols), F32),
            jax.ShapeDtypeStruct((part, cols), F32),
            jax.ShapeDtypeStruct(half, F32),
            jax.ShapeDtypeStruct((row[0], 2 * cols), F32),
            jax.ShapeDtypeStruct((1, part), F32),
            jax.ShapeDtypeStruct((1, part), F32),
            jax.ShapeDtypeStruct((part, inner), F32),
            jax.ShapeDtypeStruct((part, inner), F32),
            jax.ShapeDtypeStruct((cols, part), F32),
        ],
        in_specs=[WHOLE] * 3 + [ANY] + [WHOLE] * 7 + [ANY] * 2 + [WHOLE],
        out_specs=[WHOLE] * 10,
        scratch_shapes=[
            vmem(4, *row), vmem(nblk, part, padded), pltpu.VMEM(gains.shape, F32),
            vmem(row[0], padded), vmem(row[1], 3 * cols), pltpu.VMEM((row[1], padded), F32),
            vmem(*row), pltpu.VMEM(row, F32), vmem(4, *row), dma((6,)),
            vmem(2, row[0], cols), pltpu.VMEM(rest[1:], F32),
            vmem(2, *row), vmem(*row), vmem(*row),
            vmem(line, part, padded), vmem(line, part, padded),
            vmem(line, part, padded),
            pltpu.VMEM((2,) + half, F32),
            pltpu.VMEM(half, F32),
            pltpu.VMEM(gains.shape, F32),
            pltpu.VMEM(gains.shape[1:], F32),
            pltpu.VMEM((3,) + gains.shape[1:], F32),
            vmem(*rest), vmem(*rest), vmem(*rest), vmem(*rest),
            dma,
            dma(piece), dma(piece),
            dma((pieces,)), dma((pieces,)),
            dma((line,)), dma((line,)), dma((line,)), dma((line,)),
            dma((2,)), dma((1,)),
            dma((3,)), dma((2,)),
            dma((nblk,)), dma((nblk,)),
            dma((3,)), dma((3,)),
            dma((line,)), dma((line,)), dma((line,)), dma((line,)),
        ],
        compiler_params=pltpu.CompilerParams(
            collective_id=4, has_side_effects=True, vmem_limit_bytes=60 << 20
        ),
        name="tail",
    )(d_q, d_k, d_v, normed, w_qk, w_v, gain_m, kept_a, got_a, kept_b, got_b, tok, resid, gain)


def settle_kernel(count, *refs):
    sources, targets, sems = refs[:count], refs[count : 2 * count], refs[2 * count]
    copies = [
        pltpu.make_async_copy(source, target, sems.at[i])
        for i, (source, target) in enumerate(zip(sources, targets))
    ]
    for copy in copies:
        copy.start()
    for copy in copies:
        copy.wait()


def settle(arrays):
    count = len(arrays)
    return pl.pallas_call(
        functools.partial(settle_kernel, count),
        out_shape=[jax.ShapeDtypeStruct(a.shape, a.dtype) for a in arrays],
        in_specs=[ANY] * count,
        out_specs=[WHOLE] * count,
        scratch_shapes=[pltpu.SemaphoreType.DMA((count,))],
        name="settle",
    )(*arrays)


def statistics(values):
    center = values - jnp.mean(values, axis=-1, keepdims=True)
    scale = lax.rsqrt(jnp.mean(jnp.square(center), axis=-1, keepdims=True) + EPSILON)
    return center * scale, scale


def norm_back(grad, xhat, scale, gain):
    eg = grad * gain
    return scale * (
        eg
        - jnp.mean(eg, axis=-1, keepdims=True)
        - xhat * jnp.mean(eg * xhat, axis=-1, keepdims=True)
    )


def split_parts(values):
    high = values.astype(BF16).astype(F32)
    middle = (values - high).astype(BF16).astype(F32)
    return high, middle, values - high - middle


def front_kernel(
    nblk, parts, pieces, early, tok, first, w_q, w_k, w_v, w_up, w_down, w_out, gain_a, gain_m,
    normed, query, own, near_far, rest, qk_all, v_all, attn_gain, mlp_gain,
    tok_all, first_all, v_own, gain_all, w_qk, w_rest, gains, weight, normed_buf,
    own_sem, normed_sem, send_t, recv_t, send_s, recv_s, send_p, recv_p, send_w, recv_w,
    send_v, recv_v, qk_u, qk_ur, qk_d, qk_dr, qk_a, qk_ar, up_u, up_ur, up_d, up_dr, up_a, up_ar,
    send_x, recv_x, send_c, recv_c, send_f, recv_f, send_z, recv_z, send_y, recv_y,
):
    head, blk = lax.axis_index("head"), lax.axis_index("blk")
    side, core, beyond = xor(head, 2), xor(head, 1), 3 - head
    odd, place = lax.rem(blk, 2), lax.div(blk, 2)
    near = blk + 1 - 2 * odd
    up, down = lax.rem(blk + 2, nblk), lax.rem(blk + nblk - 2, nblk)
    greet(partners_of(head, blk, nblk))
    moved = [(tok, tok_all), (first, first_all)]
    weights = [(w_v, v_own), (gains, gain_all)]
    rows = tok.shape[0] // parts

    def part(ref, n):
        return ref.at[pl.ds(n * rows, rows)]

    def hop(sems, k, n, source, slot, target):
        dst = part(moved[k][1].at[slot], n)
        return remote(source, dst, sems[0].at[k, n], sems[1].at[k, n], target, blk)

    ts, ss, ps = (send_t, recv_t), (send_s, recv_s), (send_p, recv_p)
    order = [(k, n) for n in range(parts) for k in range(2)]
    for k, n in order:
        hop(ts, k, n, part(moved[k][0], n), head, side).start()
    cols, inner = w_q.shape[1], w_up.shape[1]
    w_qk[:, :cols] = w_q[...]
    w_qk[:, cols:] = w_k[...]
    qk_line = Line(nblk, head, blk, w_qk, qk_all, (qk_u, qk_ur), (qk_d, qk_dr), (qk_a, qk_ar))
    qk_line.begin()
    w_rest[:, :inner] = w_up[...]
    w_rest[:, inner : 2 * inner] = w_down[...]
    w_rest[:, 2 * inner :] = w_out[...].T
    line = Line(
        nblk, head, blk, w_rest, rest.at[head], (up_u, up_ur), (up_d, up_dr), (up_a, up_ar)
    )
    line.begin()
    gains[0] = gain_a[...]
    gains[1] = gain_m[...]

    def chunk(sems, slot, b, to, source=None):
        at = rest.at[slot, b]
        return remote(at if source is None else source, at, sems[0].at[b], sems[1].at[b], to, blk)

    xs, cs, fs = (send_x, recv_x), (send_c, recv_c), (send_f, recv_f)

    def to_core(b, source=None):
        chunk(cs, head, b, core, source).start()

    def to_side(b, source=None):
        @pl.when(b < early)
        def _():
            chunk(xs, head, b, side, source).start()

    to_core(blk, w_rest)
    own_rest = pltpu.make_async_copy(w_rest, rest.at[head, blk], own_sem)
    own_rest.start()

    def spread(d):
        to = lax.rem(blk + d, nblk)
        return [
            remote(src, dst.at[blk], send_w.at[i, d], recv_w.at[i, d], head, to)
            for i, (src, dst) in enumerate(weights)
        ]

    def from_peer(d):
        source = lax.rem(blk - d + nblk, nblk)
        return [
            remote(src, dst.at[source], send_w.at[i, d], recv_w.at[i, d], head, source)
            for i, (src, dst) in enumerate(weights)
        ]

    for d in range(1, nblk):
        for copy in spread(d):
            copy.start()
    for k, n in order:
        hop(ss, k, n, part(moved[k][0], n), head, core).start()
    tok_all[head] = tok[...]
    first_all[head] = first[...]
    v_own[blk] = w_v[...]
    gain_all[blk] = gains[...]
    qk_all[blk] = w_qk[...]

    def pass_on(k, n):
        landed = part(moved[k][1].at[side], n)
        hop(ts, k, n, landed, side, side).wait_recv()
        hop(ps, k, n, landed, side, core).start()

    steps = nblk // 2 - 1
    for s in range(steps):
        qk_line.step(s)
    for s in range(steps):
        line.step(s, to_core)
        for k, n in order[s * len(order) // steps : (s + 1) * len(order) // steps]:
            pass_on(k, n)
    to_side(blk, w_rest)
    for s in range(steps):

        @pl.when(place - 1 - s >= 0)
        def _():
            to_side(blk - 2 - 2 * s)

        @pl.when(place + 1 + s < nblk // 2)
        def _():
            to_side(blk + 2 + 2 * s)

    for d in range(1, nblk):
        for copy in from_peer(d):
            copy.wait_recv()
    half, kind = lax.div(head, 2), lax.rem(head, 2)
    for i in range(2):
        target = half + 2 * i

        @pl.when(target == head)
        def _():
            v_all[kind] = v_own[...]

        @pl.when(target != head)
        def _():
            remote(v_own, v_all.at[kind], send_v.at[i], recv_v.at[kind], target, blk).start()

    for o in range(nblk // 2):
        qk_line.land(o)
    for c in range(2):
        source = 2 * kind + c

        @pl.when(source != head)
        def _():
            remote(v_own, v_all.at[c], send_v.at[0], recv_v.at[c], source, blk).wait_recv()

    attn_gain[...] = jnp.concatenate([gain_all[b, 0] for b in range(nblk)], axis=1)
    mlp_gain[...] = jnp.concatenate([gain_all[b, 1] for b in range(nblk)], axis=1)

    step = own.shape[0] // pieces

    def slab(ref, n):
        return ref.at[pl.ds(n * step, step)]

    def far_copy(n, to):
        return remote(slab(own, n), slab(near_far.at[0], n), send_z.at[n], recv_z.at[n], head, to)

    def near_copy(n, src):
        return remote(src, slab(near_far.at[1], n), send_y.at[n], recv_y.at[n], head, near)

    size = HEAD_DIM
    pair = 2 * size
    width = tok.shape[1]
    block = w_q.shape[0]
    for b in range(nblk):
        at = pl.ds(b * block, block)
        both, fresh = qk_all[b], jnp.concatenate([v_all[0, b], v_all[1, b]], axis=1)
        key = both[:, cols:]
        weight[at, :pair] = key[:, :pair]
        weight[at, pair : 2 * pair] = fresh[:, :pair]
        weight[at, 2 * pair : 3 * pair] = jnp.concatenate([key[:, pair:], fresh[:, pair:]], axis=1)
        weight[at, 3 * pair :] = jnp.concatenate(
            [both[:, :cols], jnp.zeros((block, WIDTH - cols), BF16)], axis=1
        )
    def make_rows(i, carry):
        t = jnp.where(i == 0, head, jnp.where(i == 1, side, jnp.where(i == 2, core, beyond)))

        @pl.when(i == 2)
        def _():
            for k, n in order:
                hop(ss, k, n, part(moved[k][1].at[core], n), core, core).wait_recv()

        @pl.when(i == 3)
        def _():
            for k, n in order:
                hop(ps, k, n, part(moved[k][1].at[beyond], n), beyond, core).wait_recv()
        total = tok.shape[0]
        at = pl.ds(pl.multiple_of(t * total, total), total)
        xhat, _ = statistics(tok_all[t].astype(F32))
        row = (xhat * attn_gain[...]).astype(BF16)
        normed_buf[t] = row
        pltpu.make_async_copy(normed_buf.at[t], normed.at[at], normed_sem.at[i]).start()
        out = dotf(row, weight[...])
        query[at, :] = (out[:, 3 * pair :].astype(BF16).astype(F32) * size**-0.5).astype(BF16)
        done = out[:, : 3 * pair].astype(BF16)
        given = first_all[t]
        kept = jnp.where(kind == 0, given[:, :cols], given[:, cols:])
        other = jnp.concatenate(
            [done[:, :pair], kept[:, :pair], done[:, 2 * pair : 2 * pair + size], kept[:, pair:]],
            axis=1,
        )
        own[at, :] = jnp.where(half == 0, done, other)
        for n in range(pieces // 4):
            n = t * (pieces // 4) + n

            @pl.when(blk + 2 < nblk)
            def _():
                far_copy(n, up).start()

            @pl.when(odd == 0)
            def _():
                near_copy(n, slab(own, n)).start()

        return carry

    lax.fori_loop(0, 4, make_rows, 0)
    for o in range(nblk // 2):

        line.land(o)
        to_core(2 * o + 1 - odd)
        to_side(2 * o + 1 - odd)

    for i, t in enumerate((head, side, core, beyond)):
        for n in range(pieces // 4):
            n = t * (pieces // 4) + n

            @pl.when(blk >= 2)
            def _():
                far_copy(n, down).wait_recv()

            @pl.when((blk >= 2) & (odd == 1))
            def _():
                near_copy(n, slab(near_far.at[0], n)).start()

    own_rest.wait()
    for b in range(early):
        chunk(xs, side, b, side).wait_recv()
        chunk(fs, side, b, core).start()
    for b in range(nblk):
        chunk(cs, core, b, core).wait_recv()
    for b in range(early):
        chunk(fs, beyond, b, core).wait_recv()
        chunk(xs, head, b, side).wait_send()
        chunk(fs, side, b, core).wait_send()
    for b in range(nblk):
        chunk(cs, head, b, core).wait_send()
    for i in range(4):
        at = pl.ds(0, tok.shape[0])
        pltpu.make_async_copy(normed_buf.at[i], normed.at[at], normed_sem.at[i]).wait()
    for n in range(pieces):

        @pl.when((blk >= 2) | (odd == 1))
        def _():
            near_copy(n, slab(own, n)).wait_recv()

        @pl.when(blk + 2 < nblk)
        def _():
            far_copy(n, up).wait_send()

        @pl.when((blk >= 2) | (odd == 0))
        def _():
            near_copy(n, slab(own, n)).wait_send()

    for i in range(2):
        target = half + 2 * i

        @pl.when(target != head)
        def _():
            remote(v_own, v_all.at[kind], send_v.at[i], recv_v.at[kind], target, blk).wait_send()

    for k, n in order:
        hop(ts, k, n, part(moved[k][0], n), head, side).wait_send()
        hop(ss, k, n, part(moved[k][0], n), head, core).wait_send()
        hop(ps, k, n, part(moved[k][1].at[side], n), side, core).wait_send()
    for d in range(1, nblk):
        for copy in spread(d):
            copy.wait_send()
    qk_line.finish()
    line.finish()


def front(
    nblk, early, tok, first, w_q, w_k, w_v, w_up, w_down, w_out, gain_a, gain_m, parts=4, pieces=8
):
    dma = pltpu.SemaphoreType.DMA
    (rows, width), (part, cols) = tok.shape, w_q.shape
    total = 4 * rows
    both = w_up.shape[1] + w_down.shape[1] + w_out.shape[0]
    low = lambda *shape: jax.ShapeDtypeStruct(shape, BF16)
    vmem = lambda *shape: pltpu.VMEM(shape, BF16)
    line = [dma((nblk // 2,))] * 6
    return pl.pallas_call(
        functools.partial(front_kernel, nblk, parts, pieces, early),
        out_shape=[
            low(total, width),
            low(total, WIDTH),
            low(total, 2 * cols),
            low(2, total, 2 * cols),
            low(4, nblk, part, both),
            low(nblk, part, 2 * cols),
            low(2, nblk, *w_v.shape),
            jax.ShapeDtypeStruct((1, width), F32),
            jax.ShapeDtypeStruct((1, width), F32),
        ],
        in_specs=[WHOLE] * 10,
        out_specs=[ANY, WHOLE, WHOLE, ANY, ANY] + [WHOLE] * 4,
        scratch_shapes=[
            vmem(4, *tok.shape),
            vmem(4, *first.shape),
            vmem(nblk, *w_v.shape),
            pltpu.VMEM((nblk, 2) + gain_a.shape, F32),
            vmem(part, 2 * cols),
            vmem(part, both),
            pltpu.VMEM((2,) + gain_a.shape, F32),
            vmem(width, 2 * cols + WIDTH),
            vmem(4, *tok.shape),
            dma,
            dma((4,)),
        ]
        + [dma((2, parts))] * 6
        + [dma((2, nblk))] * 2
        + [dma((2,))] * 2
        + line * 2
        + [dma((nblk,))] * 6
        + [dma((pieces,))] * 4,
        compiler_params=pltpu.CompilerParams(
            collective_id=0, has_side_effects=True, vmem_limit_bytes=56 << 20
        ),
        name="front",
    )(tok, first, w_q, w_k, w_v, w_up, w_down, w_out, gain_a, gain_m)


def gelu_both(pre):
    square = pre * pre
    inner = jnp.tanh(GELU_SCALE * (pre + 0.044715 * square * pre))
    slope = GELU_SCALE * (1.0 + 3.0 * 0.044715 * square)
    outer = 0.5 * (1.0 + inner)
    return pre * outer, outer + 0.5 * pre * (1.0 - inner * inner) * slope


def middle_kernel(
    nblk, up_cols, cut, pieces, tok, mixed_parts, cot, gain, gathered, late, query,
    out, grad_resid, grad_wide, gain_part, keep_a, give_a, keep_b, give_b, query_later,
    up, down, w_out, up_grad, down_grad, out_grad, mixed, wide_parts, up_got, down_got, out_got,
    sems, out_sems, send_m, recv_m, send_g, recv_g, send_c, recv_c,
    send_z, recv_z, send_y, recv_y, hidden_all, pre_all, normed_t, cot_t, total, grad_normed, normed_rows, branch_rows, branch_t, late_far, send_l, recv_l,
):
    head, blk = lax.axis_index("head"), lax.axis_index("blk")
    x, core_index = lax.div(head, 2), lax.rem(head, 2)
    core = xor(head, 1)
    others = [xor(head, 2), 3 - head, core]
    odd = lax.rem(blk, 2)
    pair = blk + 1 - 2 * odd
    above, below = lax.rem(blk + 2, nblk), lax.rem(blk + nblk - 2, nblk)
    greet(partners_of(head, blk, nblk, blks=False) + [(head, b) for b in (pair, above, below)])
    heads_of = 4
    part = gathered.shape[2]
    cols = mixed.shape[2]
    heads = cols // HEAD_DIM

    def mixed_copy(i, to, slot):
        return remote(
            mixed_parts.at[to], mixed.at[slot], send_m.at[i], recv_m.at[i], to, blk
        )

    for i, to in enumerate(others):
        mixed_copy(i, to, head).start()
    late_copy = remote(late, late_far, send_l, recv_l, core, blk)
    late_copy.start()
    early = nblk - late.shape[0]
    piece_rows = query.shape[0] // pieces

    def slab(ref, p):
        return ref.at[pl.ds(p * piece_rows, piece_rows)]

    def far_copy(p, to):
        dst = slab(query_later.at[1], p)
        return remote(slab(query, p), dst, send_z.at[p], recv_z.at[p], head, to)

    def near_copy(p, src):
        return remote(src, slab(query_later.at[0], p), send_y.at[p], recv_y.at[p], head, pair)

    for p in range(pieces):

        @pl.when(blk >= 2)
        def _():
            far_copy(p, below).start()

        @pl.when(odd == 1)
        def _():
            near_copy(p, slab(query, p)).start()

    def relay(p):
        @pl.when(blk + 2 < nblk)
        def _():
            far_copy(p, above).wait_recv()

        @pl.when((blk + 2 < nblk) & (odd == 0))
        def _():
            near_copy(p, slab(query_later.at[1], p)).start()

    chunks = [2 * n + c for n in (1 - x, x) for c in (1 - core_index, core_index)]
    side = others[0]
    sources = (3 - head, others[0], core)

    def source(i, b):
        if b < early or i > 1:
            return gathered.at[chunks[i], b]
        return (late_far, late)[i].at[b - early]

    def load(i, which):
        target, lo, size = ((w_out, 2 * up_cols, cols), (up, 0, up_cols), (down, up_cols, up_cols))[
            which
        ]
        return [
            pltpu.make_async_copy(
                source(i, b).at[:, pl.ds(lo, size)],
                target.at[i, pl.ds(b * part, part)],
                sems.at[which, i, b],
            )
            for b in range(nblk)
        ]

    turns = (2, 3, 1, 0)
    order = [(i, 0) for i in turns] + [(i, w) for i in turns for w in (1, 2)]
    for i, which in order:
        for b, copy in enumerate(load(i, which)):
            if i or b < early:
                copy.start()
    mixed[head] = mixed_parts[head]
    late_copy.wait()
    for which in range(3):
        for copy in load(0, which)[early:]:
            copy.start()
    for i in range(heads_of):
        for copy in load(i, 0):
            copy.wait()
    for i, to in enumerate(others):
        mixed_copy(i, to, to).wait_recv()
    branch = None
    for i in range(heads_of):
        term = dotf(mixed[chunks[i]], w_out[i], NT)
        branch = term if branch is None else branch + term
    resid = tok[...].astype(F32) + branch
    xhat, scale = statistics(resid)
    normed = (xhat * gain[...]).astype(BF16)
    cotangent = cot[...]
    total[...] = resid
    grad_normed[...] = jnp.zeros_like(resid)

    def chunk_of(i):
        far = jnp.where(i < 2, 1 - x, x)
        return 2 * far + jnp.where(lax.rem(i, 2) == 0, 1 - core_index, core_index)

    def to_core(n, k):
        mine, theirs = ((up_grad, up_got), (down_grad, down_got), (out_grad, out_got))[k]
        return remote(mine.at[2 * n], theirs.at[n], send_c.at[k, n], recv_c.at[k, n], core, blk)

    normed_rows[...] = normed
    normed_t[...] = normed.T
    cot_t[...] = cotangent.T
    def arrived(which, i):
        target = (w_out, up, down)[which].at[i, pl.ds(0, part)]
        for b in range(nblk):
            pltpu.make_async_copy(target, target, sems.at[which, i, b]).wait()

    def forward(n, carry):
        i = jnp.where(n < 2, n + 2, 3 - n)
        arrived(1, i)
        arrived(2, i)
        hidden, slope = gelu_both(dotf(normed_rows[...], up[i]))
        hidden_all[i] = hidden.astype(BF16)
        pre_all[i] = (slope * dotf(cot[...], down[i])).astype(BF16)
        total[...] += dotf(hidden_all[i], down[i], NT)
        grad_normed[...] += dotf(pre_all[i], up[i], NT)

        @pl.loop(0, pieces // heads_of)
        def _(p):
            relay(n * (pieces // heads_of) + p)

        return carry

    lax.fori_loop(0, heads_of, forward, 0)
    grad = cotangent.astype(F32) + norm_back(grad_normed[...], xhat, scale, gain[...])
    branch_grad = grad.astype(BF16)
    lane = lax.broadcasted_iota(jnp.int32, (tok.shape[0], WIDTH), 1)

    def wide_copy(i, to, slot):
        return remote(
            wide_parts.at[to], grad_wide.at[slot], send_g.at[i], recv_g.at[i], to, blk
        )

    branch_rows[...] = branch_grad

    def widen(i, carry):
        h = chunk_of(i)
        rows = dotf(branch_rows[...], w_out[i]).astype(BF16).astype(F32)
        product = rows * mixed[h].astype(F32)
        wide = jnp.concatenate([rows, jnp.zeros((rows.shape[0], WIDTH - cols), F32)], axis=1)
        for k in range(heads):
            delta = jnp.sum(
                product[:, k * HEAD_DIM : (k + 1) * HEAD_DIM], axis=1, keepdims=True
            )
            for c, piece in enumerate(split_parts(-delta)):
                wide = jnp.where(lane == cols + SPLITS * k + c, piece, wide)
        wide_parts[h] = wide.astype(BF16)

        @pl.when(i < 3)
        def _():
            wide_copy(i, h, head).start()

        return carry

    lax.fori_loop(0, heads_of, widen, 0)
    grad_wide[head] = wide_parts[head]
    out[...] = total[...].astype(BF16)
    gain_part[...] = jnp.sum(grad_normed[...] * xhat, axis=0, keepdims=True)
    grad_resid[...] = grad
    branch_t[...] = branch_grad.T

    def weigh(i, carry):
        up_grad[i] = dotf(normed_t[...], pre_all[i]).astype(BF16)
        down_grad[i] = dotf(cot_t[...], hidden_all[i]).astype(BF16)
        out_grad[i] = dotf(branch_t[...], mixed[chunk_of(i)]).astype(BF16)

        @pl.when(lax.rem(i, 2) == 0)
        def _():
            for k in range(3):
                to_core(lax.div(i, 2), k).start()

        return carry

    lax.fori_loop(0, heads_of, weigh, 0)

    def store(k, source, target, lo):
        size = source.shape[1]
        return [
            pltpu.make_async_copy(
                source.at[pl.ds(b * part, part)],
                target(b).at[:, pl.ds(lo, size)],
                out_sems.at[k, b],
            )
            for b in range(nblk)
        ]

    stores = []
    for n, target in enumerate((give_a, keep_a)):
        at = 2 * n + 1
        for k, (mine, theirs) in enumerate(
            ((up_grad, up_got), (down_grad, down_got), (out_grad, out_got))
        ):
            to_core(n, k).wait_recv()
            mine[at] = (mine[at].astype(F32) + theirs[n].astype(F32)).astype(BF16)
        first_part = store(3 * n, up_grad.at[at], lambda b: target.at[b], 0)
        far_down = down_grad.at[at].at[:, pl.ds(cut, up_cols - cut)]
        first_part += store(6 + n, far_down, lambda b: target.at[b], up_cols)
        first_part += store(3 * n + 1, out_grad.at[at], lambda b: target.at[b], 2 * up_cols - cut)
        for copy in first_part:
            copy.start()
        kept = store(3 * n + 2, down_grad.at[at].at[:, pl.ds(0, cut)], lambda b: keep_b.at[n, b // 2], 0)
        given = store(3 * n + 2, down_grad.at[at].at[:, pl.ds(0, cut)], lambda b: give_b.at[n, b // 2], 0)
        for b in range(nblk):

            @pl.when(odd == b % 2)
            def _():
                kept[b].start()

            @pl.when(odd != b % 2)
            def _():
                given[b].start()

        stores += first_part + kept
    for copy in stores:
        copy.wait()
    for k in range(3):
        for n in range(2):
            to_core(n, k).wait_send()
    for i in range(3):
        wide_copy(i, chunks[i], sources[i]).wait_recv()
    for i, to in enumerate(others):
        mixed_copy(i, to, head).wait_send()
        wide_copy(i, chunks[i], head).wait_send()
    for p in range(pieces):

        @pl.when((blk + 2 < nblk) | (odd == 0))
        def _():
            near_copy(p, slab(query, p)).wait_recv()

        @pl.when(blk >= 2)
        def _():
            far_copy(p, below).wait_send()

        @pl.when((blk + 2 < nblk) | (odd == 1))
        def _():
            near_copy(p, slab(query, p)).wait_send()


def middle(nblk, tok, mixed_parts, cot, gain, gathered, late, query, up_cols, cut=512, pieces=8):
    heads_of, rows, cols = mixed_parts.shape
    width, part = tok.shape[1], gathered.shape[2]
    flops = 2 * rows * width * (6 * up_cols * heads_of + 3 * width)
    dma = pltpu.SemaphoreType.DMA
    vmem = lambda *shape: pltpu.VMEM(shape, BF16)
    return pl.pallas_call(
        functools.partial(middle_kernel, nblk, up_cols, cut, pieces),
        out_shape=[
            jax.ShapeDtypeStruct((rows, width), BF16),
            jax.ShapeDtypeStruct((rows, width), F32),
            jax.ShapeDtypeStruct((heads_of, rows, WIDTH), BF16),
            jax.ShapeDtypeStruct((1, width), F32),
            jax.ShapeDtypeStruct((nblk, part, 2 * up_cols - cut + cols), BF16),
            jax.ShapeDtypeStruct((nblk, part, 2 * up_cols - cut + cols), BF16),
            jax.ShapeDtypeStruct((2, nblk // 2, part, cut), BF16),
            jax.ShapeDtypeStruct((2, nblk // 2, part, cut), BF16),
            jax.ShapeDtypeStruct((2,) + query.shape, BF16),
        ],
        in_specs=[WHOLE] * 4 + [ANY] * 3,
        out_specs=[WHOLE] * 4 + [ANY] * 5,
        scratch_shapes=[
            vmem(heads_of, width, up_cols), vmem(heads_of, width, up_cols),
            vmem(heads_of, width, cols),
            vmem(heads_of, width, up_cols), vmem(heads_of, width, up_cols),
            vmem(heads_of, width, cols),
            vmem(heads_of, rows, cols), vmem(heads_of, rows, WIDTH),
            vmem(2, width, up_cols), vmem(2, width, up_cols), vmem(2, width, cols),
            dma((3, heads_of, nblk)), dma((8, nblk)),
            dma((3,)), dma((3,)), dma((3,)), dma((3,)), dma((3, 2)), dma((3, 2)),
            dma((pieces,)), dma((pieces,)), dma((pieces,)), dma((pieces,)),
            vmem(heads_of, rows, up_cols), vmem(heads_of, rows, up_cols),
            vmem(width, rows), vmem(width, rows),
            pltpu.VMEM((rows, width), F32), pltpu.VMEM((rows, width), F32),
            vmem(rows, width), vmem(rows, width), vmem(width, rows),
            vmem(*late.shape), dma, dma,
        ],
        compiler_params=pltpu.CompilerParams(
            collective_id=2, has_side_effects=True, vmem_limit_bytes=62 << 20
        ),
        cost_estimate=pl.CostEstimate(
            flops=flops, bytes_accessed=24 << 20, transcendentals=rows * up_cols * heads_of
        ),
        name="middle",
    )(tok, mixed_parts, cot, gain, gathered, late, query)


def pair_sum_kernel(ours_a, got_a, ours_b, got_b, keep_a, give_a, keep_b, give_b):
    odd = lax.rem(lax.axis_index("blk"), 2)
    sums = [(ours_a[n].astype(F32) + got_a[n].astype(F32)).astype(BF16) for n in range(2)]
    keep_a[0] = jnp.where(odd == 0, sums[0], sums[1])
    give_a[0] = jnp.where(odd == 0, sums[1], sums[0])
    give_b[0] = (ours_b[0, 0].astype(F32) + got_b[0, 0].astype(F32)).astype(BF16)
    keep_b[0] = (ours_b[1, 0].astype(F32) + got_b[1, 0].astype(F32)).astype(BF16)


def pair_sum(ours_a, got_a, ours_b, got_b):
    nblk, part, width = ours_a.shape
    other = ours_b.shape[3]
    a_in = pl.BlockSpec((2, part, width), lambda i: (i, 0, 0))
    b_in = pl.BlockSpec((2, 1, part, other), lambda i: (0, i, 0, 0))
    out = lambda cols: pl.BlockSpec((1, part, cols), lambda i: (i, 0, 0))
    shape = lambda cols: jax.ShapeDtypeStruct((nblk // 2, part, cols), BF16)
    return pl.pallas_call(
        pair_sum_kernel,
        grid=(nblk // 2,),
        in_specs=[a_in, a_in, b_in, b_in],
        out_specs=[out(width)] * 2 + [out(other)] * 2,
        out_shape=[shape(width)] * 2 + [shape(other)] * 2,
        cost_estimate=pl.CostEstimate(
            flops=nblk * part * width, bytes_accessed=12 * nblk * part * width, transcendentals=0
        ),
        name="pair_sum",
    )(ours_a, got_a, ours_b, got_b)


def head_rows(h, heads, shape):
    row = lax.broadcasted_iota(jnp.int32, shape, 0)
    real = heads * HEAD_DIM
    own = (row >= h * HEAD_DIM) & (row < (h + 1) * HEAD_DIM)
    return own | ((row >= real + SPLITS * h) & (row < real + SPLITS * (h + 1)))


def per_head(wide, heads, out):
    flipped = wide.T
    for h in range(heads):
        out[h] = jnp.where(head_rows(h, heads, flipped.shape), flipped, jnp.zeros_like(flipped))


def doc_start(meta, ndocs, t):
    def step(j,c):
        cum,best=c
        best=jnp.where(cum<=t,cum,best)
        return cum+meta[1+j],best
    return lax.fori_loop(0,ndocs,step,(jnp.int32(0),jnp.int32(0)),unroll=True)[1]

def doc_end(meta, ndocs, t):
    def step(j,c):
        cum,best,found=c
        cum=cum+meta[1+j]
        take=(cum>t)&(found==0)
        return cum,jnp.where(take,cum,best),jnp.where(take,1,found)
    return lax.fori_loop(0,ndocs,step,(jnp.int32(0),jnp.int32(0),jnp.int32(0)),unroll=True)[1]

def starts_vec(meta, ndocs, t):
    def step(j,c):
        cum,best=c
        return cum+meta[1+j],jnp.where(cum<=t,cum,best)
    return lax.fori_loop(0,ndocs,step,(jnp.int32(0),jnp.zeros(t.shape,jnp.int32)))[1]

def ends_vec(meta, ndocs, t):
    def step(j,c):
        cum,best=c
        ln=meta[1+j]
        return cum+ln,jnp.where(cum<=t,cum+ln,best)
    return lax.fori_loop(0,ndocs,step,(jnp.int32(0),jnp.zeros(t.shape,jnp.int32)))[1]

def widened(columns, heads):
    rows, width = columns.shape
    ones = jnp.ones((rows, SPLITS * heads), BF16)
    empty = jnp.zeros((rows, WIDTH - width - SPLITS * heads), BF16)
    return jnp.concatenate([columns, ones, empty], axis=1)


def unpack_rows(packed, heads):
    pair = 2 * HEAD_DIM
    key = jnp.concatenate([packed[:, :pair], packed[:, 2 * pair : 2 * pair + HEAD_DIM]], axis=1)
    value = jnp.concatenate([packed[:, pair : 2 * pair], packed[:, 2 * pair + HEAD_DIM :]], axis=1)
    return widened(key, heads), widened(value, heads)


STEP = 512


def build_window(heads, start, earlier, own, packed, sems, keys, values, key_rows, value_rows):
    before = earlier.shape[0] // STEP
    chunks = before + own.shape[0] // STEP

    def copy(n, source, row):
        return pltpu.make_async_copy(
            source.at[pl.ds(row * STEP, STEP)], packed.at[pl.ds(n * STEP, STEP)], sems.at[n]
        )

    def begin(n, carry):
        @pl.when(n < before)
        def _():
            copy(n, earlier, n).start()

        @pl.when(n >= before)
        def _():
            copy(n, own, n - before).start()

        return carry

    def build(n, carry):
        copy(n, own, 0).wait()
        at = pl.ds(pl.multiple_of(n * STEP, STEP), STEP)
        key, value = unpack_rows(packed[at, :], heads)
        for wide, rows, flipped in ((key, keys, key_rows), (value, values, value_rows)):
            if rows is not None:
                rows[at, :] = wide
            if flipped is not None:
                turned = wide.T
                for h in range(heads):
                    flipped[h, :HEAD_DIM, at] = turned[h * HEAD_DIM : (h + 1) * HEAD_DIM]
        return carry

    lax.fori_loop(start, chunks, begin, 0)
    lax.fori_loop(start, chunks, build, 0)


def three(lo, a, b, hi, body):
    edge = a - lo

    def masked(n, carry):
        body(jnp.where(n < edge, lo + n, b + n - edge), True)
        return carry

    def free(n, carry):
        body(n, False)
        return carry

    lax.fori_loop(0, edge + hi - b, masked, 0)
    lax.fori_loop(a, b, free, 0)


def query_tiles(meta, ndocs, t0, wbase, tq, tk):
    lo = (doc_start(meta, ndocs, t0) - wbase) // tk
    f0 = (doc_start(meta, ndocs, t0 + tq - 1) - wbase + tk - 1) // tk
    f1 = (t0 - wbase) // tk
    hi = (t0 + tq - 1 - wbase) // tk + 1
    return lo, jnp.minimum(f0, f1), f1, hi


def fwd_kernel(heads, ndocs, tq, tk, meta, q_ref, earlier, own, mix_ref, wide_ref,
               k_ref, vt_ref, qt, m_ref, acc_ref, packed, sems):
    i = pl.program_id(0)
    width = q_ref.shape[1]
    real = heads * HEAD_DIM
    base = meta[0]
    wbase = base - earlier.shape[0]

    @pl.when(i == 0)
    def _():
        vt_ref[:, HEAD_DIM:, :] = jnp.ones_like(vt_ref[:, HEAD_DIM:, :])
        start = (doc_start(meta, ndocs, base) - wbase) // tk * (tk // STEP)
        build_window(heads, start, earlier, own, packed, sems, k_ref, None, None, vt_ref)

    t0 = base + i * tq
    lo, f0, f1, hi = query_tiles(meta, ndocs, t0, wbase, tq, tk)
    q = q_ref[...]
    trow = t0 + lax.broadcasted_iota(jnp.int32, (8, tq), 1)
    srow = starts_vec(meta, ndocs, trow)[:1]
    trow = trow[:1]
    lane = lax.broadcasted_iota(jnp.int32, (tq, width), 1)

    def visible(off):
        u = wbase + off + lax.broadcasted_iota(jnp.int32, (tk, tq), 0)
        return (u >= srow) & (u <= trow)

    itself = q.astype(F32) * k_ref[pl.ds(pl.multiple_of(t0 - wbase, tq), tq), :].astype(F32)
    shifted = q.astype(F32)
    for h in range(heads):
        mine = (lane >= h * HEAD_DIM) & (lane < (h + 1) * HEAD_DIM)
        score = jnp.sum(jnp.where(mine, itself, 0.0), axis=1, keepdims=True)
        for c, piece in enumerate(split_parts(-score)):
            shifted = jnp.where(lane == real + SPLITS * h + c, piece, shifted)
    per_head(shifted.astype(BF16), heads, qt)
    acc_ref[...] = jnp.zeros_like(acc_ref)

    def quick(j, masked):
        off = pl.multiple_of(j * tk, tk)
        k = k_ref[pl.ds(off, tk), :]
        if masked:
            vis = visible(off)
        scores = [dotf(k, qt[h]) for h in range(heads)]
        for h in range(heads):
            p = jnp.exp(scores[h])
            if masked:
                p = jnp.where(vis, p, 0.0)
            acc_ref[h] += dotf(vt_ref[h, :, pl.ds(off, tk)], p.astype(BF16))

    def finish(extra):
        rows = []
        parts = []
        for h in range(heads):
            acc = acc_ref[h]
            total = acc[HEAD_DIM : HEAD_DIM + 1]
            rows.append(acc[:HEAD_DIM] / total)
            at = real + SPLITS * h
            shift = jnp.sum(qt[h, at : at + SPLITS, :].astype(F32), axis=0, keepdims=True)
            parts += split_parts(shift - extra[h] - jnp.log(total))
        rest = jnp.zeros((width - real - len(parts), tq), F32)
        turned = jnp.concatenate(rows + parts + [rest], axis=0).T
        mix_ref[0] = turned[:, :real].astype(BF16)
        wide_ref[...] = jnp.where(lane < real, q.astype(F32), turned).astype(BF16)

    three(lo, f0, f1, hi, quick)
    none = jnp.zeros((1, tq), F32)
    finish([none] * heads)
    sums = acc_ref[:, HEAD_DIM : HEAD_DIM + 1, :]
    fits = jnp.max(jnp.where(sums < 1e30, 0.0, 1.0)) == 0.0

    @pl.when(jnp.logical_not(fits))
    def _():
        acc_ref[...] = jnp.zeros_like(acc_ref)
        m_ref[...] = jnp.full_like(m_ref, EXCLUDED)

        def body(j, carry):
            off = pl.multiple_of(j * tk, tk)
            k = k_ref[pl.ds(off, tk), :]
            vis = visible(off)
            for h in range(heads):
                s = jnp.where(vis, dotf(k, qt[h]), EXCLUDED)
                old = m_ref[h, :1]
                new = jnp.maximum(old, jnp.max(s, axis=0, keepdims=True))
                m_ref[h, :1] = new
                p = jnp.exp(s - new).astype(BF16)
                acc_ref[h] = acc_ref[h] * jnp.exp(old - new) + dotf(
                    vt_ref[h, :, pl.ds(off, tk)], p
                )
            return carry

        lax.fori_loop(lo, hi, body, 0)
        finish([m_ref[h, :1] for h in range(heads)])


SCALARS = pl.BlockSpec(memory_space=pltpu.SMEM)


def attention_fwd(meta, q, earlier, own, heads, tq, tk):
    block, width = q.shape
    window = block + earlier.shape[0]
    ndocs = meta.shape[0] - 1
    return pl.pallas_call(
        functools.partial(fwd_kernel, heads, ndocs, tq, tk),
        grid=(block // tq,),
        in_specs=[
            SCALARS,
            pl.BlockSpec((tq, width), lambda i: (i, 0)),
            ANY,
            ANY,
        ],
        out_specs=[
            pl.BlockSpec((1, tq, heads * HEAD_DIM), lambda i: (i, 0, 0)),
            pl.BlockSpec((tq, width), lambda i: (i, 0)),
        ],
        out_shape=[
            jax.ShapeDtypeStruct((block // tq, tq, heads * HEAD_DIM), BF16),
            jax.ShapeDtypeStruct((block, width), BF16),
        ],
        scratch_shapes=[
            pltpu.VMEM((window, width), BF16),
            pltpu.VMEM((heads, HEAD_DIM + 16, window), BF16),
            pltpu.VMEM((heads, width, tq), BF16),
            pltpu.VMEM((heads, 8, tq), F32),
            pltpu.VMEM((heads, HEAD_DIM + 16, tq), F32),
            pltpu.VMEM((window, own.shape[1]), BF16),
            pltpu.SemaphoreType.DMA((window // STEP,)),
        ],
        compiler_params=pltpu.CompilerParams(vmem_limit_bytes=56 << 20),
        cost_estimate=pl.CostEstimate(
            flops=30_000_000_000, bytes_accessed=12 << 20, transcendentals=20_000_000
        ),
        name="attn_fwd",
    )(meta, q, earlier, own)


def dq_kernel(heads, ndocs, tq, tk, meta, q_ref, do_ref, earlier, own, dq_ref,
              k_ref, v_ref, kt_ref, qt, dot, acc_ref, packed, sems):
    i = pl.program_id(0)
    base = meta[0]
    wbase = base - earlier.shape[0]

    @pl.when(i == 0)
    def _():
        start = (doc_start(meta, ndocs, base) - wbase) // tk * (tk // STEP)
        build_window(heads, start, earlier, own, packed, sems, k_ref, v_ref, kt_ref, None)

    t0 = base + i * tq
    per_head(q_ref[...], heads, qt)
    per_head(do_ref[...], heads, dot)
    acc_ref[...] = jnp.zeros_like(acc_ref)
    trow = t0 + lax.broadcasted_iota(jnp.int32, (8, tq), 1)
    srow = starts_vec(meta, ndocs, trow)[:1]
    trow = trow[:1]

    def body(j, masked):
        off = pl.multiple_of(j * tk, tk)
        k = k_ref[pl.ds(off, tk), :]
        v = v_ref[pl.ds(off, tk), :]
        if masked:
            u = wbase + off + lax.broadcasted_iota(jnp.int32, (tk, tq), 0)
            vis = (u >= srow) & (u <= trow)
        made = [(dotf(k, qt[h]), dotf(v, dot[h])) for h in range(heads)]
        for h in range(heads):
            p = jnp.exp(made[h][0])
            if masked:
                p = jnp.where(vis, p, 0.0)
            ds = (p * made[h][1]).astype(BF16)
            acc_ref[h] += dotf(kt_ref[h, :, pl.ds(off, tk)], ds)

    three(*query_tiles(meta, ndocs, t0, wbase, tq, tk), body)
    turned = acc_ref[...].reshape(heads * HEAD_DIM, tq).T
    dq_ref[...] = (turned * (HEAD_DIM**-0.5)).astype(BF16)


def attention_dq(meta, q, do, earlier, own, heads, tq, tk):
    block, width = q.shape
    window = block + earlier.shape[0]
    ndocs = meta.shape[0] - 1
    row = lambda w: pl.BlockSpec((tq, w), lambda i: (i, 0))
    return pl.pallas_call(
        functools.partial(dq_kernel, heads, ndocs, tq, tk),
        grid=(block // tq,),
        in_specs=[SCALARS, row(width), row(width), ANY, ANY],
        out_specs=row(heads * HEAD_DIM),
        out_shape=jax.ShapeDtypeStruct((block, heads * HEAD_DIM), BF16),
        scratch_shapes=[pltpu.VMEM((window, width), BF16)] * 2
        + [pltpu.VMEM((heads, HEAD_DIM, window), BF16)]
        + [pltpu.VMEM((heads, width, tq), BF16)] * 2
        + [pltpu.VMEM((heads, HEAD_DIM, tq), F32)]
        + [pltpu.VMEM((window, own.shape[1]), BF16), pltpu.SemaphoreType.DMA((window // STEP,))],
        compiler_params=pltpu.CompilerParams(vmem_limit_bytes=56 << 20),
        cost_estimate=pl.CostEstimate(
            flops=45_000_000_000, bytes_accessed=12 << 20, transcendentals=20_000_000
        ),
        name="attn_dq",
    )(meta, q, do, earlier, own)


def dkv_kernel(heads, ndocs, tq, tk, meta, own, q_parts, do_parts, dk_ref, dv_ref,
               q_ref, do_ref, qt_ref, dot_ref, kt, vt, dk_acc, dv_acc, sems):
    i = pl.program_id(0)
    base = meta[0]

    @pl.when(i == 0)
    def _():
        block = pl.num_programs(0) * tk
        end = (doc_end(meta, ndocs, base + block - 1) - base + STEP - 1) // STEP
        sources = []
        for parts in (q_parts, do_parts):
            row, found = 0, []
            for part in parts:
                found.append((row // STEP, (row + part.shape[0]) // STEP, part))
                row += part.shape[0]
            sources.append(found)

        def copy(k, n, source, row):
            return pltpu.make_async_copy(
                source.at[pl.ds(row * STEP, STEP)],
                (q_ref, do_ref)[k].at[pl.ds(n * STEP, STEP)],
                sems.at[k, n],
            )

        def begin(n, carry):
            for k in range(2):
                for first, last, part in sources[k]:

                    @pl.when((n >= first) & (n < last))
                    def _():
                        copy(k, n, part, n - first).start()

            return carry

        def turn(n, carry):
            at = pl.ds(pl.multiple_of(n * STEP, STEP), STEP)
            for k, (rows, flipped) in enumerate(((q_ref, qt_ref), (do_ref, dot_ref))):
                copy(k, n, sources[k][0][2], 0).wait()
                turned = rows[at, :].T
                for h in range(heads):
                    flipped[h, :, at] = turned[h * HEAD_DIM : (h + 1) * HEAD_DIM]
            return carry

        lax.fori_loop(0, end, begin, 0)
        lax.fori_loop(0, end, turn, 0)

    u0 = base + i * tk
    lo = (u0 - base) // tq
    f0 = (u0 + tk - 1 - base + tq - 1) // tq
    e_first = doc_end(meta, ndocs, u0)
    e_last = doc_end(meta, ndocs, u0 + tk - 1)
    f1 = (e_first - base) // tq
    hi = (e_last - 1 - base) // tq + 1
    f0 = jnp.minimum(f0, hi)
    f1 = jnp.clip(f1, f0, hi)
    k, v = unpack_rows(own[...], heads)
    per_head(k, heads, kt)
    per_head(v, heads, vt)
    dk_acc[...] = jnp.zeros_like(dk_acc)
    dv_acc[...] = jnp.zeros_like(dv_acc)
    urow = u0 + lax.broadcasted_iota(jnp.int32, (8, tk), 1)
    erow = ends_vec(meta, ndocs, urow)[:1]
    urow = urow[:1]

    def body(j, masked):
        off = pl.multiple_of(j * tq, tq)
        at = pl.ds(off, tq)
        q = q_ref[at, :]
        do = do_ref[at, :]
        if masked:
            t = base + off + lax.broadcasted_iota(jnp.int32, (tq, tk), 0)
            vis = (t >= urow) & (t < erow)
        for h in range(heads):
            p = jnp.exp(dotf(q, kt[h]))
            if masked:
                p = jnp.where(vis, p, 0.0)
            ds = (p * dotf(do, vt[h])).astype(BF16)
            dv_acc[h] += dotf(dot_ref[h, :, at], p.astype(BF16))
            dk_acc[h] += dotf(qt_ref[h, :, at], ds)

    three(lo, f0, f1, hi, body)
    for acc, out in ((dk_acc, dk_ref), (dv_acc, dv_ref)):
        out[...] = acc[...].reshape(heads * HEAD_DIM, tk).T.astype(BF16)


def attention_dkv(meta, own, q_parts, do_parts, heads, tq, tk):
    block, width = q_parts[0].shape
    window = sum(part.shape[0] for part in q_parts)
    ndocs = meta.shape[0] - 1
    row = lambda w: pl.BlockSpec((tk, w), lambda i: (i, 0))
    return pl.pallas_call(
        functools.partial(dkv_kernel, heads, ndocs, tq, tk),
        grid=(block // tk,),
        in_specs=[SCALARS, row(own.shape[1]), [ANY] * len(q_parts), [ANY] * len(do_parts)],
        out_specs=[row(heads * HEAD_DIM)] * 2,
        out_shape=[jax.ShapeDtypeStruct((block, heads * HEAD_DIM), BF16)] * 2,
        scratch_shapes=[pltpu.VMEM((window, width), BF16)] * 2
        + [pltpu.VMEM((heads, HEAD_DIM, window), BF16)] * 2
        + [pltpu.VMEM((heads, width, tk), BF16)] * 2
        + [pltpu.VMEM((heads, HEAD_DIM, tk), F32)] * 2
        + [pltpu.SemaphoreType.DMA((2, window // STEP))],
        compiler_params=pltpu.CompilerParams(vmem_limit_bytes=56 << 20),
        cost_estimate=pl.CostEstimate(
            flops=60_000_000_000, bytes_accessed=12 << 20, transcendentals=20_000_000
        ),
        name="attn_dkv",
    )(meta, own, q_parts, do_parts)


def on_device(
    tokens, first_values, cotangent, w_query, w_key, w_value, w_out, w_up, w_down,
    gain_attn, gain_mlp, doc_lengths,
):
    width = tokens.shape[1]
    heads_of = lax.axis_size("head")
    nblk = lax.axis_size("blk")
    blk = lax.axis_index("blk")
    rows = tokens.shape[0]
    block = rows * heads_of
    heads = HEADS // heads_of
    cols = heads * HEAD_DIM
    part = width // nblk
    meta = jnp.concatenate([jnp.reshape(blk * block, (1,)).astype(jnp.int32), doc_lengths])

    up_cols = w_up.shape[1]
    early = nblk - 3 * nblk // 8
    normed, query, own, earlier, gathered, qk_all, v_all, attn_gain, mlp_gain = front(
        nblk, early, tokens, first_values, w_query, w_key, w_value, w_up, w_down.T, w_out,
        gain_attn.reshape(1, part), gain_mlp.reshape(1, part),
    )
    w_qk = qk_all.reshape(width, 2 * cols)
    w_v = v_all.reshape(2, width, w_value.shape[1])
    earlier = earlier.reshape(2 * block, 2 * cols)
    beside = [(h, (h + 2) % heads_of) for h in range(heads_of)]
    mine = lax.dynamic_index_in_dim(gathered, lax.axis_index("head"), 0, keepdims=False)[early:]
    late = lax.ppermute(mine, "head", beside)
    mixed_parts, query_wide = attention_fwd(
        meta, query, earlier, own, heads, rows, rows
    )
    late, mixed_parts = lax.optimization_barrier((late, mixed_parts))
    layer_output, grad_resid, grad_parts, gain_mlp_part, keep_a, give_a, keep_b, give_b, query_later = middle(
        nblk, tokens, mixed_parts, cotangent, mlp_gain, gathered, late, query_wide, up_cols
    )
    grad_wide = grad_parts.reshape(block, WIDTH)
    across = [(i, i + 1 - 2 * (i % 2)) for i in range(nblk)]
    got_a = lax.ppermute(give_a, "head", beside)
    got_b = lax.ppermute(give_b, "blk", across)

    grads_later = [grad_wide] + [
        lax.ppermute(grad_wide, "blk", [(i, i - d) for i in range(d, nblk)]) for d in (1, 2)
    ]
    queries_later = [query_wide, query_later.reshape(2 * block, WIDTH)]
    grad_query = attention_dq(
        meta, query_wide, grad_wide, earlier, own, heads, rows, rows
    )
    got_a, got_b, grad_query = lax.optimization_barrier((got_a, got_b, grad_query))
    keep_a, give_a, keep_b, give_b = pair_sum(keep_a, got_a, keep_b, got_b)
    got_a = lax.ppermute(give_a, "blk", across)
    got_b = lax.ppermute(give_b, "head", beside)
    keep_a, own = lax.optimization_barrier((keep_a, own))
    grad_key, grad_value = attention_dkv(
        meta, own, queries_later, grads_later, heads, rows, rows
    )
    outs = tail(
        nblk, grad_query, grad_key, grad_value, normed, w_qk, w_v, gain_mlp_part,
        keep_a, got_a, keep_b, got_b, tokens, grad_resid, attn_gain,
    )
    (
        layer_output, grad_tokens, final_query, final_key, final_value, grad_first, final_a, final_m,
        final_up, final_down, final_out,
    ) = settle([layer_output] + list(outs))
    return (
        layer_output,
        grad_tokens,
        grad_first,
        final_query,
        final_key,
        final_value,
        final_out,
        final_up,
        final_down.T,
        final_a.reshape(part),
        final_m.reshape(part),
    )


def solution(mesh):
    rows = P(("blk", "head"), None)
    specs = (P("blk", "head"),) * 3 + (P("head", "blk"), P("blk", "head"), P("head", "blk"))
    gains = (P("blk"), P("blk"))
    return jax.shard_map(
        on_device,
        mesh=mesh,
        in_specs=(rows,) * 3 + specs + gains + (P(),),
        out_specs=(rows,) * 3 + specs + gains,
        check_vma=False,
    )
```

```python
import functools

import jax
import jax.numpy as jnp
from jax import lax
from jax.experimental import pallas as pl
from jax.experimental.pallas import tpu as pltpu
from jax.sharding import PartitionSpec as P

HEADS = 12
HEAD_DIM = 64
DOC_MAX = 4096
EPSILON = 1e-05
GELU_SCALE = 0.7978845608028654
EXCLUDED = -1e30
WIDTH = 256
SPLITS = 3
BF16 = jnp.bfloat16
F32 = jnp.float32
MESH = pl.DeviceIdType.MESH
ANY = pl.BlockSpec(memory_space=pl.ANY)
WHOLE = pl.BlockSpec(memory_space=pltpu.VMEM)
NT = (((1,), (1,)), ((), ()))
TN = (((0,), (0,)), ((), ()))


def dotf(left, right, dims=None):
    if dims is None:
        dims = (((1,), (0,)), ((), ()))
    return lax.dot_general(left, right, dims, preferred_element_type=F32)


def remote(src, dst, send_sem, recv_sem, head, blk):
    return pltpu.make_async_remote_copy(
        src_ref=src,
        dst_ref=dst,
        send_sem=send_sem,
        recv_sem=recv_sem,
        device_id={"head": head, "blk": blk},
        device_id_type=MESH,
    )


def greet(partners):
    barrier = pltpu.get_barrier_semaphore()
    for head, blk in partners:
        pl.semaphore_signal(
            barrier, inc=1, device_id={"head": head, "blk": blk}, device_id_type=MESH
        )
    pl.semaphore_wait(barrier, len(partners))


def xor(value, bit):
    return value + bit - 2 * bit * (lax.div(value, bit) % 2)


def partners_of(head, blk, nblk, heads=True, blks=True):
    found = []
    if heads:
        found += [(xor(head, 1), blk), (xor(head, 2), blk), (3 - head, blk)]
    if blks:
        found += [(head, lax.rem(blk + d, nblk)) for d in range(1, nblk)]
    return found


class Line:
    def __init__(self, nblk, head, blk, source, target, up, down, across):
        self.half, self.head, self.blk = nblk // 2, head, blk
        self.place, self.parity = lax.div(blk, 2), lax.rem(blk, 2)
        self.source, self.target = source, target
        self.sems = {"up": up, "down": down, "across": across}

    def copy(self, way, origin, step, fresh=False):
        slot = 2 * origin + self.parity
        to = {
            "up": lax.rem(self.blk + 2, 2 * self.half),
            "down": lax.rem(self.blk + 2 * self.half - 2, 2 * self.half),
            "across": self.blk + 1 - 2 * self.parity,
        }[way]
        send, recv = self.sems[way]
        return remote(
            self.source if fresh else self.target.at[slot],
            self.target.at[slot], send.at[step], recv.at[step], self.head, to,
        )

    def landing(self, way, slot, step):
        send, recv = self.sems[way]
        other = self.blk + 1 - 2 * self.parity
        at = self.target.at[slot]
        return remote(at, at, send.at[step], recv.at[step], self.head, other)

    def begin(self):
        @pl.when(self.place + 1 < self.half)
        def _():
            self.copy("up", self.place, 0, True).start()

        @pl.when(self.place > 0)
        def _():
            self.copy("down", self.place, 0, True).start()

        self.copy("across", self.place, self.place, True).start()

    def step(self, s, then=None):
        low, high = self.place - 1 - s, self.place + 1 + s

        @pl.when(low >= 0)
        def _():
            self.landing("up", 2 * low + self.parity, s).wait_recv()
            if s + 1 < self.half - 1:

                @pl.when(self.place + 1 < self.half)
                def _():
                    self.copy("up", low, s + 1).start()

            self.copy("across", low, low).start()
            if then:
                then(2 * low + self.parity)

        @pl.when(high < self.half)
        def _():
            self.landing("down", 2 * high + self.parity, s).wait_recv()
            if s + 1 < self.half - 1:

                @pl.when(self.place > 0)
                def _():
                    self.copy("down", high, s + 1).start()

            self.copy("across", high, high).start()
            if then:
                then(2 * high + self.parity)

    def land(self, origin):
        self.landing("across", 2 * origin + 1 - self.parity, origin).wait_recv()

    def finish(self):
        for o in range(self.half):
            self.copy("across", o, o).wait_send()
        for s in range(self.half - 1):

            @pl.when((self.place - s >= 0) & (self.place + 1 < self.half))
            def _():
                self.copy("up", self.place - s, s).wait_send()

            @pl.when((self.place + s < self.half) & (self.place > 0))
            def _():
                self.copy("down", self.place + s, s).wait_send()


def tail_kernel(
    nblk, pieces, cols, d_q, d_k, d_v, normed, w_qk, w_v, gain_m, kept_a, got_a, kept_b, got_b, tok, resid, gain,
    out_grad, out_q, out_k, out_v, out_first, out_gain_a, out_gain_m, out_up, out_down, out_out,
    grad, weights, gains, joined, weight, acc,
    tok_buf, resid_buf, normed_buf, load_sem, first_got, rest_sum,
    core_buf, side_out, side_buf, pair_buf, line_out, line_in, v_sum, v_got,
    gain_buf, gain_sum, gain_got, up_out, up_in, down_out, down_in,
    own_sem, send_s, recv_s, send_x, recv_x, send_y, recv_y, send_l, recv_l,
    send_v, recv_v, send_f, recv_f, send_g, recv_g, send_h, recv_h, send_u, recv_u, send_d, recv_d,
):
    head, blk = lax.axis_index("head"), lax.axis_index("blk")
    side, core, far = xor(head, 2), xor(head, 1), 3 - head
    size = grad.shape[1]
    turns = (far, side, core, head)
    loads = [
        pltpu.make_async_copy(
            normed.at[pl.ds(pl.multiple_of(t * size, size), size)], normed_buf.at[i], load_sem.at[i]
        )
        for i, t in enumerate(turns)
    ]
    loads += [
        pltpu.make_async_copy(tok, tok_buf, load_sem.at[4]),
        pltpu.make_async_copy(resid, resid_buf, load_sem.at[5]),
    ]
    for copy in loads:
        copy.start()
    greet(partners_of(head, blk, nblk))
    rows = grad.shape[1] // pieces
    line, place, parity = nblk // 2, lax.div(blk, 2), lax.rem(blk, 2)
    pair = blk + 1 - 2 * parity
    above, below = lax.rem(blk + 2, nblk), lax.rem(blk + nblk - 2, nblk)

    def part(ref, p):
        return ref.at[pl.ds(p * rows, rows)]

    def to_core(i, p, slot):
        return remote(
            part(grad.at[slot], p), part(core_buf.at[i], p), send_s.at[i, p], recv_s.at[i, p],
            core, blk,
        )

    def to_side(p):
        return remote(
            part(side_out, p), part(side_buf, p), send_x.at[p], recv_x.at[p], side, blk
        )

    def sum_of(t):
        first_part = kept_b[t].astype(F32) + got_b[t].astype(F32)
        return jnp.concatenate([first_part, kept_a[t].astype(F32) + got_a[t].astype(F32)], axis=1)

    def up_copy(t, to):
        return remote(up_out.at[t], up_in.at[t], send_u.at[t], recv_u.at[t], head, to)

    def down_copy(t, to):
        return remote(down_out.at[t], down_in.at[t], send_d.at[t], recv_d.at[t], head, to)

    def first_hops():
        for n in range(line - 1):
            t = line - 1 - n

            @pl.when((place == 0) & (place < t))
            def _():
                up_out[t] = sum_of(t).astype(BF16)
                up_copy(t, above).start()

            @pl.when((place == line - 1) & (place > n))
            def _():
                down_out[n] = sum_of(n).astype(BF16)
                down_copy(n, below).start()

    def next_hops(n):
        t = line - 1 - n

        @pl.when((place > 0) & (place < t))
        def _():
            up_copy(t, above).wait_recv()
            up_out[t] = (sum_of(t) + up_in[t].astype(F32)).astype(BF16)
            up_copy(t, above).start()

        @pl.when((place < line - 1) & (place > n))
        def _():
            down_copy(n, below).wait_recv()
            down_out[n] = (sum_of(n) + down_in[n].astype(F32)).astype(BF16)
            down_copy(n, below).start()

    first_hops()
    half, kind = lax.div(head, 2), lax.rem(head, 2)

    def first_copy(i, to, slot):
        source = d_v.at[pl.ds(to * grad.shape[1], grad.shape[1])]
        return remote(source, first_got.at[slot], send_f.at[i], recv_f.at[slot], to, blk)

    def own_first(slot):
        source = d_v.at[pl.ds(head * grad.shape[1], grad.shape[1])]
        return pltpu.make_async_copy(source, first_got.at[slot], own_sem)

    @pl.when(half == 1)
    def _():
        for i, to in enumerate((core, side, far)):
            first_copy(i, to, kind).start()
        own_first(kind).start()

    mine = half == 0
    weight[:, : 2 * cols] = w_qk[...]
    fresh = jnp.concatenate([w_v[0], w_v[1]], axis=1)
    weight[:, 2 * cols :] = jnp.where(mine, fresh, jnp.zeros_like(fresh))
    gain_row = None
    for i, t in enumerate(turns):
        at = pl.ds(pl.multiple_of(t * grad.shape[1], grad.shape[1]), grad.shape[1])
        joined[:, :cols] = d_q[at, :]
        joined[:, cols : 2 * cols] = d_k[at, :]
        joined[:, 2 * cols : 3 * cols] = d_v[at, :]
        joined[:, 3 * cols :] = jnp.zeros((grad.shape[1], joined.shape[1] - 3 * cols), BF16)
        given = joined[...]
        whole = dotf(given[:, : 3 * cols], weight[...], NT)
        grad[t] = whole.astype(BF16)
        if i == 0:
            for p in range(pieces):
                to_core(0, p, far).start()
        if i == 2:
            for p in range(pieces):
                to_core(1, p, core).start()
        loads[i].wait()
        rows_in = normed_buf[i]
        term = jnp.sum(whole * rows_in.astype(F32), axis=0, keepdims=True)
        gain_row = term if gain_row is None else gain_row + term
        term = dotf(rows_in, given, TN)
        acc[...] = term if i == 0 else acc[...] + term
        if i == 2:
            for p in range(pieces):
                to_core(0, p, far).wait_recv()
                part(side_out, p)[...] = (
                    part(grad.at[side], p)[...].astype(F32)
                    + part(core_buf.at[0], p)[...].astype(F32)
                ).astype(BF16)
                to_side(p).start()
    whole_part = weights.shape[1]
    for b in range(nblk):
        weights[b] = acc[b * whole_part : (b + 1) * whole_part].astype(BF16)

    def across(n):
        return remote(
            weights.at[2 * n + 1 - parity], pair_buf.at[n], send_y.at[n], recv_y.at[n], head, pair
        )

    for n in range(line):
        across(n).start()
    gain_row = gain_row / gain[...]
    for b in range(nblk):
        gains[b, 0] = gain_row[:, b * whole_part : (b + 1) * whole_part]
        gains[b, 1] = gain_m[:, b * whole_part : (b + 1) * whole_part]

    def gain_to(d):
        to = lax.rem(blk + d, nblk)
        return remote(gains.at[to], gain_buf.at[blk], send_g.at[d], recv_g.at[d], head, to)

    def gain_from(d):
        source = lax.rem(blk - d + nblk, nblk)
        return remote(gains.at[0], gain_buf.at[source], send_g.at[d], recv_g.at[d], head, source)

    for d in range(1, nblk):
        gain_to(d).start()
    gain_buf[blk] = gains[blk]

    def along(d, to):
        return remote(
            line_out.at[to], line_in.at[d], send_l.at[d], recv_l.at[d], head, 2 * to + parity
        )

    next_hops(0)
    for n in range(line):
        across(n).wait_recv()
        line_out[n] = (
            weights[2 * n + parity].astype(F32) + pair_buf[n].astype(F32)
        ).astype(BF16)
    for d in range(1, line):
        along(d, lax.rem(place + d, line)).start()
    for d in range(1, nblk):
        gain_from(d).wait_recv()
    gain_sum[...] = jnp.sum(gain_buf[...], axis=0)
    peers = (core, side, far)

    def gain_copy(i, to):
        return remote(gain_sum, gain_got.at[i], send_h.at[i], recv_h.at[i], to, blk)

    for i, to in enumerate(peers):
        gain_copy(i, to).start()
    for n in range(1, line - 1):
        next_hops(n)
    total = line_out[place].astype(F32)
    for d in range(1, line):
        along(d, lax.rem(place - d + line, line)).wait_recv()
        total = total + line_in[d].astype(F32)
    out_q[...] = total[:, :cols]
    out_k[...] = total[:, cols : 2 * cols]
    v_sum[0] = total[:, 2 * cols : 2 * cols + cols // 2]
    v_sum[1] = total[:, 2 * cols + cols // 2 : 3 * cols]

    def give(c, to):
        return remote(v_sum.at[c], v_got, send_v.at[c], recv_v.at[0], to, blk)

    for c in range(2):
        to = 2 * head + c

        @pl.when((half == 0) & (to != head))
        def _():
            give(c, to).start()

    for copy in loads[4:]:
        copy.wait()
    for p in range(pieces):
        to_core(1, p, core).wait_recv()
        to_side(p).wait_recv()
        norm_grad = (
            part(grad.at[head], p)[...].astype(F32)
            + part(core_buf.at[1], p)[...].astype(F32)
            + part(side_buf, p)[...].astype(F32)
        )
        xhat, scale = statistics(part(tok_buf, p)[...].astype(F32))
        part(out_grad, p)[...] = part(resid_buf, p)[...] + norm_back(norm_grad, xhat, scale, gain[...])
    rest_sum[...] = sum_of(place)
    for t in range(line):

        @pl.when((place == t) & (place > 0))
        def _():
            up_copy(t, above).wait_recv()
            rest_sum[...] += up_in[t].astype(F32)

        @pl.when((place == t) & (place < line - 1))
        def _():
            down_copy(t, below).wait_recv()
            rest_sum[...] += down_in[t].astype(F32)

    inner = out_up.shape[1]
    cut = kept_b.shape[2]
    out_up[...] = rest_sum[:, cut : cut + inner]
    out_down[:, :cut] = rest_sum[:, :cut]
    out_down[:, cut:] = rest_sum[:, cut + inner : 2 * inner]
    out_out[...] = rest_sum[:, 2 * inner :].T
    for i, to in enumerate(peers):
        gain_copy(i, to).wait_recv()
    gain_total = gain_sum[...] + gain_got[0] + gain_got[1] + gain_got[2]
    out_gain_a[...] = gain_total[0]
    out_gain_m[...] = gain_total[1]

    @pl.when(head == 0)
    def _():
        out_v[...] = v_sum[0]

    @pl.when(head != 0)
    def _():
        give(0, half).wait_recv()
        out_v[...] = v_got[...]

    for slot in range(2):

        @pl.when(head == 2 + slot)
        def _():
            own_first(slot).wait()

        @pl.when(head != 2 + slot)
        def _():
            first_copy(0, 2 + slot, slot).wait_recv()

    out_first[...] = jnp.concatenate([first_got[0], first_got[1]], axis=1).astype(F32)

    @pl.when(half == 1)
    def _():
        for i, to in enumerate((core, side, far)):
            first_copy(i, to, kind).wait_send()

    for c in range(2):
        to = 2 * head + c

        @pl.when((half == 0) & (to != head))
        def _():
            give(c, to).wait_send()

    for i, to in enumerate(peers):
        gain_copy(i, to).wait_send()
    for p in range(pieces):
        to_core(0, p, far).wait_send()
        to_core(1, p, core).wait_send()
        to_side(p).wait_send()
    for d in range(1, nblk):
        gain_to(d).wait_send()
    for n in range(line):
        across(n).wait_send()
    for d in range(1, line):
        along(d, lax.rem(place + d, line)).wait_send()
    for t in range(line):

        @pl.when(place < t)
        def _():
            up_copy(t, above).wait_send()

        @pl.when(place > t)
        def _():
            down_copy(t, below).wait_send()


def tail(
    nblk, d_q, d_k, d_v, normed, w_qk, w_v, gain_m, kept_a, got_a, kept_b, got_b, tok, resid, gain,
    pieces=4,
):
    dma = pltpu.SemaphoreType.DMA
    row, part, cols = tok.shape, w_v.shape[1] // nblk, d_q.shape[1]
    rest = (nblk // 2, part, kept_a.shape[2] + kept_b.shape[2])
    inner = (rest[2] - cols) // 2
    padded = -(-3 * cols // 128) * 128
    gains = jax.ShapeDtypeStruct((nblk, 2, 1, part), F32)
    half, line = (part, cols // 2), nblk // 2
    piece = (2, pieces)
    vmem = lambda *shape: pltpu.VMEM(shape, BF16)
    return pl.pallas_call(
        functools.partial(tail_kernel, nblk, pieces, cols),
        out_shape=[
            jax.ShapeDtypeStruct(row, F32),
            jax.ShapeDtypeStruct((part, cols), F32),
            jax.ShapeDtypeStruct((part, cols), F32),
            jax.ShapeDtypeStruct(half, F32),
            jax.ShapeDtypeStruct((row[0], 2 * cols), F32),
            jax.ShapeDtypeStruct((1, part), F32),
            jax.ShapeDtypeStruct((1, part), F32),
            jax.ShapeDtypeStruct((part, inner), F32),
            jax.ShapeDtypeStruct((part, inner), F32),
            jax.ShapeDtypeStruct((cols, part), F32),
        ],
        in_specs=[WHOLE] * 3 + [ANY] + [WHOLE] * 7 + [ANY] * 2 + [WHOLE],
        out_specs=[WHOLE] * 10,
        scratch_shapes=[
            vmem(4, *row), vmem(nblk, part, padded), pltpu.VMEM(gains.shape, F32),
            vmem(row[0], padded), vmem(row[1], 3 * cols), pltpu.VMEM((row[1], padded), F32),
            vmem(*row), pltpu.VMEM(row, F32), vmem(4, *row), dma((6,)),
            vmem(2, row[0], cols), pltpu.VMEM(rest[1:], F32),
            vmem(2, *row), vmem(*row), vmem(*row),
            vmem(line, part, padded), vmem(line, part, padded),
            vmem(line, part, padded),
            pltpu.VMEM((2,) + half, F32),
            pltpu.VMEM(half, F32),
            pltpu.VMEM(gains.shape, F32),
            pltpu.VMEM(gains.shape[1:], F32),
            pltpu.VMEM((3,) + gains.shape[1:], F32),
            vmem(*rest), vmem(*rest), vmem(*rest), vmem(*rest),
            dma,
            dma(piece), dma(piece),
            dma((pieces,)), dma((pieces,)),
            dma((line,)), dma((line,)), dma((line,)), dma((line,)),
            dma((2,)), dma((1,)),
            dma((3,)), dma((2,)),
            dma((nblk,)), dma((nblk,)),
            dma((3,)), dma((3,)),
            dma((line,)), dma((line,)), dma((line,)), dma((line,)),
        ],
        compiler_params=pltpu.CompilerParams(
            collective_id=4, has_side_effects=True, vmem_limit_bytes=60 << 20
        ),
        name="tail",
    )(d_q, d_k, d_v, normed, w_qk, w_v, gain_m, kept_a, got_a, kept_b, got_b, tok, resid, gain)


def settle_kernel(count, *refs):
    sources, targets, sems = refs[:count], refs[count : 2 * count], refs[2 * count]
    copies = [
        pltpu.make_async_copy(source, target, sems.at[i])
        for i, (source, target) in enumerate(zip(sources, targets))
    ]
    for copy in copies:
        copy.start()
    for copy in copies:
        copy.wait()


def settle(arrays):
    count = len(arrays)
    return pl.pallas_call(
        functools.partial(settle_kernel, count),
        out_shape=[jax.ShapeDtypeStruct(a.shape, a.dtype) for a in arrays],
        in_specs=[ANY] * count,
        out_specs=[WHOLE] * count,
        scratch_shapes=[pltpu.SemaphoreType.DMA((count,))],
        name="settle",
    )(*arrays)


def statistics(values):
    center = values - jnp.mean(values, axis=-1, keepdims=True)
    scale = lax.rsqrt(jnp.mean(jnp.square(center), axis=-1, keepdims=True) + EPSILON)
    return center * scale, scale


def norm_back(grad, xhat, scale, gain):
    eg = grad * gain
    return scale * (
        eg
        - jnp.mean(eg, axis=-1, keepdims=True)
        - xhat * jnp.mean(eg * xhat, axis=-1, keepdims=True)
    )


def split_parts(values):
    high = values.astype(BF16).astype(F32)
    middle = (values - high).astype(BF16).astype(F32)
    return high, middle, values - high - middle


def front_kernel(
    nblk, parts, pieces, early, tok, first, w_q, w_k, w_v, w_up, w_down, w_out, gain_a, gain_m,
    normed, query, own, near_far, rest, qk_all, v_all, attn_gain, mlp_gain,
    tok_all, first_all, v_own, gain_all, w_qk, w_rest, gains, weight, normed_buf,
    own_sem, normed_sem, send_t, recv_t, send_s, recv_s, send_p, recv_p, send_w, recv_w,
    send_v, recv_v, qk_u, qk_ur, qk_d, qk_dr, qk_a, qk_ar, up_u, up_ur, up_d, up_dr, up_a, up_ar,
    send_x, recv_x, send_c, recv_c, send_f, recv_f, send_z, recv_z, send_y, recv_y,
):
    head, blk = lax.axis_index("head"), lax.axis_index("blk")
    side, core, beyond = xor(head, 2), xor(head, 1), 3 - head
    odd, place = lax.rem(blk, 2), lax.div(blk, 2)
    near = blk + 1 - 2 * odd
    up, down = lax.rem(blk + 2, nblk), lax.rem(blk + nblk - 2, nblk)
    greet(partners_of(head, blk, nblk))
    moved = [(tok, tok_all), (first, first_all)]
    weights = [(w_v, v_own), (gains, gain_all)]
    rows = tok.shape[0] // parts

    def part(ref, n):
        return ref.at[pl.ds(n * rows, rows)]

    def hop(sems, k, n, source, slot, target):
        dst = part(moved[k][1].at[slot], n)
        return remote(source, dst, sems[0].at[k, n], sems[1].at[k, n], target, blk)

    ts, ss, ps = (send_t, recv_t), (send_s, recv_s), (send_p, recv_p)
    order = [(k, n) for n in range(parts) for k in range(2)]
    for k, n in order:
        hop(ts, k, n, part(moved[k][0], n), head, side).start()
    cols, inner = w_q.shape[1], w_up.shape[1]
    w_qk[:, :cols] = w_q[...]
    w_qk[:, cols:] = w_k[...]
    qk_line = Line(nblk, head, blk, w_qk, qk_all, (qk_u, qk_ur), (qk_d, qk_dr), (qk_a, qk_ar))
    qk_line.begin()
    w_rest[:, :inner] = w_up[...]
    w_rest[:, inner : 2 * inner] = w_down[...]
    w_rest[:, 2 * inner :] = w_out[...].T
    line = Line(
        nblk, head, blk, w_rest, rest.at[head], (up_u, up_ur), (up_d, up_dr), (up_a, up_ar)
    )
    line.begin()
    gains[0] = gain_a[...]
    gains[1] = gain_m[...]

    def chunk(sems, slot, b, to, source=None):
        at = rest.at[slot, b]
        return remote(at if source is None else source, at, sems[0].at[b], sems[1].at[b], to, blk)

    xs, cs, fs = (send_x, recv_x), (send_c, recv_c), (send_f, recv_f)

    def to_core(b, source=None):
        chunk(cs, head, b, core, source).start()

    def to_side(b, source=None):
        @pl.when(b < early)
        def _():
            chunk(xs, head, b, side, source).start()

    to_core(blk, w_rest)
    own_rest = pltpu.make_async_copy(w_rest, rest.at[head, blk], own_sem)
    own_rest.start()

    def spread(d):
        to = lax.rem(blk + d, nblk)
        return [
            remote(src, dst.at[blk], send_w.at[i, d], recv_w.at[i, d], head, to)
            for i, (src, dst) in enumerate(weights)
        ]

    def from_peer(d):
        source = lax.rem(blk - d + nblk, nblk)
        return [
            remote(src, dst.at[source], send_w.at[i, d], recv_w.at[i, d], head, source)
            for i, (src, dst) in enumerate(weights)
        ]

    for d in range(1, nblk):
        for copy in spread(d):
            copy.start()
    for k, n in order:
        hop(ss, k, n, part(moved[k][0], n), head, core).start()
    tok_all[head] = tok[...]
    first_all[head] = first[...]
    v_own[blk] = w_v[...]
    gain_all[blk] = gains[...]
    qk_all[blk] = w_qk[...]

    def pass_on(k, n):
        landed = part(moved[k][1].at[side], n)
        hop(ts, k, n, landed, side, side).wait_recv()
        hop(ps, k, n, landed, side, core).start()

    steps = nblk // 2 - 1
    for s in range(steps):
        qk_line.step(s)
    for s in range(steps):
        line.step(s, to_core)
        for k, n in order[s * len(order) // steps : (s + 1) * len(order) // steps]:
            pass_on(k, n)
    to_side(blk, w_rest)
    for s in range(steps):

        @pl.when(place - 1 - s >= 0)
        def _():
            to_side(blk - 2 - 2 * s)

        @pl.when(place + 1 + s < nblk // 2)
        def _():
            to_side(blk + 2 + 2 * s)

    for d in range(1, nblk):
        for copy in from_peer(d):
            copy.wait_recv()
    half, kind = lax.div(head, 2), lax.rem(head, 2)
    for i in range(2):
        target = half + 2 * i

        @pl.when(target == head)
        def _():
            v_all[kind] = v_own[...]

        @pl.when(target != head)
        def _():
            remote(v_own, v_all.at[kind], send_v.at[i], recv_v.at[kind], target, blk).start()

    for o in range(nblk // 2):
        qk_line.land(o)
    for c in range(2):
        source = 2 * kind + c

        @pl.when(source != head)
        def _():
            remote(v_own, v_all.at[c], send_v.at[0], recv_v.at[c], source, blk).wait_recv()

    attn_gain[...] = jnp.concatenate([gain_all[b, 0] for b in range(nblk)], axis=1)
    mlp_gain[...] = jnp.concatenate([gain_all[b, 1] for b in range(nblk)], axis=1)

    step = own.shape[0] // pieces

    def slab(ref, n):
        return ref.at[pl.ds(n * step, step)]

    def far_copy(n, to):
        return remote(slab(own, n), slab(near_far.at[0], n), send_z.at[n], recv_z.at[n], head, to)

    def near_copy(n, src):
        return remote(src, slab(near_far.at[1], n), send_y.at[n], recv_y.at[n], head, near)

    size = HEAD_DIM
    pair = 2 * size
    width = tok.shape[1]
    block = w_q.shape[0]
    for b in range(nblk):
        at = pl.ds(b * block, block)
        both, fresh = qk_all[b], jnp.concatenate([v_all[0, b], v_all[1, b]], axis=1)
        key = both[:, cols:]
        weight[at, :pair] = key[:, :pair]
        weight[at, pair : 2 * pair] = fresh[:, :pair]
        weight[at, 2 * pair : 3 * pair] = jnp.concatenate([key[:, pair:], fresh[:, pair:]], axis=1)
        weight[at, 3 * pair :] = jnp.concatenate(
            [both[:, :cols], jnp.zeros((block, WIDTH - cols), BF16)], axis=1
        )
    def make_rows(i, carry):
        t = jnp.where(i == 0, head, jnp.where(i == 1, side, jnp.where(i == 2, core, beyond)))

        @pl.when(i == 2)
        def _():
            for k, n in order:
                hop(ss, k, n, part(moved[k][1].at[core], n), core, core).wait_recv()

        @pl.when(i == 3)
        def _():
            for k, n in order:
                hop(ps, k, n, part(moved[k][1].at[beyond], n), beyond, core).wait_recv()
        total = tok.shape[0]
        at = pl.ds(pl.multiple_of(t * total, total), total)
        xhat, _ = statistics(tok_all[t].astype(F32))
        row = (xhat * attn_gain[...]).astype(BF16)
        normed_buf[t] = row
        pltpu.make_async_copy(normed_buf.at[t], normed.at[at], normed_sem.at[i]).start()
        out = dotf(row, weight[...])
        query[at, :] = (out[:, 3 * pair :].astype(BF16).astype(F32) * size**-0.5).astype(BF16)
        done = out[:, : 3 * pair].astype(BF16)
        given = first_all[t]
        kept = jnp.where(kind == 0, given[:, :cols], given[:, cols:])
        other = jnp.concatenate(
            [done[:, :pair], kept[:, :pair], done[:, 2 * pair : 2 * pair + size], kept[:, pair:]],
            axis=1,
        )
        own[at, :] = jnp.where(half == 0, done, other)
        for n in range(pieces // 4):
            n = t * (pieces // 4) + n

            @pl.when(blk + 2 < nblk)
            def _():
                far_copy(n, up).start()

            @pl.when(odd == 0)
            def _():
                near_copy(n, slab(own, n)).start()

        return carry

    lax.fori_loop(0, 4, make_rows, 0)
    for o in range(nblk // 2):

        line.land(o)
        to_core(2 * o + 1 - odd)
        to_side(2 * o + 1 - odd)

    for i, t in enumerate((head, side, core, beyond)):
        for n in range(pieces // 4):
            n = t * (pieces // 4) + n

            @pl.when(blk >= 2)
            def _():
                far_copy(n, down).wait_recv()

            @pl.when((blk >= 2) & (odd == 1))
            def _():
                near_copy(n, slab(near_far.at[0], n)).start()

    own_rest.wait()
    for b in range(early):
        chunk(xs, side, b, side).wait_recv()
        chunk(fs, side, b, core).start()
    for b in range(nblk):
        chunk(cs, core, b, core).wait_recv()
    for b in range(early):
        chunk(fs, beyond, b, core).wait_recv()
        chunk(xs, head, b, side).wait_send()
        chunk(fs, side, b, core).wait_send()
    for b in range(nblk):
        chunk(cs, head, b, core).wait_send()
    for i in range(4):
        at = pl.ds(0, tok.shape[0])
        pltpu.make_async_copy(normed_buf.at[i], normed.at[at], normed_sem.at[i]).wait()
    for n in range(pieces):

        @pl.when((blk >= 2) | (odd == 1))
        def _():
            near_copy(n, slab(own, n)).wait_recv()

        @pl.when(blk + 2 < nblk)
        def _():
            far_copy(n, up).wait_send()

        @pl.when((blk >= 2) | (odd == 0))
        def _():
            near_copy(n, slab(own, n)).wait_send()

    for i in range(2):
        target = half + 2 * i

        @pl.when(target != head)
        def _():
            remote(v_own, v_all.at[kind], send_v.at[i], recv_v.at[kind], target, blk).wait_send()

    for k, n in order:
        hop(ts, k, n, part(moved[k][0], n), head, side).wait_send()
        hop(ss, k, n, part(moved[k][0], n), head, core).wait_send()
        hop(ps, k, n, part(moved[k][1].at[side], n), side, core).wait_send()
    for d in range(1, nblk):
        for copy in spread(d):
            copy.wait_send()
    qk_line.finish()
    line.finish()


def front(
    nblk, early, tok, first, w_q, w_k, w_v, w_up, w_down, w_out, gain_a, gain_m, parts=4, pieces=8
):
    dma = pltpu.SemaphoreType.DMA
    (rows, width), (part, cols) = tok.shape, w_q.shape
    total = 4 * rows
    both = w_up.shape[1] + w_down.shape[1] + w_out.shape[0]
    low = lambda *shape: jax.ShapeDtypeStruct(shape, BF16)
    vmem = lambda *shape: pltpu.VMEM(shape, BF16)
    line = [dma((nblk // 2,))] * 6
    return pl.pallas_call(
        functools.partial(front_kernel, nblk, parts, pieces, early),
        out_shape=[
            low(total, width),
            low(total, WIDTH),
            low(total, 2 * cols),
            low(2, total, 2 * cols),
            low(4, nblk, part, both),
            low(nblk, part, 2 * cols),
            low(2, nblk, *w_v.shape),
            jax.ShapeDtypeStruct((1, width), F32),
            jax.ShapeDtypeStruct((1, width), F32),
        ],
        in_specs=[WHOLE] * 10,
        out_specs=[ANY, WHOLE, WHOLE, ANY, ANY] + [WHOLE] * 4,
        scratch_shapes=[
            vmem(4, *tok.shape),
            vmem(4, *first.shape),
            vmem(nblk, *w_v.shape),
            pltpu.VMEM((nblk, 2) + gain_a.shape, F32),
            vmem(part, 2 * cols),
            vmem(part, both),
            pltpu.VMEM((2,) + gain_a.shape, F32),
            vmem(width, 2 * cols + WIDTH),
            vmem(4, *tok.shape),
            dma,
            dma((4,)),
        ]
        + [dma((2, parts))] * 6
        + [dma((2, nblk))] * 2
        + [dma((2,))] * 2
        + line * 2
        + [dma((nblk,))] * 6
        + [dma((pieces,))] * 4,
        compiler_params=pltpu.CompilerParams(
            collective_id=0, has_side_effects=True, vmem_limit_bytes=56 << 20
        ),
        name="front",
    )(tok, first, w_q, w_k, w_v, w_up, w_down, w_out, gain_a, gain_m)


def gelu_both(pre):
    square = pre * pre
    inner = jnp.tanh(GELU_SCALE * (pre + 0.044715 * square * pre))
    slope = GELU_SCALE * (1.0 + 3.0 * 0.044715 * square)
    outer = 0.5 * (1.0 + inner)
    return pre * outer, outer + 0.5 * pre * (1.0 - inner * inner) * slope


def middle_kernel(
    nblk, up_cols, cut, pieces, tok, mixed_parts, cot, gain, gathered, late, query,
    out, grad_resid, grad_wide, gain_part, keep_a, give_a, keep_b, give_b, query_later,
    up, down, w_out, up_grad, down_grad, out_grad, mixed, wide_parts, up_got, down_got, out_got,
    sems, out_sems, send_m, recv_m, send_g, recv_g, send_c, recv_c,
    send_z, recv_z, send_y, recv_y, hidden_all, pre_all, normed_t, cot_t, total, grad_normed, normed_rows, branch_rows, branch_t, late_far, send_l, recv_l,
):
    head, blk = lax.axis_index("head"), lax.axis_index("blk")
    x, core_index = lax.div(head, 2), lax.rem(head, 2)
    core = xor(head, 1)
    others = [xor(head, 2), 3 - head, core]
    odd = lax.rem(blk, 2)
    pair = blk + 1 - 2 * odd
    above, below = lax.rem(blk + 2, nblk), lax.rem(blk + nblk - 2, nblk)
    greet(partners_of(head, blk, nblk, blks=False) + [(head, b) for b in (pair, above, below)])
    heads_of = 4
    part = gathered.shape[2]
    cols = mixed.shape[2]
    heads = cols // HEAD_DIM

    def mixed_copy(i, to, slot):
        return remote(
            mixed_parts.at[to], mixed.at[slot], send_m.at[i], recv_m.at[i], to, blk
        )

    for i, to in enumerate(others):
        mixed_copy(i, to, head).start()
    late_copy = remote(late, late_far, send_l, recv_l, core, blk)
    late_copy.start()
    early = nblk - late.shape[0]
    piece_rows = query.shape[0] // pieces

    def slab(ref, p):
        return ref.at[pl.ds(p * piece_rows, piece_rows)]

    def far_copy(p, to):
        dst = slab(query_later.at[1], p)
        return remote(slab(query, p), dst, send_z.at[p], recv_z.at[p], head, to)

    def near_copy(p, src):
        return remote(src, slab(query_later.at[0], p), send_y.at[p], recv_y.at[p], head, pair)

    for p in range(pieces):

        @pl.when(blk >= 2)
        def _():
            far_copy(p, below).start()

        @pl.when(odd == 1)
        def _():
            near_copy(p, slab(query, p)).start()

    def relay(p):
        @pl.when(blk + 2 < nblk)
        def _():
            far_copy(p, above).wait_recv()

        @pl.when((blk + 2 < nblk) & (odd == 0))
        def _():
            near_copy(p, slab(query_later.at[1], p)).start()

    chunks = [2 * n + c for n in (1 - x, x) for c in (1 - core_index, core_index)]
    side = others[0]
    sources = (3 - head, others[0], core)

    def source(i, b):
        if b < early or i > 1:
            return gathered.at[chunks[i], b]
        return (late_far, late)[i].at[b - early]

    def load(i, which):
        target, lo, size = ((w_out, 2 * up_cols, cols), (up, 0, up_cols), (down, up_cols, up_cols))[
            which
        ]
        return [
            pltpu.make_async_copy(
                source(i, b).at[:, pl.ds(lo, size)],
                target.at[i, pl.ds(b * part, part)],
                sems.at[which, i, b],
            )
            for b in range(nblk)
        ]

    turns = (2, 3, 1, 0)
    order = [(i, 0) for i in turns] + [(i, w) for i in turns for w in (1, 2)]
    for i, which in order:
        for b, copy in enumerate(load(i, which)):
            if i or b < early:
                copy.start()
    mixed[head] = mixed_parts[head]
    late_copy.wait()
    for which in range(3):
        for copy in load(0, which)[early:]:
            copy.start()
    for i in range(heads_of):
        for copy in load(i, 0):
            copy.wait()
    for i, to in enumerate(others):
        mixed_copy(i, to, to).wait_recv()
    branch = None
    for i in range(heads_of):
        term = dotf(mixed[chunks[i]], w_out[i], NT)
        branch = term if branch is None else branch + term
    resid = tok[...].astype(F32) + branch
    xhat, scale = statistics(resid)
    normed = (xhat * gain[...]).astype(BF16)
    cotangent = cot[...]
    total[...] = resid
    grad_normed[...] = jnp.zeros_like(resid)

    def chunk_of(i):
        far = jnp.where(i < 2, 1 - x, x)
        return 2 * far + jnp.where(lax.rem(i, 2) == 0, 1 - core_index, core_index)

    def to_core(n, k):
        mine, theirs = ((up_grad, up_got), (down_grad, down_got), (out_grad, out_got))[k]
        return remote(mine.at[2 * n], theirs.at[n], send_c.at[k, n], recv_c.at[k, n], core, blk)

    normed_rows[...] = normed
    normed_t[...] = normed.T
    cot_t[...] = cotangent.T
    def arrived(which, i):
        target = (w_out, up, down)[which].at[i, pl.ds(0, part)]
        for b in range(nblk):
            pltpu.make_async_copy(target, target, sems.at[which, i, b]).wait()

    def forward(n, carry):
        i = jnp.where(n < 2, n + 2, 3 - n)
        arrived(1, i)
        arrived(2, i)
        hidden, slope = gelu_both(dotf(normed_rows[...], up[i]))
        hidden_all[i] = hidden.astype(BF16)
        pre_all[i] = (slope * dotf(cot[...], down[i])).astype(BF16)
        total[...] += dotf(hidden_all[i], down[i], NT)
        grad_normed[...] += dotf(pre_all[i], up[i], NT)

        @pl.loop(0, pieces // heads_of)
        def _(p):
            relay(n * (pieces // heads_of) + p)

        return carry

    lax.fori_loop(0, heads_of, forward, 0)
    grad = cotangent.astype(F32) + norm_back(grad_normed[...], xhat, scale, gain[...])
    branch_grad = grad.astype(BF16)
    lane = lax.broadcasted_iota(jnp.int32, (tok.shape[0], WIDTH), 1)

    def wide_copy(i, to, slot):
        return remote(
            wide_parts.at[to], grad_wide.at[slot], send_g.at[i], recv_g.at[i], to, blk
        )

    branch_rows[...] = branch_grad

    def widen(i, carry):
        h = chunk_of(i)
        rows = dotf(branch_rows[...], w_out[i]).astype(BF16).astype(F32)
        product = rows * mixed[h].astype(F32)
        wide = jnp.concatenate([rows, jnp.zeros((rows.shape[0], WIDTH - cols), F32)], axis=1)
        for k in range(heads):
            delta = jnp.sum(
                product[:, k * HEAD_DIM : (k + 1) * HEAD_DIM], axis=1, keepdims=True
            )
            for c, piece in enumerate(split_parts(-delta)):
                wide = jnp.where(lane == cols + SPLITS * k + c, piece, wide)
        wide_parts[h] = wide.astype(BF16)

        @pl.when(i < 3)
        def _():
            wide_copy(i, h, head).start()

        return carry

    lax.fori_loop(0, heads_of, widen, 0)
    grad_wide[head] = wide_parts[head]
    out[...] = total[...].astype(BF16)
    gain_part[...] = jnp.sum(grad_normed[...] * xhat, axis=0, keepdims=True)
    grad_resid[...] = grad
    branch_t[...] = branch_grad.T

    def weigh(i, carry):
        up_grad[i] = dotf(normed_t[...], pre_all[i]).astype(BF16)
        down_grad[i] = dotf(cot_t[...], hidden_all[i]).astype(BF16)
        out_grad[i] = dotf(branch_t[...], mixed[chunk_of(i)]).astype(BF16)

        @pl.when(lax.rem(i, 2) == 0)
        def _():
            for k in range(3):
                to_core(lax.div(i, 2), k).start()

        return carry

    lax.fori_loop(0, heads_of, weigh, 0)

    def store(k, source, target, lo):
        size = source.shape[1]
        return [
            pltpu.make_async_copy(
                source.at[pl.ds(b * part, part)],
                target(b).at[:, pl.ds(lo, size)],
                out_sems.at[k, b],
            )
            for b in range(nblk)
        ]

    stores = []
    for n, target in enumerate((give_a, keep_a)):
        at = 2 * n + 1
        for k, (mine, theirs) in enumerate(
            ((up_grad, up_got), (down_grad, down_got), (out_grad, out_got))
        ):
            to_core(n, k).wait_recv()
            mine[at] = (mine[at].astype(F32) + theirs[n].astype(F32)).astype(BF16)
        first_part = store(3 * n, up_grad.at[at], lambda b: target.at[b], 0)
        far_down = down_grad.at[at].at[:, pl.ds(cut, up_cols - cut)]
        first_part += store(6 + n, far_down, lambda b: target.at[b], up_cols)
        first_part += store(3 * n + 1, out_grad.at[at], lambda b: target.at[b], 2 * up_cols - cut)
        for copy in first_part:
            copy.start()
        kept = store(3 * n + 2, down_grad.at[at].at[:, pl.ds(0, cut)], lambda b: keep_b.at[n, b // 2], 0)
        given = store(3 * n + 2, down_grad.at[at].at[:, pl.ds(0, cut)], lambda b: give_b.at[n, b // 2], 0)
        for b in range(nblk):

            @pl.when(odd == b % 2)
            def _():
                kept[b].start()

            @pl.when(odd != b % 2)
            def _():
                given[b].start()

        stores += first_part + kept
    for copy in stores:
        copy.wait()
    for k in range(3):
        for n in range(2):
            to_core(n, k).wait_send()
    for i in range(3):
        wide_copy(i, chunks[i], sources[i]).wait_recv()
    for i, to in enumerate(others):
        mixed_copy(i, to, head).wait_send()
        wide_copy(i, chunks[i], head).wait_send()
    for p in range(pieces):

        @pl.when((blk + 2 < nblk) | (odd == 0))
        def _():
            near_copy(p, slab(query, p)).wait_recv()

        @pl.when(blk >= 2)
        def _():
            far_copy(p, below).wait_send()

        @pl.when((blk + 2 < nblk) | (odd == 1))
        def _():
            near_copy(p, slab(query, p)).wait_send()


def middle(nblk, tok, mixed_parts, cot, gain, gathered, late, query, up_cols, cut=512, pieces=8):
    heads_of, rows, cols = mixed_parts.shape
    width, part = tok.shape[1], gathered.shape[2]
    flops = 2 * rows * width * (6 * up_cols * heads_of + 3 * width)
    dma = pltpu.SemaphoreType.DMA
    vmem = lambda *shape: pltpu.VMEM(shape, BF16)
    return pl.pallas_call(
        functools.partial(middle_kernel, nblk, up_cols, cut, pieces),
        out_shape=[
            jax.ShapeDtypeStruct((rows, width), BF16),
            jax.ShapeDtypeStruct((rows, width), F32),
            jax.ShapeDtypeStruct((heads_of, rows, WIDTH), BF16),
            jax.ShapeDtypeStruct((1, width), F32),
            jax.ShapeDtypeStruct((nblk, part, 2 * up_cols - cut + cols), BF16),
            jax.ShapeDtypeStruct((nblk, part, 2 * up_cols - cut + cols), BF16),
            jax.ShapeDtypeStruct((2, nblk // 2, part, cut), BF16),
            jax.ShapeDtypeStruct((2, nblk // 2, part, cut), BF16),
            jax.ShapeDtypeStruct((2,) + query.shape, BF16),
        ],
        in_specs=[WHOLE] * 4 + [ANY] * 3,
        out_specs=[WHOLE] * 4 + [ANY] * 5,
        scratch_shapes=[
            vmem(heads_of, width, up_cols), vmem(heads_of, width, up_cols),
            vmem(heads_of, width, cols),
            vmem(heads_of, width, up_cols), vmem(heads_of, width, up_cols),
            vmem(heads_of, width, cols),
            vmem(heads_of, rows, cols), vmem(heads_of, rows, WIDTH),
            vmem(2, width, up_cols), vmem(2, width, up_cols), vmem(2, width, cols),
            dma((3, heads_of, nblk)), dma((8, nblk)),
            dma((3,)), dma((3,)), dma((3,)), dma((3,)), dma((3, 2)), dma((3, 2)),
            dma((pieces,)), dma((pieces,)), dma((pieces,)), dma((pieces,)),
            vmem(heads_of, rows, up_cols), vmem(heads_of, rows, up_cols),
            vmem(width, rows), vmem(width, rows),
            pltpu.VMEM((rows, width), F32), pltpu.VMEM((rows, width), F32),
            vmem(rows, width), vmem(rows, width), vmem(width, rows),
            vmem(*late.shape), dma, dma,
        ],
        compiler_params=pltpu.CompilerParams(
            collective_id=2, has_side_effects=True, vmem_limit_bytes=62 << 20
        ),
        cost_estimate=pl.CostEstimate(
            flops=flops, bytes_accessed=24 << 20, transcendentals=rows * up_cols * heads_of
        ),
        name="middle",
    )(tok, mixed_parts, cot, gain, gathered, late, query)


def pair_sum_kernel(ours_a, got_a, ours_b, got_b, keep_a, give_a, keep_b, give_b):
    odd = lax.rem(lax.axis_index("blk"), 2)
    for j in range(keep_a.shape[0]):
        sums = [
            (ours_a[2 * j + n].astype(F32) + got_a[2 * j + n].astype(F32)).astype(BF16)
            for n in range(2)
        ]
        keep_a[j] = jnp.where(odd == 0, sums[0], sums[1])
        give_a[j] = jnp.where(odd == 0, sums[1], sums[0])
        give_b[j] = (ours_b[0, j].astype(F32) + got_b[0, j].astype(F32)).astype(BF16)
        keep_b[j] = (ours_b[1, j].astype(F32) + got_b[1, j].astype(F32)).astype(BF16)


def pair_sum(ours_a, got_a, ours_b, got_b, step=2):
    nblk, part, width = ours_a.shape
    other = ours_b.shape[3]
    a_in = pl.BlockSpec((2 * step, part, width), lambda i: (i, 0, 0))
    b_in = pl.BlockSpec((2, step, part, other), lambda i: (0, i, 0, 0))
    out = lambda cols: pl.BlockSpec((step, part, cols), lambda i: (i, 0, 0))
    shape = lambda cols: jax.ShapeDtypeStruct((nblk // 2, part, cols), BF16)
    return pl.pallas_call(
        pair_sum_kernel,
        grid=(nblk // 2 // step,),
        in_specs=[a_in, a_in, b_in, b_in],
        out_specs=[out(width)] * 2 + [out(other)] * 2,
        out_shape=[shape(width)] * 2 + [shape(other)] * 2,
        cost_estimate=pl.CostEstimate(
            flops=nblk * part * width, bytes_accessed=12 * nblk * part * width, transcendentals=0
        ),
        compiler_params=pltpu.CompilerParams(vmem_limit_bytes=32 << 20),
        name="pair_sum",
    )(ours_a, got_a, ours_b, got_b)


def head_rows(h, heads, shape):
    row = lax.broadcasted_iota(jnp.int32, shape, 0)
    real = heads * HEAD_DIM
    own = (row >= h * HEAD_DIM) & (row < (h + 1) * HEAD_DIM)
    return own | ((row >= real + SPLITS * h) & (row < real + SPLITS * (h + 1)))


def per_head(wide, heads, out):
    flipped = wide.T
    for h in range(heads):
        out[h] = jnp.where(head_rows(h, heads, flipped.shape), flipped, jnp.zeros_like(flipped))


def doc_start(meta, ndocs, t):
    def step(j,c):
        cum,best=c
        best=jnp.where(cum<=t,cum,best)
        return cum+meta[1+j],best
    return lax.fori_loop(0,ndocs,step,(jnp.int32(0),jnp.int32(0)),unroll=True)[1]

def doc_end(meta, ndocs, t):
    def step(j,c):
        cum,best,found=c
        cum=cum+meta[1+j]
        take=(cum>t)&(found==0)
        return cum,jnp.where(take,cum,best),jnp.where(take,1,found)
    return lax.fori_loop(0,ndocs,step,(jnp.int32(0),jnp.int32(0),jnp.int32(0)),unroll=True)[1]

def starts_vec(meta, ndocs, t):
    def step(j,c):
        cum,best=c
        return cum+meta[1+j],jnp.where(cum<=t,cum,best)
    return lax.fori_loop(0,ndocs,step,(jnp.int32(0),jnp.zeros(t.shape,jnp.int32)))[1]

def ends_vec(meta, ndocs, t):
    def step(j,c):
        cum,best=c
        ln=meta[1+j]
        return cum+ln,jnp.where(cum<=t,cum+ln,best)
    return lax.fori_loop(0,ndocs,step,(jnp.int32(0),jnp.zeros(t.shape,jnp.int32)))[1]

def widened(columns, heads):
    rows, width = columns.shape
    ones = jnp.ones((rows, SPLITS * heads), BF16)
    empty = jnp.zeros((rows, WIDTH - width - SPLITS * heads), BF16)
    return jnp.concatenate([columns, ones, empty], axis=1)


def unpack_rows(packed, heads):
    pair = 2 * HEAD_DIM
    key = jnp.concatenate([packed[:, :pair], packed[:, 2 * pair : 2 * pair + HEAD_DIM]], axis=1)
    value = jnp.concatenate([packed[:, pair : 2 * pair], packed[:, 2 * pair + HEAD_DIM :]], axis=1)
    return widened(key, heads), widened(value, heads)


STEP = 512


def build_window(heads, start, earlier, own, packed, sems, keys, values, key_rows, value_rows):
    before = earlier.shape[0] // STEP
    chunks = before + own.shape[0] // STEP

    def copy(n, source, row):
        return pltpu.make_async_copy(
            source.at[pl.ds(row * STEP, STEP)], packed.at[pl.ds(n * STEP, STEP)], sems.at[n]
        )

    def begin(n, carry):
        @pl.when(n < before)
        def _():
            copy(n, earlier, n).start()

        @pl.when(n >= before)
        def _():
            copy(n, own, n - before).start()

        return carry

    def build(n, carry):
        copy(n, own, 0).wait()
        at = pl.ds(pl.multiple_of(n * STEP, STEP), STEP)
        key, value = unpack_rows(packed[at, :], heads)
        for wide, rows, flipped in ((key, keys, key_rows), (value, values, value_rows)):
            if rows is not None:
                rows[at, :] = wide
            if flipped is not None:
                turned = wide.T
                for h in range(heads):
                    flipped[h, :HEAD_DIM, at] = turned[h * HEAD_DIM : (h + 1) * HEAD_DIM]
        return carry

    lax.fori_loop(start, chunks, begin, 0)
    lax.fori_loop(start, chunks, build, 0)


def three(lo, a, b, hi, body):
    edge = a - lo

    def masked(n, carry):
        body(jnp.where(n < edge, lo + n, b + n - edge), True)
        return carry

    def free(n, carry):
        body(n, False)
        return carry

    lax.fori_loop(0, edge + hi - b, masked, 0)
    lax.fori_loop(a, b, free, 0)


def query_tiles(meta, ndocs, t0, wbase, tq, tk):
    lo = (doc_start(meta, ndocs, t0) - wbase) // tk
    f0 = (doc_start(meta, ndocs, t0 + tq - 1) - wbase + tk - 1) // tk
    f1 = (t0 - wbase) // tk
    hi = (t0 + tq - 1 - wbase) // tk + 1
    return lo, jnp.minimum(f0, f1), f1, hi


def fwd_kernel(heads, ndocs, tq, tk, meta, q_ref, earlier, own, mix_ref, wide_ref,
               k_ref, vt_ref, qt, m_ref, acc_ref, packed, sems):
    i = pl.program_id(0)
    width = q_ref.shape[1]
    real = heads * HEAD_DIM
    base = meta[0]
    wbase = base - earlier.shape[0]

    @pl.when(i == 0)
    def _():
        vt_ref[:, HEAD_DIM:, :] = jnp.ones_like(vt_ref[:, HEAD_DIM:, :])
        start = (doc_start(meta, ndocs, base) - wbase) // tk * (tk // STEP)
        build_window(heads, start, earlier, own, packed, sems, k_ref, None, None, vt_ref)

    t0 = base + i * tq
    lo, f0, f1, hi = query_tiles(meta, ndocs, t0, wbase, tq, tk)
    q = q_ref[...]
    trow = t0 + lax.broadcasted_iota(jnp.int32, (8, tq), 1)
    srow = starts_vec(meta, ndocs, trow)[:1]
    trow = trow[:1]
    lane = lax.broadcasted_iota(jnp.int32, (tq, width), 1)

    def visible(off):
        u = wbase + off + lax.broadcasted_iota(jnp.int32, (tk, tq), 0)
        return (u >= srow) & (u <= trow)

    itself = q.astype(F32) * k_ref[pl.ds(pl.multiple_of(t0 - wbase, tq), tq), :].astype(F32)
    shifted = q.astype(F32)
    for h in range(heads):
        mine = (lane >= h * HEAD_DIM) & (lane < (h + 1) * HEAD_DIM)
        score = jnp.sum(jnp.where(mine, itself, 0.0), axis=1, keepdims=True)
        for c, piece in enumerate(split_parts(-score)):
            shifted = jnp.where(lane == real + SPLITS * h + c, piece, shifted)
    per_head(shifted.astype(BF16), heads, qt)
    acc_ref[...] = jnp.zeros_like(acc_ref)

    def quick(j, masked):
        off = pl.multiple_of(j * tk, tk)
        k = k_ref[pl.ds(off, tk), :]
        if masked:
            vis = visible(off)
        scores = [dotf(k, qt[h]) for h in range(heads)]
        for h in range(heads):
            p = jnp.exp(scores[h])
            if masked:
                p = jnp.where(vis, p, 0.0)
            acc_ref[h] += dotf(vt_ref[h, :, pl.ds(off, tk)], p.astype(BF16))

    def finish(extra):
        rows = []
        parts = []
        for h in range(heads):
            acc = acc_ref[h]
            total = acc[HEAD_DIM : HEAD_DIM + 1]
            rows.append(acc[:HEAD_DIM] / total)
            at = real + SPLITS * h
            shift = jnp.sum(qt[h, at : at + SPLITS, :].astype(F32), axis=0, keepdims=True)
            parts += split_parts(shift - extra[h] - jnp.log(total))
        rest = jnp.zeros((width - real - len(parts), tq), F32)
        turned = jnp.concatenate(rows + parts + [rest], axis=0).T
        mix_ref[0] = turned[:, :real].astype(BF16)
        wide_ref[...] = jnp.where(lane < real, q.astype(F32), turned).astype(BF16)

    three(lo, f0, f1, hi, quick)
    none = jnp.zeros((1, tq), F32)
    finish([none] * heads)
    sums = acc_ref[:, HEAD_DIM : HEAD_DIM + 1, :]
    fits = jnp.max(jnp.where(sums < 1e30, 0.0, 1.0)) == 0.0

    @pl.when(jnp.logical_not(fits))
    def _():
        acc_ref[...] = jnp.zeros_like(acc_ref)
        m_ref[...] = jnp.full_like(m_ref, EXCLUDED)

        def body(j, carry):
            off = pl.multiple_of(j * tk, tk)
            k = k_ref[pl.ds(off, tk), :]
            vis = visible(off)
            for h in range(heads):
                s = jnp.where(vis, dotf(k, qt[h]), EXCLUDED)
                old = m_ref[h, :1]
                new = jnp.maximum(old, jnp.max(s, axis=0, keepdims=True))
                m_ref[h, :1] = new
                p = jnp.exp(s - new).astype(BF16)
                acc_ref[h] = acc_ref[h] * jnp.exp(old - new) + dotf(
                    vt_ref[h, :, pl.ds(off, tk)], p
                )
            return carry

        lax.fori_loop(lo, hi, body, 0)
        finish([m_ref[h, :1] for h in range(heads)])


SCALARS = pl.BlockSpec(memory_space=pltpu.SMEM)


def attention_fwd(meta, q, earlier, own, heads, tq, tk):
    block, width = q.shape
    window = block + earlier.shape[0]
    ndocs = meta.shape[0] - 1
    return pl.pallas_call(
        functools.partial(fwd_kernel, heads, ndocs, tq, tk),
        grid=(block // tq,),
        in_specs=[
            SCALARS,
            pl.BlockSpec((tq, width), lambda i: (i, 0)),
            ANY,
            ANY,
        ],
        out_specs=[
            pl.BlockSpec((1, tq, heads * HEAD_DIM), lambda i: (i, 0, 0)),
            pl.BlockSpec((tq, width), lambda i: (i, 0)),
        ],
        out_shape=[
            jax.ShapeDtypeStruct((block // tq, tq, heads * HEAD_DIM), BF16),
            jax.ShapeDtypeStruct((block, width), BF16),
        ],
        scratch_shapes=[
            pltpu.VMEM((window, width), BF16),
            pltpu.VMEM((heads, HEAD_DIM + 16, window), BF16),
            pltpu.VMEM((heads, width, tq), BF16),
            pltpu.VMEM((heads, 8, tq), F32),
            pltpu.VMEM((heads, HEAD_DIM + 16, tq), F32),
            pltpu.VMEM((window, own.shape[1]), BF16),
            pltpu.SemaphoreType.DMA((window // STEP,)),
        ],
        compiler_params=pltpu.CompilerParams(vmem_limit_bytes=56 << 20),
        cost_estimate=pl.CostEstimate(
            flops=30_000_000_000, bytes_accessed=12 << 20, transcendentals=20_000_000
        ),
        name="attn_fwd",
    )(meta, q, earlier, own)


def dq_kernel(heads, ndocs, tq, tk, meta, q_ref, do_ref, earlier, own, dq_ref,
              k_ref, v_ref, kt_ref, qt, dot, acc_ref, packed, sems):
    i = pl.program_id(0)
    base = meta[0]
    wbase = base - earlier.shape[0]

    @pl.when(i == 0)
    def _():
        start = (doc_start(meta, ndocs, base) - wbase) // tk * (tk // STEP)
        build_window(heads, start, earlier, own, packed, sems, k_ref, v_ref, kt_ref, None)

    t0 = base + i * tq
    per_head(q_ref[...], heads, qt)
    per_head(do_ref[...], heads, dot)
    acc_ref[...] = jnp.zeros_like(acc_ref)
    trow = t0 + lax.broadcasted_iota(jnp.int32, (8, tq), 1)
    srow = starts_vec(meta, ndocs, trow)[:1]
    trow = trow[:1]

    def body(j, masked):
        off = pl.multiple_of(j * tk, tk)
        k = k_ref[pl.ds(off, tk), :]
        v = v_ref[pl.ds(off, tk), :]
        if masked:
            u = wbase + off + lax.broadcasted_iota(jnp.int32, (tk, tq), 0)
            vis = (u >= srow) & (u <= trow)
        made = [(dotf(k, qt[h]), dotf(v, dot[h])) for h in range(heads)]
        for h in range(heads):
            p = jnp.exp(made[h][0])
            if masked:
                p = jnp.where(vis, p, 0.0)
            ds = (p * made[h][1]).astype(BF16)
            acc_ref[h] += dotf(kt_ref[h, :, pl.ds(off, tk)], ds)

    three(*query_tiles(meta, ndocs, t0, wbase, tq, tk), body)
    turned = acc_ref[...].reshape(heads * HEAD_DIM, tq).T
    dq_ref[...] = (turned * (HEAD_DIM**-0.5)).astype(BF16)


def attention_dq(meta, q, do, earlier, own, heads, tq, tk):
    block, width = q.shape
    window = block + earlier.shape[0]
    ndocs = meta.shape[0] - 1
    row = lambda w: pl.BlockSpec((tq, w), lambda i: (i, 0))
    return pl.pallas_call(
        functools.partial(dq_kernel, heads, ndocs, tq, tk),
        grid=(block // tq,),
        in_specs=[SCALARS, row(width), row(width), ANY, ANY],
        out_specs=row(heads * HEAD_DIM),
        out_shape=jax.ShapeDtypeStruct((block, heads * HEAD_DIM), BF16),
        scratch_shapes=[pltpu.VMEM((window, width), BF16)] * 2
        + [pltpu.VMEM((heads, HEAD_DIM, window), BF16)]
        + [pltpu.VMEM((heads, width, tq), BF16)] * 2
        + [pltpu.VMEM((heads, HEAD_DIM, tq), F32)]
        + [pltpu.VMEM((window, own.shape[1]), BF16), pltpu.SemaphoreType.DMA((window // STEP,))],
        compiler_params=pltpu.CompilerParams(vmem_limit_bytes=56 << 20),
        cost_estimate=pl.CostEstimate(
            flops=45_000_000_000, bytes_accessed=12 << 20, transcendentals=20_000_000
        ),
        name="attn_dq",
    )(meta, q, do, earlier, own)


def dkv_kernel(heads, ndocs, tq, tk, meta, own, q_parts, do_parts, dk_ref, dv_ref,
               q_ref, do_ref, qt_ref, dot_ref, kt, vt, dk_acc, dv_acc, sems):
    i = pl.program_id(0)
    base = meta[0]

    @pl.when(i == 0)
    def _():
        block = pl.num_programs(0) * tk
        end = (doc_end(meta, ndocs, base + block - 1) - base + STEP - 1) // STEP
        sources = []
        for parts in (q_parts, do_parts):
            row, found = 0, []
            for part in parts:
                found.append((row // STEP, (row + part.shape[0]) // STEP, part))
                row += part.shape[0]
            sources.append(found)

        def copy(k, n, source, row):
            return pltpu.make_async_copy(
                source.at[pl.ds(row * STEP, STEP)],
                (q_ref, do_ref)[k].at[pl.ds(n * STEP, STEP)],
                sems.at[k, n],
            )

        def begin(n, carry):
            for k in range(2):
                for first, last, part in sources[k]:

                    @pl.when((n >= first) & (n < last))
                    def _():
                        copy(k, n, part, n - first).start()

            return carry

        def turn(n, carry):
            at = pl.ds(pl.multiple_of(n * STEP, STEP), STEP)
            for k, (rows, flipped) in enumerate(((q_ref, qt_ref), (do_ref, dot_ref))):
                copy(k, n, sources[k][0][2], 0).wait()
                turned = rows[at, :].T
                for h in range(heads):
                    flipped[h, :, at] = turned[h * HEAD_DIM : (h + 1) * HEAD_DIM]
            return carry

        lax.fori_loop(0, end, begin, 0)
        lax.fori_loop(0, end, turn, 0)

    u0 = base + i * tk
    lo = (u0 - base) // tq
    f0 = (u0 + tk - 1 - base + tq - 1) // tq
    e_first = doc_end(meta, ndocs, u0)
    e_last = doc_end(meta, ndocs, u0 + tk - 1)
    f1 = (e_first - base) // tq
    hi = (e_last - 1 - base) // tq + 1
    f0 = jnp.minimum(f0, hi)
    f1 = jnp.clip(f1, f0, hi)
    k, v = unpack_rows(own[...], heads)
    per_head(k, heads, kt)
    per_head(v, heads, vt)
    dk_acc[...] = jnp.zeros_like(dk_acc)
    dv_acc[...] = jnp.zeros_like(dv_acc)
    urow = u0 + lax.broadcasted_iota(jnp.int32, (8, tk), 1)
    erow = ends_vec(meta, ndocs, urow)[:1]
    urow = urow[:1]

    def body(j, masked):
        off = pl.multiple_of(j * tq, tq)
        at = pl.ds(off, tq)
        q = q_ref[at, :]
        do = do_ref[at, :]
        if masked:
            t = base + off + lax.broadcasted_iota(jnp.int32, (tq, tk), 0)
            vis = (t >= urow) & (t < erow)
        for h in range(heads):
            p = jnp.exp(dotf(q, kt[h]))
            if masked:
                p = jnp.where(vis, p, 0.0)
            ds = (p * dotf(do, vt[h])).astype(BF16)
            dv_acc[h] += dotf(dot_ref[h, :, at], p.astype(BF16))
            dk_acc[h] += dotf(qt_ref[h, :, at], ds)

    three(lo, f0, f1, hi, body)
    for acc, out in ((dk_acc, dk_ref), (dv_acc, dv_ref)):
        out[...] = acc[...].reshape(heads * HEAD_DIM, tk).T.astype(BF16)


def attention_dkv(meta, own, q_parts, do_parts, heads, tq, tk):
    block, width = q_parts[0].shape
    window = sum(part.shape[0] for part in q_parts)
    ndocs = meta.shape[0] - 1
    row = lambda w: pl.BlockSpec((tk, w), lambda i: (i, 0))
    return pl.pallas_call(
        functools.partial(dkv_kernel, heads, ndocs, tq, tk),
        grid=(block // tk,),
        in_specs=[SCALARS, row(own.shape[1]), [ANY] * len(q_parts), [ANY] * len(do_parts)],
        out_specs=[row(heads * HEAD_DIM)] * 2,
        out_shape=[jax.ShapeDtypeStruct((block, heads * HEAD_DIM), BF16)] * 2,
        scratch_shapes=[pltpu.VMEM((window, width), BF16)] * 2
        + [pltpu.VMEM((heads, HEAD_DIM, window), BF16)] * 2
        + [pltpu.VMEM((heads, width, tk), BF16)] * 2
        + [pltpu.VMEM((heads, HEAD_DIM, tk), F32)] * 2
        + [pltpu.SemaphoreType.DMA((2, window // STEP))],
        compiler_params=pltpu.CompilerParams(vmem_limit_bytes=56 << 20),
        cost_estimate=pl.CostEstimate(
            flops=60_000_000_000, bytes_accessed=12 << 20, transcendentals=20_000_000
        ),
        name="attn_dkv",
    )(meta, own, q_parts, do_parts)


def on_device(
    tokens, first_values, cotangent, w_query, w_key, w_value, w_out, w_up, w_down,
    gain_attn, gain_mlp, doc_lengths,
):
    width = tokens.shape[1]
    heads_of = lax.axis_size("head")
    nblk = lax.axis_size("blk")
    blk = lax.axis_index("blk")
    rows = tokens.shape[0]
    block = rows * heads_of
    heads = HEADS // heads_of
    cols = heads * HEAD_DIM
    part = width // nblk
    meta = jnp.concatenate([jnp.reshape(blk * block, (1,)).astype(jnp.int32), doc_lengths])

    up_cols = w_up.shape[1]
    early = nblk - 3 * nblk // 8
    normed, query, own, earlier, gathered, qk_all, v_all, attn_gain, mlp_gain = front(
        nblk, early, tokens, first_values, w_query, w_key, w_value, w_up, w_down.T, w_out,
        gain_attn.reshape(1, part), gain_mlp.reshape(1, part),
    )
    w_qk = qk_all.reshape(width, 2 * cols)
    w_v = v_all.reshape(2, width, w_value.shape[1])
    earlier = earlier.reshape(2 * block, 2 * cols)
    beside = [(h, (h + 2) % heads_of) for h in range(heads_of)]
    mine = lax.dynamic_index_in_dim(gathered, lax.axis_index("head"), 0, keepdims=False)[early:]
    late = lax.ppermute(mine, "head", beside)
    mixed_parts, query_wide = attention_fwd(
        meta, query, earlier, own, heads, rows, rows
    )
    late, mixed_parts = lax.optimization_barrier((late, mixed_parts))
    layer_output, grad_resid, grad_parts, gain_mlp_part, keep_a, give_a, keep_b, give_b, query_later = middle(
        nblk, tokens, mixed_parts, cotangent, mlp_gain, gathered, late, query_wide, up_cols
    )
    grad_wide = grad_parts.reshape(block, WIDTH)
    across = [(i, i + 1 - 2 * (i % 2)) for i in range(nblk)]
    got_a = lax.ppermute(give_a, "head", beside)
    got_b = lax.ppermute(give_b, "blk", across)

    grads_later = [grad_wide] + [
        lax.ppermute(grad_wide, "blk", [(i, i - d) for i in range(d, nblk)]) for d in (1, 2)
    ]
    queries_later = [query_wide, query_later.reshape(2 * block, WIDTH)]
    grad_query = attention_dq(
        meta, query_wide, grad_wide, earlier, own, heads, rows, rows
    )
    got_a, got_b, grad_query = lax.optimization_barrier((got_a, got_b, grad_query))
    keep_a, give_a, keep_b, give_b = pair_sum(keep_a, got_a, keep_b, got_b)
    got_a = lax.ppermute(give_a, "blk", across)
    got_b = lax.ppermute(give_b, "head", beside)
    keep_a, own = lax.optimization_barrier((keep_a, own))
    grad_key, grad_value = attention_dkv(
        meta, own, queries_later, grads_later, heads, rows, rows
    )
    outs = tail(
        nblk, grad_query, grad_key, grad_value, normed, w_qk, w_v, gain_mlp_part,
        keep_a, got_a, keep_b, got_b, tokens, grad_resid, attn_gain,
    )
    (
        layer_output, grad_tokens, final_query, final_key, final_value, grad_first, final_a, final_m,
        final_up, final_down, final_out,
    ) = settle([layer_output] + list(outs))
    return (
        layer_output,
        grad_tokens,
        grad_first,
        final_query,
        final_key,
        final_value,
        final_out,
        final_up,
        final_down.T,
        final_a.reshape(part),
        final_m.reshape(part),
    )


def solution(mesh):
    rows = P(("blk", "head"), None)
    specs = (P("blk", "head"),) * 3 + (P("head", "blk"), P("blk", "head"), P("head", "blk"))
    gains = (P("blk"), P("blk"))
    return jax.shard_map(
        on_device,
        mesh=mesh,
        in_specs=(rows,) * 3 + specs + gains + (P(),),
        out_specs=(rows,) * 3 + specs + gains,
        check_vma=False,
    )
```
